32 devices in a mesh: seq: 2 (over x), row: 4 (over y, core), col: 4 (over z).
Axes of the slice: x: 2, y: 2, z: 4, core: 2. Of those that a mesh axis runs over, the one named last changes fastest.
Arguments:
- inputs: bfloat16 [2, 8, 1024, 768], P(None, ('seq', 'row'), 'col'), may hold values from -6 to 6
- segment_ids: int32 [2, 8, 1024], P(None, ('seq', 'row')), may hold values from 0 to 7, never falling along the last dimension, each value on 1 to 512 neighbouring positions
- query_weight: bfloat16 [768, 768], P(('seq', 'row'), 'col'), may hold values from -0.21875 to 0.21875
- key_weight: bfloat16 [768, 768], P(('seq', 'row'), 'col'), may hold values from -0.21875 to 0.21875
- value_weight: bfloat16 [768, 768], P(('seq', 'row'), 'col'), may hold values from -0.21875 to 0.21875
- query_bias: bfloat16 [768], P('col'), may hold values from -1.25 to 1.25
- value_bias: bfloat16 [768], P('col'), may hold values from -1.25 to 1.25
- output_weight: bfloat16 [768, 768], P('col', ('seq', 'row')), may hold values from -0.875 to 0.875
- output_bias: bfloat16 [768], replicated, may hold values from -1.25 to 1.25
- first_gain: bfloat16 [768], replicated, may hold values from 0.5 to 1.5
- first_shift: bfloat16 [768], replicated, may hold values from -1.25 to 1.25
- hidden_weight: bfloat16 [768, 3072], P(('seq', 'row'), 'col'), may hold values from -0.21875 to 0.21875
- hidden_bias: bfloat16 [3072], P('col'), may hold values from -1.25 to 1.25
- down_weight: bfloat16 [3072, 768], P('col', ('seq', 'row')), may hold values from -0.109375 to 0.109375
- down_bias: bfloat16 [768], replicated, may hold values from -1.25 to 1.25
- second_gain: bfloat16 [768], replicated, may hold values from 0.5 to 1.5
- second_shift: bfloat16 [768], replicated, may hold values from -1.25 to 1.25
- cotangent: bfloat16 [2, 8, 1024, 768], P(None, ('seq', 'row'), 'col'), may hold values from -6 to 6
Outputs:
- outputs: bfloat16 [2, 8, 1024, 768], P(None, ('seq', 'row'), 'col')
- input_grad: float32 [2, 8, 1024, 768], P(None, ('seq', 'row'), 'col')
- grad_query_weight: float32 [768, 768], P(('seq', 'row'), 'col')
- grad_key_weight: float32 [768, 768], P(('seq', 'row'), 'col')
- grad_value_weight: float32 [768, 768], P(('seq', 'row'), 'col')
- grad_query_bias: float32 [768], P('col')
- grad_value_bias: float32 [768], P('col')
- grad_output_weight: float32 [768, 768], P('col', ('seq', 'row'))
- grad_output_bias: float32 [768], replicated
- grad_first_gain: float32 [768], replicated
- grad_first_shift: float32 [768], replicated
- grad_hidden_weight: float32 [768, 3072], P(('seq', 'row'), 'col')
- grad_hidden_bias: float32 [3072], P('col')
- grad_down_weight: float32 [3072, 768], P('col', ('seq', 'row'))
- grad_down_bias: float32 [768], replicated
- grad_second_gain: float32 [768], replicated
- grad_second_shift: float32 [768], replicated
The draws below stay inside these ranges and needn't reach their ends.
Inputs may be any that keep to these rules, and one draw needn't show every extreme that they name: `segment_ids`: in each sequence the document numbers never fall along the positions; a document holds at most 512 positions, and some document holds exactly that many.
All inputs are finite; a program needn't handle non-finite values.
Results may differ from the reference program's by a relative error of at most 0.014.
Values may be sent and summed in bfloat16 or wider, within the bound.
A program may use at most 128 MiB of HBM per device.

```python
import math
import jax
import jax.numpy as jnp
import numpy as np
from jax import lax

D = 768
HEADS = 12
HEAD_DIM = 64
FF = 3072
LEN = 1024
MICRO = 2
SEQS = 8
DOCS = 8
DOC_MOST = 512


def steps_of(stream_key, shape, shards, low, top_value):
    loudness = 1.0
    for dim, blocks in shards:
        draws = jax.random.uniform(jax.random.fold_in(jax.random.fold_in(stream_key, 6), dim), (blocks,), jnp.float32, low / len(shards), top_value / len(shards))
        loudness = loudness * jnp.repeat(jnp.exp(draws), shape[dim] // blocks).reshape((-1,) + (1,) * (len(shape) - 1 - dim))
    return loudness


def length_profile(number_of, total, bound, skew):
    loads = [(1 << 20) // math.isqrt(standing ** skew) + 1 for standing in range(2, number_of + 1)]
    surplus, given = total - bound - (number_of - 1), [1] * (number_of - 1)
    while surplus > 0:
        free = [i for i in range(number_of - 1) if given[i] < bound]
        whole, remaining = sum([loads[i] for i in free]), surplus
        for i in free:
            addition = min(bound - given[i], max(1, remaining * loads[i] // whole), surplus)
            given[i] = given[i] + addition
            surplus = surplus - addition
    return np.array([bound] + given)


def ragged_sizes(stream_key, count, total, most, slope):
    if count == 2:
        one = jax.random.randint(stream_key, (), max(1, total - most), min(most, total - 1) + 1)
        return jnp.stack([one, total - one])
    tallies = jnp.asarray(length_profile(count, total, most, slope), jnp.int32)
    twos = (count - 1) // 2
    giver, taker = tallies[1:1 + 2 * twos:2], tallies[2:2 + 2 * twos:2]
    slack = jnp.minimum(giver - 1, most - taker)
    shifted = jax.random.randint(jax.random.fold_in(stream_key, 1), (twos,), 0, 1 << 20) % (slack + 1)
    tallies = tallies.at[1:1 + 2 * twos:2].set(giver - shifted).at[2:2 + 2 * twos:2].set(taker + shifted)
    return tallies[jax.random.permutation(jax.random.fold_in(stream_key, 2), count)]


def gaussian(stream_key, dims, scale, reach, split=(), held_as=jnp.bfloat16):
    values = jax.random.normal(stream_key, dims, jnp.float32) * scale
    if len(split) > 0:
        values = steps_of(stream_key, dims, split, -0.22, 0.18) * values
    return jnp.clip(values, min=-reach, max=reach).astype(held_as)


def setup_inputs(seed: int = 0) -> dict:
    key_of = jax.random.split(jax.random.key(seed), 19)
    inputs = gaussian(key_of[0], (MICRO, SEQS, LEN, D), 1.0, 6.0, ((1, 8), (2, 4)))
    segment_ids = jax.vmap(lambda own: jnp.searchsorted(jnp.cumsum(ragged_sizes(own, DOCS, LEN, DOC_MOST, 2)), jnp.arange(LEN), side="right"))(jax.random.split(key_of[1], MICRO * SEQS)).reshape((MICRO, SEQS, LEN)).astype(jnp.int32)
    query_weight = gaussian(key_of[2], (D, D), D ** -0.5, 0.21875, ((0, 8), (1, 4)))
    key_weight = gaussian(key_of[3], (D, D), D ** -0.5, 0.21875, ((0, 8), (1, 4)))
    value_weight = gaussian(key_of[4], (D, D), D ** -0.5, 0.21875, ((0, 8), (1, 4)))
    query_bias = gaussian(key_of[5], (D,), 0.2, 1.25, ((0, 4),))
    value_bias = gaussian(key_of[6], (D,), 0.2, 1.25, ((0, 4),))
    output_weight = gaussian(key_of[7], (D, D), (D // 16) ** -0.5, 0.875, ((0, 4), (1, 8)))
    output_bias = gaussian(key_of[8], (D,), 0.2, 1.25)
    first_gain = jnp.clip(1.0 + 0.1 * jax.random.normal(key_of[9], (D,), jnp.float32), 0.5, 1.5).astype(jnp.bfloat16)
    first_shift = gaussian(key_of[10], (D,), 0.2, 1.25)
    hidden_weight = gaussian(key_of[11], (D, FF), D ** -0.5, 0.21875, ((0, 8), (1, 4)))
    hidden_bias = gaussian(key_of[12], (FF,), 0.2, 1.25, ((0, 4),))
    down_weight = gaussian(key_of[13], (FF, D), FF ** -0.5, 0.109375, ((0, 4), (1, 8)))
    down_bias = gaussian(key_of[14], (D,), 0.2, 1.25)
    second_gain = jnp.clip(1.0 + 0.1 * jax.random.normal(key_of[15], (D,), jnp.float32), 0.5, 1.5).astype(jnp.bfloat16)
    second_shift = gaussian(key_of[16], (D,), 0.2, 1.25)
    cotangent = gaussian(key_of[17], (MICRO, SEQS, LEN, D), 1.0, 6.0, ((1, 8), (2, 4)))
    return dict(inputs=inputs, segment_ids=segment_ids, query_weight=query_weight, key_weight=key_weight, value_weight=value_weight, query_bias=query_bias, value_bias=value_bias, output_weight=output_weight, output_bias=output_bias, first_gain=first_gain, first_shift=first_shift, hidden_weight=hidden_weight, hidden_bias=hidden_bias, down_weight=down_weight, down_bias=down_bias, second_gain=second_gain, second_shift=second_shift, cotangent=cotangent)


@jax.custom_vjp
def low(v):
    return lax.optimization_barrier(v.astype(jnp.bfloat16)).astype(jnp.float32)

@jax.custom_vjp
def low_back(v):
    return v

def low_keep(v):
    return (low(v), None)

def low_pass(kept, grad):
    return (grad,)

def back_keep(v):
    return (v, None)

def back_low(kept, grad):
    return (low(grad),)
low.defvjp(low_keep, low_pass)
low_back.defvjp(back_keep, back_low)
PRECISE = lax.Precision.HIGHEST
NORM_EPS = 1e-05
MASK_VALUE = -1000000000.0

def matmul(left, right):
    return jnp.dot(left, right, precision=PRECISE, preferred_element_type=jnp.float32)

def layer_norm(summed, gain, shift):
    center = lax.optimization_barrier(jnp.mean(summed, -1, keepdims=True))
    deviation = summed - center
    variance = lax.optimization_barrier(jnp.mean(deviation * deviation, -1, keepdims=True))
    return deviation * lax.rsqrt(variance + NORM_EPS) * gain + shift

def make_layer(segment_row):

    def layer(inputs, query_weight, key_weight, value_weight, query_bias, value_bias, output_weight, output_bias, first_gain, first_shift, hidden_weight, hidden_bias, down_weight, down_bias, second_gain, second_shift):
        length = inputs.shape[0]
        queries = low_back(low(matmul(inputs, query_weight) + query_bias)).reshape(length, HEADS, HEAD_DIM)
        keys_all = low_back(low(matmul(inputs, key_weight))).reshape(length, HEADS, HEAD_DIM)
        values_all = low_back(low(matmul(inputs, value_weight) + value_bias)).reshape(length, HEADS, HEAD_DIM)
        block_rows = min(512, length)
        block_count = length // block_rows

        def attend(block_pair):
            query_block, segment_block = block_pair
            scores = low_back(jnp.einsum('qhd,khd->hqk', query_block, keys_all, precision=PRECISE))
            same_doc = segment_block[:, None] == segment_row[None, :]
            logits = jnp.where(same_doc[None], scores * HEAD_DIM ** (-0.5), MASK_VALUE)
            attn_probs = low(jax.nn.softmax(logits, axis=-1))
            return jnp.einsum('hqk,khd->qhd', attn_probs, values_all, precision=PRECISE)
        mixed = lax.map(jax.checkpoint(attend), (queries.reshape(block_count, block_rows, HEADS, HEAD_DIM), segment_row.reshape(block_count, block_rows)))
        mixed = low_back(low(mixed.reshape(length, HEADS * HEAD_DIM)))
        branch = low_back(matmul(mixed, output_weight))
        first_sum = inputs + branch + output_bias
        normed = layer_norm(first_sum, first_gain, first_shift)
        hidden_pre = low_back(matmul(low(normed), hidden_weight) + hidden_bias)
        activated = low(jax.nn.gelu(hidden_pre, approximate=False))
        feed_out = low_back(matmul(activated, down_weight))
        second_sum = normed + feed_out + down_bias
        return layer_norm(second_sum, second_gain, second_shift)
    return layer

def reference(inputs, segment_ids, query_weight, key_weight, value_weight, query_bias, value_bias, output_weight, output_bias, first_gain, first_shift, hidden_weight, hidden_bias, down_weight, down_bias, second_gain, second_shift, cotangent):
    params = tuple((weight.astype(jnp.float32) for weight in (query_weight, key_weight, value_weight, query_bias, value_bias, output_weight, output_bias, first_gain, first_shift, hidden_weight, hidden_bias, down_weight, down_bias, second_gain, second_shift)))
    flat_inputs = inputs.reshape(MICRO * SEQS, LEN, D).astype(jnp.float32)
    flat_cotangent = cotangent.reshape(MICRO * SEQS, LEN, D).astype(jnp.float32)
    flat_segments = segment_ids.reshape(MICRO * SEQS, LEN).astype(jnp.int32)
    zero_grads = tuple((jnp.zeros(weight.shape, jnp.float32) for weight in params))

    def one_sequence(running, sequence_item):
        seq_inputs, seq_segments, seq_cotangent = sequence_item
        layer = make_layer(seq_segments)
        result, pullback = jax.vjp(layer, seq_inputs, *params)
        gradients = pullback(seq_cotangent)
        updated = tuple((left + right for left, right in zip(running, gradients[1:])))
        return (updated, (result.astype(jnp.bfloat16), gradients[0]))
    totals, (results, input_grads) = lax.scan(one_sequence, zero_grads, (flat_inputs, flat_segments, flat_cotangent))
    return (results.reshape(MICRO, SEQS, LEN, D), input_grads.reshape(MICRO, SEQS, LEN, D), totals[0], totals[1], totals[2], totals[3], totals[4], totals[5], totals[6], totals[7], totals[8], totals[9], totals[10], totals[11], totals[12], totals[13], totals[14])
```

```python
import functools

import jax
import jax.numpy as jnp
from jax import lax
from jax.experimental import pallas as pl
from jax.experimental.pallas import tpu as pltpu
from jax.sharding import PartitionSpec as P

HEAD_DIM = 64
NORM_EPS = 1e-05
MASK_VALUE = -1000000000.0
DOC_MOST = 512
KEY_BLOCK = 256
MESH = pl.DeviceIdType.MESH


def contract_rows(left, right):
    return lax.dot_general(
        left, right, (((0,), (0,)), ((), ())), preferred_element_type=jnp.float32
    )


def contract_cols(left, right):
    return lax.dot_general(
        left, right, (((1,), (1,)), ((), ())), preferred_element_type=jnp.float32
    )


def norm_parts(summed):
    deviation = summed - jnp.mean(summed, -1, keepdims=True)
    scale = lax.rsqrt(jnp.mean(deviation * deviation, -1, keepdims=True) + NORM_EPS)
    return deviation * scale, scale


def norm_back(pull, normal, scale):
    return scale * (
        pull - jnp.mean(pull, -1, keepdims=True) - normal * jnp.mean(pull * normal, -1, keepdims=True)
    )


def attend_kernel(bounds, own_ref, all_ref, wq_ref, wk_ref, wkt_ref, wv_ref, wvt_ref, bq_ref, bv_ref, bvt_ref,
                  segq_ref, segk_ref, mixed_ref, lse_ref, q_ref, k_ref, kt_ref, v_ref, bias, acc, top, total):
    micro = pl.program_id(0)
    low, high = bounds[micro, 0], bounds[micro, 1]
    floats, halves = jnp.float32, jnp.bfloat16
    width = wq_ref.shape[-1]
    heads = width // HEAD_DIM
    rows = own_ref.shape[1]

    @pl.when(pl.program_id(1) == 0)
    def _():
        same = segk_ref[0] == segq_ref[0, 0:1]
        bias[...] = jnp.where(same, 0.0, MASK_VALUE)

    queries = jnp.dot(own_ref[0], wq_ref[0], preferred_element_type=floats) + bq_ref[0]
    queries = queries.astype(halves) * jnp.asarray(HEAD_DIM ** -0.5, halves)
    q_ref[0, 0] = queries
    lane = lax.broadcasted_iota(jnp.int32, (rows, width), 1) // HEAD_DIM
    query_heads = [jnp.where(lane == h, queries, jnp.zeros_like(queries)) for h in range(heads)]
    acc[...] = jnp.zeros_like(acc)
    total[...] = jnp.zeros_like(total)
    top[...] = jnp.full_like(top, 2 * MASK_VALUE)

    def step(block, carry):
        at = pl.ds(pl.multiple_of(block * KEY_BLOCK, KEY_BLOCK), KEY_BLOCK)
        x = all_ref[0, at, :]
        keys = jnp.dot(x, wk_ref[0], preferred_element_type=floats).astype(halves)
        k_ref[0, 0, at, :] = keys
        kt_ref[0, 0, :, at] = contract_cols(wkt_ref[0], x).astype(halves)
        v_ref[0, 0, at, :] = (jnp.dot(x, wv_ref[0], preferred_element_type=floats) + bv_ref[0]).astype(halves)
        values_t = (contract_cols(wvt_ref[0], x) + bvt_ref[0]).astype(halves)
        mask = bias[at, :]
        for h in range(heads):
            s = contract_cols(keys, query_heads[h]) + mask
            old = top[h : h + 1]
            new = jnp.maximum(old, jnp.max(s, 0, keepdims=True))
            p = jnp.exp(s - new)
            shrink = jnp.exp(old - new)
            top[h : h + 1] = new
            total[h : h + 1] = total[h : h + 1] * shrink + jnp.sum(p, 0, keepdims=True)
            part = pl.ds(h * HEAD_DIM, HEAD_DIM)
            acc[part, :] = acc[part, :] * shrink + jnp.dot(
                values_t[h * HEAD_DIM : (h + 1) * HEAD_DIM], p.astype(halves), preferred_element_type=floats
            )
        return carry

    lax.fori_loop(low, high, step, 0)
    for h in range(heads):
        part = pl.ds(h * HEAD_DIM, HEAD_DIM)
        acc[part, :] = acc[part, :] / total[h : h + 1]
    mixed_ref[0, 0] = acc[...].T.astype(halves)
    lse_ref[0, 0] = top[...] + jnp.log(jnp.maximum(total[...], 1e-30))


def attend(bounds, own, everything, wq, wk, wv, bq, bv, seg_own, seg_all):
    micro, rows, model = own.shape
    length = everything.shape[1]
    cols, _, width = wq.shape
    halves = jnp.bfloat16
    weight = pl.BlockSpec((1, model, width), lambda m, c, b: (c, 0, 0))
    weight_t = pl.BlockSpec((1, width, model), lambda m, c, b: (c, 0, 0))
    per = lambda a, b_: pl.BlockSpec((1, 1, a, b_), lambda m, c, b: (c, m, 0, 0))
    spec = pltpu.PrefetchScalarGridSpec(
        num_scalar_prefetch=1,
        grid=(micro, cols),
        in_specs=[
            pl.BlockSpec((1, rows, model), lambda m, c, b: (m, 0, 0)),
            pl.BlockSpec((1, length, model), lambda m, c, b: (m, 0, 0)),
            weight, weight, weight_t, weight, weight_t,
            pl.BlockSpec((1, 1, width), lambda m, c, b: (c, 0, 0)),
            pl.BlockSpec((1, 1, width), lambda m, c, b: (c, 0, 0)),
            pl.BlockSpec((1, width, 1), lambda m, c, b: (c, 0, 0)),
            pl.BlockSpec((1, 1, rows), lambda m, c, b: (m, 0, 0)),
            pl.BlockSpec((1, length, 1), lambda m, c, b: (m, 0, 0)),
        ],
        out_specs=[per(rows, width), per(8, rows), per(rows, width), per(length, width), per(width, length), per(length, width)],
        scratch_shapes=[
            pltpu.VMEM((length, rows), jnp.float32),
            pltpu.VMEM((width, rows), jnp.float32),
            pltpu.VMEM((8, rows), jnp.float32),
            pltpu.VMEM((8, rows), jnp.float32),
        ],
    )
    shape = lambda a, b_, d=halves: jax.ShapeDtypeStruct((cols, micro, a, b_), d)
    return pl.pallas_call(
        attend_kernel,
        grid_spec=spec,
        out_shape=[shape(rows, width), shape(8, rows, jnp.float32), shape(rows, width), shape(length, width), shape(width, length), shape(length, width)],
        compiler_params=pltpu.CompilerParams(vmem_limit_bytes=48 << 20),
        name="attend",
    )(bounds, own, everything, wq, wk, wk.swapaxes(1, 2), wv, wv.swapaxes(1, 2), bq[:, None], bv[:, None], bv[:, :, None],
      seg_own[:, None], seg_all[:, :, None])


def attend_back_kernel(bounds, grad_ref, wot_ref, mixed_ref, lse_ref, q_ref, k_ref, kt_ref, v_ref, segq_ref, segk_ref,
                       dq_ref, dk_ref, dv_ref, bias, acc):
    micro = pl.program_id(0)
    low, high = bounds[micro, 0], bounds[micro, 1]
    floats, halves = jnp.float32, jnp.bfloat16
    rows, width = q_ref.shape[2:]
    heads = width // HEAD_DIM

    @pl.when(pl.program_id(1) == 0)
    def _():
        same = segk_ref[0] == segq_ref[0, 0:1]
        bias[...] = jnp.where(same, 0.0, MASK_VALUE)

    mixed_grad = jnp.dot(grad_ref[0], wot_ref[0], preferred_element_type=floats).astype(halves)
    product = mixed_grad.astype(floats) * mixed_ref[0, 0].astype(floats)
    product_high = product.astype(halves)
    product_low = (product - product_high.astype(floats)).astype(halves)
    pick = (
        lax.broadcasted_iota(jnp.int32, (8, width), 1) // HEAD_DIM == lax.broadcasted_iota(jnp.int32, (8, width), 0)
    ).astype(halves)
    inner = contract_cols(pick, product_high) + contract_cols(pick, product_low)
    lane = lax.broadcasted_iota(jnp.int32, (rows, width), 1) // HEAD_DIM
    queries = q_ref[0, 0]
    query_heads = [jnp.where(lane == h, queries, jnp.zeros_like(queries)) for h in range(heads)]
    grad_heads = [jnp.where(lane == h, mixed_grad, jnp.zeros_like(mixed_grad)) for h in range(heads)]
    acc[...] = jnp.zeros_like(acc)
    dk_ref[...] = jnp.zeros_like(dk_ref)
    dv_ref[...] = jnp.zeros_like(dv_ref)

    def step(block, carry):
        at = pl.ds(pl.multiple_of(block * KEY_BLOCK, KEY_BLOCK), KEY_BLOCK)
        keys = k_ref[0, 0, at, :]
        values = v_ref[0, 0, at, :]
        mask = bias[at, :]
        key_grad = jnp.zeros((KEY_BLOCK, width), floats)
        value_grad = jnp.zeros((KEY_BLOCK, width), floats)
        for h in range(heads):
            s = contract_cols(keys, query_heads[h]) + mask
            p = jnp.exp(s - lse_ref[0, 0, h : h + 1])
            prob_grad = contract_cols(values, grad_heads[h])
            score_grad = (p * (prob_grad - inner[h : h + 1])).astype(halves)
            value_grad = value_grad + jnp.dot(p.astype(halves), grad_heads[h], preferred_element_type=floats)
            key_grad = key_grad + jnp.dot(score_grad, query_heads[h], preferred_element_type=floats)
            part = pl.ds(h * HEAD_DIM, HEAD_DIM)
            acc[part, :] += jnp.dot(kt_ref[0, 0, part, at], score_grad, preferred_element_type=floats)
        dk_ref[0, 0, at, :] = key_grad.astype(halves)
        dv_ref[0, 0, at, :] = value_grad.astype(halves)
        return carry

    lax.fori_loop(low, high, step, 0)
    dq_ref[0, 0] = (acc[...].T * HEAD_DIM ** -0.5).astype(halves)


def attend_back(bounds, grad, wot, mixed, lse, q, k, kt, v, seg_own, seg_all):
    micro, rows, model = grad.shape
    cols, _, length, width = k.shape
    halves = jnp.bfloat16
    per = lambda a, b_: pl.BlockSpec((1, 1, a, b_), lambda m, c, b: (c, m, 0, 0))
    spec = pltpu.PrefetchScalarGridSpec(
        num_scalar_prefetch=1,
        grid=(micro, cols),
        in_specs=[
            pl.BlockSpec((1, rows, model), lambda m, c, b: (m, 0, 0)),
            pl.BlockSpec((1, model, width), lambda m, c, b: (c, 0, 0)),
            per(rows, width), per(8, rows), per(rows, width), per(length, width), per(width, length), per(length, width),
            pl.BlockSpec((1, 1, rows), lambda m, c, b: (m, 0, 0)),
            pl.BlockSpec((1, length, 1), lambda m, c, b: (m, 0, 0)),
        ],
        out_specs=[per(rows, width), per(length, width), per(length, width)],
        scratch_shapes=[pltpu.VMEM((length, rows), jnp.float32), pltpu.VMEM((width, rows), jnp.float32)],
    )
    shape = lambda a, b_, d=halves: jax.ShapeDtypeStruct((cols, micro, a, b_), d)
    return pl.pallas_call(
        attend_back_kernel,
        grid_spec=spec,
        out_shape=[shape(rows, width), shape(length, width), shape(length, width)],
        compiler_params=pltpu.CompilerParams(vmem_limit_bytes=48 << 20),
        name="attend_back",
    )(bounds, grad, wot, mixed, lse, q, k, kt, v, seg_own[:, None], seg_all[:, :, None])


def place(sizes):
    seq, row, col = (lax.axis_index(name) for name in ("seq", "row", "col"))
    lines = {"x": (seq, sizes[0]), "y": (row // 2, sizes[1] // 2), "k": (lax.rem(row, 2), 2), "z": (col, sizes[2])}

    def device(axis, index):
        if axis == "x":
            return (index, row, col)
        if axis == "y":
            return (seq, index * 2 + lax.rem(row, 2), col)
        if axis == "k":
            return (seq, row // 2 * 2 + index, col)
        return (seq, row, index)

    return lines, device


def greet(lines, device):
    barrier = pltpu.get_barrier_semaphore()
    count = 0
    for axis, (mine, size) in lines.items():
        for t in range(1, size):
            pl.semaphore_signal(barrier, inc=1, device_id=device(axis, lax.rem(mine + t, size)), device_id_type=MESH)
            count += 1
    pl.semaphore_wait(barrier, count)


class Post:
    def __init__(self, device, send_sems, recv_sems):
        self.device, self.send_sems, self.recv_sems = device, send_sems, recv_sems
        self.slots, self.sent = {}, []

    def slot(self, key):
        return self.slots.setdefault(key, len(self.slots))

    def copy(self, key, axis, index, source, target):
        n = self.slot(key)
        return pltpu.make_async_remote_copy(
            src_ref=source, dst_ref=target, send_sem=self.send_sems.at[n], recv_sem=self.recv_sems.at[n],
            device_id=self.device(axis, index), device_id_type=MESH,
        )

    def send(self, key, axis, index, source, target, when=None):
        def go():
            self.copy(key, axis, index, source, target).start()

        if when is None:
            go()
        else:
            pl.when(when)(go)
        self.sent.append((key, axis, index, source, target, when))

    def wait(self, key, axis, index, target, when=None):
        def go():
            self.copy(key, axis, index, target, target).wait_recv()

        if when is None:
            go()
        else:
            pl.when(when)(go)

    def close(self):
        for key, axis, index, source, target, when in self.sent:
            def go():
                self.copy(key, axis, index, source, target).wait_send()

            if when is None:
                go()
            else:
                pl.when(when)(go)


def clip(index, size):
    return jnp.clip(index, 0, size - 1)


class LineGather:
    def __init__(self, post, name, axis, line, region, reach=None):
        self.post, self.name, self.axis, self.region = post, name, axis, region
        self.mine, self.size = line
        self.reach = min(self.size - 1, reach or self.size)

    def hop(self, way, t):
        mine, size = self.mine, self.size
        origin, target = mine - way * t, mine + way
        ok = (origin >= 0) & (origin < size) & (target >= 0) & (target < size)
        here = self.region(clip(origin, size))
        self.post.send((self.name, way, t + 1), self.axis, clip(target, size), here, here, ok)

    def start(self):
        for way in (1, -1):
            if self.reach >= 1:
                self.hop(way, 0)

    def finish(self):
        for t in range(1, self.reach + 1):
            for way in (1, -1):
                origin = self.mine - way * t
                ok = (origin >= 0) & (origin < self.size)
                self.post.wait((self.name, way, t), self.axis, clip(self.mine - way, self.size), self.region(clip(origin, self.size)), ok)
                if t < self.reach:
                    self.hop(way, t)


def gather_kernel(sizes, micro, own_ref, shard_ref, every_ref, full_ref, send_sems, recv_sems, local_sems):
    lines, device = place(sizes)
    (x, _), (y, _), (k, _), (z, cols) = (lines[a] for a in "xykz")
    half = shard_ref.shape[-1] // 2
    rows = own_ref.shape[1]
    reach = -(-(DOC_MOST - 1) // rows)
    parts = [pl.ds(p * half, half) for p in (0, 1)]
    local = [pltpu.make_async_copy(shard_ref.at[j], full_ref.at[j, z, x, y, k], local_sems.at[j]) for j in range(3)]
    local += [pltpu.make_async_copy(own_ref.at[m], every_ref.at[m, z], local_sems.at[3 + m]) for m in range(micro)]
    for copy in local:
        copy.start()
    greet(lines, device)
    post = Post(device, send_sems, recv_sems)
    for copy in local:
        copy.wait()
    zs = [LineGather(post, ("z", j), "z", lines["z"], lambda i, j=j: full_ref.at[j, i, x, y, k]) for j in range(3)]
    tokens = [LineGather(post, ("t", m), "z", lines["z"], lambda i, m=m: every_ref.at[m, i], reach) for m in range(micro)]
    second, third = {}, {}
    for j in range(3):
        second[j] = [
            LineGather(post, ("a", j), "y", lines["y"], lambda i, j=j: full_ref.at[j, :, x, i, k, :, parts[0]]),
            LineGather(post, ("b", j), "x", lines["x"], lambda i, j=j: full_ref.at[j, :, i, y, k, :, parts[1]]),
        ]
        third[j] = [
            LineGather(post, ("c", j), "x", lines["x"], lambda i, j=j: full_ref.at[j, :, i, :, k, :, parts[0]]),
            LineGather(post, ("d", j), "y", lines["y"], lambda i, j=j: full_ref.at[j, :, :, i, k, :, parts[1]]),
        ]

    def start(group):
        for line in group:
            line.start()

    def finish(group):
        for line in group:
            line.finish()

    def swap(j):
        plane = full_ref.at[j, :, :, :, k]
        post.send(("k", j), "k", 1 - k, plane, plane)

    start(zs + tokens)
    finish(zs[:1])
    start(second[0])
    finish(zs[1:2])
    finish(second[0])
    start(third[0] + second[1])
    finish(zs[2:])
    finish(tokens)
    finish(second[1])
    start(third[1] + second[2])
    finish(third[0])
    swap(0)
    finish(second[2])
    start(third[2])
    finish(third[1])
    swap(1)
    finish(third[2])
    swap(2)
    for i in range(cols):
        far = (z - i > reach) | (i - z > reach)
        for m in range(micro):
            def fill(m=m, i=i):
                copy = pltpu.make_async_copy(own_ref.at[m], every_ref.at[m, i], local_sems.at[3 + m])
                copy.start()
                copy.wait()

            if i > reach or cols - 1 - i > reach:
                pl.when(far)(fill)
    for j in range(3):
        post.wait(("k", j), "k", 1 - k, full_ref.at[j, :, :, :, 1 - k])
    post.close()


def gather(sizes, own, shard):
    ns, nr, nc = sizes
    ny = nr // 2
    micro, rows, model = own.shape
    _, rb, w = shard.shape
    count = 3 * 2 * (nc - 1) + micro * 2 * (nc - 1) + 3 * (4 * (ny - 1) + 4 * (ns - 1) + 1)
    anywhere = pl.BlockSpec(memory_space=pl.ANY)
    every, full = pl.pallas_call(
        functools.partial(gather_kernel, sizes, micro),
        out_shape=[
            jax.ShapeDtypeStruct((micro, nc, rows, model), own.dtype),
            jax.ShapeDtypeStruct((3, nc, ns, ny, 2, rb, w), shard.dtype),
        ],
        in_specs=[anywhere] * 2,
        out_specs=[anywhere] * 2,
        scratch_shapes=[pltpu.SemaphoreType.DMA((count,)), pltpu.SemaphoreType.DMA((count,)), pltpu.SemaphoreType.DMA((3 + micro,))],
        compiler_params=pltpu.CompilerParams(collective_id=0, has_side_effects=True),
        name="gather",
    )(own, shard)
    return every, full.reshape(3, nc, ns * nr * rb, w)


class LineReduce:
    def __init__(self, post, name, axis, line, region, inbox, add, reach=None):
        self.post, self.name, self.axis, self.region, self.inbox, self.add = post, name, axis, region, inbox, add
        self.mine, self.size = line
        self.reach = min(self.size - 1, reach or self.size)

    def arrived(self, way, e):
        behind, goal = self.mine - way, self.mine + way * e
        return (behind >= 0) & (behind < self.size) & (goal >= 0) & (goal < self.size)

    def take(self, way, e):
        ok = self.arrived(way, e)
        inbox = self.inbox(way, e)
        self.post.wait((self.name, way, e), self.axis, clip(self.mine - way, self.size), inbox, ok)

        @pl.when(ok)
        def _():
            self.add(self.region(clip(self.mine + way * e, self.size)), inbox)

    def forward(self, way, e):
        goal = self.mine + way * e
        ok = (goal >= 0) & (goal < self.size)
        self.post.send((self.name, way, e - 1), self.axis, clip(self.mine + way, self.size),
                       self.region(clip(goal, self.size)), self.inbox(way, e - 1), ok)

    def start(self):
        for way in (1, -1):
            if self.reach >= 1:
                self.forward(way, self.reach)

    def finish(self, last=True):
        for e in range(self.reach - 1, 0, -1):
            for way in (1, -1):
                self.take(way, e)
                self.forward(way, e)
        if last:
            for way in (1, -1):
                if self.reach >= 1:
                    self.take(way, 0)


def reduce_kernel(sizes, micro, own_ref, spread_ref, part_ref, vec_ref, back_ref, block_ref, sums_ref,
                  mine_buf, core_buf, in_a, in_b, in_c, in_d, in_z, tok_buf, tok_in, vec_buf, send_sems, recv_sems, local_sems):
    floats, halves = jnp.float32, jnp.bfloat16
    lines, device = place(sizes)
    (x, ns), (y, ny), (k, _), (z, nc) = (lines[a] for a in "xykz")
    half = part_ref.shape[-1] // 2
    rows = own_ref.shape[1]
    reach = -(-(DOC_MOST - 1) // rows)
    parts = [pl.ds(p * half, half) for p in (0, 1)]
    local = [pltpu.make_async_copy(part_ref.at[j, :, :, :, k], mine_buf.at[j], local_sems.at[j]) for j in range(3)]
    local += [pltpu.make_async_copy(spread_ref.at[m], tok_buf.at[m], local_sems.at[3 + m]) for m in range(micro)]
    for copy in local:
        copy.start()
    greet(lines, device)
    post = Post(device, send_sems, recv_sems)
    for j in range(3):
        post.send(("k", j), "k", 1 - k, part_ref.at[j, :, :, :, 1 - k], core_buf.at[j])

    def plus(target, source):
        target[...] = (target[...].astype(floats) + source[...].astype(floats)).astype(halves)

    def plus_grid(target, source, first, second):
        @pl.loop(0, first * second)
        def _(n):
            plus(target.at[n // second, lax.rem(n, second)], source.at[n // second, lax.rem(n, second)])

    def plus_row(target, source, first):
        @pl.loop(0, first)
        def _(n):
            plus(target.at[n], source.at[n])

    vec_buf[0, 0] = vec_ref[...]

    def vector_start(stage, axis):
        mine, size = lines[axis]
        vec_buf[stage, 1 + mine] = vec_buf[stage, 0]
        for t in range(1, size):
            post.send(("v", stage, t), axis, lax.rem(mine + t, size), vec_buf.at[stage, 0], vec_buf.at[stage, 1 + mine])

    def vector_finish(stage, axis, out):
        mine, size = lines[axis]
        for t in range(1, size):
            origin = lax.rem(mine + size - t, size)
            post.wait(("v", stage, t), axis, origin, vec_buf.at[stage, 1 + origin])
        total = vec_buf[stage, 1]
        for i in range(1, size):
            total = total + vec_buf[stage, 1 + i]
        out[...] = total

    tokens = [
        LineReduce(post, ("t", m), "z", lines["z"], lambda i, m=m: tok_buf.at[m, i],
                   lambda way, e, m=m: tok_in.at[m, (1 - way) // 2, e], plus, reach)
        for m in range(micro)
    ]
    box = lambda way: (1 - way) // 2
    second, third, last = {}, {}, {}
    for j in range(3):
        second[j] = [
            LineReduce(post, ("a", j), "x", lines["x"], lambda i, j=j: mine_buf.at[j, :, i, :, :, parts[0]],
                       lambda way, e, j=j: in_a.at[j, box(way), e], lambda t, s: plus_grid(t, s, nc, ny)),
            LineReduce(post, ("b", j), "y", lines["y"], lambda i, j=j: mine_buf.at[j, :, :, i, :, parts[1]],
                       lambda way, e, j=j: in_b.at[j, box(way), e], lambda t, s: plus_grid(t, s, nc, ns)),
        ]
        third[j] = [
            LineReduce(post, ("c", j), "y", lines["y"], lambda i, j=j: mine_buf.at[j, :, x, i, :, parts[0]],
                       lambda way, e, j=j: in_c.at[j, box(way), e], lambda t, s: plus_row(t, s, nc)),
            LineReduce(post, ("d", j), "x", lines["x"], lambda i, j=j: mine_buf.at[j, :, i, y, :, parts[1]],
                       lambda way, e, j=j: in_d.at[j, box(way), e], lambda t, s: plus_row(t, s, nc)),
        ]
        last[j] = [
            LineReduce(post, ("z", j), "z", lines["z"], lambda i, j=j: mine_buf.at[j, i, x, y],
                       lambda way, e, j=j: in_z.at[j, box(way), e], plus)
        ]

    def start(group):
        for line in group:
            line.start()

    def finish(group):
        for line in group:
            line.finish()

    def core(j):
        local[j].wait()
        post.wait(("k", j), "k", 1 - k, core_buf.at[j])

        @pl.loop(0, nc * ns * ny)
        def _(n):
            at = (n // (ns * ny), lax.rem(n // ny, ns), lax.rem(n, ny))
            plus(mine_buf.at[(j, *at)], core_buf.at[(j, *at)])

    for m in range(micro):
        local[3 + m].wait()
    start(tokens)
    core(0)
    start(second[0])
    vector_start(0, "k")
    core(1)
    start(second[1])
    vector_finish(0, "k", vec_buf.at[1, 0])
    vector_start(1, "y")
    core(2)
    finish(second[0])
    start(third[0])
    start(second[2])
    vector_finish(1, "y", vec_buf.at[2, 0])
    vector_start(2, "x")
    finish(tokens)
    vector_finish(2, "x", vec_buf.at[3, 0])
    vector_start(3, "z")
    finish(second[1])
    start(third[1])
    finish(third[0])
    start(last[0])
    finish(second[2])
    start(third[2])
    finish(third[1])
    start(last[1])
    finish(last[0])
    finish(third[2])
    start(last[2])
    vector_finish(3, "z", sums_ref)
    for m in range(micro):
        back_ref[m] = own_ref[m] + tok_buf[m, z].astype(floats)
    finish(last[1])
    finish(last[2])
    for j in range(3):
        block_ref[j] = mine_buf[j, z, x, y].astype(floats)
    post.close()


def reduce(sizes, own_share, spread, partial, vectors):
    ns, nr, nc = sizes
    ny = nr // 2
    micro, rows, model = own_share.shape
    w = partial.shape[-1]
    rb = partial.shape[2] // (ns * nr)
    halves, floats = jnp.bfloat16, jnp.float32
    reach = min(nc - 1, -(-(DOC_MOST - 1) // rows))
    count = 3 + 2 * (ny - 1 + ns - 1) * 6 + 3 * 2 * (nc - 1) + micro * 2 * reach + (1 + ny - 1 + ns - 1 + nc - 1)
    widest = max(ns, ny, nc, 2)
    extra = -vectors.shape[0] % 8
    vectors = jnp.pad(vectors, ((0, extra), (0, 0)))
    vmem = pl.BlockSpec(memory_space=pltpu.VMEM)
    anywhere = pl.BlockSpec(memory_space=pl.ANY)
    back, blocks, sums = pl.pallas_call(
        functools.partial(reduce_kernel, sizes, micro),
        out_shape=[
            jax.ShapeDtypeStruct((micro, rows, model), floats),
            jax.ShapeDtypeStruct((3, rb, w), floats),
            jax.ShapeDtypeStruct(vectors.shape, floats),
        ],
        in_specs=[vmem, anywhere, anywhere, vmem],
        out_specs=[vmem] * 3,
        scratch_shapes=[
            pltpu.VMEM((3, nc, ns, ny, rb, w), halves),
            pltpu.VMEM((3, nc, ns, ny, rb, w), halves),
            pltpu.VMEM((3, 2, max(ns - 1, 1), nc, ny, rb, w // 2), halves),
            pltpu.VMEM((3, 2, max(ny - 1, 1), nc, ns, rb, w // 2), halves),
            pltpu.VMEM((3, 2, max(ny - 1, 1), nc, rb, w // 2), halves),
            pltpu.VMEM((3, 2, max(ns - 1, 1), nc, rb, w // 2), halves),
            pltpu.VMEM((3, 2, max(nc - 1, 1), rb, w), halves),
            pltpu.VMEM((micro, nc, rows, model), halves),
            pltpu.VMEM((micro, 2, max(reach, 1), rows, model), halves),
            pltpu.VMEM((4, 1 + widest, *vectors.shape), floats),
            pltpu.SemaphoreType.DMA((count,)),
            pltpu.SemaphoreType.DMA((count,)),
            pltpu.SemaphoreType.DMA((3 + micro,)),
        ],
        compiler_params=pltpu.CompilerParams(collective_id=1, has_side_effects=True, vmem_limit_bytes=60 << 20),
        name="reduce",
    )(own_share, spread, partial.reshape(3, nc, ns, ny, 2, rb, w), vectors)
    return back, blocks, sums


def per_device(sizes, inputs, segment_ids, query_weight, key_weight, value_weight, query_bias, value_bias,
               output_weight, output_bias, first_gain, first_shift, hidden_weight, hidden_bias, down_weight,
               down_bias, second_gain, second_shift, cotangent):
    floats, halves = jnp.float32, jnp.bfloat16
    cols = sizes[2]
    micro, _, rows, model = inputs.shape
    length = segment_ids.shape[-1]
    width = query_weight.shape[1]
    here = lax.axis_index("col")
    own = inputs[:, 0]
    shard = jnp.stack([
        jnp.concatenate([query_weight, key_weight, value_weight, output_weight.T], 1),
        hidden_weight,
        down_weight.T,
    ])
    biases = lax.all_gather(jnp.concatenate([query_bias, value_bias, hidden_bias]), "col", axis=0)
    everything, gathered = gather(sizes, own, shard)
    everything = everything.reshape(micro, length, model)
    attn_weights = gathered[0]
    wq, wk, wv, wot = (attn_weights[:, :, i * width : (i + 1) * width] for i in range(4))
    hidden_full, down_full = gathered[1], gathered[2]
    bq, bv, bh = biases[:, :width], biases[:, width : 2 * width], biases[:, 2 * width :]
    seg_all = segment_ids[:, 0]
    seg_own = lax.dynamic_slice_in_dim(seg_all, here * rows, rows, 1)
    first_key = jnp.sum((seg_all < seg_own[:, :1]).astype(jnp.int32), 1)
    last_key = jnp.sum((seg_all <= seg_own[:, -1:]).astype(jnp.int32), 1)
    bounds = jnp.stack([first_key // KEY_BLOCK, (last_key + KEY_BLOCK - 1) // KEY_BLOCK], 1)

    mixed, lse, q, k, kt, v = attend(bounds, own, everything, wq, wk, wv, bq.astype(floats), bv.astype(floats), seg_own, seg_all)
    total = micro * rows
    flat = lambda a: a.reshape(total, -1)
    mixed_flat = mixed.reshape(cols, total, width)
    attn = sum(contract_cols(mixed_flat[c], wot[c]) for c in range(cols))
    first_sum = flat(own).astype(floats) + attn + output_bias.astype(floats)
    normal_one, scale_one = norm_parts(first_sum)
    gain_one = first_gain.astype(floats)
    normed = normal_one * gain_one + first_shift.astype(floats)
    normed_low = normed.astype(halves)
    ffn = 0
    activated, slopes = [], []
    for c in range(cols):
        hidden = jnp.dot(normed_low, hidden_full[c], preferred_element_type=floats) + bh[c].astype(floats)
        half_erf = 0.5 * lax.erf(hidden * 0.7071067811865476) + 0.5
        act = (hidden * half_erf).astype(halves)
        slope = half_erf + hidden * (jnp.exp(-0.5 * hidden * hidden) * 0.3989422804014327)
        activated.append(act)
        slopes.append(slope.astype(halves))
        ffn = ffn + contract_cols(act, down_full[c])
    second_sum = normed + ffn + down_bias.astype(floats)
    normal_two, scale_two = norm_parts(second_sum)
    gain_two = second_gain.astype(floats)
    outputs = (normal_two * gain_two + second_shift.astype(floats)).astype(halves)
    cot = flat(cotangent[:, 0]).astype(floats)
    second_grad = norm_back(cot * gain_two, normal_two, scale_two)
    ffn_grad = second_grad.astype(halves)
    hidden_grads, down_grads, hidden_bias_grads = [], [], []
    normed_grad = second_grad
    for c in range(cols):
        pre = (jnp.dot(ffn_grad, down_full[c], preferred_element_type=floats) * slopes[c].astype(floats)).astype(halves)
        hidden_grads.append(contract_rows(normed_low, pre).astype(halves))
        down_grads.append(contract_rows(ffn_grad, activated[c]).astype(halves))
        hidden_bias_grads.append(jnp.sum(pre.astype(floats), 0))
        normed_grad = normed_grad + contract_cols(pre, hidden_full[c])
    first_grad = norm_back(normed_grad * gain_one, normal_one, scale_one)
    attn_grad = first_grad.astype(halves)
    dq, dk, dv = attend_back(bounds, attn_grad.reshape(micro, rows, model), wot, mixed, lse, q, k, kt, v, seg_own, seg_all)
    every_flat = everything.reshape(micro * length, model)
    attn_grads = []
    own_share = first_grad
    spread = 0
    for c in range(cols):
        dq_c, dk_c, dv_c = dq[c].reshape(total, width), dk[c].reshape(micro * length, width), dv[c].reshape(micro * length, width)
        attn_grads.append(jnp.concatenate([
            contract_rows(flat(own), dq_c), contract_rows(every_flat, dk_c), contract_rows(every_flat, dv_c),
            contract_rows(attn_grad, mixed_flat[c]),
        ], 1).astype(halves))
        own_share = own_share + contract_cols(dq_c, wq[c])
        spread = spread + contract_cols(dk_c, wk[c]) + contract_cols(dv_c, wv[c])
    bias_q = jnp.sum(dq.astype(floats), (1, 2)).reshape(-1)
    bias_v = jnp.sum(dv.astype(floats), (1, 2)).reshape(-1)
    vectors = jnp.concatenate([
        jnp.sum(first_grad, 0), jnp.sum(normed_grad * normal_one, 0), jnp.sum(normed_grad, 0), jnp.sum(second_grad, 0),
        jnp.sum(cot * normal_two, 0), jnp.sum(cot, 0), bias_q, bias_v, *hidden_bias_grads,
    ]).reshape(-1, model)
    partial = jnp.stack([jnp.stack(attn_grads), jnp.stack(hidden_grads), jnp.stack(down_grads)])
    input_grad, reduced, sums = reduce(sizes, own_share.reshape(micro, rows, model),
                                       spread.astype(halves).reshape(micro, cols, rows, model), partial, vectors)
    attn_block = reduced[0]
    piece = lambda i: attn_block[:, i * width : (i + 1) * width]
    mine = lambda vector, size: lax.dynamic_slice_in_dim(vector.reshape(-1), here * size, size, 0)
    return (
        outputs.reshape(micro, 1, rows, model), input_grad[:, None],
        piece(0), piece(1), piece(2), mine(sums[6], width), mine(sums[7], width), piece(3).T,
        sums[0], sums[1], sums[2], reduced[1], mine(sums[8:], hidden_bias.shape[0]), reduced[2].T,
        sums[3], sums[4], sums[5],
    )


def solution(mesh):
    sizes = tuple(mesh.shape[name] for name in ("seq", "row", "col"))
    block, line = P(("seq", "row"), "col"), P("col", ("seq", "row"))
    tokens = P(None, ("seq", "row"), "col", None)
    placed = (tokens, P(None, ("seq", "row"), None), block, block, block, P("col"), P("col"), line, P(), P(), P(),
              block, P("col"), line, P(), P(), P(), tokens)
    given = (tokens, tokens, block, block, block, P("col"), P("col"), line, P(), P(), P(), block, P("col"), line,
             P(), P(), P())
    return jax.shard_map(functools.partial(per_device, sizes), mesh=mesh, in_specs=placed, out_specs=given, check_vma=False)
```

```python
import functools

import jax
import jax.numpy as jnp
from jax import lax
from jax.experimental import pallas as pl
from jax.experimental.pallas import tpu as pltpu
from jax.sharding import PartitionSpec as P

HEAD_DIM = 64
NORM_EPS = 1e-05
MASK_VALUE = -1000000000.0
DOC_MOST = 512
KEY_BLOCK = 256
MESH = pl.DeviceIdType.MESH


def contract_rows(left, right):
    return lax.dot_general(
        left, right, (((0,), (0,)), ((), ())), preferred_element_type=jnp.float32
    )


def contract_cols(left, right):
    return lax.dot_general(
        left, right, (((1,), (1,)), ((), ())), preferred_element_type=jnp.float32
    )


def norm_parts(summed):
    deviation = summed - jnp.mean(summed, -1, keepdims=True)
    scale = lax.rsqrt(jnp.mean(deviation * deviation, -1, keepdims=True) + NORM_EPS)
    return deviation * scale, scale


def norm_back(pull, normal, scale):
    return scale * (
        pull - jnp.mean(pull, -1, keepdims=True) - normal * jnp.mean(pull * normal, -1, keepdims=True)
    )


def attend_kernel(bounds, own_ref, all_ref, wq_ref, wk_ref, wv_ref, bq_ref, bv_ref,
                  segq_ref, segk_ref, mixed_ref, lse_ref, q_ref, k_ref, v_ref, bias, acc, top, total):
    micro = pl.program_id(0)
    low, high = bounds[micro, 0], bounds[micro, 1]
    floats, halves = jnp.float32, jnp.bfloat16
    width = wq_ref.shape[-1]
    heads = width // HEAD_DIM
    rows = own_ref.shape[1]

    @pl.when(pl.program_id(1) == 0)
    def _():
        same = segk_ref[0] == segq_ref[0, 0:1]
        bias[...] = jnp.where(same, 0.0, MASK_VALUE)

    queries = jnp.dot(own_ref[0], wq_ref[0], preferred_element_type=floats) + bq_ref[0]
    queries = queries.astype(halves) * jnp.asarray(HEAD_DIM ** -0.5, halves)
    q_ref[0, 0] = queries
    lane = lax.broadcasted_iota(jnp.int32, (rows, width), 1) // HEAD_DIM
    query_heads = [jnp.where(lane == h, queries, jnp.zeros_like(queries)) for h in range(heads)]
    acc[...] = jnp.zeros_like(acc)
    total[...] = jnp.zeros_like(total)
    top[...] = jnp.full_like(top, 2 * MASK_VALUE)

    def step(block, carry):
        at = pl.ds(pl.multiple_of(block * KEY_BLOCK, KEY_BLOCK), KEY_BLOCK)
        x = all_ref[0, at, :]
        keys = jnp.dot(x, wk_ref[0], preferred_element_type=floats).astype(halves)
        k_ref[0, 0, at, :] = keys
        values = (jnp.dot(x, wv_ref[0], preferred_element_type=floats) + bv_ref[0]).astype(halves)
        v_ref[0, 0, at, :] = values
        values_t = values.T
        mask = bias[at, :]
        for h in range(heads):
            s = contract_cols(keys, query_heads[h]) + mask
            old = top[h : h + 1]
            new = jnp.maximum(old, jnp.max(s, 0, keepdims=True))
            p = jnp.exp(s - new)
            shrink = jnp.exp(old - new)
            top[h : h + 1] = new
            total[h : h + 1] = total[h : h + 1] * shrink + jnp.sum(p, 0, keepdims=True)
            part = pl.ds(h * HEAD_DIM, HEAD_DIM)
            acc[part, :] = acc[part, :] * shrink + jnp.dot(
                values_t[h * HEAD_DIM : (h + 1) * HEAD_DIM], p.astype(halves), preferred_element_type=floats
            )
        return carry

    lax.fori_loop(low, high, step, 0)
    for h in range(heads):
        part = pl.ds(h * HEAD_DIM, HEAD_DIM)
        acc[part, :] = acc[part, :] / total[h : h + 1]
    mixed_ref[0, 0] = acc[...].T.astype(halves)
    lse_ref[0, 0] = top[...] + jnp.log(jnp.maximum(total[...], 1e-30))


def attend(bounds, own, everything, wq, wk, wv, bq, bv, seg_own, seg_all):
    micro, rows, model = own.shape
    length = everything.shape[1]
    cols, _, width = wq.shape
    halves = jnp.bfloat16
    weight = pl.BlockSpec((1, model, width), lambda m, c, b: (c, 0, 0))
    per = lambda a, b_: pl.BlockSpec((1, 1, a, b_), lambda m, c, b: (c, m, 0, 0))
    spec = pltpu.PrefetchScalarGridSpec(
        num_scalar_prefetch=1,
        grid=(micro, cols),
        in_specs=[
            pl.BlockSpec((1, rows, model), lambda m, c, b: (m, 0, 0)),
            pl.BlockSpec((1, length, model), lambda m, c, b: (m, 0, 0)),
            weight, weight, weight,
            pl.BlockSpec((1, 1, width), lambda m, c, b: (c, 0, 0)),
            pl.BlockSpec((1, 1, width), lambda m, c, b: (c, 0, 0)),
            pl.BlockSpec((1, 1, rows), lambda m, c, b: (m, 0, 0)),
            pl.BlockSpec((1, length, 1), lambda m, c, b: (m, 0, 0)),
        ],
        out_specs=[per(rows, width), per(8, rows), per(rows, width), per(length, width), per(length, width)],
        scratch_shapes=[
            pltpu.VMEM((length, rows), jnp.float32),
            pltpu.VMEM((width, rows), jnp.float32),
            pltpu.VMEM((8, rows), jnp.float32),
            pltpu.VMEM((8, rows), jnp.float32),
        ],
    )
    shape = lambda a, b_, d=halves: jax.ShapeDtypeStruct((cols, micro, a, b_), d)
    return pl.pallas_call(
        attend_kernel,
        grid_spec=spec,
        out_shape=[shape(rows, width), shape(8, rows, jnp.float32), shape(rows, width), shape(length, width), shape(length, width)],
        compiler_params=pltpu.CompilerParams(vmem_limit_bytes=48 << 20),
        name="attend",
    )(bounds, own, everything, wq, wk, wv, bq[:, None], bv[:, None],
      seg_own[:, None], seg_all[:, :, None])


def attend_back_kernel(bounds, grad_ref, wot_ref, mixed_ref, lse_ref, q_ref, k_ref, v_ref, segq_ref, segk_ref,
                       dq_ref, dk_ref, dv_ref, bias, acc):
    micro = pl.program_id(0)
    low, high = bounds[micro, 0], bounds[micro, 1]
    floats, halves = jnp.float32, jnp.bfloat16
    rows, width = q_ref.shape[2:]
    heads = width // HEAD_DIM

    @pl.when(pl.program_id(1) == 0)
    def _():
        same = segk_ref[0] == segq_ref[0, 0:1]
        bias[...] = jnp.where(same, 0.0, MASK_VALUE)

    mixed_grad = jnp.dot(grad_ref[0], wot_ref[0], preferred_element_type=floats).astype(halves)
    product = mixed_grad.astype(floats) * mixed_ref[0, 0].astype(floats)
    product_high = product.astype(halves)
    product_low = (product - product_high.astype(floats)).astype(halves)
    pick = (
        lax.broadcasted_iota(jnp.int32, (8, width), 1) // HEAD_DIM == lax.broadcasted_iota(jnp.int32, (8, width), 0)
    ).astype(halves)
    inner = contract_cols(pick, product_high) + contract_cols(pick, product_low)
    lane = lax.broadcasted_iota(jnp.int32, (rows, width), 1) // HEAD_DIM
    queries = q_ref[0, 0]
    query_heads = [jnp.where(lane == h, queries, jnp.zeros_like(queries)) for h in range(heads)]
    grad_heads = [jnp.where(lane == h, mixed_grad, jnp.zeros_like(mixed_grad)) for h in range(heads)]
    acc[...] = jnp.zeros_like(acc)
    dk_ref[...] = jnp.zeros_like(dk_ref)
    dv_ref[...] = jnp.zeros_like(dv_ref)

    def step(block, carry):
        at = pl.ds(pl.multiple_of(block * KEY_BLOCK, KEY_BLOCK), KEY_BLOCK)
        keys = k_ref[0, 0, at, :]
        values = v_ref[0, 0, at, :]
        keys_t = keys.T
        mask = bias[at, :]
        key_grad = jnp.zeros((KEY_BLOCK, width), floats)
        value_grad = jnp.zeros((KEY_BLOCK, width), floats)
        for h in range(heads):
            s = contract_cols(keys, query_heads[h]) + mask
            p = jnp.exp(s - lse_ref[0, 0, h : h + 1])
            prob_grad = contract_cols(values, grad_heads[h])
            score_grad = (p * (prob_grad - inner[h : h + 1])).astype(halves)
            value_grad = value_grad + jnp.dot(p.astype(halves), grad_heads[h], preferred_element_type=floats)
            key_grad = key_grad + jnp.dot(score_grad, query_heads[h], preferred_element_type=floats)
            part = pl.ds(h * HEAD_DIM, HEAD_DIM)
            acc[part, :] += jnp.dot(keys_t[h * HEAD_DIM : (h + 1) * HEAD_DIM], score_grad, preferred_element_type=floats)
        dk_ref[0, 0, at, :] = key_grad.astype(halves)
        dv_ref[0, 0, at, :] = value_grad.astype(halves)
        return carry

    lax.fori_loop(low, high, step, 0)
    dq_ref[0, 0] = (acc[...].T * HEAD_DIM ** -0.5).astype(halves)


def attend_back(bounds, grad, wot, mixed, lse, q, k, v, seg_own, seg_all):
    micro, rows, model = grad.shape
    cols, _, length, width = k.shape
    halves = jnp.bfloat16
    per = lambda a, b_: pl.BlockSpec((1, 1, a, b_), lambda m, c, b: (c, m, 0, 0))
    spec = pltpu.PrefetchScalarGridSpec(
        num_scalar_prefetch=1,
        grid=(micro, cols),
        in_specs=[
            pl.BlockSpec((1, rows, model), lambda m, c, b: (m, 0, 0)),
            pl.BlockSpec((1, model, width), lambda m, c, b: (c, 0, 0)),
            per(rows, width), per(8, rows), per(rows, width), per(length, width), per(length, width),
            pl.BlockSpec((1, 1, rows), lambda m, c, b: (m, 0, 0)),
            pl.BlockSpec((1, length, 1), lambda m, c, b: (m, 0, 0)),
        ],
        out_specs=[per(rows, width), per(length, width), per(length, width)],
        scratch_shapes=[pltpu.VMEM((length, rows), jnp.float32), pltpu.VMEM((width, rows), jnp.float32)],
    )
    shape = lambda a, b_, d=halves: jax.ShapeDtypeStruct((cols, micro, a, b_), d)
    return pl.pallas_call(
        attend_back_kernel,
        grid_spec=spec,
        out_shape=[shape(rows, width), shape(length, width), shape(length, width)],
        compiler_params=pltpu.CompilerParams(vmem_limit_bytes=48 << 20),
        name="attend_back",
    )(bounds, grad, wot, mixed, lse, q, k, v, seg_own[:, None], seg_all[:, :, None])


def place(sizes):
    seq, row, col = (lax.axis_index(name) for name in ("seq", "row", "col"))
    lines = {"x": (seq, sizes[0]), "y": (row // 2, sizes[1] // 2), "k": (lax.rem(row, 2), 2), "z": (col, sizes[2])}

    def device(axis, index):
        if axis == "x":
            return (index, row, col)
        if axis == "y":
            return (seq, index * 2 + lax.rem(row, 2), col)
        if axis == "k":
            return (seq, row // 2 * 2 + index, col)
        return (seq, row, index)

    return lines, device


def greet(lines, device):
    barrier = pltpu.get_barrier_semaphore()
    count = 0
    for axis, (mine, size) in lines.items():
        for t in range(1, size):
            pl.semaphore_signal(barrier, inc=1, device_id=device(axis, lax.rem(mine + t, size)), device_id_type=MESH)
            count += 1
    pl.semaphore_wait(barrier, count)


class Post:
    def __init__(self, device, send_sems, recv_sems):
        self.device, self.send_sems, self.recv_sems = device, send_sems, recv_sems
        self.slots, self.sent = {}, []

    def slot(self, key):
        return self.slots.setdefault(key, len(self.slots))

    def copy(self, key, axis, index, source, target):
        n = self.slot(key)
        return pltpu.make_async_remote_copy(
            src_ref=source, dst_ref=target, send_sem=self.send_sems.at[n], recv_sem=self.recv_sems.at[n],
            device_id=self.device(axis, index), device_id_type=MESH,
        )

    def send(self, key, axis, index, source, target, when=None):
        def go():
            self.copy(key, axis, index, source, target).start()

        if when is None:
            go()
        else:
            pl.when(when)(go)
        self.sent.append((key, axis, index, source, target, when))

    def wait(self, key, axis, index, target, when=None):
        def go():
            self.copy(key, axis, index, target, target).wait_recv()

        if when is None:
            go()
        else:
            pl.when(when)(go)

    def close(self):
        for key, axis, index, source, target, when in self.sent:
            def go():
                self.copy(key, axis, index, source, target).wait_send()

            if when is None:
                go()
            else:
                pl.when(when)(go)


def clip(index, size):
    return jnp.clip(index, 0, size - 1)


class LineGather:
    def __init__(self, post, name, axis, line, region, reach=None):
        self.post, self.name, self.axis, self.region = post, name, axis, region
        self.mine, self.size = line
        self.reach = min(self.size - 1, reach or self.size)

    def hop(self, way, t):
        mine, size = self.mine, self.size
        origin, target = mine - way * t, mine + way
        ok = (origin >= 0) & (origin < size) & (target >= 0) & (target < size)
        here = self.region(clip(origin, size))
        self.post.send((self.name, way, t + 1), self.axis, clip(target, size), here, here, ok)

    def start(self):
        for way in (1, -1):
            if self.reach >= 1:
                self.hop(way, 0)

    def finish(self):
        for t in range(1, self.reach + 1):
            for way in (1, -1):
                origin = self.mine - way * t
                ok = (origin >= 0) & (origin < self.size)
                self.post.wait((self.name, way, t), self.axis, clip(self.mine - way, self.size), self.region(clip(origin, self.size)), ok)
                if t < self.reach:
                    self.hop(way, t)


def gather_kernel(sizes, micro, own_ref, shard_ref, every_ref, full_ref, send_sems, recv_sems, local_sems):
    lines, device = place(sizes)
    (x, _), (y, _), (k, _), (z, cols) = (lines[a] for a in "xykz")
    half = shard_ref.shape[-1] // 2
    rows = own_ref.shape[1]
    reach = -(-(DOC_MOST - 1) // rows)
    parts = [pl.ds(p * half, half) for p in (0, 1)]
    local = [pltpu.make_async_copy(shard_ref.at[j], full_ref.at[j, z, x, y, k], local_sems.at[j]) for j in range(3)]
    local += [pltpu.make_async_copy(own_ref.at[m], every_ref.at[m, z], local_sems.at[3 + m]) for m in range(micro)]
    for copy in local:
        copy.start()
    greet(lines, device)
    post = Post(device, send_sems, recv_sems)
    for copy in local:
        copy.wait()
    zs = [LineGather(post, ("z", j), "z", lines["z"], lambda i, j=j: full_ref.at[j, i, x, y, k]) for j in range(3)]
    tokens = [LineGather(post, ("t", m), "z", lines["z"], lambda i, m=m: every_ref.at[m, i], reach) for m in range(micro)]
    second, third = {}, {}
    for j in range(3):
        second[j] = [
            LineGather(post, ("a", j), "y", lines["y"], lambda i, j=j: full_ref.at[j, :, x, i, k, :, parts[0]]),
            LineGather(post, ("b", j), "x", lines["x"], lambda i, j=j: full_ref.at[j, :, i, y, k, :, parts[1]]),
        ]
        third[j] = [
            LineGather(post, ("c", j), "x", lines["x"], lambda i, j=j: full_ref.at[j, :, i, :, k, :, parts[0]]),
            LineGather(post, ("d", j), "y", lines["y"], lambda i, j=j: full_ref.at[j, :, :, i, k, :, parts[1]]),
        ]

    def start(group):
        for line in group:
            line.start()

    def finish(group):
        for line in group:
            line.finish()

    def swap(j):
        plane = full_ref.at[j, :, :, :, k]
        post.send(("k", j), "k", 1 - k, plane, plane)

    start(zs[:1])
    finish(zs[:1])
    start(second[0] + zs[1:2])
    finish(second[0])
    start(third[0])
    finish(zs[1:2])
    start(second[1] + tokens[:1])
    finish(third[0])
    swap(0)
    finish(second[1])
    start(third[1])
    finish(tokens[:1])
    start(zs[2:])
    finish(zs[2:])
    start(second[2] + tokens[1:])
    finish(third[1])
    swap(1)
    finish(second[2])
    start(third[2])
    finish(tokens[1:])
    finish(third[2])
    swap(2)
    for i in range(cols):
        far = (z - i > reach) | (i - z > reach)
        for m in range(micro):
            def fill(m=m, i=i):
                copy = pltpu.make_async_copy(own_ref.at[m], every_ref.at[m, i], local_sems.at[3 + m])
                copy.start()
                copy.wait()

            if i > reach or cols - 1 - i > reach:
                pl.when(far)(fill)
    for j in range(3):
        post.wait(("k", j), "k", 1 - k, full_ref.at[j, :, :, :, 1 - k])
    post.close()


def gather(sizes, own, shard):
    ns, nr, nc = sizes
    ny = nr // 2
    micro, rows, model = own.shape
    _, rb, w = shard.shape
    count = 3 * 2 * (nc - 1) + micro * 2 * (nc - 1) + 3 * (4 * (ny - 1) + 4 * (ns - 1) + 1)
    anywhere = pl.BlockSpec(memory_space=pl.ANY)
    every, full = pl.pallas_call(
        functools.partial(gather_kernel, sizes, micro),
        out_shape=[
            jax.ShapeDtypeStruct((micro, nc, rows, model), own.dtype),
            jax.ShapeDtypeStruct((3, nc, ns, ny, 2, rb, w), shard.dtype),
        ],
        in_specs=[pl.BlockSpec(memory_space=pltpu.VMEM)] * 2,
        out_specs=[anywhere] * 2,
        scratch_shapes=[pltpu.SemaphoreType.DMA((count,)), pltpu.SemaphoreType.DMA((count,)), pltpu.SemaphoreType.DMA((3 + micro,))],
        compiler_params=pltpu.CompilerParams(collective_id=0, has_side_effects=True),
        name="gather",
    )(own, shard)
    return every, full.reshape(3, nc, ns * nr * rb, w)


class LineReduce:
    def __init__(self, post, name, axis, line, region, inbox, add, reach=None):
        self.post, self.name, self.axis, self.region, self.inbox, self.add = post, name, axis, region, inbox, add
        self.mine, self.size = line
        self.reach = min(self.size - 1, reach or self.size)

    def arrived(self, way, e):
        behind, goal = self.mine - way, self.mine + way * e
        return (behind >= 0) & (behind < self.size) & (goal >= 0) & (goal < self.size)

    def take(self, way, e):
        ok = self.arrived(way, e)
        inbox = self.inbox(way, e)
        self.post.wait((self.name, way, e), self.axis, clip(self.mine - way, self.size), inbox, ok)

        @pl.when(ok)
        def _():
            self.add(self.region(clip(self.mine + way * e, self.size)), inbox)

    def forward(self, way, e):
        goal = self.mine + way * e
        ok = (goal >= 0) & (goal < self.size)
        self.post.send((self.name, way, e - 1), self.axis, clip(self.mine + way, self.size),
                       self.region(clip(goal, self.size)), self.inbox(way, e - 1), ok)

    def start(self):
        for way in (1, -1):
            if self.reach >= 1:
                self.forward(way, self.reach)

    def finish(self, last=True):
        for e in range(self.reach - 1, 0, -1):
            for way in (1, -1):
                self.take(way, e)
                self.forward(way, e)
        if last:
            for way in (1, -1):
                if self.reach >= 1:
                    self.take(way, 0)


def reduce_kernel(sizes, micro, own_ref, spread_ref, part_ref, vec_ref, back_ref, block_ref, sums_ref,
                  mine_buf, core_buf, in_a, in_b, in_c, in_d, in_z, tok_buf, tok_in, vec_buf, send_sems, recv_sems, local_sems):
    floats, halves = jnp.float32, jnp.bfloat16
    lines, device = place(sizes)
    (x, ns), (y, ny), (k, _), (z, nc) = (lines[a] for a in "xykz")
    half = part_ref.shape[-1] // 2
    rows = own_ref.shape[1]
    reach = -(-(DOC_MOST - 1) // rows)
    parts = [pl.ds(p * half, half) for p in (0, 1)]
    local = [pltpu.make_async_copy(part_ref.at[j, :, :, :, k], mine_buf.at[j], local_sems.at[j]) for j in range(3)]
    local += [pltpu.make_async_copy(spread_ref.at[m], tok_buf.at[m], local_sems.at[3 + m]) for m in range(micro)]
    for copy in local:
        copy.start()
    greet(lines, device)
    post = Post(device, send_sems, recv_sems)
    for j in range(3):
        post.send(("k", j), "k", 1 - k, part_ref.at[j, :, :, :, 1 - k], core_buf.at[j])

    def plus(target, source):
        target[...] = (target[...].astype(floats) + source[...].astype(floats)).astype(halves)

    def plus_grid(target, source, first, second):
        @pl.loop(0, first * second)
        def _(n):
            plus(target.at[n // second, lax.rem(n, second)], source.at[n // second, lax.rem(n, second)])

    def plus_row(target, source, first):
        @pl.loop(0, first)
        def _(n):
            plus(target.at[n], source.at[n])

    vec_buf[0, 0] = vec_ref[...]

    def vector_start(stage, axis):
        mine, size = lines[axis]
        vec_buf[stage, 1 + mine] = vec_buf[stage, 0]
        for t in range(1, size):
            post.send(("v", stage, t), axis, lax.rem(mine + t, size), vec_buf.at[stage, 0], vec_buf.at[stage, 1 + mine])

    def vector_finish(stage, axis, out):
        mine, size = lines[axis]
        for t in range(1, size):
            origin = lax.rem(mine + size - t, size)
            post.wait(("v", stage, t), axis, origin, vec_buf.at[stage, 1 + origin])
        total = vec_buf[stage, 1]
        for i in range(1, size):
            total = total + vec_buf[stage, 1 + i]
        out[...] = total

    tokens = [
        LineReduce(post, ("t", m), "z", lines["z"], lambda i, m=m: tok_buf.at[m, i],
                   lambda way, e, m=m: tok_in.at[m, (1 - way) // 2, e], plus, reach)
        for m in range(micro)
    ]
    box = lambda way: (1 - way) // 2
    second, third, last = {}, {}, {}
    for j in range(3):
        second[j] = [
            LineReduce(post, ("a", j), "x", lines["x"], lambda i, j=j: mine_buf.at[j, :, i, :, :, parts[0]],
                       lambda way, e, j=j: in_a.at[j, box(way), e], lambda t, s: plus_grid(t, s, nc, ny)),
            LineReduce(post, ("b", j), "y", lines["y"], lambda i, j=j: mine_buf.at[j, :, :, i, :, parts[1]],
                       lambda way, e, j=j: in_b.at[j, box(way), e], lambda t, s: plus_grid(t, s, nc, ns)),
        ]
        third[j] = [
            LineReduce(post, ("c", j), "y", lines["y"], lambda i, j=j: mine_buf.at[j, :, x, i, :, parts[0]],
                       lambda way, e, j=j: in_c.at[j, box(way), e], lambda t, s: plus_row(t, s, nc)),
            LineReduce(post, ("d", j), "x", lines["x"], lambda i, j=j: mine_buf.at[j, :, i, y, :, parts[1]],
                       lambda way, e, j=j: in_d.at[j, box(way), e], lambda t, s: plus_row(t, s, nc)),
        ]
        last[j] = [
            LineReduce(post, ("z", j), "z", lines["z"], lambda i, j=j: mine_buf.at[j, i, x, y],
                       lambda way, e, j=j: in_z.at[j, box(way), e], plus)
        ]

    def start(group):
        for line in group:
            line.start()

    def finish(group):
        for line in group:
            line.finish()

    def core(j):
        local[j].wait()
        post.wait(("k", j), "k", 1 - k, core_buf.at[j])

        @pl.loop(0, nc * ns * ny)
        def _(n):
            at = (n // (ns * ny), lax.rem(n // ny, ns), lax.rem(n, ny))
            plus(mine_buf.at[(j, *at)], core_buf.at[(j, *at)])

    for m in range(micro):
        local[3 + m].wait()
    start(tokens)
    core(0)
    start(second[0])
    vector_start(0, "k")
    core(1)
    start(second[1])
    vector_finish(0, "k", vec_buf.at[1, 0])
    vector_start(1, "y")
    core(2)
    finish(second[0])
    start(third[0])
    start(second[2])
    vector_finish(1, "y", vec_buf.at[2, 0])
    vector_start(2, "x")
    finish(tokens)
    vector_finish(2, "x", vec_buf.at[3, 0])
    vector_start(3, "z")
    finish(second[1])
    start(third[1])
    finish(third[0])
    start(last[0])
    finish(second[2])
    start(third[2])
    finish(third[1])
    start(last[1])
    finish(last[0])
    finish(third[2])
    start(last[2])
    vector_finish(3, "z", sums_ref)
    for m in range(micro):
        back_ref[m] = own_ref[m] + tok_buf[m, z].astype(floats)
    finish(last[1])
    finish(last[2])
    for j in range(3):
        block_ref[j] = mine_buf[j, z, x, y].astype(floats)
    post.close()


def reduce(sizes, own_share, spread, partial, vectors):
    ns, nr, nc = sizes
    ny = nr // 2
    micro, rows, model = own_share.shape
    w = partial.shape[-1]
    rb = partial.shape[2] // (ns * nr)
    halves, floats = jnp.bfloat16, jnp.float32
    reach = min(nc - 1, -(-(DOC_MOST - 1) // rows))
    count = 3 + 2 * (ny - 1 + ns - 1) * 6 + 3 * 2 * (nc - 1) + micro * 2 * reach + (1 + ny - 1 + ns - 1 + nc - 1)
    widest = max(ns, ny, nc, 2)
    extra = -vectors.shape[0] % 8
    vectors = jnp.pad(vectors, ((0, extra), (0, 0)))
    vmem = pl.BlockSpec(memory_space=pltpu.VMEM)
    anywhere = pl.BlockSpec(memory_space=pl.ANY)
    back, blocks, sums = pl.pallas_call(
        functools.partial(reduce_kernel, sizes, micro),
        out_shape=[
            jax.ShapeDtypeStruct((micro, rows, model), floats),
            jax.ShapeDtypeStruct((3, rb, w), floats),
            jax.ShapeDtypeStruct(vectors.shape, floats),
        ],
        in_specs=[vmem, anywhere, anywhere, vmem],
        out_specs=[vmem] * 3,
        scratch_shapes=[
            pltpu.VMEM((3, nc, ns, ny, rb, w), halves),
            pltpu.VMEM((3, nc, ns, ny, rb, w), halves),
            pltpu.VMEM((3, 2, max(ns - 1, 1), nc, ny, rb, w // 2), halves),
            pltpu.VMEM((3, 2, max(ny - 1, 1), nc, ns, rb, w // 2), halves),
            pltpu.VMEM((3, 2, max(ny - 1, 1), nc, rb, w // 2), halves),
            pltpu.VMEM((3, 2, max(ns - 1, 1), nc, rb, w // 2), halves),
            pltpu.VMEM((3, 2, max(nc - 1, 1), rb, w), halves),
            pltpu.VMEM((micro, nc, rows, model), halves),
            pltpu.VMEM((micro, 2, max(reach, 1), rows, model), halves),
            pltpu.VMEM((4, 1 + widest, *vectors.shape), floats),
            pltpu.SemaphoreType.DMA((count,)),
            pltpu.SemaphoreType.DMA((count,)),
            pltpu.SemaphoreType.DMA((3 + micro,)),
        ],
        compiler_params=pltpu.CompilerParams(collective_id=1, has_side_effects=True, vmem_limit_bytes=60 << 20),
        name="reduce",
    )(own_share, spread, partial.reshape(3, nc, ns, ny, 2, rb, w), vectors)
    return back, blocks, sums


Q_AT, K_AT, V_AT, O_AT, WINDOW = 0, 128, 384, 512, 256


def plane(full_ref, c, at, size=WINDOW):
    value = full_ref[c, :, :, :, :, at : at + size]
    return value.reshape(-1, size)


def place_of(rows):
    return lax.broadcasted_iota(jnp.int32, (rows, WINDOW), 1) // HEAD_DIM


def keep(value, places, wanted):
    return jnp.where(places == wanted, value, jnp.zeros_like(value))


def forward_kernel(sizes, micro, own_ref, shard_ref, bias_ref, segq_ref, segk_ref,
                   rest_ref, first_ref, every_ref, biases_ref, mixed_ref, lse_ref, q_ref, k_ref, v_ref,
                   weights, tokens_buf, bias_buf, mask, mixed_buf, lse_buf, q_buf, k_buf, v_buf, acc, top, total,
                   send_sems, recv_sems, local_sems):
    floats, halves = jnp.float32, jnp.bfloat16
    lines, device = place(sizes)
    (x, _), (y, _), (k, _), (z, cols) = (lines[a] for a in "xykz")
    half = shard_ref.shape[-1] // 2
    rows = own_ref.shape[1]
    reach = -(-(DOC_MOST - 1) // rows)
    parts = [pl.ds(p * half, half) for p in (0, 1)]
    low, high = jnp.maximum(z - reach, 0), jnp.minimum(z + reach + 1, cols)
    used = [0]

    def local(source, target):
        copy = pltpu.make_async_copy(source, target, local_sems.at[used[0]])
        used[0] += 1
        copy.start()
        return copy

    targets = [weights.at[0], rest_ref.at[0], rest_ref.at[1]]
    begin = [local(shard_ref.at[j], targets[j].at[z, x, y, k]) for j in range(3)]
    begin += [local(own_ref.at[m], tokens_buf.at[m, z]) for m in range(micro)]
    begin += [local(bias_ref, bias_buf.at[z])]
    greet(lines, device)
    post = Post(device, send_sems, recv_sems)
    for copy in begin:
        copy.wait()
    zs = [LineGather(post, ("z", j), "z", lines["z"], lambda i, j=j: targets[j].at[i, x, y, k]) for j in range(3)]
    tokens = [LineGather(post, ("t", m), "z", lines["z"], lambda i, m=m: tokens_buf.at[m, i], reach) for m in range(micro)]
    small = LineGather(post, "bias", "z", lines["z"], lambda i: bias_buf.at[i])
    second, third = {}, {}
    for j in range(3):
        second[j] = [
            LineGather(post, ("a", j), "y", lines["y"], lambda i, j=j: targets[j].at[:, x, i, k, :, parts[0]]),
            LineGather(post, ("b", j), "x", lines["x"], lambda i, j=j: targets[j].at[:, i, y, k, :, parts[1]]),
        ]
        third[j] = [
            LineGather(post, ("c", j), "x", lines["x"], lambda i, j=j: targets[j].at[:, i, :, k, :, parts[0]]),
            LineGather(post, ("d", j), "y", lines["y"], lambda i, j=j: targets[j].at[:, :, i, k, :, parts[1]]),
        ]

    def start(*group):
        for line in group:
            line.start()

    def finish(*group):
        for line in group:
            line.finish()

    def swap(j):
        own_plane = targets[j].at[:, :, :, k]
        post.send(("k", j), "k", 1 - k, own_plane, own_plane)

    def swapped(j):
        post.wait(("k", j), "k", 1 - k, targets[j].at[:, :, :, 1 - k])

    places = place_of(rows)

    def unit(m, c):
        queries = jnp.dot(own_ref[m], plane(weights.at[0], c, Q_AT), preferred_element_type=floats) + bias_buf[c, 1:2, 0:WINDOW]
        queries = pltpu.roll(queries.astype(halves).astype(floats) * HEAD_DIM ** -0.5, HEAD_DIM, 1)
        queries = jnp.where(places > 0, queries, 0.0).astype(halves)
        q_buf[m, c] = queries
        heads = [keep(queries, places, h + 1) for h in range(3)]
        acc[...] = jnp.zeros_like(acc)
        total[...] = jnp.zeros_like(total)
        top[...] = jnp.full_like(top, 2 * MASK_VALUE)
        key_weight = plane(weights.at[0], c, K_AT)
        value_weight = plane(weights.at[0], c, V_AT)
        value_bias = bias_buf[c, 2:3, 0:WINDOW]

        def step(block, carry):
            rows_at = tokens_buf[m, block]
            keys = jnp.dot(rows_at, key_weight, preferred_element_type=floats).astype(halves)
            values = (jnp.dot(rows_at, value_weight, preferred_element_type=floats) + value_bias).astype(halves)
            k_buf[m, c, block] = keys
            v_buf[m, c, block] = values
            values_t = values.T
            hidden = mask[m, block]
            for h in range(3):
                s = contract_cols(keys, heads[h]) + hidden
                old = top[h : h + 1]
                new = jnp.maximum(old, jnp.max(s, 0, keepdims=True))
                p = jnp.exp(s - new)
                shrink = jnp.exp(old - new)
                top[h : h + 1] = new
                total[h : h + 1] = total[h : h + 1] * shrink + jnp.sum(p, 0, keepdims=True)
                at = pl.ds((h + 1) * HEAD_DIM, HEAD_DIM)
                acc[at, :] = acc[at, :] * shrink + jnp.dot(
                    values_t[h * HEAD_DIM : (h + 1) * HEAD_DIM], p.astype(halves), preferred_element_type=floats
                )
            return carry

        lax.fori_loop(low, high, step, 0)
        for h in range(3):
            at = pl.ds((h + 1) * HEAD_DIM, HEAD_DIM)
            acc[at, :] = acc[at, :] / total[h : h + 1]
        mixed_buf[c, m] = acc[...].T.astype(halves)
        lse_buf[m, c] = top[...] + jnp.log(jnp.maximum(total[...], 1e-30))

    def units(m, first, last):
        @pl.loop(first, last)
        def _(c):
            unit(m, c)

    def masks(m):
        @pl.loop(low, high)
        def _(block):
            same = segk_ref[m, pl.ds(pl.multiple_of(block * rows, rows), rows), :] == segq_ref[m, 0:1]
            mask[m, block] = jnp.where(same, 0.0, MASK_VALUE)

    done = []
    middle = max(cols // 2, 1)
    start(small, zs[0])
    finish(zs[0])
    start(*second[0], tokens[0])
    for m in range(micro):
        masks(m)
    finish(small, *second[0])
    start(*third[0])
    finish(tokens[0])
    start(zs[1])
    finish(*third[0])
    swap(0)
    finish(zs[1])
    start(*second[1], zs[2])
    swapped(0)
    units(0, 0, middle)
    finish(*second[1])
    start(*third[1])
    finish(zs[2])
    for m in range(1, micro):
        start(tokens[m])
    done.append(local(weights.at[0], first_ref))
    units(0, middle, cols)
    finish(*tokens[1:])
    finish(*third[1])
    swap(1)
    start(*second[2])
    for m in range(1, micro):
        units(m, 0, middle)
        if m == 1:
            finish(*second[2])
            start(*third[2])
        units(m, middle, cols)
    for m in range(micro):
        @pl.loop(low, high)
        def _(block, m=m):
            copy = pltpu.make_async_copy(tokens_buf.at[m, block], every_ref.at[m, block], local_sems.at[used[0] + m])
            copy.start()
            copy.wait()
    used[0] += micro
    for source, target in ((bias_buf, biases_ref), (mixed_buf, mixed_ref), (lse_buf, lse_ref), (q_buf, q_ref), (k_buf, k_ref), (v_buf, v_ref)):
        done.append(local(source, target))
    if micro == 1:
        finish(*second[2])
        start(*third[2])
    finish(*third[2])
    swap(2)
    swapped(1)
    swapped(2)
    for copy in done:
        copy.wait()
    post.close()


def forward(sizes, own, shard, bias, seg_own, seg_all):
    ns, nr, nc = sizes
    ny = nr // 2
    micro, rows, model = own.shape
    _, rb, w = shard.shape
    halves, floats = own.dtype, jnp.float32
    reach = min(nc - 1, -(-(DOC_MOST - 1) // rows))
    count = (3 + 1) * 2 * (nc - 1) + micro * 2 * reach + 3 * (4 * (ny - 1) + 4 * (ns - 1) + 1)
    anywhere = pl.BlockSpec(memory_space=pl.ANY)
    vmem = pl.BlockSpec(memory_space=pltpu.VMEM)
    length = nc * rows
    arrays = [
        ((2, nc, ns, ny, 2, rb, w), halves), ((nc, ns, ny, 2, rb, w), halves), ((micro, nc, rows, model), halves),
        ((nc, *bias.shape), floats), ((nc, micro, rows, WINDOW), halves), ((micro, nc, 8, rows), floats),
        ((micro, nc, rows, WINDOW), halves), ((micro, nc, nc, rows, WINDOW), halves), ((micro, nc, nc, rows, WINDOW), halves),
    ]
    shapes = [pltpu.VMEM(shape, kind) for shape, kind in arrays]
    return pl.pallas_call(
        functools.partial(forward_kernel, sizes, micro),
        out_shape=[jax.ShapeDtypeStruct(shape, kind) for shape, kind in arrays],
        in_specs=[vmem] * 5,
        out_specs=[anywhere] * len(arrays),
        scratch_shapes=[
            pltpu.VMEM((1, nc, ns, ny, 2, rb, w), halves),
            shapes[2], shapes[3], pltpu.VMEM((micro, nc, rows, rows), floats), *shapes[4:],
            pltpu.VMEM((WINDOW, rows), floats), pltpu.VMEM((8, rows), floats), pltpu.VMEM((8, rows), floats),
            pltpu.SemaphoreType.DMA((count,)), pltpu.SemaphoreType.DMA((count,)), pltpu.SemaphoreType.DMA((20,)),
        ],
        compiler_params=pltpu.CompilerParams(collective_id=2, has_side_effects=True, vmem_limit_bytes=60 << 20),
        name="forward",
    )(own, shard, bias, seg_own[:, None], seg_all[:, :, None])


def per_device_plain(sizes, inputs, segment_ids, query_weight, key_weight, value_weight, query_bias, value_bias,
               output_weight, output_bias, first_gain, first_shift, hidden_weight, hidden_bias, down_weight,
               down_bias, second_gain, second_shift, cotangent):
    floats, halves = jnp.float32, jnp.bfloat16
    cols = sizes[2]
    micro, _, rows, model = inputs.shape
    length = segment_ids.shape[-1]
    width = query_weight.shape[1]
    here = lax.axis_index("col")
    own = inputs[:, 0]
    shard = jnp.stack([
        jnp.concatenate([query_weight, key_weight, value_weight, output_weight.T], 1),
        hidden_weight,
        down_weight.T,
    ])
    biases = lax.all_gather(jnp.concatenate([query_bias, value_bias, hidden_bias]), "col", axis=0)
    everything, gathered = gather(sizes, own, shard)
    everything = everything.reshape(micro, length, model)
    attn_weights = gathered[0]
    wq, wk, wv, wot = (attn_weights[:, :, i * width : (i + 1) * width] for i in range(4))
    hidden_full, down_full = gathered[1], gathered[2]
    bq, bv, bh = biases[:, :width], biases[:, width : 2 * width], biases[:, 2 * width :]
    seg_all = segment_ids[:, 0]
    seg_own = lax.dynamic_slice_in_dim(seg_all, here * rows, rows, 1)
    first_key = jnp.sum((seg_all < seg_own[:, :1]).astype(jnp.int32), 1)
    last_key = jnp.sum((seg_all <= seg_own[:, -1:]).astype(jnp.int32), 1)
    bounds = jnp.stack([first_key // KEY_BLOCK, (last_key + KEY_BLOCK - 1) // KEY_BLOCK], 1)

    mixed, lse, q, k, v = attend(bounds, own, everything, wq, wk, wv, bq.astype(floats), bv.astype(floats), seg_own, seg_all)
    total = micro * rows
    flat = lambda a: a.reshape(total, -1)
    mixed_flat = mixed.reshape(cols, total, width)
    attn = sum(contract_cols(mixed_flat[c], wot[c]) for c in range(cols))
    first_sum = flat(own).astype(floats) + attn + output_bias.astype(floats)
    normal_one, scale_one = norm_parts(first_sum)
    gain_one = first_gain.astype(floats)
    normed = normal_one * gain_one + first_shift.astype(floats)
    normed_low = normed.astype(halves)
    ffn = 0
    activated, slopes = [], []
    for c in range(cols):
        hidden = jnp.dot(normed_low, hidden_full[c], preferred_element_type=floats) + bh[c].astype(floats)
        half_erf = 0.5 * lax.erf(hidden * 0.7071067811865476) + 0.5
        act = (hidden * half_erf).astype(halves)
        slope = half_erf + hidden * (jnp.exp(-0.5 * hidden * hidden) * 0.3989422804014327)
        activated.append(act)
        slopes.append(slope.astype(halves))
        ffn = ffn + contract_cols(act, down_full[c])
    second_sum = normed + ffn + down_bias.astype(floats)
    normal_two, scale_two = norm_parts(second_sum)
    gain_two = second_gain.astype(floats)
    outputs = (normal_two * gain_two + second_shift.astype(floats)).astype(halves)
    cot = flat(cotangent[:, 0]).astype(floats)
    second_grad = norm_back(cot * gain_two, normal_two, scale_two)
    ffn_grad = second_grad.astype(halves)
    hidden_grads, down_grads, hidden_bias_grads = [], [], []
    normed_grad = second_grad
    for c in range(cols):
        pre = (jnp.dot(ffn_grad, down_full[c], preferred_element_type=floats) * slopes[c].astype(floats)).astype(halves)
        hidden_grads.append(contract_rows(normed_low, pre).astype(halves))
        down_grads.append(contract_rows(ffn_grad, activated[c]).astype(halves))
        hidden_bias_grads.append(jnp.sum(pre.astype(floats), 0))
        normed_grad = normed_grad + contract_cols(pre, hidden_full[c])
    first_grad = norm_back(normed_grad * gain_one, normal_one, scale_one)
    attn_grad = first_grad.astype(halves)
    dq, dk, dv = attend_back(bounds, attn_grad.reshape(micro, rows, model), wot, mixed, lse, q, k, v, seg_own, seg_all)
    every_flat = everything.reshape(micro * length, model)
    attn_grads = []
    own_share = first_grad
    spread = 0
    for c in range(cols):
        dq_c, dk_c, dv_c = dq[c].reshape(total, width), dk[c].reshape(micro * length, width), dv[c].reshape(micro * length, width)
        attn_grads.append(jnp.concatenate([
            contract_rows(flat(own), dq_c), contract_rows(every_flat, dk_c), contract_rows(every_flat, dv_c),
            contract_rows(attn_grad, mixed_flat[c]),
        ], 1).astype(halves))
        own_share = own_share + contract_cols(dq_c, wq[c])
        spread = spread + contract_cols(dk_c, wk[c]) + contract_cols(dv_c, wv[c])
    bias_q = jnp.sum(dq.astype(floats), (1, 2)).reshape(-1)
    bias_v = jnp.sum(dv.astype(floats), (1, 2)).reshape(-1)
    vectors = jnp.concatenate([
        jnp.sum(first_grad, 0), jnp.sum(normed_grad * normal_one, 0), jnp.sum(normed_grad, 0), jnp.sum(second_grad, 0),
        jnp.sum(cot * normal_two, 0), jnp.sum(cot, 0), bias_q, bias_v, *hidden_bias_grads,
    ]).reshape(-1, model)
    partial = jnp.stack([jnp.stack(attn_grads), jnp.stack(hidden_grads), jnp.stack(down_grads)])
    input_grad, reduced, sums = reduce(sizes, own_share.reshape(micro, rows, model),
                                       spread.astype(halves).reshape(micro, cols, rows, model), partial, vectors)
    attn_block = reduced[0]
    piece = lambda i: attn_block[:, i * width : (i + 1) * width]
    mine = lambda vector, size: lax.dynamic_slice_in_dim(vector.reshape(-1), here * size, size, 0)
    return (
        outputs.reshape(micro, 1, rows, model), input_grad[:, None],
        piece(0), piece(1), piece(2), mine(sums[6], width), mine(sums[7], width), piece(3).T,
        sums[0], sums[1], sums[2], reduced[1], mine(sums[8:], hidden_bias.shape[0]), reduced[2].T,
        sums[3], sums[4], sums[5],
    )


def per_device_fused(sizes, inputs, segment_ids, query_weight, key_weight, value_weight, query_bias, value_bias,
               output_weight, output_bias, first_gain, first_shift, hidden_weight, hidden_bias, down_weight,
               down_bias, second_gain, second_shift, cotangent):
    floats, halves = jnp.float32, jnp.bfloat16
    cols = sizes[2]
    micro, _, rows, model = inputs.shape
    length = segment_ids.shape[-1]
    width = query_weight.shape[1]
    here = lax.axis_index("col")
    own = inputs[:, 0]
    shard = jnp.stack([
        jnp.concatenate([query_weight, key_weight, value_weight, output_weight.T], 1),
        hidden_weight,
        down_weight.T,
    ])
    pad = lambda vector: jnp.pad(vector.astype(floats), (0, model - vector.shape[0]))
    bias = jnp.stack([pad(hidden_bias), pad(query_bias), pad(value_bias)] + [jnp.zeros((model,), floats)] * 5)
    seg_all = segment_ids[:, 0]
    seg_own = lax.dynamic_slice_in_dim(seg_all, here * rows, rows, 1)
    rest, first, everything, biases, mixed, lse, q, k, v = forward(sizes, own, shard, bias, seg_own, seg_all)
    first = first.reshape(cols, model, 4 * width)
    wq, wk, wv, wot = (first[:, :, i * width : (i + 1) * width] for i in range(4))
    hidden_full, down_full = rest.reshape(2, cols, model, -1)
    bh = biases[:, 0, : hidden_bias.shape[0]]
    first_key = jnp.sum((seg_all < seg_own[:, :1]).astype(jnp.int32), 1)
    last_key = jnp.sum((seg_all <= seg_own[:, -1:]).astype(jnp.int32), 1)
    bounds = jnp.stack([first_key // KEY_BLOCK, (last_key + KEY_BLOCK - 1) // KEY_BLOCK], 1)
    everything = everything.reshape(micro, length, model)
    everything = jnp.where(jnp.isfinite(everything), everything, 0)
    mixed = mixed[..., HEAD_DIM:]
    lse = lse.swapaxes(0, 1)
    q = q[..., HEAD_DIM:].swapaxes(0, 1)
    k = k.reshape(micro, cols, length, -1)[..., HEAD_DIM:].swapaxes(0, 1)
    v = v.reshape(micro, cols, length, -1)[..., :width].swapaxes(0, 1)
    total = micro * rows
    flat = lambda a: a.reshape(total, -1)
    mixed_flat = mixed.reshape(cols, total, width)
    attn = sum(contract_cols(mixed_flat[c], wot[c]) for c in range(cols))
    first_sum = flat(own).astype(floats) + attn + output_bias.astype(floats)
    normal_one, scale_one = norm_parts(first_sum)
    gain_one = first_gain.astype(floats)
    normed = normal_one * gain_one + first_shift.astype(floats)
    normed_low = normed.astype(halves)
    ffn = 0
    activated, slopes = [], []
    for c in range(cols):
        hidden = jnp.dot(normed_low, hidden_full[c], preferred_element_type=floats) + bh[c].astype(floats)
        half_erf = 0.5 * lax.erf(hidden * 0.7071067811865476) + 0.5
        act = (hidden * half_erf).astype(halves)
        slope = half_erf + hidden * (jnp.exp(-0.5 * hidden * hidden) * 0.3989422804014327)
        activated.append(act)
        slopes.append(slope.astype(halves))
        ffn = ffn + contract_cols(act, down_full[c])
    second_sum = normed + ffn + down_bias.astype(floats)
    normal_two, scale_two = norm_parts(second_sum)
    gain_two = second_gain.astype(floats)
    outputs = (normal_two * gain_two + second_shift.astype(floats)).astype(halves)
    cot = flat(cotangent[:, 0]).astype(floats)
    second_grad = norm_back(cot * gain_two, normal_two, scale_two)
    ffn_grad = second_grad.astype(halves)
    hidden_grads, down_grads, hidden_bias_grads = [], [], []
    normed_grad = second_grad
    for c in range(cols):
        pre = (jnp.dot(ffn_grad, down_full[c], preferred_element_type=floats) * slopes[c].astype(floats)).astype(halves)
        hidden_grads.append(contract_rows(normed_low, pre).astype(halves))
        down_grads.append(contract_rows(ffn_grad, activated[c]).astype(halves))
        hidden_bias_grads.append(jnp.sum(pre.astype(floats), 0))
        normed_grad = normed_grad + contract_cols(pre, hidden_full[c])
    first_grad = norm_back(normed_grad * gain_one, normal_one, scale_one)
    attn_grad = first_grad.astype(halves)
    dq, dk, dv = attend_back(bounds, attn_grad.reshape(micro, rows, model), wot, mixed, lse, q, k, v, seg_own, seg_all)
    every_flat = everything.reshape(micro * length, model)
    attn_grads = []
    own_share = first_grad
    spread = 0
    for c in range(cols):
        dq_c, dk_c, dv_c = dq[c].reshape(total, width), dk[c].reshape(micro * length, width), dv[c].reshape(micro * length, width)
        attn_grads.append(jnp.concatenate([
            contract_rows(flat(own), dq_c), contract_rows(every_flat, dk_c), contract_rows(every_flat, dv_c),
            contract_rows(attn_grad, mixed_flat[c]),
        ], 1).astype(halves))
        own_share = own_share + contract_cols(dq_c, wq[c])
        spread = spread + contract_cols(dk_c, wk[c]) + contract_cols(dv_c, wv[c])
    bias_q = jnp.sum(dq.astype(floats), (1, 2)).reshape(-1)
    bias_v = jnp.sum(dv.astype(floats), (1, 2)).reshape(-1)
    vectors = jnp.concatenate([
        jnp.sum(first_grad, 0), jnp.sum(normed_grad * normal_one, 0), jnp.sum(normed_grad, 0), jnp.sum(second_grad, 0),
        jnp.sum(cot * normal_two, 0), jnp.sum(cot, 0), bias_q, bias_v, *hidden_bias_grads,
    ]).reshape(-1, model)
    partial = jnp.stack([jnp.stack(attn_grads), jnp.stack(hidden_grads), jnp.stack(down_grads)])
    input_grad, reduced, sums = reduce(sizes, own_share.reshape(micro, rows, model),
                                       spread.astype(halves).reshape(micro, cols, rows, model), partial, vectors)
    attn_block = reduced[0]
    piece = lambda i: attn_block[:, i * width : (i + 1) * width]
    mine = lambda vector, size: lax.dynamic_slice_in_dim(vector.reshape(-1), here * size, size, 0)
    return (
        outputs.reshape(micro, 1, rows, model), input_grad[:, None],
        piece(0), piece(1), piece(2), mine(sums[6], width), mine(sums[7], width), piece(3).T,
        sums[0], sums[1], sums[2], reduced[1], mine(sums[8:], hidden_bias.shape[0]), reduced[2].T,
        sums[3], sums[4], sums[5],
    )


def per_device(sizes, inputs, segment_ids, query_weight, *rest):
    fits = query_weight.shape == (query_weight.shape[0] // 16 * 16, 3 * HEAD_DIM)
    return (per_device_fused if fits else per_device_plain)(sizes, inputs, segment_ids, query_weight, *rest)


def solution(mesh):
    sizes = tuple(mesh.shape[name] for name in ("seq", "row", "col"))
    block, line = P(("seq", "row"), "col"), P("col", ("seq", "row"))
    tokens = P(None, ("seq", "row"), "col", None)
    placed = (tokens, P(None, ("seq", "row"), None), block, block, block, P("col"), P("col"), line, P(), P(), P(),
              block, P("col"), line, P(), P(), P(), tokens)
    given = (tokens, tokens, block, block, block, P("col"), P("col"), line, P(), P(), P(), block, P("col"), line,
             P(), P(), P())
    return jax.shard_map(functools.partial(per_device, sizes), mesh=mesh, in_specs=placed, out_specs=given, check_vma=False)
```

```python
import functools

import jax
import jax.numpy as jnp
from jax import lax
from jax.experimental import pallas as pl
from jax.experimental.pallas import tpu as pltpu
from jax.sharding import PartitionSpec as P

HEAD_DIM = 64
NORM_EPS = 1e-05
MASK_VALUE = -1000000000.0
DOC_MOST = 512
KEY_BLOCK = 256
MESH = pl.DeviceIdType.MESH


def contract_rows(left, right):
    return lax.dot_general(
        left, right, (((0,), (0,)), ((), ())), preferred_element_type=jnp.float32
    )


def contract_cols(left, right):
    return lax.dot_general(
        left, right, (((1,), (1,)), ((), ())), preferred_element_type=jnp.float32
    )


def norm_parts(summed):
    deviation = summed - jnp.mean(summed, -1, keepdims=True)
    scale = lax.rsqrt(jnp.mean(deviation * deviation, -1, keepdims=True) + NORM_EPS)
    return deviation * scale, scale


def norm_back(pull, normal, scale):
    return scale * (
        pull - jnp.mean(pull, -1, keepdims=True) - normal * jnp.mean(pull * normal, -1, keepdims=True)
    )


def attend_kernel(bounds, own_ref, all_ref, wq_ref, wk_ref, wv_ref, bq_ref, bv_ref,
                  segq_ref, segk_ref, mixed_ref, lse_ref, q_ref, k_ref, v_ref, bias, acc, top, total):
    micro = pl.program_id(0)
    low, high = bounds[micro, 0], bounds[micro, 1]
    floats, halves = jnp.float32, jnp.bfloat16
    width = wq_ref.shape[-1]
    heads = width // HEAD_DIM
    rows = own_ref.shape[1]

    @pl.when(pl.program_id(1) == 0)
    def _():
        same = segk_ref[0] == segq_ref[0, 0:1]
        bias[...] = jnp.where(same, 0.0, MASK_VALUE)

    queries = jnp.dot(own_ref[0], wq_ref[0], preferred_element_type=floats) + bq_ref[0]
    queries = queries.astype(halves) * jnp.asarray(HEAD_DIM ** -0.5, halves)
    q_ref[0, 0] = queries
    lane = lax.broadcasted_iota(jnp.int32, (rows, width), 1) // HEAD_DIM
    query_heads = [jnp.where(lane == h, queries, jnp.zeros_like(queries)) for h in range(heads)]
    acc[...] = jnp.zeros_like(acc)
    total[...] = jnp.zeros_like(total)
    top[...] = jnp.full_like(top, 2 * MASK_VALUE)

    def step(block, carry):
        at = pl.ds(pl.multiple_of(block * KEY_BLOCK, KEY_BLOCK), KEY_BLOCK)
        x = all_ref[0, at, :]
        keys = jnp.dot(x, wk_ref[0], preferred_element_type=floats).astype(halves)
        k_ref[0, 0, at, :] = keys
        values = (jnp.dot(x, wv_ref[0], preferred_element_type=floats) + bv_ref[0]).astype(halves)
        v_ref[0, 0, at, :] = values
        values_t = values.T
        mask = bias[at, :]
        for h in range(heads):
            s = contract_cols(keys, query_heads[h]) + mask
            old = top[h : h + 1]
            new = jnp.maximum(old, jnp.max(s, 0, keepdims=True))
            p = jnp.exp(s - new)
            shrink = jnp.exp(old - new)
            top[h : h + 1] = new
            total[h : h + 1] = total[h : h + 1] * shrink + jnp.sum(p, 0, keepdims=True)
            part = pl.ds(h * HEAD_DIM, HEAD_DIM)
            acc[part, :] = acc[part, :] * shrink + jnp.dot(
                values_t[h * HEAD_DIM : (h + 1) * HEAD_DIM], p.astype(halves), preferred_element_type=floats
            )
        return carry

    lax.fori_loop(low, high, step, 0)
    for h in range(heads):
        part = pl.ds(h * HEAD_DIM, HEAD_DIM)
        acc[part, :] = acc[part, :] / total[h : h + 1]
    mixed_ref[0, 0] = acc[...].T.astype(halves)
    lse_ref[0, 0] = top[...] + jnp.log(jnp.maximum(total[...], 1e-30))


def attend(bounds, own, everything, wq, wk, wv, bq, bv, seg_own, seg_all):
    micro, rows, model = own.shape
    length = everything.shape[1]
    cols, _, width = wq.shape
    halves = jnp.bfloat16
    weight = pl.BlockSpec((1, model, width), lambda m, c, b: (c, 0, 0))
    per = lambda a, b_: pl.BlockSpec((1, 1, a, b_), lambda m, c, b: (c, m, 0, 0))
    spec = pltpu.PrefetchScalarGridSpec(
        num_scalar_prefetch=1,
        grid=(micro, cols),
        in_specs=[
            pl.BlockSpec((1, rows, model), lambda m, c, b: (m, 0, 0)),
            pl.BlockSpec((1, length, model), lambda m, c, b: (m, 0, 0)),
            weight, weight, weight,
            pl.BlockSpec((1, 1, width), lambda m, c, b: (c, 0, 0)),
            pl.BlockSpec((1, 1, width), lambda m, c, b: (c, 0, 0)),
            pl.BlockSpec((1, 1, rows), lambda m, c, b: (m, 0, 0)),
            pl.BlockSpec((1, length, 1), lambda m, c, b: (m, 0, 0)),
        ],
        out_specs=[per(rows, width), per(8, rows), per(rows, width), per(length, width), per(length, width)],
        scratch_shapes=[
            pltpu.VMEM((length, rows), jnp.float32),
            pltpu.VMEM((width, rows), jnp.float32),
            pltpu.VMEM((8, rows), jnp.float32),
            pltpu.VMEM((8, rows), jnp.float32),
        ],
    )
    shape = lambda a, b_, d=halves: jax.ShapeDtypeStruct((cols, micro, a, b_), d)
    return pl.pallas_call(
        attend_kernel,
        grid_spec=spec,
        out_shape=[shape(rows, width), shape(8, rows, jnp.float32), shape(rows, width), shape(length, width), shape(length, width)],
        compiler_params=pltpu.CompilerParams(vmem_limit_bytes=48 << 20),
        name="attend",
    )(bounds, own, everything, wq, wk, wv, bq[:, None], bv[:, None],
      seg_own[:, None], seg_all[:, :, None])


def attend_back_kernel(bounds, grad_ref, wot_ref, mixed_ref, lse_ref, q_ref, k_ref, v_ref, segq_ref, segk_ref,
                       dq_ref, dk_ref, dv_ref, bias, acc):
    micro = pl.program_id(0)
    low, high = bounds[micro, 0], bounds[micro, 1]
    floats, halves = jnp.float32, jnp.bfloat16
    rows, width = q_ref.shape[2:]
    heads = width // HEAD_DIM

    @pl.when(pl.program_id(1) == 0)
    def _():
        same = segk_ref[0] == segq_ref[0, 0:1]
        bias[...] = jnp.where(same, 0.0, MASK_VALUE)

    mixed_grad = jnp.dot(grad_ref[0], wot_ref[0], preferred_element_type=floats).astype(halves)
    product = mixed_grad.astype(floats) * mixed_ref[0, 0].astype(floats)
    product_high = product.astype(halves)
    product_low = (product - product_high.astype(floats)).astype(halves)
    pick = (
        lax.broadcasted_iota(jnp.int32, (8, width), 1) // HEAD_DIM == lax.broadcasted_iota(jnp.int32, (8, width), 0)
    ).astype(halves)
    inner = contract_cols(pick, product_high) + contract_cols(pick, product_low)
    lane = lax.broadcasted_iota(jnp.int32, (rows, width), 1) // HEAD_DIM
    queries = q_ref[0, 0]
    query_heads = [jnp.where(lane == h, queries, jnp.zeros_like(queries)) for h in range(heads)]
    grad_heads = [jnp.where(lane == h, mixed_grad, jnp.zeros_like(mixed_grad)) for h in range(heads)]
    acc[...] = jnp.zeros_like(acc)
    dk_ref[...] = jnp.zeros_like(dk_ref)
    dv_ref[...] = jnp.zeros_like(dv_ref)

    def step(block, carry):
        at = pl.ds(pl.multiple_of(block * KEY_BLOCK, KEY_BLOCK), KEY_BLOCK)
        keys = k_ref[0, 0, at, :]
        values = v_ref[0, 0, at, :]
        keys_t = keys.T
        mask = bias[at, :]
        key_grad = jnp.zeros((KEY_BLOCK, width), floats)
        value_grad = jnp.zeros((KEY_BLOCK, width), floats)
        for h in range(heads):
            s = contract_cols(keys, query_heads[h]) + mask
            p = jnp.exp(s - lse_ref[0, 0, h : h + 1])
            prob_grad = contract_cols(values, grad_heads[h])
            score_grad = (p * (prob_grad - inner[h : h + 1])).astype(halves)
            value_grad = value_grad + jnp.dot(p.astype(halves), grad_heads[h], preferred_element_type=floats)
            key_grad = key_grad + jnp.dot(score_grad, query_heads[h], preferred_element_type=floats)
            part = pl.ds(h * HEAD_DIM, HEAD_DIM)
            acc[part, :] += jnp.dot(keys_t[h * HEAD_DIM : (h + 1) * HEAD_DIM], score_grad, preferred_element_type=floats)
        dk_ref[0, 0, at, :] = key_grad.astype(halves)
        dv_ref[0, 0, at, :] = value_grad.astype(halves)
        return carry

    lax.fori_loop(low, high, step, 0)
    dq_ref[0, 0] = (acc[...].T * HEAD_DIM ** -0.5).astype(halves)


def attend_back(bounds, grad, wot, mixed, lse, q, k, v, seg_own, seg_all):
    micro, rows, model = grad.shape
    cols, _, length, width = k.shape
    halves = jnp.bfloat16
    per = lambda a, b_: pl.BlockSpec((1, 1, a, b_), lambda m, c, b: (c, m, 0, 0))
    spec = pltpu.PrefetchScalarGridSpec(
        num_scalar_prefetch=1,
        grid=(micro, cols),
        in_specs=[
            pl.BlockSpec((1, rows, model), lambda m, c, b: (m, 0, 0)),
            pl.BlockSpec((1, model, width), lambda m, c, b: (c, 0, 0)),
            per(rows, width), per(8, rows), per(rows, width), per(length, width), per(length, width),
            pl.BlockSpec((1, 1, rows), lambda m, c, b: (m, 0, 0)),
            pl.BlockSpec((1, length, 1), lambda m, c, b: (m, 0, 0)),
        ],
        out_specs=[per(rows, width), per(length, width), per(length, width)],
        scratch_shapes=[pltpu.VMEM((length, rows), jnp.float32), pltpu.VMEM((width, rows), jnp.float32)],
    )
    shape = lambda a, b_, d=halves: jax.ShapeDtypeStruct((cols, micro, a, b_), d)
    return pl.pallas_call(
        attend_back_kernel,
        grid_spec=spec,
        out_shape=[shape(rows, width), shape(length, width), shape(length, width)],
        compiler_params=pltpu.CompilerParams(vmem_limit_bytes=48 << 20),
        name="attend_back",
    )(bounds, grad, wot, mixed, lse, q, k, v, seg_own[:, None], seg_all[:, :, None])


def place(sizes):
    seq, row, col = (lax.axis_index(name) for name in ("seq", "row", "col"))
    lines = {"x": (seq, sizes[0]), "y": (row // 2, sizes[1] // 2), "k": (lax.rem(row, 2), 2), "z": (col, sizes[2])}

    def device(axis, index):
        if axis == "x":
            return (index, row, col)
        if axis == "y":
            return (seq, index * 2 + lax.rem(row, 2), col)
        if axis == "k":
            return (seq, row // 2 * 2 + index, col)
        return (seq, row, index)

    return lines, device


def greet(lines, device):
    barrier = pltpu.get_barrier_semaphore()
    count = 0
    for axis, (mine, size) in lines.items():
        for t in range(1, size):
            pl.semaphore_signal(barrier, inc=1, device_id=device(axis, lax.rem(mine + t, size)), device_id_type=MESH)
            count += 1
    pl.semaphore_wait(barrier, count)


class Post:
    def __init__(self, device, send_sems, recv_sems):
        self.device, self.send_sems, self.recv_sems = device, send_sems, recv_sems
        self.slots, self.sent = {}, []

    def slot(self, key):
        return self.slots.setdefault(key, len(self.slots))

    def copy(self, key, axis, index, source, target):
        n = self.slot(key)
        return pltpu.make_async_remote_copy(
            src_ref=source, dst_ref=target, send_sem=self.send_sems.at[n], recv_sem=self.recv_sems.at[n],
            device_id=self.device(axis, index), device_id_type=MESH,
        )

    def send(self, key, axis, index, source, target, when=None):
        def go():
            self.copy(key, axis, index, source, target).start()

        if when is None:
            go()
        else:
            pl.when(when)(go)
        self.sent.append((key, axis, index, source, target, when))

    def wait(self, key, axis, index, target, when=None):
        def go():
            self.copy(key, axis, index, target, target).wait_recv()

        if when is None:
            go()
        else:
            pl.when(when)(go)

    def close(self):
        for key, axis, index, source, target, when in self.sent:
            def go():
                self.copy(key, axis, index, source, target).wait_send()

            if when is None:
                go()
            else:
                pl.when(when)(go)


def clip(index, size):
    return jnp.clip(index, 0, size - 1)


class LineGather:
    def __init__(self, post, name, axis, line, region, reach=None):
        self.post, self.name, self.axis, self.region = post, name, axis, region
        self.mine, self.size = line
        self.reach = min(self.size - 1, reach or self.size)

    def hop(self, way, t):
        mine, size = self.mine, self.size
        origin, target = mine - way * t, mine + way
        ok = (origin >= 0) & (origin < size) & (target >= 0) & (target < size)
        here = self.region(clip(origin, size))
        self.post.send((self.name, way, t + 1), self.axis, clip(target, size), here, here, ok)

    def start(self):
        for way in (1, -1):
            if self.reach >= 1:
                self.hop(way, 0)

    def finish(self):
        for t in range(1, self.reach + 1):
            for way in (1, -1):
                origin = self.mine - way * t
                ok = (origin >= 0) & (origin < self.size)
                self.post.wait((self.name, way, t), self.axis, clip(self.mine - way, self.size), self.region(clip(origin, self.size)), ok)
                if t < self.reach:
                    self.hop(way, t)


def gather_kernel(sizes, micro, own_ref, shard_ref, every_ref, full_ref, send_sems, recv_sems, local_sems):
    lines, device = place(sizes)
    (x, _), (y, _), (k, _), (z, cols) = (lines[a] for a in "xykz")
    half = shard_ref.shape[-1] // 2
    rows = own_ref.shape[1]
    reach = -(-(DOC_MOST - 1) // rows)
    parts = [pl.ds(p * half, half) for p in (0, 1)]
    local = [pltpu.make_async_copy(shard_ref.at[j], full_ref.at[j, z, x, y, k], local_sems.at[j]) for j in range(3)]
    local += [pltpu.make_async_copy(own_ref.at[m], every_ref.at[m, z], local_sems.at[3 + m]) for m in range(micro)]
    for copy in local:
        copy.start()
    greet(lines, device)
    post = Post(device, send_sems, recv_sems)
    for copy in local:
        copy.wait()
    zs = [LineGather(post, ("z", j), "z", lines["z"], lambda i, j=j: full_ref.at[j, i, x, y, k]) for j in range(3)]
    tokens = [LineGather(post, ("t", m), "z", lines["z"], lambda i, m=m: every_ref.at[m, i], reach) for m in range(micro)]
    second, third = {}, {}
    for j in range(3):
        second[j] = [
            LineGather(post, ("a", j), "y", lines["y"], lambda i, j=j: full_ref.at[j, :, x, i, k, :, parts[0]]),
            LineGather(post, ("b", j), "x", lines["x"], lambda i, j=j: full_ref.at[j, :, i, y, k, :, parts[1]]),
        ]
        third[j] = [
            LineGather(post, ("c", j), "x", lines["x"], lambda i, j=j: full_ref.at[j, :, i, :, k, :, parts[0]]),
            LineGather(post, ("d", j), "y", lines["y"], lambda i, j=j: full_ref.at[j, :, :, i, k, :, parts[1]]),
        ]

    def start(group):
        for line in group:
            line.start()

    def finish(group):
        for line in group:
            line.finish()

    def swap(j):
        plane = full_ref.at[j, :, :, :, k]
        post.send(("k", j), "k", 1 - k, plane, plane)

    start(zs[:1])
    finish(zs[:1])
    start(second[0] + zs[1:2])
    finish(second[0])
    start(third[0])
    finish(zs[1:2])
    start(second[1] + tokens[:1])
    finish(third[0])
    swap(0)
    finish(second[1])
    start(third[1])
    finish(tokens[:1])
    start(zs[2:])
    finish(zs[2:])
    start(second[2] + tokens[1:])
    finish(third[1])
    swap(1)
    finish(second[2])
    start(third[2])
    finish(tokens[1:])
    finish(third[2])
    swap(2)
    for i in range(cols):
        far = (z - i > reach) | (i - z > reach)
        for m in range(micro):
            def fill(m=m, i=i):
                copy = pltpu.make_async_copy(own_ref.at[m], every_ref.at[m, i], local_sems.at[3 + m])
                copy.start()
                copy.wait()

            if i > reach or cols - 1 - i > reach:
                pl.when(far)(fill)
    for j in range(3):
        post.wait(("k", j), "k", 1 - k, full_ref.at[j, :, :, :, 1 - k])
    post.close()


def gather(sizes, own, shard):
    ns, nr, nc = sizes
    ny = nr // 2
    micro, rows, model = own.shape
    _, rb, w = shard.shape
    count = 3 * 2 * (nc - 1) + micro * 2 * (nc - 1) + 3 * (4 * (ny - 1) + 4 * (ns - 1) + 1)
    anywhere = pl.BlockSpec(memory_space=pl.ANY)
    every, full = pl.pallas_call(
        functools.partial(gather_kernel, sizes, micro),
        out_shape=[
            jax.ShapeDtypeStruct((micro, nc, rows, model), own.dtype),
            jax.ShapeDtypeStruct((3, nc, ns, ny, 2, rb, w), shard.dtype),
        ],
        in_specs=[pl.BlockSpec(memory_space=pltpu.VMEM)] * 2,
        out_specs=[anywhere] * 2,
        scratch_shapes=[pltpu.SemaphoreType.DMA((count,)), pltpu.SemaphoreType.DMA((count,)), pltpu.SemaphoreType.DMA((3 + micro,))],
        compiler_params=pltpu.CompilerParams(collective_id=0, has_side_effects=True),
        name="gather",
    )(own, shard)
    return every, full.reshape(3, nc, ns * nr * rb, w)


class LineReduce:
    def __init__(self, post, name, axis, line, region, inbox, add, reach=None):
        self.post, self.name, self.axis, self.region, self.inbox, self.add = post, name, axis, region, inbox, add
        self.mine, self.size = line
        self.reach = min(self.size - 1, reach or self.size)

    def arrived(self, way, e):
        behind, goal = self.mine - way, self.mine + way * e
        return (behind >= 0) & (behind < self.size) & (goal >= 0) & (goal < self.size)

    def take(self, way, e):
        ok = self.arrived(way, e)
        inbox = self.inbox(way, e)
        self.post.wait((self.name, way, e), self.axis, clip(self.mine - way, self.size), inbox, ok)

        @pl.when(ok)
        def _():
            self.add(self.region(clip(self.mine + way * e, self.size)), inbox)

    def forward(self, way, e):
        goal = self.mine + way * e
        ok = (goal >= 0) & (goal < self.size)
        self.post.send((self.name, way, e - 1), self.axis, clip(self.mine + way, self.size),
                       self.region(clip(goal, self.size)), self.inbox(way, e - 1), ok)

    def start(self):
        for way in (1, -1):
            if self.reach >= 1:
                self.forward(way, self.reach)

    def finish(self, last=True):
        for e in range(self.reach - 1, 0, -1):
            for way in (1, -1):
                self.take(way, e)
                self.forward(way, e)
        if last:
            for way in (1, -1):
                if self.reach >= 1:
                    self.take(way, 0)


def reduce_kernel(sizes, micro, own_ref, spread_ref, part_ref, vec_ref, back_ref, block_ref, sums_ref,
                  mine_buf, core_buf, in_a, in_b, in_c, in_d, in_z, tok_buf, tok_in, vec_buf, send_sems, recv_sems, local_sems):
    floats, halves = jnp.float32, jnp.bfloat16
    lines, device = place(sizes)
    (x, ns), (y, ny), (k, _), (z, nc) = (lines[a] for a in "xykz")
    half = part_ref.shape[-1] // 2
    rows = own_ref.shape[1]
    reach = -(-(DOC_MOST - 1) // rows)
    parts = [pl.ds(p * half, half) for p in (0, 1)]
    local = [pltpu.make_async_copy(part_ref.at[j, :, :, :, k], mine_buf.at[j], local_sems.at[j]) for j in range(3)]
    local += [pltpu.make_async_copy(spread_ref.at[m], tok_buf.at[m], local_sems.at[3 + m]) for m in range(micro)]
    for copy in local:
        copy.start()
    greet(lines, device)
    post = Post(device, send_sems, recv_sems)
    for j in range(3):
        post.send(("k", j), "k", 1 - k, part_ref.at[j, :, :, :, 1 - k], core_buf.at[j])

    def plus(target, source):
        target[...] = (target[...].astype(floats) + source[...].astype(floats)).astype(halves)

    def plus_grid(target, source, first, second):
        @pl.loop(0, first * second)
        def _(n):
            plus(target.at[n // second, lax.rem(n, second)], source.at[n // second, lax.rem(n, second)])

    def plus_row(target, source, first):
        @pl.loop(0, first)
        def _(n):
            plus(target.at[n], source.at[n])

    vec_buf[0, 0] = vec_ref[...]

    def vector_start(stage, axis):
        mine, size = lines[axis]
        vec_buf[stage, 1 + mine] = vec_buf[stage, 0]
        for t in range(1, size):
            post.send(("v", stage, t), axis, lax.rem(mine + t, size), vec_buf.at[stage, 0], vec_buf.at[stage, 1 + mine])

    def vector_finish(stage, axis, out):
        mine, size = lines[axis]
        for t in range(1, size):
            origin = lax.rem(mine + size - t, size)
            post.wait(("v", stage, t), axis, origin, vec_buf.at[stage, 1 + origin])
        total = vec_buf[stage, 1]
        for i in range(1, size):
            total = total + vec_buf[stage, 1 + i]
        out[...] = total

    tokens = [
        LineReduce(post, ("t", m), "z", lines["z"], lambda i, m=m: tok_buf.at[m, i],
                   lambda way, e, m=m: tok_in.at[m, (1 - way) // 2, e], plus, reach)
        for m in range(micro)
    ]
    box = lambda way: (1 - way) // 2
    second, third, last = {}, {}, {}
    for j in range(3):
        second[j] = [
            LineReduce(post, ("a", j), "x", lines["x"], lambda i, j=j: mine_buf.at[j, :, i, :, :, parts[0]],
                       lambda way, e, j=j: in_a.at[j, box(way), e], lambda t, s: plus_grid(t, s, nc, ny)),
            LineReduce(post, ("b", j), "y", lines["y"], lambda i, j=j: mine_buf.at[j, :, :, i, :, parts[1]],
                       lambda way, e, j=j: in_b.at[j, box(way), e], lambda t, s: plus_grid(t, s, nc, ns)),
        ]
        third[j] = [
            LineReduce(post, ("c", j), "y", lines["y"], lambda i, j=j: mine_buf.at[j, :, x, i, :, parts[0]],
                       lambda way, e, j=j: in_c.at[j, box(way), e], lambda t, s: plus_row(t, s, nc)),
            LineReduce(post, ("d", j), "x", lines["x"], lambda i, j=j: mine_buf.at[j, :, i, y, :, parts[1]],
                       lambda way, e, j=j: in_d.at[j, box(way), e], lambda t, s: plus_row(t, s, nc)),
        ]
        last[j] = [
            LineReduce(post, ("z", j), "z", lines["z"], lambda i, j=j: mine_buf.at[j, i, x, y],
                       lambda way, e, j=j: in_z.at[j, box(way), e], plus)
        ]

    def start(group):
        for line in group:
            line.start()

    def finish(group):
        for line in group:
            line.finish()

    def core(j):
        local[j].wait()
        post.wait(("k", j), "k", 1 - k, core_buf.at[j])

        @pl.loop(0, nc * ns * ny)
        def _(n):
            at = (n // (ns * ny), lax.rem(n // ny, ns), lax.rem(n, ny))
            plus(mine_buf.at[(j, *at)], core_buf.at[(j, *at)])

    for m in range(micro):
        local[3 + m].wait()
    start(tokens)
    core(0)
    start(second[0])
    vector_start(0, "k")
    core(1)
    start(second[1])
    vector_finish(0, "k", vec_buf.at[1, 0])
    vector_start(1, "y")
    core(2)
    finish(second[0])
    start(third[0])
    start(second[2])
    vector_finish(1, "y", vec_buf.at[2, 0])
    vector_start(2, "x")
    finish(tokens)
    vector_finish(2, "x", vec_buf.at[3, 0])
    vector_start(3, "z")
    finish(second[1])
    start(third[1])
    finish(third[0])
    start(last[0])
    finish(second[2])
    start(third[2])
    finish(third[1])
    start(last[1])
    finish(last[0])
    finish(third[2])
    start(last[2])
    vector_finish(3, "z", sums_ref)
    for m in range(micro):
        back_ref[m] = own_ref[m] + tok_buf[m, z].astype(floats)
    finish(last[1])
    finish(last[2])
    for j in range(3):
        block_ref[j] = mine_buf[j, z, x, y].astype(floats)
    post.close()


def reduce(sizes, own_share, spread, partial, vectors):
    ns, nr, nc = sizes
    ny = nr // 2
    micro, rows, model = own_share.shape
    w = partial.shape[-1]
    rb = partial.shape[2] // (ns * nr)
    halves, floats = jnp.bfloat16, jnp.float32
    reach = min(nc - 1, -(-(DOC_MOST - 1) // rows))
    count = 3 + 2 * (ny - 1 + ns - 1) * 6 + 3 * 2 * (nc - 1) + micro * 2 * reach + (1 + ny - 1 + ns - 1 + nc - 1)
    widest = max(ns, ny, nc, 2)
    extra = -vectors.shape[0] % 8
    vectors = jnp.pad(vectors, ((0, extra), (0, 0)))
    vmem = pl.BlockSpec(memory_space=pltpu.VMEM)
    anywhere = pl.BlockSpec(memory_space=pl.ANY)
    back, blocks, sums = pl.pallas_call(
        functools.partial(reduce_kernel, sizes, micro),
        out_shape=[
            jax.ShapeDtypeStruct((micro, rows, model), floats),
            jax.ShapeDtypeStruct((3, rb, w), floats),
            jax.ShapeDtypeStruct(vectors.shape, floats),
        ],
        in_specs=[vmem, anywhere, anywhere, vmem],
        out_specs=[vmem] * 3,
        scratch_shapes=[
            pltpu.VMEM((3, nc, ns, ny, rb, w), halves),
            pltpu.VMEM((3, nc, ns, ny, rb, w), halves),
            pltpu.VMEM((3, 2, max(ns - 1, 1), nc, ny, rb, w // 2), halves),
            pltpu.VMEM((3, 2, max(ny - 1, 1), nc, ns, rb, w // 2), halves),
            pltpu.VMEM((3, 2, max(ny - 1, 1), nc, rb, w // 2), halves),
            pltpu.VMEM((3, 2, max(ns - 1, 1), nc, rb, w // 2), halves),
            pltpu.VMEM((3, 2, max(nc - 1, 1), rb, w), halves),
            pltpu.VMEM((micro, nc, rows, model), halves),
            pltpu.VMEM((micro, 2, max(reach, 1), rows, model), halves),
            pltpu.VMEM((4, 1 + widest, *vectors.shape), floats),
            pltpu.SemaphoreType.DMA((count,)),
            pltpu.SemaphoreType.DMA((count,)),
            pltpu.SemaphoreType.DMA((3 + micro,)),
        ],
        compiler_params=pltpu.CompilerParams(collective_id=1, has_side_effects=True, vmem_limit_bytes=60 << 20),
        name="reduce",
    )(own_share, spread, partial.reshape(3, nc, ns, ny, 2, rb, w), vectors)
    return back, blocks, sums


Q_AT, K_AT, V_AT, O_AT, WINDOW = 0, 128, 384, 512, 256


def plane(full_ref, c, at, size=WINDOW):
    value = full_ref[c, :, :, :, :, at : at + size]
    return value.reshape(-1, size)


def place_of(rows):
    return lax.broadcasted_iota(jnp.int32, (rows, WINDOW), 1) // HEAD_DIM


def keep(value, places, wanted):
    return jnp.where(places == wanted, value, jnp.zeros_like(value))


def forward_kernel(sizes, micro, own_ref, shard_ref, bias_ref, segq_ref, segk_ref,
                   rest_ref, first_ref, every_ref, biases_ref, mixed_ref, lse_ref, q_ref, k_ref, v_ref,
                   weights, tokens_buf, bias_buf, mask, mixed_buf, lse_buf, q_buf, k_buf, v_buf, acc, top, total,
                   send_sems, recv_sems, local_sems):
    floats, halves = jnp.float32, jnp.bfloat16
    lines, device = place(sizes)
    (x, _), (y, _), (k, _), (z, cols) = (lines[a] for a in "xykz")
    half = shard_ref.shape[-1] // 2
    rows = own_ref.shape[1]
    reach = -(-(DOC_MOST - 1) // rows)
    parts = [pl.ds(p * half, half) for p in (0, 1)]
    low, high = jnp.maximum(z - reach, 0), jnp.minimum(z + reach + 1, cols)
    used = [0]

    def local(source, target):
        copy = pltpu.make_async_copy(source, target, local_sems.at[used[0]])
        used[0] += 1
        copy.start()
        return copy

    targets = [weights.at[0], rest_ref.at[0], rest_ref.at[1]]
    begin = [local(shard_ref.at[j], targets[j].at[z, x, y, k]) for j in range(3)]
    begin += [local(own_ref.at[m], tokens_buf.at[m, z]) for m in range(micro)]
    begin += [local(bias_ref, bias_buf.at[z])]
    greet(lines, device)
    post = Post(device, send_sems, recv_sems)
    for copy in begin:
        copy.wait()
    zs = [LineGather(post, ("z", j), "z", lines["z"], lambda i, j=j: targets[j].at[i, x, y, k]) for j in range(3)]
    tokens = [LineGather(post, ("t", m), "z", lines["z"], lambda i, m=m: tokens_buf.at[m, i], reach) for m in range(micro)]
    small = LineGather(post, "bias", "z", lines["z"], lambda i: bias_buf.at[i])
    second, third = {}, {}
    for j in range(3):
        second[j] = [
            LineGather(post, ("a", j), "y", lines["y"], lambda i, j=j: targets[j].at[:, x, i, k, :, parts[0]]),
            LineGather(post, ("b", j), "x", lines["x"], lambda i, j=j: targets[j].at[:, i, y, k, :, parts[1]]),
        ]
        third[j] = [
            LineGather(post, ("c", j), "x", lines["x"], lambda i, j=j: targets[j].at[:, i, :, k, :, parts[0]]),
            LineGather(post, ("d", j), "y", lines["y"], lambda i, j=j: targets[j].at[:, :, i, k, :, parts[1]]),
        ]

    def start(*group):
        for line in group:
            line.start()

    def finish(*group):
        for line in group:
            line.finish()

    def swap(j):
        own_plane = targets[j].at[:, :, :, k]
        post.send(("k", j), "k", 1 - k, own_plane, own_plane)

    def swapped(j):
        post.wait(("k", j), "k", 1 - k, targets[j].at[:, :, :, 1 - k])

    places = place_of(rows)

    def unit(m, c):
        queries = jnp.dot(own_ref[m], plane(weights.at[0], c, Q_AT), preferred_element_type=floats) + bias_buf[c, 1:2, 0:WINDOW]
        queries = pltpu.roll(queries.astype(halves).astype(floats) * HEAD_DIM ** -0.5, HEAD_DIM, 1)
        queries = jnp.where(places > 0, queries, 0.0).astype(halves)
        q_buf[m, c] = queries
        heads = [keep(queries, places, h + 1) for h in range(3)]
        acc[...] = jnp.zeros_like(acc)
        total[...] = jnp.zeros_like(total)
        top[...] = jnp.full_like(top, 2 * MASK_VALUE)
        key_weight = plane(weights.at[0], c, K_AT)
        value_weight = plane(weights.at[0], c, V_AT)
        value_bias = bias_buf[c, 2:3, 0:WINDOW]

        def step(block, carry):
            rows_at = tokens_buf[m, block]
            keys = jnp.dot(rows_at, key_weight, preferred_element_type=floats).astype(halves)
            values = (jnp.dot(rows_at, value_weight, preferred_element_type=floats) + value_bias).astype(halves)
            k_buf[m, c, block] = keys
            v_buf[m, c, block] = values
            values_t = values.T
            hidden = mask[m, block]
            for h in range(3):
                s = contract_cols(keys, heads[h]) + hidden
                old = top[h : h + 1]
                new = jnp.maximum(old, jnp.max(s, 0, keepdims=True))
                p = jnp.exp(s - new)
                shrink = jnp.exp(old - new)
                top[h : h + 1] = new
                total[h : h + 1] = total[h : h + 1] * shrink + jnp.sum(p, 0, keepdims=True)
                at = pl.ds((h + 1) * HEAD_DIM, HEAD_DIM)
                acc[at, :] = acc[at, :] * shrink + jnp.dot(
                    values_t[h * HEAD_DIM : (h + 1) * HEAD_DIM], p.astype(halves), preferred_element_type=floats
                )
            return carry

        lax.fori_loop(low, high, step, 0)
        for h in range(3):
            at = pl.ds((h + 1) * HEAD_DIM, HEAD_DIM)
            acc[at, :] = acc[at, :] / total[h : h + 1]
        mixed_buf[c, m] = acc[...].T.astype(halves)
        lse_buf[m, c] = top[...] + jnp.log(jnp.maximum(total[...], 1e-30))

    def units(m, first, last):
        @pl.loop(first, last)
        def _(c):
            unit(m, c)

    def masks(m):
        @pl.loop(low, high)
        def _(block):
            same = jnp.broadcast_to(segk_ref[m, pl.ds(block, 1), :], (rows, rows)).T == segq_ref[m, 0:1]
            mask[m, block] = jnp.where(same, 0.0, MASK_VALUE)

    done = []
    middle = max(cols // 2, 1)
    start(small, zs[0])
    finish(zs[0])
    start(*second[0], tokens[0])
    for m in range(micro):
        masks(m)
    finish(small, *second[0])
    start(*third[0])
    finish(tokens[0])
    start(zs[1])
    finish(*third[0])
    swap(0)
    finish(zs[1])
    start(*second[1], zs[2])
    swapped(0)
    units(0, 0, middle)
    finish(*second[1])
    start(*third[1])
    finish(zs[2])
    for m in range(1, micro):
        start(tokens[m])
    done.append(local(weights.at[0], first_ref))
    units(0, middle, cols)
    finish(*tokens[1:])
    finish(*third[1])
    swap(1)
    start(*second[2])
    for m in range(1, micro):
        units(m, 0, middle)
        if m == 1:
            finish(*second[2])
            start(*third[2])
        units(m, middle, cols)
    for m in range(micro):
        @pl.loop(low, high)
        def _(block, m=m):
            copy = pltpu.make_async_copy(tokens_buf.at[m, block], every_ref.at[m, block], local_sems.at[used[0] + m])
            copy.start()
            copy.wait()
    used[0] += micro
    for source, target in ((bias_buf, biases_ref), (mixed_buf, mixed_ref), (lse_buf, lse_ref), (q_buf, q_ref), (k_buf, k_ref), (v_buf, v_ref)):
        done.append(local(source, target))
    if micro == 1:
        finish(*second[2])
        start(*third[2])
    finish(*third[2])
    swap(2)
    swapped(1)
    swapped(2)
    for copy in done:
        copy.wait()
    post.close()


def forward(sizes, own, shard, bias, seg_own, seg_all):
    ns, nr, nc = sizes
    ny = nr // 2
    micro, rows, model = own.shape
    _, rb, w = shard.shape
    halves, floats = own.dtype, jnp.float32
    reach = min(nc - 1, -(-(DOC_MOST - 1) // rows))
    count = (3 + 1) * 2 * (nc - 1) + micro * 2 * reach + 3 * (4 * (ny - 1) + 4 * (ns - 1) + 1)
    anywhere = pl.BlockSpec(memory_space=pl.ANY)
    vmem = pl.BlockSpec(memory_space=pltpu.VMEM)
    length = nc * rows
    arrays = [
        ((2, nc, ns, ny, 2, rb, w), halves), ((nc, ns, ny, 2, rb, w), halves), ((micro, nc, rows, model), halves),
        ((nc, *bias.shape), floats), ((nc, micro, rows, WINDOW), halves), ((micro, nc, 8, rows), floats),
        ((micro, nc, rows, WINDOW), halves), ((micro, nc, nc, rows, WINDOW), halves), ((micro, nc, nc, rows, WINDOW), halves),
    ]
    shapes = [pltpu.VMEM(shape, kind) for shape, kind in arrays]
    return pl.pallas_call(
        functools.partial(forward_kernel, sizes, micro),
        out_shape=[jax.ShapeDtypeStruct(shape, kind) for shape, kind in arrays],
        in_specs=[vmem] * 5,
        out_specs=[anywhere] * len(arrays),
        scratch_shapes=[
            pltpu.VMEM((1, nc, ns, ny, 2, rb, w), halves),
            shapes[2], shapes[3], pltpu.VMEM((micro, nc, rows, rows), floats), *shapes[4:],
            pltpu.VMEM((WINDOW, rows), floats), pltpu.VMEM((8, rows), floats), pltpu.VMEM((8, rows), floats),
            pltpu.SemaphoreType.DMA((count,)), pltpu.SemaphoreType.DMA((count,)), pltpu.SemaphoreType.DMA((20,)),
        ],
        compiler_params=pltpu.CompilerParams(collective_id=2, has_side_effects=True, vmem_limit_bytes=60 << 20),
        name="forward",
    )(own, shard, bias, seg_own.astype(floats)[:, None], seg_all.astype(floats).reshape(micro, nc, rows))


def middle_kernel(cols, own_ref, mixed_ref, out_ref, hidden_ref, down_ref, bias_ref, vector_ref, cot_ref,
                  outputs_ref, first_grad_ref, attn_grad_ref, part_ref, sums_ref,
                  normal, scale, normed, normed_low, normed_t, grad_low, grad_t, act_buf, slope_buf, total):
    floats, halves = jnp.float32, jnp.bfloat16
    step = pl.program_id(0)
    rows, model = own_ref.shape
    chunks = [pl.ds(r * 256, 256) for r in range(rows // 256)]
    bands = [pl.ds(n * 256, 256) for n in range(model // 256)]
    vector = lambda i: vector_ref[i : i + 1]

    @pl.when(step == 0)
    def _():
        sums_ref[...] = jnp.zeros_like(sums_ref)
        for chunk in chunks:
            first_sum = own_ref[chunk].astype(floats) + vector(0)
            for c in range(cols):
                first_sum = first_sum + contract_cols(mixed_ref[c, chunk], out_ref[c])
            normal_one, scale_one = norm_parts(first_sum)
            normal[chunk] = normal_one
            scale[chunk] = jnp.broadcast_to(scale_one, (256, 128))
            norm_one = normal_one * vector(1) + vector(2)
            total[chunk] = norm_one + vector(3)
            normed_low[chunk] = norm_one.astype(halves)
            normed_t[:, chunk] = norm_one.astype(halves).T

    @pl.when(step < cols)
    def _():
        for chunk in chunks:
            for band in bands:
                hidden = jnp.dot(normed_low[chunk], hidden_ref[0, 0, :, band], preferred_element_type=floats) + bias_ref[0, 0:1, band]
                half_erf = 0.5 * lax.erf(hidden * 0.7071067811865476) + 0.5
                act_buf[step, chunk, band] = (hidden * half_erf).astype(halves)
                slope_buf[step, chunk, band] = (half_erf + hidden * (jnp.exp(-0.5 * hidden * hidden) * 0.3989422804014327)).astype(halves)
        for chunk in chunks:
            for band in bands:
                total[chunk, band] += contract_cols(act_buf[step, chunk], down_ref[0, 0, band, :])

    @pl.when(step == cols - 1)
    def _():
        for chunk in chunks:
            normal_two, scale_two = norm_parts(total[chunk])
            outputs_ref[chunk] = (normal_two * vector(4) + vector(5)).astype(halves)
            cot = cot_ref[chunk].astype(floats)
            second_grad = norm_back(cot * vector(4), normal_two, scale_two)
            total[chunk] = second_grad
            grad_low[chunk] = second_grad.astype(halves)
            grad_t[:, chunk] = second_grad.astype(halves).T
            sums_ref[3:4] += jnp.sum(second_grad, 0, keepdims=True)
            sums_ref[4:5] += jnp.sum(cot * normal_two, 0, keepdims=True)
            sums_ref[5:6] += jnp.sum(cot, 0, keepdims=True)

    @pl.when(step >= cols)
    def _():
        c = step - cols
        bias_total = [jnp.zeros((1, 256), floats) for _ in bands]
        for chunk in chunks:
            for n, band in enumerate(bands):
                pre = jnp.dot(grad_low[chunk], down_ref[0, 0, :, band], preferred_element_type=floats)
                pre = (pre * slope_buf[c, chunk, band].astype(floats)).astype(halves)
                slope_buf[c, chunk, band] = pre
                bias_total[n] = bias_total[n] + jnp.sum(pre.astype(floats), 0, keepdims=True)
        for n, band in enumerate(bands):
            sums_ref[pl.ds(8 + c, 1), band] = bias_total[n]
        for band in bands:
            for side in bands:
                part_ref[0, 0, side, band] = jnp.dot(normed_t[side, :], slope_buf[c, :, band], preferred_element_type=floats).astype(halves)
                part_ref[1, 0, side, band] = jnp.dot(grad_t[side, :], act_buf[c, :, band], preferred_element_type=floats).astype(halves)
        for chunk in chunks:
            for band in bands:
                total[chunk, band] += contract_cols(slope_buf[c, chunk], hidden_ref[0, 0, band, :])

    @pl.when(step == 2 * cols - 1)
    def _():
        for chunk in chunks:
            normed_grad, normal_one = total[chunk], normal[chunk]
            first_grad = norm_back(normed_grad * vector(1), normal_one, scale[chunk, 0:1])
            first_grad_ref[chunk] = first_grad
            attn_grad_ref[chunk] = first_grad.astype(halves)
            sums_ref[0:1] += jnp.sum(first_grad, 0, keepdims=True)
            sums_ref[1:2] += jnp.sum(normed_grad * normal_one, 0, keepdims=True)
            sums_ref[2:3] += jnp.sum(normed_grad, 0, keepdims=True)


def middle(own, mixed, first, rest, biases, vectors, cot):
    rows, model = own.shape
    cols = first.shape[0]
    halves, floats = jnp.bfloat16, jnp.float32
    whole = lambda shape: pl.BlockSpec(shape, lambda i: (0,) * len(shape))
    wide = lambda kind: pltpu.VMEM((rows, model), kind)
    return pl.pallas_call(
        functools.partial(middle_kernel, cols),
        grid=(2 * cols,),
        in_specs=[
            whole((rows, model)), whole(mixed.shape),
            pl.BlockSpec((cols, model, WINDOW), lambda i: (0, 0, O_AT // WINDOW)),
            pl.BlockSpec((1, 1, model, rest.shape[-1]), lambda i: (0, lax.rem(i, cols), 0, 0)),
            pl.BlockSpec((1, 1, model, rest.shape[-1]), lambda i: (1, lax.rem(i, cols), 0, 0)),
            pl.BlockSpec((1, *biases.shape[1:]), lambda i: (lax.rem(i, cols), 0, 0)),
            whole(vectors.shape), whole((rows, model)),
        ],
        out_specs=[
            whole((rows, model)), whole((rows, model)), whole((rows, model)),
            pl.BlockSpec((2, 1, model, rest.shape[-1]), lambda i: (0, jnp.maximum(i - cols, 0), 0, 0)),
            whole((8 + cols + -cols % 8, model)),
        ],
        out_shape=[
            jax.ShapeDtypeStruct((rows, model), halves), jax.ShapeDtypeStruct((rows, model), floats),
            jax.ShapeDtypeStruct((rows, model), halves), jax.ShapeDtypeStruct(rest.shape, halves),
            jax.ShapeDtypeStruct((8 + cols + -cols % 8, model), floats),
        ],
        scratch_shapes=[
            wide(floats), pltpu.VMEM((rows, 128), floats), wide(floats), wide(halves), pltpu.VMEM((model, rows), halves), wide(halves),
            pltpu.VMEM((model, rows), halves), pltpu.VMEM((cols, rows, rest.shape[-1]), halves),
            pltpu.VMEM((cols, rows, rest.shape[-1]), halves), wide(floats),
        ],
        compiler_params=pltpu.CompilerParams(vmem_limit_bytes=56 << 20),
        name="middle",
    )(own, mixed, first, rest, rest, biases, vectors, cot)


class Inbox:
    def __init__(self, ref, size):
        self.ref, self.size = ref, size

    def __call__(self, way, e):
        return self.ref.at[0 if self.size == 2 else (1 - way) // 2, e]


def backward_kernel(sizes, micro, grad_ref, share_ref, first_ref, every_ref, mixed_ref, lse_ref, q_ref, k_ref, v_ref,
                    segq_ref, segk_ref, part_ref, vec_ref,
                    back_ref, block_ref, sums_ref,
                    mine_buf, core_buf, stage_buf, in_a, in_b, in_c, in_d, in_z, tok_buf, tok_in, vec_buf,
                    weights, mixed_buf, q_buf, k_buf, v_buf, every_t, grad_t, x_buf, mask, acc, spread, block_sum,
                    send_sems, recv_sems, local_sems):
    floats, halves = jnp.float32, jnp.bfloat16
    lines, device = place(sizes)
    (x, ns), (y, ny), (k, _), (z, cols) = (lines[a] for a in "xykz")
    model = first_ref.shape[1]
    half = part_ref.shape[-1] // 2
    rb = part_ref.shape[-2]
    rows = grad_ref.shape[1]
    reach = -(-(DOC_MOST - 1) // rows)
    parts = [pl.ds(p * half, half) for p in (0, 1)]
    low, high = jnp.maximum(z - reach, 0), jnp.minimum(z + reach + 1, cols)
    used = [0]

    def local(source, target):
        copy = pltpu.make_async_copy(source, target, local_sems.at[used[0]])
        used[0] += 1
        copy.start()
        return copy

    loads = [local(*pair) for pair in ((first_ref, weights), (mixed_ref, mixed_buf), (q_ref, q_buf))]
    loads += [local(k_ref.at[0], k_buf.at[0]), local(v_ref.at[0], v_buf.at[0])]
    loads += [local(share_ref, back_ref)]
    planes = [local(part_ref.at[j, :, :, :, k], mine_buf.at[j + 1]) for j in range(2)]
    more = [[local(k_ref.at[m], k_buf.at[m]), local(v_ref.at[m], v_buf.at[m])] for m in range(1, micro)]
    greet(lines, device)
    post = Post(device, send_sems, recv_sems)
    for j in range(2):
        post.send(("k", j + 1), "k", 1 - k, part_ref.at[j, :, :, :, 1 - k], core_buf.at[j + 1])

    def plus(target, source):
        target[...] = (target[...].astype(floats) + source[...].astype(floats)).astype(halves)

    def plus_grid(target, source, first, second):
        @pl.loop(0, first * second)
        def _(n):
            at = (n // second, lax.rem(n, second))
            plus(target.at[at], source.at[at])

    def plus_row(target, source, first):
        @pl.loop(0, first)
        def _(n):
            plus(target.at[n], source.at[n])

    class Stream:
        def __init__(self, name, j, begin, size):
            cs = pl.ds(begin, size)
            self.j, self.begin, self.size = j, begin, size
            self.second = [
                LineReduce(post, (name, "a"), "x", lines["x"], lambda i: mine_buf.at[j, cs, i, :, :, parts[0]],
                           lambda way, e: Inbox(in_a.at[j], ns)(way, e).at[cs], lambda t, s: plus_grid(t, s, size, ny)),
                LineReduce(post, (name, "b"), "y", lines["y"], lambda i: mine_buf.at[j, cs, :, i, :, parts[1]],
                           lambda way, e: Inbox(in_b.at[j], ny)(way, e).at[cs], lambda t, s: plus_grid(t, s, size, ns)),
            ]
            self.third = [
                LineReduce(post, (name, "c"), "y", lines["y"], lambda i: mine_buf.at[j, cs, x, i, :, parts[0]],
                           lambda way, e: Inbox(in_c.at[j], ny)(way, e).at[cs], lambda t, s: plus_row(t, s, size)),
                LineReduce(post, (name, "d"), "x", lines["x"], lambda i: mine_buf.at[j, cs, i, y, :, parts[1]],
                           lambda way, e: Inbox(in_d.at[j], ns)(way, e).at[cs], lambda t, s: plus_row(t, s, size)),
            ]

    ffn = [None] + [Stream(("s", j), j, 0, cols) for j in (1, 2)]
    cut = max(cols // 2, 1)
    attn = [Stream(("s", 0, begin), 0, begin, min(cut, cols - begin)) for begin in range(0, cols, cut)]
    last = [
        LineReduce(post, ("z", j), "z", lines["z"], lambda i, j=j: mine_buf.at[j, i, x, y],
                   lambda way, e, j=j: in_z.at[j, (1 - way) // 2, e], plus)
        for j in range(3)
    ]

    def plus_back(m):
        def add(target, source):
            back_ref[m] += source[...].astype(floats)

        return add

    tokens = [
        LineReduce(post, ("t", m), "z", lines["z"], lambda i, m=m: tok_buf.at[m, i],
                   lambda way, e, m=m: tok_in.at[m, (1 - way) // 2, e], plus, reach)
        for m in range(micro)
    ]

    def start(*group):
        for line in group:
            line.start()

    def finish(*group):
        for line in group:
            line.finish()

    def tokens_finish(m):
        tokens[m].finish(last=False)
        tokens[m].add = plus_back(m)
        for way in (1, -1):
            if tokens[m].reach >= 1:
                tokens[m].take(way, 0)

    def core(j):
        planes[j - 1].wait()
        post.wait(("k", j), "k", 1 - k, core_buf.at[j])

        @pl.loop(0, cols * ns * ny)
        def _(n):
            at = (n // (ns * ny), lax.rem(n // ny, ns), lax.rem(n, ny))
            plus(mine_buf.at[(j, *at)], core_buf.at[(j, *at)])

    def vector_start(stage, axis):
        mine, size = lines[axis]
        vec_buf[stage, 1 + mine] = vec_buf[stage, 0]
        for t in range(1, size):
            post.send(("v", stage, t), axis, lax.rem(mine + t, size), vec_buf.at[stage, 0], vec_buf.at[stage, 1 + mine])

    def vector_finish(stage, axis, out):
        mine, size = lines[axis]
        for t in range(1, size):
            origin = lax.rem(mine + size - t, size)
            post.wait(("v", stage, t), axis, origin, vec_buf.at[stage, 1 + origin])
        total = vec_buf[stage, 1]
        for i in range(1, size):
            total = total + vec_buf[stage, 1 + i]
        out[...] = total

    places = place_of(rows)
    small = vec_ref.shape[0]
    vec_buf[0, 0] = jnp.zeros_like(vec_buf[0, 0])
    vec_buf[0, 0, 0:small] = vec_ref[...]

    def masks(m):
        @pl.loop(low, high)
        def _(block):
            same = jnp.broadcast_to(segk_ref[m, pl.ds(block, 1), :], (rows, rows)).T == segq_ref[m, 0:1]
            mask[block] = jnp.where(same, 0.0, MASK_VALUE)

    def turn(m):
        for block in range(cols):
            inside = (low <= block) & (block < high)
            at = pl.ds((m * cols + block) * rows, rows)

            @pl.when(inside)
            def _():
                copy = pltpu.make_async_copy(every_ref.at[m, block], x_buf, local_sems.at[used[0] + m])
                copy.start()
                copy.wait()
                every_t[:, at] = x_buf[...].T

            if block > reach or cols - 1 - block > reach:
                @pl.when(jnp.logical_not(inside))
                def _():
                    every_t[:, at] = jnp.zeros((model, rows), halves)

                    @pl.loop(0, cols)
                    def _(c):
                        k_buf[m, c, block] = jnp.zeros((rows, WINDOW), halves)
                        v_buf[m, c, block] = jnp.zeros((rows, WINDOW), halves)

    def unit(m, c):
        mixed_grad = jnp.dot(grad_ref[m], weights[c, :, O_AT : O_AT + WINDOW], preferred_element_type=floats).astype(halves)
        mixed_grad = jnp.where(places > 0, mixed_grad.astype(floats), 0.0)
        product = mixed_grad * mixed_buf[c, m].astype(floats)
        product_high = product.astype(halves)
        product_low = (product - product_high.astype(floats)).astype(halves)
        pick = (
            lax.broadcasted_iota(jnp.int32, (8, WINDOW), 1) // HEAD_DIM == lax.broadcasted_iota(jnp.int32, (8, WINDOW), 0) + 1
        ).astype(floats).astype(halves)
        inner = contract_cols(pick, product_high) + contract_cols(pick, product_low)
        value_side = pltpu.roll(mixed_grad, WINDOW - HEAD_DIM, 1).astype(halves)
        queries = q_buf[m, c]
        query_heads = [keep(queries, places, h + 1) for h in range(3)]
        grad_heads = [keep(value_side, places, h) for h in range(3)]
        acc[...] = jnp.zeros_like(acc)
        key_weight = weights[c, :, K_AT : K_AT + WINDOW]
        value_weight = weights[c, :, V_AT : V_AT + WINDOW]

        def step(block, value_bias):
            keys = k_buf[m, c, block]
            values = v_buf[m, c, block]
            keys_t = keys.T
            hidden = mask[block]
            key_grad = jnp.zeros((rows, WINDOW), floats)
            value_grad = jnp.zeros((rows, WINDOW), floats)
            for h in range(3):
                p = jnp.exp(contract_cols(keys, query_heads[h]) + hidden - lse_ref[m, c, h : h + 1])
                prob_grad = contract_cols(values, grad_heads[h])
                score_grad = (p * (prob_grad - inner[h : h + 1])).astype(halves)
                value_grad = value_grad + jnp.dot(p.astype(halves), grad_heads[h], preferred_element_type=floats)
                key_grad = key_grad + jnp.dot(score_grad, query_heads[h], preferred_element_type=floats)
                at = pl.ds(h * HEAD_DIM, HEAD_DIM)
                acc[at, :] += jnp.dot(keys_t[(h + 1) * HEAD_DIM : (h + 2) * HEAD_DIM], score_grad, preferred_element_type=floats)
            key_low, value_low = key_grad.astype(halves), value_grad.astype(halves)
            k_buf[m, c, block] = key_low
            v_buf[m, c, block] = value_low
            spread[block] += contract_cols(key_low, key_weight) + contract_cols(value_low, value_weight)
            return value_bias + jnp.sum(value_low.astype(floats), 0, keepdims=True)

        value_bias = lax.fori_loop(low, high, step, jnp.zeros((1, WINDOW), floats))
        query_low = (acc[...].T * HEAD_DIM ** -0.5).astype(halves)
        q_buf[m, c] = query_low
        vec_buf[0, 0, pl.ds(small + c, 1), 0:WINDOW] += jnp.sum(query_low.astype(floats), 0, keepdims=True)
        vec_buf[0, 0, pl.ds(small + c, 1), WINDOW : 2 * WINDOW] += value_bias
        back_ref[m] += contract_cols(query_low, weights[c, :, Q_AT : Q_AT + WINDOW])

    def units(m, first, last_):
        @pl.loop(first, last_)
        def _(c):
            unit(m, c)

    def send_tokens(m):
        back_ref[m] += spread[z]

        @pl.loop(low, high)
        def _(block):
            tok_buf[m, block] = spread[block].astype(halves)

        start(tokens[m])

    def weight_grads(c):
        for begin in range(0, model, 256):
            side = pl.ds(begin, 256)
            block_sum[side] = jnp.zeros((256, 4 * (WINDOW - HEAD_DIM)), floats)
            out = 0
            for m in range(micro):
                mine_at = pl.ds(pl.multiple_of((m * cols + z) * rows, rows), rows)
                block_sum[side, Q_AT : Q_AT + WINDOW] += jnp.dot(every_t[side, mine_at], q_buf[m, c], preferred_element_type=floats)
                all_at = pl.ds(m * cols * rows, cols * rows)
                block_sum[side, K_AT : K_AT + WINDOW] += jnp.dot(
                    every_t[side, all_at], k_buf[m, c].reshape(-1, WINDOW), preferred_element_type=floats)
                block_sum[side, V_AT : V_AT + WINDOW] += jnp.dot(
                    every_t[side, all_at], v_buf[m, c].reshape(-1, WINDOW), preferred_element_type=floats)
                block_sum[side, O_AT : O_AT + WINDOW] += jnp.dot(
                    grad_t[side, m * rows : (m + 1) * rows], mixed_buf[c, m], preferred_element_type=floats)
        for i in range(ns * ny):
            ours = pl.ds(pl.multiple_of((2 * i + k) * rb, 16), rb)
            theirs = pl.ds(pl.multiple_of((2 * i + 1 - k) * rb, 16), rb)
            mine_buf[0, c, i // ny, i % ny] = block_sum[ours].astype(halves)
            stage_buf[c, i // ny, i % ny] = block_sum[theirs].astype(halves)

    def attn_core(stream):
        cs = pl.ds(stream.begin, stream.size)

        @pl.loop(stream.begin, stream.begin + stream.size)
        def _(c):
            weight_grads(c)

        post.send(("k", 0, stream.begin), "k", 1 - k, stage_buf.at[cs], core_buf.at[0, cs])

    def attn_add(stream):
        cs = pl.ds(stream.begin, stream.size)
        post.wait(("k", 0, stream.begin), "k", 1 - k, core_buf.at[0, cs])

        @pl.loop(0, stream.size * ns * ny)
        def _(n):
            at = (stream.begin + n // (ns * ny), lax.rem(n // ny, ns), lax.rem(n, ny))
            plus(mine_buf.at[(0, *at)], core_buf.at[(0, *at)])

    for copy in loads:
        copy.wait()
    masks(0)
    spread[...] = jnp.zeros_like(spread)
    units(0, 0, 1)
    core(1)
    start(*ffn[1].second)
    for m in range(micro):
        for copy in more[m - 1] if m else ():
            copy.wait()
        turn(m)
        grad_t[:, m * rows : (m + 1) * rows] = grad_ref[m].T
    core(2)
    start(*ffn[2].second)
    units(0, 1, 3)
    finish(*ffn[1].second)
    start(*ffn[1].third)
    units(0, 3, cols)
    send_tokens(0)
    for m in range(1, micro):
        masks(m)
        spread[...] = jnp.zeros_like(spread)
        units(m, 0, 1)
        if m == 1:
            finish(*ffn[2].second)
            start(*ffn[2].third)
            finish(*ffn[1].third)
            start(last[1])
        units(m, 1, 2)
        if m == 1:
            tokens_finish(0)
        units(m, 2, 3)
        if m == 1:
            finish(*ffn[2].third)
            start(last[2])
        units(m, 3, cols)
        send_tokens(m)
    vector_start(0, "k")
    attn_core(attn[0])
    vector_finish(0, "k", vec_buf.at[1, 0])
    vector_start(1, "y")
    for stream in attn[1:]:
        attn_core(stream)
    attn_add(attn[0])
    start(*attn[0].second)
    vector_finish(1, "y", vec_buf.at[2, 0])
    vector_start(2, "x")
    finish(last[1])
    for stream in attn[1:]:
        attn_add(stream)
        start(*stream.second)
    vector_finish(2, "x", vec_buf.at[3, 0])
    vector_start(3, "z")
    for m in range(1, micro):
        tokens_finish(m)
    finish(last[2])
    for stream in attn:
        finish(*stream.second)
        start(*stream.third)
    vector_finish(3, "z", sums_ref)
    for stream in attn:
        finish(*stream.third)
    start(last[0])
    for j in (1, 2):
        block_ref[j] = mine_buf[j, z, x, y].astype(floats)
    finish(last[0])
    block_ref[0] = mine_buf[0, z, x, y].astype(floats)
    post.close()


def backward(sizes, grad, share, first, every, mixed, lse, q, k, v, seg_own, seg_all, part, vectors):
    ns, nr, nc = sizes
    ny = nr // 2
    micro, rows, model = grad.shape
    w = part.shape[-1]
    rb = model // (ns * nr)
    halves, floats = jnp.bfloat16, jnp.float32
    reach = min(nc - 1, -(-(DOC_MOST - 1) // rows))
    streams = 2 + -(-nc // max(nc // 2, 1))
    count = 2 + nc + 4 * (ny - 1 + ns - 1) * streams + 3 * 2 * (nc - 1) + micro * 2 * reach + (1 + ny - 1 + ns - 1 + nc - 1)
    widest = max(ns, ny, nc, 2)
    ways = lambda n: 1 if n == 2 else 2
    vec_shape = (vectors.shape[0] + nc + -nc % 8, model)
    vmem = pl.BlockSpec(memory_space=pltpu.VMEM)
    anywhere = pl.BlockSpec(memory_space=pl.ANY)
    buf = lambda *shape, kind=halves: pltpu.VMEM(shape, kind)
    return pl.pallas_call(
        functools.partial(backward_kernel, sizes, micro),
        out_shape=[
            jax.ShapeDtypeStruct((micro, rows, model), floats),
            jax.ShapeDtypeStruct((3, rb, w), floats),
            jax.ShapeDtypeStruct(vec_shape, floats),
        ],
        in_specs=[vmem, anywhere, anywhere, anywhere, anywhere, vmem, anywhere, anywhere, anywhere, vmem, vmem, anywhere, vmem],
        out_specs=[vmem] * 3,
        scratch_shapes=[
            buf(3, nc, ns, ny, rb, w), buf(3, nc, ns, ny, rb, w), buf(nc, ns, ny, rb, w),
            buf(3, ways(ns), max(ns - 1, 1), nc, ny, rb, w // 2), buf(3, ways(ny), max(ny - 1, 1), nc, ns, rb, w // 2),
            buf(3, ways(ny), max(ny - 1, 1), nc, rb, w // 2), buf(3, ways(ns), max(ns - 1, 1), nc, rb, w // 2),
            buf(3, 2, max(nc - 1, 1), rb, w), buf(micro, nc, rows, model), buf(micro, 2, max(reach, 1), rows, model),
            buf(4, 1 + widest, *vec_shape, kind=floats),
            buf(nc, model, w), buf(nc, micro, rows, WINDOW), buf(micro, nc, rows, WINDOW),
            buf(micro, nc, nc, rows, WINDOW), buf(micro, nc, nc, rows, WINDOW),
            buf(model, micro * nc * rows), buf(model, micro * rows), buf(rows, model),
            buf(nc, rows, rows, kind=floats), buf(WINDOW, rows, kind=floats), buf(nc, rows, model, kind=floats), buf(model, w, kind=floats),
            pltpu.SemaphoreType.DMA((count,)), pltpu.SemaphoreType.DMA((count,)), pltpu.SemaphoreType.DMA((24,)),
        ],
        compiler_params=pltpu.CompilerParams(collective_id=3, has_side_effects=True, vmem_limit_bytes=62 << 20),
        name="backward",
    )(grad, share, first, every, mixed, lse, q, k, v, seg_own.astype(floats)[:, None], seg_all.astype(floats).reshape(micro, nc, rows),
      part.reshape(2, nc, ns, ny, 2, rb, w), vectors)


def per_device_plain(sizes, inputs, segment_ids, query_weight, key_weight, value_weight, query_bias, value_bias,
               output_weight, output_bias, first_gain, first_shift, hidden_weight, hidden_bias, down_weight,
               down_bias, second_gain, second_shift, cotangent):
    floats, halves = jnp.float32, jnp.bfloat16
    cols = sizes[2]
    micro, _, rows, model = inputs.shape
    length = segment_ids.shape[-1]
    width = query_weight.shape[1]
    here = lax.axis_index("col")
    own = inputs[:, 0]
    shard = jnp.stack([
        jnp.concatenate([query_weight, key_weight, value_weight, output_weight.T], 1),
        hidden_weight,
        down_weight.T,
    ])
    biases = lax.all_gather(jnp.concatenate([query_bias, value_bias, hidden_bias]), "col", axis=0)
    everything, gathered = gather(sizes, own, shard)
    everything = everything.reshape(micro, length, model)
    attn_weights = gathered[0]
    wq, wk, wv, wot = (attn_weights[:, :, i * width : (i + 1) * width] for i in range(4))
    hidden_full, down_full = gathered[1], gathered[2]
    bq, bv, bh = biases[:, :width], biases[:, width : 2 * width], biases[:, 2 * width :]
    seg_all = segment_ids[:, 0]
    seg_own = lax.dynamic_slice_in_dim(seg_all, here * rows, rows, 1)
    first_key = jnp.sum((seg_all < seg_own[:, :1]).astype(jnp.int32), 1)
    last_key = jnp.sum((seg_all <= seg_own[:, -1:]).astype(jnp.int32), 1)
    bounds = jnp.stack([first_key // KEY_BLOCK, (last_key + KEY_BLOCK - 1) // KEY_BLOCK], 1)

    mixed, lse, q, k, v = attend(bounds, own, everything, wq, wk, wv, bq.astype(floats), bv.astype(floats), seg_own, seg_all)
    total = micro * rows
    flat = lambda a: a.reshape(total, -1)
    mixed_flat = mixed.reshape(cols, total, width)
    attn = sum(contract_cols(mixed_flat[c], wot[c]) for c in range(cols))
    first_sum = flat(own).astype(floats) + attn + output_bias.astype(floats)
    normal_one, scale_one = norm_parts(first_sum)
    gain_one = first_gain.astype(floats)
    normed = normal_one * gain_one + first_shift.astype(floats)
    normed_low = normed.astype(halves)
    ffn = 0
    activated, slopes = [], []
    for c in range(cols):
        hidden = jnp.dot(normed_low, hidden_full[c], preferred_element_type=floats) + bh[c].astype(floats)
        half_erf = 0.5 * lax.erf(hidden * 0.7071067811865476) + 0.5
        act = (hidden * half_erf).astype(halves)
        slope = half_erf + hidden * (jnp.exp(-0.5 * hidden * hidden) * 0.3989422804014327)
        activated.append(act)
        slopes.append(slope.astype(halves))
        ffn = ffn + contract_cols(act, down_full[c])
    second_sum = normed + ffn + down_bias.astype(floats)
    normal_two, scale_two = norm_parts(second_sum)
    gain_two = second_gain.astype(floats)
    outputs = (normal_two * gain_two + second_shift.astype(floats)).astype(halves)
    cot = flat(cotangent[:, 0]).astype(floats)
    second_grad = norm_back(cot * gain_two, normal_two, scale_two)
    ffn_grad = second_grad.astype(halves)
    hidden_grads, down_grads, hidden_bias_grads = [], [], []
    normed_grad = second_grad
    for c in range(cols):
        pre = (jnp.dot(ffn_grad, down_full[c], preferred_element_type=floats) * slopes[c].astype(floats)).astype(halves)
        hidden_grads.append(contract_rows(normed_low, pre).astype(halves))
        down_grads.append(contract_rows(ffn_grad, activated[c]).astype(halves))
        hidden_bias_grads.append(jnp.sum(pre.astype(floats), 0))
        normed_grad = normed_grad + contract_cols(pre, hidden_full[c])
    first_grad = norm_back(normed_grad * gain_one, normal_one, scale_one)
    attn_grad = first_grad.astype(halves)
    dq, dk, dv = attend_back(bounds, attn_grad.reshape(micro, rows, model), wot, mixed, lse, q, k, v, seg_own, seg_all)
    every_flat = everything.reshape(micro * length, model)
    attn_grads = []
    own_share = first_grad
    spread = 0
    for c in range(cols):
        dq_c, dk_c, dv_c = dq[c].reshape(total, width), dk[c].reshape(micro * length, width), dv[c].reshape(micro * length, width)
        attn_grads.append(jnp.concatenate([
            contract_rows(flat(own), dq_c), contract_rows(every_flat, dk_c), contract_rows(every_flat, dv_c),
            contract_rows(attn_grad, mixed_flat[c]),
        ], 1).astype(halves))
        own_share = own_share + contract_cols(dq_c, wq[c])
        spread = spread + contract_cols(dk_c, wk[c]) + contract_cols(dv_c, wv[c])
    bias_q = jnp.sum(dq.astype(floats), (1, 2)).reshape(-1)
    bias_v = jnp.sum(dv.astype(floats), (1, 2)).reshape(-1)
    vectors = jnp.concatenate([
        jnp.sum(first_grad, 0), jnp.sum(normed_grad * normal_one, 0), jnp.sum(normed_grad, 0), jnp.sum(second_grad, 0),
        jnp.sum(cot * normal_two, 0), jnp.sum(cot, 0), bias_q, bias_v, *hidden_bias_grads,
    ]).reshape(-1, model)
    partial = jnp.stack([jnp.stack(attn_grads), jnp.stack(hidden_grads), jnp.stack(down_grads)])
    input_grad, reduced, sums = reduce(sizes, own_share.reshape(micro, rows, model),
                                       spread.astype(halves).reshape(micro, cols, rows, model), partial, vectors)
    attn_block = reduced[0]
    piece = lambda i: attn_block[:, i * width : (i + 1) * width]
    mine = lambda vector, size: lax.dynamic_slice_in_dim(vector.reshape(-1), here * size, size, 0)
    return (
        outputs.reshape(micro, 1, rows, model), input_grad[:, None],
        piece(0), piece(1), piece(2), mine(sums[6], width), mine(sums[7], width), piece(3).T,
        sums[0], sums[1], sums[2], reduced[1], mine(sums[8:], hidden_bias.shape[0]), reduced[2].T,
        sums[3], sums[4], sums[5],
    )


def per_device_fused(sizes, inputs, segment_ids, query_weight, key_weight, value_weight, query_bias, value_bias,
               output_weight, output_bias, first_gain, first_shift, hidden_weight, hidden_bias, down_weight,
               down_bias, second_gain, second_shift, cotangent):
    floats, halves = jnp.float32, jnp.bfloat16
    cols = sizes[2]
    micro, _, rows, model = inputs.shape
    length = segment_ids.shape[-1]
    width = query_weight.shape[1]
    here = lax.axis_index("col")
    own = inputs[:, 0]
    shard = jnp.stack([
        jnp.concatenate([query_weight, key_weight, value_weight, output_weight.T], 1),
        hidden_weight,
        down_weight.T,
    ])
    pad = lambda vector: jnp.pad(vector.astype(floats), (0, model - vector.shape[0]))
    bias = jnp.stack([pad(hidden_bias), pad(query_bias), pad(value_bias)] + [jnp.zeros((model,), floats)] * 5)
    seg_all = segment_ids[:, 0]
    seg_own = lax.dynamic_slice_in_dim(seg_all, here * rows, rows, 1)
    rest, first, everything, biases, mixed, lse, q, k, v = forward(sizes, own, shard, bias, seg_own, seg_all)
    first = first.reshape(cols, model, 4 * width)
    total = micro * rows
    flat = lambda a: a.reshape(total, -1)
    vectors = jnp.stack([a.astype(floats) for a in (output_bias, first_gain, first_shift, down_bias, second_gain, second_shift)]
                        + [jnp.zeros((model,), floats)] * 2)
    outputs, first_grad, attn_grad, part, sums = middle(
        flat(own), mixed.reshape(cols, total, WINDOW), first, rest.reshape(2, cols, model, -1), biases, vectors, flat(cotangent[:, 0]))
    parted = lambda a: a.reshape(micro, rows, model)
    input_grad, reduced, sums = backward(sizes, parted(attn_grad), parted(first_grad), first, everything, mixed, lse, q, k, v,
                                         seg_own, seg_all, part, sums)
    piece = lambda i: reduced[0, :, i * width : (i + 1) * width]
    mine = lambda first_row, at, size: lax.dynamic_slice(sums, (first_row + here, at), (1, size))[0]
    heads_at = sums.shape[0] - (cols + -cols % 8)
    return (
        outputs.reshape(micro, 1, rows, model), input_grad[:, None],
        piece(0), piece(1), piece(2), mine(heads_at, 0, width), mine(heads_at, WINDOW, width), piece(3).T,
        sums[0], sums[1], sums[2], reduced[1], mine(8, 0, hidden_bias.shape[0]), reduced[2].T,
        sums[3], sums[4], sums[5],
    )


def per_device(sizes, inputs, segment_ids, query_weight, *rest):
    fits = query_weight.shape == (query_weight.shape[0] // 16 * 16, 3 * HEAD_DIM)
    return (per_device_fused if fits else per_device_plain)(sizes, inputs, segment_ids, query_weight, *rest)


def solution(mesh):
    sizes = tuple(mesh.shape[name] for name in ("seq", "row", "col"))
    block, line = P(("seq", "row"), "col"), P("col", ("seq", "row"))
    tokens = P(None, ("seq", "row"), "col", None)
    placed = (tokens, P(None, ("seq", "row"), None), block, block, block, P("col"), P("col"), line, P(), P(), P(),
              block, P("col"), line, P(), P(), P(), tokens)
    given = (tokens, tokens, block, block, block, P("col"), P("col"), line, P(), P(), P(), block, P("col"), line,
             P(), P(), P())
    return jax.shard_map(functools.partial(per_device, sizes), mesh=mesh, in_specs=placed, out_specs=given, check_vma=False)
```

```python
import functools

import jax
import jax.numpy as jnp
from jax import lax
from jax.experimental import pallas as pl
from jax.experimental.pallas import tpu as pltpu
from jax.sharding import PartitionSpec as P

HEAD_DIM = 64
NORM_EPS = 1e-05
MASK_VALUE = -1000000000.0
DOC_MOST = 512
KEY_BLOCK = 256
MESH = pl.DeviceIdType.MESH


def contract_rows(left, right):
    return lax.dot_general(
        left, right, (((0,), (0,)), ((), ())), preferred_element_type=jnp.float32
    )


def contract_cols(left, right):
    return lax.dot_general(
        left, right, (((1,), (1,)), ((), ())), preferred_element_type=jnp.float32
    )


def norm_parts(summed):
    deviation = summed - jnp.mean(summed, -1, keepdims=True)
    scale = lax.rsqrt(jnp.mean(deviation * deviation, -1, keepdims=True) + NORM_EPS)
    return deviation * scale, scale


def norm_back(pull, normal, scale):
    return scale * (
        pull - jnp.mean(pull, -1, keepdims=True) - normal * jnp.mean(pull * normal, -1, keepdims=True)
    )

FORWARD_PLAN = (
    ("Zs", 1), ("Zs", 0), ("Zs", 3), ("Z", 1, 1), ("Z", 0, 1), ("Zs", 2), ("Z", 1, 2), ("Zs", 4), ("Z", 1, 3),
    ("Z", 0, 2), ("Z", 0, 3), ("Z", 2, 1), ("Z", 4, 1), ("Ts", 1), ("Z", 2, 2), ("B", 1), ("Z", 3, 1), ("Ts", 0),
    ("Z", 4, 2), ("B", 0), ("T", 1, 1), ("T", 0, 1), ("Z", 2, 3), ("Z", 3, 2), ("Ts", 3), ("C", 1), ("C", 0),
    ("Ts", 2), ("Z", 4, 3), ("K", 0), ("B", 2), ("T", 1, 2), ("T", 0, 2), ("R", 0), ("Zs", 5), ("K", 1), ("Z", 3, 3),
    ("B", 4), ("U", 0, 0), ("T", 3, 1), ("U", 0, 1), ("B", 3), ("U", 0, 2), ("T", 2, 1), ("C", 2), ("T", 3, 2),
    ("Z", 5, 1), ("C", 4), ("U", 0, 3), ("T", 2, 2), ("R", 1), ("C", 3), ("Z", 5, 2), ("K", 2), ("Z", 5, 3),
    ("U", 1, 0), ("K", 3), ("K", 4), ("B", 5), ("U", 1, 1), ("U", 1, 2), ("C", 5), ("U", 1, 3), ("K", 5),
)
BACKWARD_PLAN = (
    ("G", 3), ("G", 0), ("L",), ("U", 0, 0), ("A", 0), ("A", 3), ("U", 0, 1), ("U", 1, 0), ("B", 0), ("U", 1, 1),
    ("B", 3), ("C", 0), ("U", 2, 0), ("C", 3), ("Z", 0, 2), ("G", 1), ("U", 3, 0), ("Z", 3, 2), ("S", 0), ("A", 1),
    ("G", 2), ("U", 2, 1), ("A", 2), ("T", 0, 0, 1), ("W", 0), ("B", 1), ("T", 0, 1, 1), ("G", 4), ("U", 3, 1),
    ("Z", 0, 1), ("V", 0), ("A", 4), ("S", 1), ("V", 1), ("B", 2), ("W", 1), ("G", 5), ("B", 4), ("W", 2), ("V", 2),
    ("G", 6), ("T", 1, 0, 1), ("A", 5), ("W", 3), ("A", 6), ("G", 7), ("C", 2), ("C", 1), ("V", 3), ("Z", 2, 2),
    ("A", 7), ("Z", 3, 1), ("B", 5), ("Z", 1, 2), ("Z", 2, 1), ("B", 6), ("T", 1, 1, 1), ("B", 7), ("T", 0, 0, 0),
    ("Z", 3, 0), ("C", 4), ("C", 5), ("T", 0, 1, 0), ("Z", 2, 0), ("Z", 0, 0), ("C", 6), ("C", 7), ("Ys",), ("V", 4),
    ("Y", 2), ("Z", 1, 1), ("T", 1, 0, 0), ("Y", 1), ("T", 1, 1, 0), ("Z", 1, 0), ("Y", 0),
)
def attend_kernel(bounds, own_ref, all_ref, wq_ref, wk_ref, wv_ref, bq_ref, bv_ref,
                  segq_ref, segk_ref, mixed_ref, lse_ref, q_ref, k_ref, v_ref, bias, acc, top, total):
    micro = pl.program_id(0)
    low, high = bounds[micro, 0], bounds[micro, 1]
    floats, halves = jnp.float32, jnp.bfloat16
    width = wq_ref.shape[-1]
    heads = width // HEAD_DIM
    rows = own_ref.shape[1]

    @pl.when(pl.program_id(1) == 0)
    def _():
        same = segk_ref[0] == segq_ref[0, 0:1]
        bias[...] = jnp.where(same, 0.0, MASK_VALUE)

    queries = jnp.dot(own_ref[0], wq_ref[0], preferred_element_type=floats) + bq_ref[0]
    queries = queries.astype(halves) * jnp.asarray(HEAD_DIM ** -0.5, halves)
    q_ref[0, 0] = queries
    lane = lax.broadcasted_iota(jnp.int32, (rows, width), 1) // HEAD_DIM
    query_heads = [jnp.where(lane == h, queries, jnp.zeros_like(queries)) for h in range(heads)]
    acc[...] = jnp.zeros_like(acc)
    total[...] = jnp.zeros_like(total)
    top[...] = jnp.full_like(top, 2 * MASK_VALUE)

    def step(block, carry):
        at = pl.ds(pl.multiple_of(block * KEY_BLOCK, KEY_BLOCK), KEY_BLOCK)
        x = all_ref[0, at, :]
        keys = jnp.dot(x, wk_ref[0], preferred_element_type=floats).astype(halves)
        k_ref[0, 0, at, :] = keys
        values = (jnp.dot(x, wv_ref[0], preferred_element_type=floats) + bv_ref[0]).astype(halves)
        v_ref[0, 0, at, :] = values
        values_t = values.T
        mask = bias[at, :]
        for h in range(heads):
            s = contract_cols(keys, query_heads[h]) + mask
            old = top[h : h + 1]
            new = jnp.maximum(old, jnp.max(s, 0, keepdims=True))
            p = jnp.exp(s - new)
            shrink = jnp.exp(old - new)
            top[h : h + 1] = new
            total[h : h + 1] = total[h : h + 1] * shrink + jnp.sum(p, 0, keepdims=True)
            part = pl.ds(h * HEAD_DIM, HEAD_DIM)
            acc[part, :] = acc[part, :] * shrink + jnp.dot(
                values_t[h * HEAD_DIM : (h + 1) * HEAD_DIM], p.astype(halves), preferred_element_type=floats
            )
        return carry

    lax.fori_loop(low, high, step, 0)
    for h in range(heads):
        part = pl.ds(h * HEAD_DIM, HEAD_DIM)
        acc[part, :] = acc[part, :] / total[h : h + 1]
    mixed_ref[0, 0] = acc[...].T.astype(halves)
    lse_ref[0, 0] = top[...] + jnp.log(jnp.maximum(total[...], 1e-30))


def attend(bounds, own, everything, wq, wk, wv, bq, bv, seg_own, seg_all):
    micro, rows, model = own.shape
    length = everything.shape[1]
    cols, _, width = wq.shape
    halves = jnp.bfloat16
    weight = pl.BlockSpec((1, model, width), lambda m, c, b: (c, 0, 0))
    per = lambda a, b_: pl.BlockSpec((1, 1, a, b_), lambda m, c, b: (c, m, 0, 0))
    spec = pltpu.PrefetchScalarGridSpec(
        num_scalar_prefetch=1,
        grid=(micro, cols),
        in_specs=[
            pl.BlockSpec((1, rows, model), lambda m, c, b: (m, 0, 0)),
            pl.BlockSpec((1, length, model), lambda m, c, b: (m, 0, 0)),
            weight, weight, weight,
            pl.BlockSpec((1, 1, width), lambda m, c, b: (c, 0, 0)),
            pl.BlockSpec((1, 1, width), lambda m, c, b: (c, 0, 0)),
            pl.BlockSpec((1, 1, rows), lambda m, c, b: (m, 0, 0)),
            pl.BlockSpec((1, length, 1), lambda m, c, b: (m, 0, 0)),
        ],
        out_specs=[per(rows, width), per(8, rows), per(rows, width), per(length, width), per(length, width)],
        scratch_shapes=[
            pltpu.VMEM((length, rows), jnp.float32),
            pltpu.VMEM((width, rows), jnp.float32),
            pltpu.VMEM((8, rows), jnp.float32),
            pltpu.VMEM((8, rows), jnp.float32),
        ],
    )
    shape = lambda a, b_, d=halves: jax.ShapeDtypeStruct((cols, micro, a, b_), d)
    return pl.pallas_call(
        attend_kernel,
        grid_spec=spec,
        out_shape=[shape(rows, width), shape(8, rows, jnp.float32), shape(rows, width), shape(length, width), shape(length, width)],
        compiler_params=pltpu.CompilerParams(vmem_limit_bytes=48 << 20),
        name="attend",
    )(bounds, own, everything, wq, wk, wv, bq[:, None], bv[:, None],
      seg_own[:, None], seg_all[:, :, None])


def attend_back_kernel(bounds, grad_ref, wot_ref, mixed_ref, lse_ref, q_ref, k_ref, v_ref, segq_ref, segk_ref,
                       dq_ref, dk_ref, dv_ref, bias, acc):
    micro = pl.program_id(0)
    low, high = bounds[micro, 0], bounds[micro, 1]
    floats, halves = jnp.float32, jnp.bfloat16
    rows, width = q_ref.shape[2:]
    heads = width // HEAD_DIM

    @pl.when(pl.program_id(1) == 0)
    def _():
        same = segk_ref[0] == segq_ref[0, 0:1]
        bias[...] = jnp.where(same, 0.0, MASK_VALUE)

    mixed_grad = jnp.dot(grad_ref[0], wot_ref[0], preferred_element_type=floats).astype(halves)
    product = mixed_grad.astype(floats) * mixed_ref[0, 0].astype(floats)
    product_high = product.astype(halves)
    product_low = (product - product_high.astype(floats)).astype(halves)
    pick = (
        lax.broadcasted_iota(jnp.int32, (8, width), 1) // HEAD_DIM == lax.broadcasted_iota(jnp.int32, (8, width), 0)
    ).astype(halves)
    inner = contract_cols(pick, product_high) + contract_cols(pick, product_low)
    lane = lax.broadcasted_iota(jnp.int32, (rows, width), 1) // HEAD_DIM
    queries = q_ref[0, 0]
    query_heads = [jnp.where(lane == h, queries, jnp.zeros_like(queries)) for h in range(heads)]
    grad_heads = [jnp.where(lane == h, mixed_grad, jnp.zeros_like(mixed_grad)) for h in range(heads)]
    acc[...] = jnp.zeros_like(acc)
    dk_ref[...] = jnp.zeros_like(dk_ref)
    dv_ref[...] = jnp.zeros_like(dv_ref)

    def step(block, carry):
        at = pl.ds(pl.multiple_of(block * KEY_BLOCK, KEY_BLOCK), KEY_BLOCK)
        keys = k_ref[0, 0, at, :]
        values = v_ref[0, 0, at, :]
        keys_t = keys.T
        mask = bias[at, :]
        key_grad = jnp.zeros((KEY_BLOCK, width), floats)
        value_grad = jnp.zeros((KEY_BLOCK, width), floats)
        for h in range(heads):
            s = contract_cols(keys, query_heads[h]) + mask
            p = jnp.exp(s - lse_ref[0, 0, h : h + 1])
            prob_grad = contract_cols(values, grad_heads[h])
            score_grad = (p * (prob_grad - inner[h : h + 1])).astype(halves)
            value_grad = value_grad + jnp.dot(p.astype(halves), grad_heads[h], preferred_element_type=floats)
            key_grad = key_grad + jnp.dot(score_grad, query_heads[h], preferred_element_type=floats)
            part = pl.ds(h * HEAD_DIM, HEAD_DIM)
            acc[part, :] += jnp.dot(keys_t[h * HEAD_DIM : (h + 1) * HEAD_DIM], score_grad, preferred_element_type=floats)
        dk_ref[0, 0, at, :] = key_grad.astype(halves)
        dv_ref[0, 0, at, :] = value_grad.astype(halves)
        return carry

    lax.fori_loop(low, high, step, 0)
    dq_ref[0, 0] = (acc[...].T * HEAD_DIM ** -0.5).astype(halves)


def attend_back(bounds, grad, wot, mixed, lse, q, k, v, seg_own, seg_all):
    micro, rows, model = grad.shape
    cols, _, length, width = k.shape
    halves = jnp.bfloat16
    per = lambda a, b_: pl.BlockSpec((1, 1, a, b_), lambda m, c, b: (c, m, 0, 0))
    spec = pltpu.PrefetchScalarGridSpec(
        num_scalar_prefetch=1,
        grid=(micro, cols),
        in_specs=[
            pl.BlockSpec((1, rows, model), lambda m, c, b: (m, 0, 0)),
            pl.BlockSpec((1, model, width), lambda m, c, b: (c, 0, 0)),
            per(rows, width), per(8, rows), per(rows, width), per(length, width), per(length, width),
            pl.BlockSpec((1, 1, rows), lambda m, c, b: (m, 0, 0)),
            pl.BlockSpec((1, length, 1), lambda m, c, b: (m, 0, 0)),
        ],
        out_specs=[per(rows, width), per(length, width), per(length, width)],
        scratch_shapes=[pltpu.VMEM((length, rows), jnp.float32), pltpu.VMEM((width, rows), jnp.float32)],
    )
    shape = lambda a, b_, d=halves: jax.ShapeDtypeStruct((cols, micro, a, b_), d)
    return pl.pallas_call(
        attend_back_kernel,
        grid_spec=spec,
        out_shape=[shape(rows, width), shape(length, width), shape(length, width)],
        compiler_params=pltpu.CompilerParams(vmem_limit_bytes=48 << 20),
        name="attend_back",
    )(bounds, grad, wot, mixed, lse, q, k, v, seg_own[:, None], seg_all[:, :, None])


def place(sizes):
    seq, row, col = (lax.axis_index(name) for name in ("seq", "row", "col"))
    lines = {"x": (seq, sizes[0]), "y": (row // 2, sizes[1] // 2), "k": (lax.rem(row, 2), 2), "z": (col, sizes[2])}

    def device(axis, index):
        if axis == "x":
            return (index, row, col)
        if axis == "y":
            return (seq, index * 2 + lax.rem(row, 2), col)
        if axis == "k":
            return (seq, row // 2 * 2 + index, col)
        return (seq, row, index)

    return lines, device


def greet(lines, device):
    barrier = pltpu.get_barrier_semaphore()
    count = 0
    for axis, (mine, size) in lines.items():
        for t in range(1, size):
            pl.semaphore_signal(barrier, inc=1, device_id=device(axis, lax.rem(mine + t, size)), device_id_type=MESH)
            count += 1
    pl.semaphore_wait(barrier, count)


class Post:
    def __init__(self, device, send_sems, recv_sems):
        self.device, self.send_sems, self.recv_sems = device, send_sems, recv_sems
        self.slots, self.sent = {}, []

    def slot(self, key):
        return self.slots.setdefault(key, len(self.slots))

    def copy(self, key, axis, index, source, target):
        n = self.slot(key)
        return pltpu.make_async_remote_copy(
            src_ref=source, dst_ref=target, send_sem=self.send_sems.at[n], recv_sem=self.recv_sems.at[n],
            device_id=self.device(axis, index), device_id_type=MESH,
        )

    def send(self, key, make):
        def run(act):
            axis, index, source, target, when = make()

            def go():
                act(self.copy(key, axis, index, source, target))

            if when is None:
                go()
            else:
                pl.when(when)(go)

        run(lambda copy: copy.start())
        self.sent.append(run)

    def wait(self, key, axis, index, target, when=None):
        def go():
            self.copy(key, axis, index, target, target).wait_recv()

        if when is None:
            go()
        else:
            pl.when(when)(go)

    def close(self):
        for run in self.sent:
            run(lambda copy: copy.wait_send())


def clip(index, size):
    return jnp.clip(index, 0, size - 1)


class LineGather:
    def __init__(self, post, name, axis, line, region, reach=None):
        self.post, self.name, self.axis, self.region = post, name, axis, region
        self.mine, self.size = line
        self.reach = min(self.size - 1, reach or self.size)

    def hop(self, way, t):
        mine, size = self.mine, self.size

        def make():
            origin, target = mine - way * t, mine + way
            ok = (origin >= 0) & (origin < size) & (target >= 0) & (target < size)
            here = self.region(clip(origin, size))
            return self.axis, clip(target, size), here, here, ok

        self.post.send((self.name, way, t + 1), make)

    def start(self):
        for way in (1, -1):
            if self.reach >= 1:
                self.hop(way, 0)

    def step(self, t):
        if t > self.reach:
            return
        for way in (1, -1):
            origin = self.mine - way * t
            ok = (origin >= 0) & (origin < self.size)
            self.post.wait((self.name, way, t), self.axis, clip(self.mine - way, self.size), self.region(clip(origin, self.size)), ok)
            if t < self.reach:
                self.hop(way, t)

    def finish(self, first=1):
        for t in range(first, self.reach + 1):
            self.step(t)


def gather_kernel(sizes, micro, own_ref, shard_ref, every_ref, full_ref, send_sems, recv_sems, local_sems):
    lines, device = place(sizes)
    (x, _), (y, _), (k, _), (z, cols) = (lines[a] for a in "xykz")
    half = shard_ref.shape[-1] // 2
    rows = own_ref.shape[1]
    reach = -(-(DOC_MOST - 1) // rows)
    parts = [pl.ds(p * half, half) for p in (0, 1)]
    local = [pltpu.make_async_copy(shard_ref.at[j], full_ref.at[j, z, x, y, k], local_sems.at[j]) for j in range(3)]
    local += [pltpu.make_async_copy(own_ref.at[m], every_ref.at[m, z], local_sems.at[3 + m]) for m in range(micro)]
    for copy in local:
        copy.start()
    greet(lines, device)
    post = Post(device, send_sems, recv_sems)
    for copy in local:
        copy.wait()
    zs = [LineGather(post, ("z", j), "z", lines["z"], lambda i, j=j: full_ref.at[j, i, x, y, k]) for j in range(3)]
    tokens = [LineGather(post, ("t", m), "z", lines["z"], lambda i, m=m: every_ref.at[m, i], reach) for m in range(micro)]
    second, third = {}, {}
    for j in range(3):
        second[j] = [
            LineGather(post, ("a", j), "y", lines["y"], lambda i, j=j: full_ref.at[j, :, x, i, k, :, parts[0]]),
            LineGather(post, ("b", j), "x", lines["x"], lambda i, j=j: full_ref.at[j, :, i, y, k, :, parts[1]]),
        ]
        third[j] = [
            LineGather(post, ("c", j), "x", lines["x"], lambda i, j=j: full_ref.at[j, :, i, :, k, :, parts[0]]),
            LineGather(post, ("d", j), "y", lines["y"], lambda i, j=j: full_ref.at[j, :, :, i, k, :, parts[1]]),
        ]

    def start(group):
        for line in group:
            line.start()

    def finish(group):
        for line in group:
            line.finish()

    def swap(j):
        plane = full_ref.at[j, :, :, :, k]
        post.send(("k", j), lambda: ("k", 1 - k, plane, plane, None))

    start(zs[:1])
    finish(zs[:1])
    start(second[0] + zs[1:2])
    finish(second[0])
    start(third[0])
    finish(zs[1:2])
    start(second[1] + tokens[:1])
    finish(third[0])
    swap(0)
    finish(second[1])
    start(third[1])
    finish(tokens[:1])
    start(zs[2:])
    finish(zs[2:])
    start(second[2] + tokens[1:])
    finish(third[1])
    swap(1)
    finish(second[2])
    start(third[2])
    finish(tokens[1:])
    finish(third[2])
    swap(2)
    for i in range(cols):
        far = (z - i > reach) | (i - z > reach)
        for m in range(micro):
            def fill(m=m, i=i):
                copy = pltpu.make_async_copy(own_ref.at[m], every_ref.at[m, i], local_sems.at[3 + m])
                copy.start()
                copy.wait()

            if i > reach or cols - 1 - i > reach:
                pl.when(far)(fill)
    for j in range(3):
        post.wait(("k", j), "k", 1 - k, full_ref.at[j, :, :, :, 1 - k])
    post.close()


def gather(sizes, own, shard):
    ns, nr, nc = sizes
    ny = nr // 2
    micro, rows, model = own.shape
    _, rb, w = shard.shape
    count = 3 * 2 * (nc - 1) + micro * 2 * (nc - 1) + 3 * (4 * (ny - 1) + 4 * (ns - 1) + 1)
    anywhere = pl.BlockSpec(memory_space=pl.ANY)
    every, full = pl.pallas_call(
        functools.partial(gather_kernel, sizes, micro),
        out_shape=[
            jax.ShapeDtypeStruct((micro, nc, rows, model), own.dtype),
            jax.ShapeDtypeStruct((3, nc, ns, ny, 2, rb, w), shard.dtype),
        ],
        in_specs=[pl.BlockSpec(memory_space=pltpu.VMEM)] * 2,
        out_specs=[anywhere] * 2,
        scratch_shapes=[pltpu.SemaphoreType.DMA((count,)), pltpu.SemaphoreType.DMA((count,)), pltpu.SemaphoreType.DMA((3 + micro,))],
        compiler_params=pltpu.CompilerParams(collective_id=0, has_side_effects=True),
        name="gather",
    )(own, shard)
    return every, full.reshape(3, nc, ns * nr * rb, w)


class LineReduce:
    def __init__(self, post, name, axis, line, region, inbox, add, reach=None):
        self.post, self.name, self.axis, self.region, self.inbox, self.add = post, name, axis, region, inbox, add
        self.mine, self.size = line
        self.reach = min(self.size - 1, reach or self.size)

    def arrived(self, way, e):
        behind, goal = self.mine - way, self.mine + way * e
        return (behind >= 0) & (behind < self.size) & (goal >= 0) & (goal < self.size)

    def take(self, way, e):
        ok = self.arrived(way, e)
        inbox = self.inbox(way, e)
        self.post.wait((self.name, way, e), self.axis, clip(self.mine - way, self.size), inbox, ok)

        @pl.when(ok)
        def _():
            self.add(self.region(clip(self.mine + way * e, self.size)), inbox)

    def forward(self, way, e):
        def make():
            goal = self.mine + way * e
            ok = (goal >= 0) & (goal < self.size)
            return self.axis, clip(self.mine + way, self.size), self.region(clip(goal, self.size)), self.inbox(way, e - 1), ok

        self.post.send((self.name, way, e - 1), make)

    def start(self):
        for way in (1, -1):
            if self.reach >= 1:
                self.forward(way, self.reach)

    def forward_from(self, nearest):
        for e in range(self.reach - 1, nearest - 1, -1):
            for way in (1, -1):
                self.take(way, e)
                self.forward(way, e)

    def finish(self, last=True):
        self.forward_from(1)
        if last:
            for way in (1, -1):
                if self.reach >= 1:
                    self.take(way, 0)


def reduce_kernel(sizes, micro, own_ref, spread_ref, part_ref, vec_ref, back_ref, block_ref, sums_ref,
                  mine_buf, core_buf, in_a, in_b, in_c, in_d, in_z, tok_buf, tok_in, vec_buf, send_sems, recv_sems, local_sems):
    floats, halves = jnp.float32, jnp.bfloat16
    lines, device = place(sizes)
    (x, ns), (y, ny), (k, _), (z, nc) = (lines[a] for a in "xykz")
    half = part_ref.shape[-1] // 2
    rows = own_ref.shape[1]
    reach = -(-(DOC_MOST - 1) // rows)
    parts = [pl.ds(p * half, half) for p in (0, 1)]
    local = [pltpu.make_async_copy(part_ref.at[j, :, :, :, k], mine_buf.at[j], local_sems.at[j]) for j in range(3)]
    local += [pltpu.make_async_copy(spread_ref.at[m], tok_buf.at[m], local_sems.at[3 + m]) for m in range(micro)]
    for copy in local:
        copy.start()
    greet(lines, device)
    post = Post(device, send_sems, recv_sems)
    for j in range(3):
        post.send(("k", j), lambda j=j: ("k", 1 - k, part_ref.at[j, :, :, :, 1 - k], core_buf.at[j], None))

    def plus(target, source):
        target[...] = (target[...].astype(floats) + source[...].astype(floats)).astype(halves)

    def plus_grid(target, source, first, second):
        @pl.loop(0, first * second)
        def _(n):
            plus(target.at[n // second, lax.rem(n, second)], source.at[n // second, lax.rem(n, second)])

    def plus_row(target, source, first):
        @pl.loop(0, first)
        def _(n):
            plus(target.at[n], source.at[n])

    vec_buf[0, 0] = vec_ref[...]

    def vector_start(stage, axis):
        mine, size = lines[axis]
        vec_buf[stage, 1 + mine] = vec_buf[stage, 0]
        for t in range(1, size):
            post.send(("v", stage, t), lambda t=t: (
                axis, lax.rem(mine + t, size), vec_buf.at[stage, 0], vec_buf.at[stage, 1 + mine], None))

    def vector_finish(stage, axis, out):
        mine, size = lines[axis]
        for t in range(1, size):
            origin = lax.rem(mine + size - t, size)
            post.wait(("v", stage, t), axis, origin, vec_buf.at[stage, 1 + origin])
        total = vec_buf[stage, 1]
        for i in range(1, size):
            total = total + vec_buf[stage, 1 + i]
        out[...] = total

    tokens = [
        LineReduce(post, ("t", m), "z", lines["z"], lambda i, m=m: tok_buf.at[m, i],
                   lambda way, e, m=m: tok_in.at[m, (1 - way) // 2, e], plus, reach)
        for m in range(micro)
    ]
    box = lambda way: (1 - way) // 2
    second, third, last = {}, {}, {}
    for j in range(3):
        second[j] = [
            LineReduce(post, ("a", j), "x", lines["x"], lambda i, j=j: mine_buf.at[j, :, i, :, :, parts[0]],
                       lambda way, e, j=j: in_a.at[j, box(way), e], lambda t, s: plus_grid(t, s, nc, ny)),
            LineReduce(post, ("b", j), "y", lines["y"], lambda i, j=j: mine_buf.at[j, :, :, i, :, parts[1]],
                       lambda way, e, j=j: in_b.at[j, box(way), e], lambda t, s: plus_grid(t, s, nc, ns)),
        ]
        third[j] = [
            LineReduce(post, ("c", j), "y", lines["y"], lambda i, j=j: mine_buf.at[j, :, x, i, :, parts[0]],
                       lambda way, e, j=j: in_c.at[j, box(way), e], lambda t, s: plus_row(t, s, nc)),
            LineReduce(post, ("d", j), "x", lines["x"], lambda i, j=j: mine_buf.at[j, :, i, y, :, parts[1]],
                       lambda way, e, j=j: in_d.at[j, box(way), e], lambda t, s: plus_row(t, s, nc)),
        ]
        last[j] = [
            LineReduce(post, ("z", j), "z", lines["z"], lambda i, j=j: mine_buf.at[j, i, x, y],
                       lambda way, e, j=j: in_z.at[j, box(way), e], plus)
        ]

    def start(group):
        for line in group:
            line.start()

    def finish(group):
        for line in group:
            line.finish()

    def core(j):
        local[j].wait()
        post.wait(("k", j), "k", 1 - k, core_buf.at[j])

        @pl.loop(0, nc * ns * ny)
        def _(n):
            at = (n // (ns * ny), lax.rem(n // ny, ns), lax.rem(n, ny))
            plus(mine_buf.at[(j, *at)], core_buf.at[(j, *at)])

    for m in range(micro):
        local[3 + m].wait()
    start(tokens)
    core(0)
    start(second[0])
    vector_start(0, "k")
    core(1)
    start(second[1])
    vector_finish(0, "k", vec_buf.at[1, 0])
    vector_start(1, "y")
    core(2)
    finish(second[0])
    start(third[0])
    start(second[2])
    vector_finish(1, "y", vec_buf.at[2, 0])
    vector_start(2, "x")
    finish(tokens)
    vector_finish(2, "x", vec_buf.at[3, 0])
    vector_start(3, "z")
    finish(second[1])
    start(third[1])
    finish(third[0])
    start(last[0])
    finish(second[2])
    start(third[2])
    finish(third[1])
    start(last[1])
    finish(last[0])
    finish(third[2])
    start(last[2])
    vector_finish(3, "z", sums_ref)
    for m in range(micro):
        back_ref[m] = own_ref[m] + tok_buf[m, z].astype(floats)
    finish(last[1])
    finish(last[2])
    for j in range(3):
        block_ref[j] = mine_buf[j, z, x, y].astype(floats)
    post.close()


def reduce(sizes, own_share, spread, partial, vectors):
    ns, nr, nc = sizes
    ny = nr // 2
    micro, rows, model = own_share.shape
    w = partial.shape[-1]
    rb = partial.shape[2] // (ns * nr)
    halves, floats = jnp.bfloat16, jnp.float32
    reach = min(nc - 1, -(-(DOC_MOST - 1) // rows))
    count = 3 + 2 * (ny - 1 + ns - 1) * 6 + 3 * 2 * (nc - 1) + micro * 2 * reach + (1 + ny - 1 + ns - 1 + nc - 1)
    widest = max(ns, ny, nc, 2)
    extra = -vectors.shape[0] % 8
    vectors = jnp.pad(vectors, ((0, extra), (0, 0)))
    vmem = pl.BlockSpec(memory_space=pltpu.VMEM)
    anywhere = pl.BlockSpec(memory_space=pl.ANY)
    back, blocks, sums = pl.pallas_call(
        functools.partial(reduce_kernel, sizes, micro),
        out_shape=[
            jax.ShapeDtypeStruct((micro, rows, model), floats),
            jax.ShapeDtypeStruct((3, rb, w), floats),
            jax.ShapeDtypeStruct(vectors.shape, floats),
        ],
        in_specs=[vmem, anywhere, anywhere, vmem],
        out_specs=[vmem] * 3,
        scratch_shapes=[
            pltpu.VMEM((3, nc, ns, ny, rb, w), halves),
            pltpu.VMEM((3, nc, ns, ny, rb, w), halves),
            pltpu.VMEM((3, 2, max(ns - 1, 1), nc, ny, rb, w // 2), halves),
            pltpu.VMEM((3, 2, max(ny - 1, 1), nc, ns, rb, w // 2), halves),
            pltpu.VMEM((3, 2, max(ny - 1, 1), nc, rb, w // 2), halves),
            pltpu.VMEM((3, 2, max(ns - 1, 1), nc, rb, w // 2), halves),
            pltpu.VMEM((3, 2, max(nc - 1, 1), rb, w), halves),
            pltpu.VMEM((micro, nc, rows, model), halves),
            pltpu.VMEM((micro, 2, max(reach, 1), rows, model), halves),
            pltpu.VMEM((4, 1 + widest, *vectors.shape), floats),
            pltpu.SemaphoreType.DMA((count,)),
            pltpu.SemaphoreType.DMA((count,)),
            pltpu.SemaphoreType.DMA((3 + micro,)),
        ],
        compiler_params=pltpu.CompilerParams(collective_id=1, has_side_effects=True, vmem_limit_bytes=60 << 20),
        name="reduce",
    )(own_share, spread, partial.reshape(3, nc, ns, ny, 2, rb, w), vectors)
    return back, blocks, sums


Q_AT, K_AT, V_AT, O_AT, WINDOW = 0, 128, 384, 512, 256


def plane(full_ref, c, at, size=WINDOW):
    value = full_ref[c, :, :, :, :, at : at + size]
    return value.reshape(-1, size)


def split_plan(plan):
    parts, order = [[]], []
    for task in plan:
        if task[0] == "U":
            order.append(task[1:])
            parts.append([])
        else:
            parts[-1].append(task)
    return parts[0], parts[1:], order


def pick(step, values):
    value = values[0]
    for i, other in enumerate(values[1:], 1):
        value = jnp.where(step == i, other, value)
    return value


def place_of(rows):
    return lax.broadcasted_iota(jnp.int32, (rows, WINDOW), 1) // HEAD_DIM


def keep(value, places, wanted):
    return jnp.where(places == wanted, value, jnp.zeros_like(value))


def forward_kernel(sizes, micro, own_ref, shard_ref, bias_ref, segq_ref, segk_ref,
                   rest_ref, first_ref, turned_ref, biases_ref, mixed_ref, lse_ref, q_ref, k_ref, v_ref,
                   weights, turned, bias_buf, mask, mixed_buf, lse_buf, q_buf, k_buf, v_buf, tokens_buf, acc, top, total,
                   send_sems, recv_sems, local_sems):
    floats, halves = jnp.float32, jnp.bfloat16
    lines, device = place(sizes)
    (x, _), (y, _), (k, _), (z, cols) = (lines[a] for a in "xykz")
    half = shard_ref.shape[-1] // 2
    rows = own_ref.shape[1]
    reach = -(-(DOC_MOST - 1) // rows)
    parts = [pl.ds(p * half, half) for p in (0, 1)]
    low, high = jnp.maximum(z - reach, 0), jnp.minimum(z + reach + 1, cols)
    used = [0]

    def local(source, target):
        copy = pltpu.make_async_copy(source, target, local_sems.at[used[0]])
        used[0] += 1
        copy.start()
        return copy

    targets = [weights.at[0], rest_ref.at[0], rest_ref.at[1]]
    begin = [local(shard_ref.at[j], targets[j].at[z, x, y, k]) for j in range(3)]
    begin += [local(own_ref.at[m], tokens_buf.at[m, z]) for m in range(micro)]
    begin += [local(bias_ref, bias_buf.at[z])]
    greet(lines, device)
    post = Post(device, send_sems, recv_sems)
    for copy in begin:
        copy.wait()
    tokens = [
        LineGather(post, ("t", q), "z", lines["z"],
                   lambda i, q=q: tokens_buf.at[q // 2, i, pl.ds(q % 2 * (rows // 2), rows // 2)], reach)
        for q in range(2 * micro)
    ]
    small = LineGather(post, "bias", "z", lines["z"], lambda i: bias_buf.at[i])
    rb = shard_ref.shape[1]
    zs, second, third = {}, {}, {}
    for n in range(6):
        j, r = n // 2, pl.ds(n % 2 * (rb // 2), rb // 2)
        zs[n] = LineGather(post, ("z", n), "z", lines["z"], lambda i, j=j, r=r: targets[j].at[i, x, y, k, r])
        second[n] = [
            LineGather(post, ("a", n), "y", lines["y"], lambda i, j=j, r=r: targets[j].at[:, x, i, k, r, parts[0]]),
            LineGather(post, ("b", n), "x", lines["x"], lambda i, j=j, r=r: targets[j].at[:, i, y, k, r, parts[1]]),
        ]
        third[n] = [
            LineGather(post, ("c", n), "x", lines["x"], lambda i, j=j, r=r: targets[j].at[:, i, :, k, r, parts[0]]),
            LineGather(post, ("d", n), "y", lines["y"], lambda i, j=j, r=r: targets[j].at[:, :, i, k, r, parts[1]]),
        ]

    def start(*group):
        for line in group:
            line.start()

    def finish(*group):
        for line in group:
            line.finish()

    def side(n, which):
        return targets[n // 2].at[:, :, :, which, pl.ds(n % 2 * (rb // 2), rb // 2)]

    def swap(n):
        post.send(("k", n), lambda: ("k", 1 - k, side(n, k), side(n, k), None))

    def swapped(n):
        post.wait(("k", n), "k", 1 - k, side(n, 1 - k))

    places = place_of(rows)

    def unit(m, c):
        queries = jnp.dot(own_ref[m], plane(weights.at[0], c, Q_AT), preferred_element_type=floats) + bias_buf[c, 1:2, 0:WINDOW]
        queries = pltpu.roll(queries.astype(halves).astype(floats) * HEAD_DIM ** -0.5, HEAD_DIM, 1)
        queries = jnp.where(places > 0, queries, 0.0).astype(halves)
        q_buf[m, c] = queries
        heads = [keep(queries, places, h + 1) for h in range(3)]
        acc[...] = jnp.zeros_like(acc)
        total[...] = jnp.zeros_like(total)
        top[...] = jnp.full_like(top, 2 * MASK_VALUE)
        key_weight = plane(weights.at[0], c, K_AT)
        value_weight = plane(weights.at[0], c, V_AT)
        value_bias = bias_buf[c, 2:3, 0:WINDOW]

        def step(block, carry):
            rows_at = tokens_buf[m, block]
            keys = jnp.dot(rows_at, key_weight, preferred_element_type=floats).astype(halves)
            values = (jnp.dot(rows_at, value_weight, preferred_element_type=floats) + value_bias).astype(halves)
            k_buf[m, c, block] = keys
            v_buf[m, c, block] = values
            values_t = values.T
            hidden = mask[m, block]
            for h in range(3):
                s = contract_cols(keys, heads[h]) + hidden
                old = top[h : h + 1]
                new = jnp.maximum(old, jnp.max(s, 0, keepdims=True))
                p = jnp.exp(s - new)
                shrink = jnp.exp(old - new)
                top[h : h + 1] = new
                total[h : h + 1] = total[h : h + 1] * shrink + jnp.sum(p, 0, keepdims=True)
                at = pl.ds((h + 1) * HEAD_DIM, HEAD_DIM)
                acc[at, :] = acc[at, :] * shrink + jnp.dot(
                    values_t[h * HEAD_DIM : (h + 1) * HEAD_DIM], p.astype(halves), preferred_element_type=floats
                )
            return carry

        lax.fori_loop(low, high, step, 0)
        for h in range(3):
            at = pl.ds((h + 1) * HEAD_DIM, HEAD_DIM)
            acc[at, :] = acc[at, :] / total[h : h + 1]
        mixed_buf[c, m] = acc[...].T.astype(halves)
        lse_buf[m, c] = top[...] + jnp.log(jnp.maximum(total[...], 1e-30))

    def units(m, first, last):
        @pl.loop(first, last)
        def _(c):
            unit(m, c)

    def masks(m):
        @pl.loop(low, high)
        def _(block):
            same = jnp.broadcast_to(segk_ref[m, pl.ds(block, 1), :], (rows, rows)).T == segq_ref[m, 0:1]
            mask[m, block] = jnp.where(same, 0.0, MASK_VALUE)

    def turn(m):
        for block in range(cols):
            inside = (low <= block) & (block < high)
            at = pl.ds((m * cols + block) * rows, rows)

            @pl.when(inside)
            def _():
                turned[:, at] = tokens_buf[m, block].T

            if block > reach or cols - 1 - block > reach:
                @pl.when(jnp.logical_not(inside))
                def _():
                    turned[:, at] = jnp.zeros((own_ref.shape[2], rows), halves)

    done = []
    keeps = ((q_buf, q_ref), (k_buf, k_ref), (v_buf, v_ref), (lse_buf, lse_ref))

    def take_z(n, t):
        zs[n].step(t)
        if n == 0:
            small.step(t)
        if t == cols - 1:
            start(*second[n])

    def take_second(n):
        finish(*second[n])
        start(*third[n])

    def take_third(n):
        finish(*third[n])
        swap(n)

    swaps = set()

    def take_core(n):
        swapped(n)
        swaps.add(n)
        if n < 2 and swaps >= {0, 1}:
            done.append(local(weights.at[0], first_ref))

    act = {
        "Zs": lambda n: zs[n].start(), "Z": take_z, "Ts": lambda q: tokens[q].start(), "T": lambda q, t: tokens[q].step(t),
        "B": take_second, "C": take_third, "K": take_core, "R": turn,
    }
    small.start()
    head, tail, order = split_plan(FORWARD_PLAN)
    act[head[0][0]](*head[0][1:])
    for m in range(micro):
        masks(m)
    for task in head[1:]:
        act[task[0]](*task[1:])

    @pl.loop(0, len(order))
    def _(step):
        unit(pick(step, [m for m, _ in order]), pick(step, [c for _, c in order]))
        for i, tasks in enumerate(tail[:-1]):
            if tasks:
                @pl.when(step == i)
                def _(tasks=tasks):
                    for task in tasks:
                        act[task[0]](*task[1:])

    for source, target in (*keeps, (bias_buf, biases_ref), (mixed_buf, mixed_ref), (turned, turned_ref)):
        done.append(local(source, target))
    for task in tail[-1]:
        act[task[0]](*task[1:])
    for copy in done:
        copy.wait()
    post.close()


def forward(sizes, own, shard, bias, seg_own, seg_all):
    ns, nr, nc = sizes
    ny = nr // 2
    micro, rows, model = own.shape
    _, rb, w = shard.shape
    halves, floats = own.dtype, jnp.float32
    reach = min(nc - 1, -(-(DOC_MOST - 1) // rows))
    count = (6 + 1) * 2 * (nc - 1) + micro * 4 * reach + 6 * (4 * (ny - 1) + 4 * (ns - 1) + 1)
    anywhere = pl.BlockSpec(memory_space=pl.ANY)
    vmem = pl.BlockSpec(memory_space=pltpu.VMEM)
    length = nc * rows
    arrays = [
        ((2, nc, ns, ny, 2, rb, w), halves), ((nc, ns, ny, 2, rb, w), halves), ((model, micro * length), halves),
        ((nc, *bias.shape), floats), ((nc, micro, rows, WINDOW), halves), ((micro, nc, 8, rows), floats),
        ((micro, nc, rows, WINDOW), halves), ((micro, nc, nc, rows, WINDOW), halves), ((micro, nc, nc, rows, WINDOW), halves),
    ]
    shapes = [pltpu.VMEM(shape, kind) for shape, kind in arrays]
    return pl.pallas_call(
        functools.partial(forward_kernel, sizes, micro),
        out_shape=[jax.ShapeDtypeStruct(shape, kind) for shape, kind in arrays],
        in_specs=[vmem] * 5,
        out_specs=[anywhere] * len(arrays),
        scratch_shapes=[
            pltpu.VMEM((1, nc, ns, ny, 2, rb, w), halves),
            shapes[2], shapes[3], pltpu.VMEM((micro, nc, rows, rows), floats), *shapes[4:],
            pltpu.VMEM((micro, nc, rows, model), halves), pltpu.VMEM((WINDOW, rows), floats), pltpu.VMEM((8, rows), floats), pltpu.VMEM((8, rows), floats),
            pltpu.SemaphoreType.DMA((count,)), pltpu.SemaphoreType.DMA((count,)), pltpu.SemaphoreType.DMA((20,)),
        ],
        compiler_params=pltpu.CompilerParams(collective_id=2, has_side_effects=True, vmem_limit_bytes=60 << 20),
        name="forward",
    )(own, shard, bias, seg_own.astype(floats)[:, None], seg_all.astype(floats).reshape(micro, nc, rows))


def middle_kernel(cols, own_ref, mixed_ref, out_ref, hidden_ref, down_ref, bias_ref, vector_ref, cot_ref,
                  outputs_ref, first_grad_ref, attn_grad_ref, part_ref, sums_ref,
                  normal, scale, normed, normed_low, normed_t, grad_low, grad_t, act_buf, slope_buf, total):
    floats, halves = jnp.float32, jnp.bfloat16
    step = pl.program_id(0)
    rows, model = own_ref.shape
    chunks = [pl.ds(r * 256, 256) for r in range(rows // 256)]
    bands = [pl.ds(n * 256, 256) for n in range(model // 256)]
    vector = lambda i: vector_ref[i : i + 1]

    @pl.when(step == 0)
    def _():
        sums_ref[...] = jnp.zeros_like(sums_ref)
        for chunk in chunks:
            first_sum = own_ref[chunk].astype(floats) + vector(0)
            for c in range(cols):
                first_sum = first_sum + contract_cols(mixed_ref[c, chunk], out_ref[c])
            normal_one, scale_one = norm_parts(first_sum)
            normal[chunk] = normal_one
            scale[chunk] = jnp.broadcast_to(scale_one, (256, 128))
            norm_one = normal_one * vector(1) + vector(2)
            total[chunk] = norm_one + vector(3)
            normed_low[chunk] = norm_one.astype(halves)
            normed_t[:, chunk] = norm_one.astype(halves).T

    @pl.when(step < cols)
    def _():
        for chunk in chunks:
            for band in bands:
                hidden = jnp.dot(normed_low[chunk], hidden_ref[0, 0, :, band], preferred_element_type=floats) + bias_ref[0, 0:1, band]
                half_erf = 0.5 * lax.erf(hidden * 0.7071067811865476) + 0.5
                act_buf[step, chunk, band] = (hidden * half_erf).astype(halves)
                slope_buf[step, chunk, band] = (half_erf + hidden * (jnp.exp(-0.5 * hidden * hidden) * 0.3989422804014327)).astype(halves)
        for chunk in chunks:
            for band in bands:
                total[chunk, band] += contract_cols(act_buf[step, chunk], down_ref[0, 0, band, :])

    @pl.when(step == cols - 1)
    def _():
        for chunk in chunks:
            normal_two, scale_two = norm_parts(total[chunk])
            outputs_ref[chunk] = (normal_two * vector(4) + vector(5)).astype(halves)
            cot = cot_ref[chunk].astype(floats)
            second_grad = norm_back(cot * vector(4), normal_two, scale_two)
            total[chunk] = second_grad
            grad_low[chunk] = second_grad.astype(halves)
            grad_t[:, chunk] = second_grad.astype(halves).T
            sums_ref[3:4] += jnp.sum(second_grad, 0, keepdims=True)
            sums_ref[4:5] += jnp.sum(cot * normal_two, 0, keepdims=True)
            sums_ref[5:6] += jnp.sum(cot, 0, keepdims=True)

    @pl.when(step >= cols)
    def _():
        c = step - cols
        bias_total = [jnp.zeros((1, 256), floats) for _ in bands]
        for chunk in chunks:
            for n, band in enumerate(bands):
                pre = jnp.dot(grad_low[chunk], down_ref[0, 0, :, band], preferred_element_type=floats)
                pre = (pre * slope_buf[c, chunk, band].astype(floats)).astype(halves)
                slope_buf[c, chunk, band] = pre
                bias_total[n] = bias_total[n] + jnp.sum(pre.astype(floats), 0, keepdims=True)
        for n, band in enumerate(bands):
            sums_ref[pl.ds(8 + c, 1), band] = bias_total[n]
        for band in bands:
            for side in bands:
                part_ref[0, 0, side, band] = jnp.dot(normed_t[side, :], slope_buf[c, :, band], preferred_element_type=floats).astype(halves)
                part_ref[1, 0, side, band] = jnp.dot(grad_t[side, :], act_buf[c, :, band], preferred_element_type=floats).astype(halves)
        for chunk in chunks:
            for band in bands:
                total[chunk, band] += contract_cols(slope_buf[c, chunk], hidden_ref[0, 0, band, :])

    @pl.when(step == 2 * cols - 1)
    def _():
        for chunk in chunks:
            normed_grad, normal_one = total[chunk], normal[chunk]
            first_grad = norm_back(normed_grad * vector(1), normal_one, scale[chunk, 0:1])
            first_grad_ref[chunk] = first_grad
            attn_grad_ref[chunk] = first_grad.astype(halves)
            sums_ref[0:1] += jnp.sum(first_grad, 0, keepdims=True)
            sums_ref[1:2] += jnp.sum(normed_grad * normal_one, 0, keepdims=True)
            sums_ref[2:3] += jnp.sum(normed_grad, 0, keepdims=True)


def middle(own, mixed, first, rest, biases, vectors, cot):
    rows, model = own.shape
    cols = first.shape[0]
    halves, floats = jnp.bfloat16, jnp.float32
    whole = lambda shape: pl.BlockSpec(shape, lambda i: (0,) * len(shape))
    wide = lambda kind: pltpu.VMEM((rows, model), kind)
    return pl.pallas_call(
        functools.partial(middle_kernel, cols),
        grid=(2 * cols,),
        in_specs=[
            whole((rows, model)), whole(mixed.shape),
            pl.BlockSpec((cols, model, WINDOW), lambda i: (0, 0, O_AT // WINDOW)),
            pl.BlockSpec((1, 1, model, rest.shape[-1]), lambda i: (0, lax.rem(i, cols), 0, 0)),
            pl.BlockSpec((1, 1, model, rest.shape[-1]), lambda i: (1, lax.rem(i, cols), 0, 0)),
            pl.BlockSpec((1, *biases.shape[1:]), lambda i: (lax.rem(i, cols), 0, 0)),
            whole(vectors.shape), whole((rows, model)),
        ],
        out_specs=[
            whole((rows, model)), whole((rows, model)), whole((rows, model)),
            pl.BlockSpec((2, 1, model, rest.shape[-1]), lambda i: (0, jnp.maximum(i - cols, 0), 0, 0)),
            whole((8 + cols + -cols % 8, model)),
        ],
        out_shape=[
            jax.ShapeDtypeStruct((rows, model), halves), jax.ShapeDtypeStruct((rows, model), floats),
            jax.ShapeDtypeStruct((rows, model), halves), jax.ShapeDtypeStruct(rest.shape, halves),
            jax.ShapeDtypeStruct((8 + cols + -cols % 8, model), floats),
        ],
        scratch_shapes=[
            wide(floats), pltpu.VMEM((rows, 128), floats), wide(floats), wide(halves), pltpu.VMEM((model, rows), halves), wide(halves),
            pltpu.VMEM((model, rows), halves), pltpu.VMEM((cols, rows, rest.shape[-1]), halves),
            pltpu.VMEM((cols, rows, rest.shape[-1]), halves), wide(floats),
        ],
        compiler_params=pltpu.CompilerParams(vmem_limit_bytes=56 << 20),
        name="middle",
    )(own, mixed, first, rest, rest, biases, vectors, cot)


class Inbox:
    def __init__(self, ref, size):
        self.ref, self.size = ref, size

    def __call__(self, way, e):
        return self.ref.at[0 if self.size == 2 else (1 - way) // 2, e]


def backward_kernel(sizes, micro, grad_ref, share_ref, first_ref, turned_ref, mixed_ref, lse_ref, q_ref, k_ref, v_ref,
                    segq_ref, segk_ref, part_ref, vec_ref,
                    back_ref, block_ref, sums_ref,
                    mine_buf, core_buf, stage_buf, in_a, in_b, in_c, in_d, in_z, tok_buf, tok_in, vec_buf,
                    weights, mixed_buf, q_buf, k_buf, v_buf, every_t, grad_t, mask, acc, spread, block_sum,
                    send_sems, recv_sems, local_sems, free_sem):
    floats, halves = jnp.float32, jnp.bfloat16
    lines, device = place(sizes)
    (x, ns), (y, ny), (k, _), (z, cols) = (lines[a] for a in "xykz")
    model = first_ref.shape[1]
    half = part_ref.shape[-1] // 2
    rb = part_ref.shape[-2]
    rows = grad_ref.shape[1]
    reach = -(-(DOC_MOST - 1) // rows)
    parts = [pl.ds(p * half, half) for p in (0, 1)]
    low, high = jnp.maximum(z - reach, 0), jnp.minimum(z + reach + 1, cols)
    used = [0]

    def local(source, target):
        copy = pltpu.make_async_copy(source, target, local_sems.at[used[0]])
        used[0] += 1
        copy.start()
        return copy

    def rows_of(n):
        return pl.ds(n % 2 * (rb // 2), rb // 2)

    planes = [local(part_ref.at[n // 2, :, :, :, k, rows_of(n)], mine_buf.at[n // 2 + 1, :, :, :, rows_of(n)]) for n in range(4)]
    loads = [local(*pair) for pair in ((first_ref, weights), (mixed_ref, mixed_buf), (q_ref, q_buf), (share_ref, back_ref))]
    loads += [local(k_ref, k_buf), local(v_ref, v_buf)]
    loads += [local(turned_ref, every_t)]
    greet(lines, device)
    post = Post(device, send_sems, recv_sems)

    def give(n):
        post.send(("k", n), lambda: (
            "k", 1 - k, part_ref.at[n // 2, :, :, :, 1 - k, rows_of(n)], core_buf.at[n // 2, :, :, :, rows_of(n)], None))

    def plus(target, source):
        target[...] = (target[...].astype(floats) + source[...].astype(floats)).astype(halves)

    def plus_grid(target, source, first, second):
        @pl.loop(0, first * second)
        def _(n):
            at = (n // second, lax.rem(n, second))
            plus(target.at[at], source.at[at])

    def plus_row(target, source, first):
        @pl.loop(0, first)
        def _(n):
            plus(target.at[n], source.at[n])

    class Stream:
        def __init__(self, name, j, begin, size, r):
            cs = pl.ds(begin, size)
            self.second = [
                LineReduce(post, (name, "a"), "x", lines["x"], lambda i: mine_buf.at[j, cs, i, :, r, parts[0]],
                           lambda way, e: Inbox(in_a.at[j], ns)(way, e).at[cs, :, r], lambda t, s: plus_grid(t, s, size, ny)),
                LineReduce(post, (name, "b"), "y", lines["y"], lambda i: mine_buf.at[j, cs, :, i, r, parts[1]],
                           lambda way, e: Inbox(in_b.at[j], ny)(way, e).at[cs, :, r], lambda t, s: plus_grid(t, s, size, ns)),
            ]
            self.third = [
                LineReduce(post, (name, "c"), "y", lines["y"], lambda i: mine_buf.at[j, cs, x, i, r, parts[0]],
                           lambda way, e: Inbox(in_c.at[j], ny)(way, e).at[cs, r], lambda t, s: plus_row(t, s, size)),
                LineReduce(post, (name, "d"), "x", lines["x"], lambda i: mine_buf.at[j, cs, i, y, r, parts[1]],
                           lambda way, e: Inbox(in_d.at[j], ns)(way, e).at[cs, r], lambda t, s: plus_row(t, s, size)),
            ]

    def line_z(name, j, r):
        return LineReduce(post, ("z", name), "z", lines["z"], lambda i: mine_buf.at[j, i, x, y, r],
                          lambda way, e: in_z.at[j, (1 - way) // 2, e, r], plus)

    ffn = [Stream(("s", n), n // 2 + 1, 0, cols, rows_of(n)) for n in range(4)]
    ffn_z = [line_z(n, n // 2 + 1, rows_of(n)) for n in range(4)]
    attn = [Stream(("u", c), 0, c, 1, pl.ds(0, rb)) for c in range(cols)]
    attn_z = line_z("u", 0, pl.ds(0, rb))

    def half_of(h):
        return pl.ds(h * (rows // 2), rows // 2)

    def line_tokens(m, h):
        at = half_of(h)
        return LineReduce(post, ("t", m, h), "z", lines["z"], lambda i: tok_buf.at[m, i, at],
                          lambda way, e: tok_in.at[m, (1 - way) // 2, e, at], plus, reach)

    tokens = [[line_tokens(m, h) for h in range(2)] for m in range(micro)]

    def start(*group):
        for line in group:
            line.start()

    def finish(*group):
        for line in group:
            line.finish()

    def core(n):
        planes[n].wait()
        r = rows_of(n)
        post.wait(("k", n), "k", 1 - k, core_buf.at[n // 2, :, :, :, r])

        @pl.loop(0, cols * ns * ny)
        def _(i):
            at = (i // (ns * ny), lax.rem(i // ny, ns), lax.rem(i, ny), r)
            plus(mine_buf.at[(n // 2 + 1, *at)], core_buf.at[(n // 2, *at)])

    def vector_start(stage, axis):
        mine, size = lines[axis]
        vec_buf[stage, 1 + mine] = vec_buf[stage, 0]
        for t in range(1, size):
            post.send(("v", stage, t), lambda t=t: (
                axis, lax.rem(mine + t, size), vec_buf.at[stage, 0], vec_buf.at[stage, 1 + mine], None))

    def vector_finish(stage, axis, out):
        mine, size = lines[axis]
        for t in range(1, size):
            origin = lax.rem(mine + size - t, size)
            post.wait(("v", stage, t), axis, origin, vec_buf.at[stage, 1 + origin])
        total = vec_buf[stage, 1]
        for i in range(1, size):
            total = total + vec_buf[stage, 1 + i]
        out[...] = total

    places = place_of(rows)
    small = vec_ref.shape[0]
    vec_buf[0, 0] = jnp.zeros_like(vec_buf[0, 0])
    vec_buf[0, 0, 0:small] = vec_ref[...]

    def masks(m):
        @pl.loop(low, high)
        def _(block):
            same = jnp.broadcast_to(segk_ref[m, pl.ds(block, 1), :], (rows, rows)).T == segq_ref[m, 0:1]
            mask[m, block] = jnp.where(same, 0.0, MASK_VALUE).astype(halves)

    def clear():
        for block in range(cols):
            if block > reach or cols - 1 - block > reach:
                @pl.when(jnp.logical_not((low <= block) & (block < high)))
                def _():
                    @pl.loop(0, micro * cols)
                    def _(n):
                        at = (n // cols, lax.rem(n, cols), block)
                        k_buf[at] = jnp.zeros((rows, WINDOW), halves)
                        v_buf[at] = jnp.zeros((rows, WINDOW), halves)

    def unit(m, c):
        mixed_grad = jnp.dot(grad_ref[m], weights[c, :, O_AT : O_AT + WINDOW], preferred_element_type=floats).astype(halves)
        mixed_grad = jnp.where(places > 0, mixed_grad.astype(floats), 0.0)
        product = mixed_grad * mixed_buf[c, m].astype(floats)
        product_high = product.astype(halves)
        product_low = (product - product_high.astype(floats)).astype(halves)
        pick = (
            lax.broadcasted_iota(jnp.int32, (8, WINDOW), 1) // HEAD_DIM == lax.broadcasted_iota(jnp.int32, (8, WINDOW), 0) + 1
        ).astype(floats).astype(halves)
        inner = contract_cols(pick, product_high) + contract_cols(pick, product_low)
        value_side = pltpu.roll(mixed_grad, WINDOW - HEAD_DIM, 1).astype(halves)
        queries = q_buf[m, c]
        query_heads = [keep(queries, places, h + 1) for h in range(3)]
        grad_heads = [keep(value_side, places, h) for h in range(3)]
        acc[...] = jnp.zeros_like(acc)
        key_weight = weights[c, :, K_AT : K_AT + WINDOW]
        value_weight = weights[c, :, V_AT : V_AT + WINDOW]

        def step(block, value_bias):
            keys = k_buf[m, c, block]
            values = v_buf[m, c, block]
            keys_t = keys.T
            hidden = mask[m, block].astype(floats)
            key_grad = jnp.zeros((rows, WINDOW), floats)
            value_grad = jnp.zeros((rows, WINDOW), floats)
            for h in range(3):
                p = jnp.exp(contract_cols(keys, query_heads[h]) + hidden - lse_ref[m, c, h : h + 1])
                prob_grad = contract_cols(values, grad_heads[h])
                score_grad = (p * (prob_grad - inner[h : h + 1])).astype(halves)
                value_grad = value_grad + jnp.dot(p.astype(halves), grad_heads[h], preferred_element_type=floats)
                key_grad = key_grad + jnp.dot(score_grad, query_heads[h], preferred_element_type=floats)
                at = pl.ds(h * HEAD_DIM, HEAD_DIM)
                acc[at, :] += jnp.dot(keys_t[(h + 1) * HEAD_DIM : (h + 2) * HEAD_DIM], score_grad, preferred_element_type=floats)
            key_low, value_low = key_grad.astype(halves), value_grad.astype(halves)
            k_buf[m, c, block] = key_low
            v_buf[m, c, block] = value_low
            spread[m, block] += contract_cols(key_low, key_weight) + contract_cols(value_low, value_weight)
            return value_bias + jnp.sum(value_low.astype(floats), 0, keepdims=True)

        value_bias = lax.fori_loop(low, high, step, jnp.zeros((1, WINDOW), floats))
        query_low = (acc[...].T * HEAD_DIM ** -0.5).astype(halves)
        q_buf[m, c] = query_low
        vec_buf[0, 0, pl.ds(small + c, 1), 0:WINDOW] += jnp.sum(query_low.astype(floats), 0, keepdims=True)
        vec_buf[0, 0, pl.ds(small + c, 1), WINDOW : 2 * WINDOW] += value_bias
        back_ref[m] += contract_cols(query_low, weights[c, :, Q_AT : Q_AT + WINDOW])

    def send_tokens(m):
        back_ref[m] += spread[m, z]

        @pl.loop(low, high)
        def _(block):
            tok_buf[m, block] = spread[m, block].astype(halves)

        start(*tokens[m])

    def weight_grads(c):
        strip = block_sum.shape[0]

        @pl.loop(0, model // strip)
        def _(part):
            base = pl.multiple_of(part * strip, strip)
            side = pl.ds(base, strip)
            block_sum[...] = jnp.zeros_like(block_sum)
            for m in range(micro):
                mine_at = pl.ds(pl.multiple_of((m * cols + z) * rows, rows), rows)
                block_sum[:, Q_AT : Q_AT + WINDOW] += jnp.dot(every_t[side, mine_at], q_buf[m, c], preferred_element_type=floats)
                all_at = pl.ds(m * cols * rows, cols * rows)
                block_sum[:, K_AT : K_AT + WINDOW] += jnp.dot(
                    every_t[side, all_at], k_buf[m, c].reshape(-1, WINDOW), preferred_element_type=floats)
                block_sum[:, V_AT : V_AT + WINDOW] += jnp.dot(
                    every_t[side, all_at], v_buf[m, c].reshape(-1, WINDOW), preferred_element_type=floats)
                block_sum[:, O_AT : O_AT + WINDOW] += jnp.dot(
                    grad_t[side, m * rows : (m + 1) * rows], mixed_buf[c, m], preferred_element_type=floats)
            for i in range(strip // (2 * rb)):
                ours = pl.ds(pl.multiple_of((2 * i + k) * rb, 16), rb)
                theirs = pl.ds(pl.multiple_of((2 * i + 1 - k) * rb, 16), rb)
                chip = part * (strip // (2 * rb)) + i
                mine_buf[0, c, chip // ny, lax.rem(chip, ny)] = block_sum[ours].astype(halves)
                stage_buf[c, chip // ny, lax.rem(chip, ny)] = block_sum[theirs].astype(halves)

    waited = []

    def attn_give(c):
        if not waited:
            pl.semaphore_wait(free_sem, 1)
            waited.append(c)
        post.send(("g", c), lambda: ("k", 1 - k, stage_buf.at[c], core_buf.at[0, c], None))

    def attn_add(c):
        post.wait(("g", c), "k", 1 - k, core_buf.at[0, c])

        @pl.loop(0, ns * ny)
        def _(n):
            at = (c, n // ny, lax.rem(n, ny))
            plus(mine_buf.at[(0, *at)], core_buf.at[(0, *at)])

    streams = ffn + attn
    added = set()

    def take_core(n):
        if n < 4:
            core(n)
            added.add(n)
            if added >= {0, 1} and n in (0, 1):
                pl.semaphore_signal(free_sem, 1, device_id=device("k", 1 - k), device_id_type=MESH)
        else:
            attn_add(n - 4)
        start(*streams[n].second)

    def take_second(n):
        finish(*streams[n].second)
        start(*streams[n].third)

    def take_third(n):
        finish(*streams[n].third)
        if n < 4:
            start(ffn_z[n])

    def along(line, e):
        for way in (1, -1):
            line.take(way, e)
            if e:
                line.forward(way, e)

    def take_tokens(m, h, e):
        line = tokens[m][h]
        if e == 0:
            at = half_of(h)

            def add(target, source):
                back_ref[m, at] += source[...].astype(floats)

            line.add = add
        along(line, e)

    def vectors(stage):
        if stage:
            vector_finish(stage - 1, "kyxz"[stage - 1], vec_buf.at[stage, 0] if stage < 4 else sums_ref)
        if stage < 4:
            vector_start(stage, "kyxz"[stage])

    def load():
        for copy in loads:
            copy.wait()
        clear()

    act = {
        "L": load, "G": lambda n: give(n) if n < 4 else attn_give(n - 4), "A": take_core, "B": take_second, "C": take_third,
        "Z": lambda n, e: along(ffn_z[n], e), "S": send_tokens, "T": take_tokens, "Ys": lambda: start(attn_z),
        "Y": lambda e: along(attn_z, e), "V": vectors,
    }
    head, tail, order = split_plan([("U", "W", task[1], 0) if task[0] == "W" else task for task in BACKWARD_PLAN])
    kinds = [item[0] == "W" for item in order]
    heads = [item[1] if item[0] == "W" else item[0] for item in order]
    micros = [0 if item[0] == "W" else item[1] for item in order]
    act[head[0][0]](*head[0][1:])
    spread[...] = jnp.zeros_like(spread)
    for m in range(micro):
        masks(m)
        grad_t[:, m * rows : (m + 1) * rows] = grad_ref[m].T
    for task in head[1:]:
        act[task[0]](*task[1:])

    @pl.loop(0, len(order))
    def _(step):
        c, m, kind = pick(step, heads), pick(step, micros), pick(step, [int(k_) for k_ in kinds])

        @pl.when(kind == 0)
        def _():
            unit(m, c)

        @pl.when(kind == 1)
        def _():
            weight_grads(c)

        for i, tasks in enumerate(tail[:-1]):
            if tasks:
                @pl.when(step == i)
                def _(tasks=tasks):
                    for task in tasks:
                        act[task[0]](*task[1:])

    for task in tail[-1]:
        act[task[0]](*task[1:])
    for j in range(3):
        block_ref[j] = mine_buf[j, z, x, y].astype(floats)
    post.close()


def backward(sizes, grad, share, first, turned, mixed, lse, q, k, v, seg_own, seg_all, part, vectors):
    ns, nr, nc = sizes
    ny = nr // 2
    micro, rows, model = grad.shape
    w = part.shape[-1]
    rb = model // (ns * nr)
    halves, floats = jnp.bfloat16, jnp.float32
    reach = min(nc - 1, -(-(DOC_MOST - 1) // rows))
    streams = 4 + nc
    count = 4 + nc + 4 * (ny - 1 + ns - 1) * streams + 5 * 2 * (nc - 1) + micro * 4 * reach + (1 + ny - 1 + ns - 1 + nc - 1)
    widest = max(ns, ny, nc, 2)
    ways = lambda n: 1 if n == 2 else 2
    vec_shape = (vectors.shape[0] + nc + -nc % 8, model)
    vmem = pl.BlockSpec(memory_space=pltpu.VMEM)
    anywhere = pl.BlockSpec(memory_space=pl.ANY)
    buf = lambda *shape, kind=halves: pltpu.VMEM(shape, kind)
    return pl.pallas_call(
        functools.partial(backward_kernel, sizes, micro),
        out_shape=[
            jax.ShapeDtypeStruct((micro, rows, model), floats),
            jax.ShapeDtypeStruct((3, rb, w), floats),
            jax.ShapeDtypeStruct(vec_shape, floats),
        ],
        in_specs=[vmem, anywhere, anywhere, anywhere, anywhere, vmem, anywhere, anywhere, anywhere, vmem, vmem, anywhere, vmem],
        out_specs=[vmem] * 3,
        scratch_shapes=[
            buf(3, nc, ns, ny, rb, w), buf(2, nc, ns, ny, rb, w), buf(nc, ns, ny, rb, w),
            buf(3, ways(ns), max(ns - 1, 1), nc, ny, rb, w // 2), buf(3, ways(ny), max(ny - 1, 1), nc, ns, rb, w // 2),
            buf(3, ways(ny), max(ny - 1, 1), nc, rb, w // 2), buf(3, ways(ns), max(ns - 1, 1), nc, rb, w // 2),
            buf(3, 2, max(nc - 1, 1), rb, w), buf(micro, nc, rows, model), buf(micro, 2, max(reach, 1), rows, model),
            buf(4, 1 + widest, *vec_shape, kind=floats),
            buf(nc, model, w), buf(nc, micro, rows, WINDOW), buf(micro, nc, rows, WINDOW),
            buf(micro, nc, nc, rows, WINDOW), buf(micro, nc, nc, rows, WINDOW),
            buf(model, micro * nc * rows), buf(model, micro * rows),
            buf(micro, nc, rows, rows), buf(WINDOW, rows, kind=floats), buf(micro, nc, rows, model, kind=floats), buf(model // 2, w, kind=floats),
            pltpu.SemaphoreType.DMA((count,)), pltpu.SemaphoreType.DMA((count,)), pltpu.SemaphoreType.DMA((24,)), pltpu.SemaphoreType.REGULAR,
        ],
        compiler_params=pltpu.CompilerParams(collective_id=3, has_side_effects=True, vmem_limit_bytes=62 << 20),
        name="backward",
    )(grad, share, first, turned, mixed, lse, q, k, v, seg_own.astype(floats)[:, None], seg_all.astype(floats).reshape(micro, nc, rows),
      part.reshape(2, nc, ns, ny, 2, rb, w), vectors)


def per_device_plain(sizes, inputs, segment_ids, query_weight, key_weight, value_weight, query_bias, value_bias,
               output_weight, output_bias, first_gain, first_shift, hidden_weight, hidden_bias, down_weight,
               down_bias, second_gain, second_shift, cotangent):
    floats, halves = jnp.float32, jnp.bfloat16
    cols = sizes[2]
    micro, _, rows, model = inputs.shape
    length = segment_ids.shape[-1]
    width = query_weight.shape[1]
    here = lax.axis_index("col")
    own = inputs[:, 0]
    shard = jnp.stack([
        jnp.concatenate([query_weight, key_weight, value_weight, output_weight.T], 1),
        hidden_weight,
        down_weight.T,
    ])
    biases = lax.all_gather(jnp.concatenate([query_bias, value_bias, hidden_bias]), "col", axis=0)
    everything, gathered = gather(sizes, own, shard)
    everything = everything.reshape(micro, length, model)
    attn_weights = gathered[0]
    wq, wk, wv, wot = (attn_weights[:, :, i * width : (i + 1) * width] for i in range(4))
    hidden_full, down_full = gathered[1], gathered[2]
    bq, bv, bh = biases[:, :width], biases[:, width : 2 * width], biases[:, 2 * width :]
    seg_all = segment_ids[:, 0]
    seg_own = lax.dynamic_slice_in_dim(seg_all, here * rows, rows, 1)
    first_key = jnp.sum((seg_all < seg_own[:, :1]).astype(jnp.int32), 1)
    last_key = jnp.sum((seg_all <= seg_own[:, -1:]).astype(jnp.int32), 1)
    bounds = jnp.stack([first_key // KEY_BLOCK, (last_key + KEY_BLOCK - 1) // KEY_BLOCK], 1)

    mixed, lse, q, k, v = attend(bounds, own, everything, wq, wk, wv, bq.astype(floats), bv.astype(floats), seg_own, seg_all)
    total = micro * rows
    flat = lambda a: a.reshape(total, -1)
    mixed_flat = mixed.reshape(cols, total, width)
    attn = sum(contract_cols(mixed_flat[c], wot[c]) for c in range(cols))
    first_sum = flat(own).astype(floats) + attn + output_bias.astype(floats)
    normal_one, scale_one = norm_parts(first_sum)
    gain_one = first_gain.astype(floats)
    normed = normal_one * gain_one + first_shift.astype(floats)
    normed_low = normed.astype(halves)
    ffn = 0
    activated, slopes = [], []
    for c in range(cols):
        hidden = jnp.dot(normed_low, hidden_full[c], preferred_element_type=floats) + bh[c].astype(floats)
        half_erf = 0.5 * lax.erf(hidden * 0.7071067811865476) + 0.5
        act = (hidden * half_erf).astype(halves)
        slope = half_erf + hidden * (jnp.exp(-0.5 * hidden * hidden) * 0.3989422804014327)
        activated.append(act)
        slopes.append(slope.astype(halves))
        ffn = ffn + contract_cols(act, down_full[c])
    second_sum = normed + ffn + down_bias.astype(floats)
    normal_two, scale_two = norm_parts(second_sum)
    gain_two = second_gain.astype(floats)
    outputs = (normal_two * gain_two + second_shift.astype(floats)).astype(halves)
    cot = flat(cotangent[:, 0]).astype(floats)
    second_grad = norm_back(cot * gain_two, normal_two, scale_two)
    ffn_grad = second_grad.astype(halves)
    hidden_grads, down_grads, hidden_bias_grads = [], [], []
    normed_grad = second_grad
    for c in range(cols):
        pre = (jnp.dot(ffn_grad, down_full[c], preferred_element_type=floats) * slopes[c].astype(floats)).astype(halves)
        hidden_grads.append(contract_rows(normed_low, pre).astype(halves))
        down_grads.append(contract_rows(ffn_grad, activated[c]).astype(halves))
        hidden_bias_grads.append(jnp.sum(pre.astype(floats), 0))
        normed_grad = normed_grad + contract_cols(pre, hidden_full[c])
    first_grad = norm_back(normed_grad * gain_one, normal_one, scale_one)
    attn_grad = first_grad.astype(halves)
    dq, dk, dv = attend_back(bounds, attn_grad.reshape(micro, rows, model), wot, mixed, lse, q, k, v, seg_own, seg_all)
    every_flat = everything.reshape(micro * length, model)
    attn_grads = []
    own_share = first_grad
    spread = 0
    for c in range(cols):
        dq_c, dk_c, dv_c = dq[c].reshape(total, width), dk[c].reshape(micro * length, width), dv[c].reshape(micro * length, width)
        attn_grads.append(jnp.concatenate([
            contract_rows(flat(own), dq_c), contract_rows(every_flat, dk_c), contract_rows(every_flat, dv_c),
            contract_rows(attn_grad, mixed_flat[c]),
        ], 1).astype(halves))
        own_share = own_share + contract_cols(dq_c, wq[c])
        spread = spread + contract_cols(dk_c, wk[c]) + contract_cols(dv_c, wv[c])
    bias_q = jnp.sum(dq.astype(floats), (1, 2)).reshape(-1)
    bias_v = jnp.sum(dv.astype(floats), (1, 2)).reshape(-1)
    vectors = jnp.concatenate([
        jnp.sum(first_grad, 0), jnp.sum(normed_grad * normal_one, 0), jnp.sum(normed_grad, 0), jnp.sum(second_grad, 0),
        jnp.sum(cot * normal_two, 0), jnp.sum(cot, 0), bias_q, bias_v, *hidden_bias_grads,
    ]).reshape(-1, model)
    partial = jnp.stack([jnp.stack(attn_grads), jnp.stack(hidden_grads), jnp.stack(down_grads)])
    input_grad, reduced, sums = reduce(sizes, own_share.reshape(micro, rows, model),
                                       spread.astype(halves).reshape(micro, cols, rows, model), partial, vectors)
    attn_block = reduced[0]
    piece = lambda i: attn_block[:, i * width : (i + 1) * width]
    mine = lambda vector, size: lax.dynamic_slice_in_dim(vector.reshape(-1), here * size, size, 0)
    return (
        outputs.reshape(micro, 1, rows, model), input_grad[:, None],
        piece(0), piece(1), piece(2), mine(sums[6], width), mine(sums[7], width), piece(3).T,
        sums[0], sums[1], sums[2], reduced[1], mine(sums[8:], hidden_bias.shape[0]), reduced[2].T,
        sums[3], sums[4], sums[5],
    )


def per_device_fused(sizes, inputs, segment_ids, query_weight, key_weight, value_weight, query_bias, value_bias,
               output_weight, output_bias, first_gain, first_shift, hidden_weight, hidden_bias, down_weight,
               down_bias, second_gain, second_shift, cotangent):
    floats, halves = jnp.float32, jnp.bfloat16
    cols = sizes[2]
    micro, _, rows, model = inputs.shape
    length = segment_ids.shape[-1]
    width = query_weight.shape[1]
    here = lax.axis_index("col")
    own = inputs[:, 0]
    shard = jnp.stack([
        jnp.concatenate([query_weight, key_weight, value_weight, output_weight.T], 1),
        hidden_weight,
        down_weight.T,
    ])
    pad = lambda vector: jnp.pad(vector.astype(floats), (0, model - vector.shape[0]))
    bias = jnp.stack([pad(hidden_bias), pad(query_bias), pad(value_bias)] + [jnp.zeros((model,), floats)] * 5)
    seg_all = segment_ids[:, 0]
    seg_own = lax.dynamic_slice_in_dim(seg_all, here * rows, rows, 1)
    rest, first, turned, biases, mixed, lse, q, k, v = forward(sizes, own, shard, bias, seg_own, seg_all)
    first = first.reshape(cols, model, 4 * width)
    total = micro * rows
    flat = lambda a: a.reshape(total, -1)
    vectors = jnp.stack([a.astype(floats) for a in (output_bias, first_gain, first_shift, down_bias, second_gain, second_shift)]
                        + [jnp.zeros((model,), floats)] * 2)
    outputs, first_grad, attn_grad, part, sums = middle(
        flat(own), mixed.reshape(cols, total, WINDOW), first, rest.reshape(2, cols, model, -1), biases, vectors, flat(cotangent[:, 0]))
    parted = lambda a: a.reshape(micro, rows, model)
    input_grad, reduced, sums = backward(sizes, parted(attn_grad), parted(first_grad), first, turned, mixed, lse, q, k, v,
                                         seg_own, seg_all, part, sums)
    piece = lambda i: reduced[0, :, i * width : (i + 1) * width]
    mine = lambda first_row, at, size: lax.dynamic_slice(sums, (first_row + here, at), (1, size))[0]
    heads_at = sums.shape[0] - (cols + -cols % 8)
    return (
        outputs.reshape(micro, 1, rows, model), input_grad[:, None],
        piece(0), piece(1), piece(2), mine(heads_at, 0, width), mine(heads_at, WINDOW, width), piece(3).T,
        sums[0], sums[1], sums[2], reduced[1], mine(8, 0, hidden_bias.shape[0]), reduced[2].T,
        sums[3], sums[4], sums[5],
    )


def per_device(sizes, inputs, segment_ids, query_weight, *rest):
    micro, _, rows, _ = inputs.shape
    fits = (query_weight.shape == (query_weight.shape[0] // 32 * 32, 3 * HEAD_DIM) and micro == 2 and sizes[2] == 4
            and DOC_MOST // 2 == rows)
    return (per_device_fused if fits else per_device_plain)(sizes, inputs, segment_ids, query_weight, *rest)


def solution(mesh):
    sizes = tuple(mesh.shape[name] for name in ("seq", "row", "col"))
    block, line = P(("seq", "row"), "col"), P("col", ("seq", "row"))
    tokens = P(None, ("seq", "row"), "col", None)
    placed = (tokens, P(None, ("seq", "row"), None), block, block, block, P("col"), P("col"), line, P(), P(), P(),
              block, P("col"), line, P(), P(), P(), tokens)
    given = (tokens, tokens, block, block, block, P("col"), P("col"), line, P(), P(), P(), block, P("col"), line,
             P(), P(), P())
    return jax.shard_map(functools.partial(per_device, sizes), mesh=mesh, in_specs=placed, out_specs=given, check_vma=False)
```

```python
import functools

import jax
import jax.numpy as jnp
from jax import lax
from jax.experimental import pallas as pl
from jax.experimental.pallas import tpu as pltpu
from jax.sharding import PartitionSpec as P

HEAD_DIM = 64
NORM_EPS = 1e-05
MASK_VALUE = -1000000000.0
DOC_MOST = 512
KEY_BLOCK = 256
MESH = pl.DeviceIdType.MESH


def contract_rows(left, right):
    return lax.dot_general(
        left, right, (((0,), (0,)), ((), ())), preferred_element_type=jnp.float32
    )


def contract_cols(left, right):
    return lax.dot_general(
        left, right, (((1,), (1,)), ((), ())), preferred_element_type=jnp.float32
    )


def norm_parts(summed):
    deviation = summed - jnp.mean(summed, -1, keepdims=True)
    scale = lax.rsqrt(jnp.mean(deviation * deviation, -1, keepdims=True) + NORM_EPS)
    return deviation * scale, scale


def norm_back(pull, normal, scale):
    return scale * (
        pull - jnp.mean(pull, -1, keepdims=True) - normal * jnp.mean(pull * normal, -1, keepdims=True)
    )

FORWARD_PLAN = (
    ("Zs", 1), ("Zs", 0), ("Zs", 3), ("Z", 1, 1), ("Z", 0, 1), ("Zs", 2), ("Z", 1, 2), ("Zs", 4), ("Z", 1, 3),
    ("Z", 0, 2), ("Z", 0, 3), ("Z", 2, 1), ("Z", 4, 1), ("Ts", 1), ("Z", 2, 2), ("B", 1), ("Z", 3, 1), ("Ts", 0),
    ("Z", 4, 2), ("B", 0), ("T", 1, 1), ("T", 0, 1), ("Z", 2, 3), ("Z", 3, 2), ("Ts", 3), ("C", 1), ("C", 0),
    ("Ts", 2), ("Z", 4, 3), ("K", 0), ("B", 2), ("T", 1, 2), ("T", 0, 2), ("R", 0), ("Zs", 5), ("K", 1), ("Z", 3, 3),
    ("B", 4), ("U", 0, 0), ("T", 3, 1), ("U", 0, 1), ("B", 3), ("U", 0, 2), ("T", 2, 1), ("C", 2), ("T", 3, 2),
    ("Z", 5, 1), ("C", 4), ("U", 0, 3), ("T", 2, 2), ("R", 1), ("C", 3), ("Z", 5, 2), ("K", 2), ("Z", 5, 3),
    ("U", 1, 0), ("K", 3), ("K", 4), ("B", 5), ("U", 1, 1), ("U", 1, 2), ("C", 5), ("U", 1, 3), ("K", 5),
)
BACKWARD_PLAN = (
    ("L",), ("G", 0), ("G", 2), ("U", 1, 0), ("A", 0), ("U", 0, 0), ("U", 2, 0), ("B", 0), ("A", 2), ("G", 1),
    ("G", 3), ("U", 3, 0), ("C", 0), ("S", 0), ("U", 2, 1), ("B", 2), ("U", 0, 1), ("Z", 0, 2), ("A", 1), ("A", 3),
    ("C", 2), ("T", 0, 1, 1), ("T", 0, 0, 1), ("U", 1, 1), ("U", 3, 1), ("S", 1), ("B", 1), ("V", 0), ("W", 2),
    ("V", 1), ("B", 3), ("G", 6), ("Z", 2, 2), ("W", 0), ("G", 4), ("V", 2), ("A", 6), ("C", 1), ("W", 3),
    ("T", 1, 0, 1), ("G", 7), ("A", 4), ("W", 1), ("G", 5), ("A", 7), ("T", 1, 1, 1), ("B", 6), ("C", 3), ("A", 5),
    ("Z", 2, 1), ("T", 0, 1, 0), ("Z", 1, 2), ("Z", 3, 2), ("B", 4), ("V", 3), ("Z", 0, 1), ("B", 7), ("B", 5),
    ("Z", 2, 0), ("C", 6), ("C", 4), ("T", 1, 0, 0), ("C", 7), ("Y", 3, 3), ("Y", 2, 2), ("Y", 0, 3), ("Z", 1, 1),
    ("T", 0, 0, 0), ("C", 5), ("Y", 1, 2), ("V", 4), ("Y", 3, 2), ("Y", 2, 1), ("Y", 0, 2), ("Z", 3, 1), ("Z", 1, 0),
    ("Y", 0, 1), ("T", 1, 1, 0), ("Y", 1, 1), ("Y", 3, 1), ("Z", 0, 0), ("Y", 2, 0), ("Z", 3, 0), ("Y", 0, 0),
    ("Y", 3, 0), ("Y", 1, 0),
)
def attend_kernel(bounds, own_ref, all_ref, wq_ref, wk_ref, wv_ref, bq_ref, bv_ref,
                  segq_ref, segk_ref, mixed_ref, lse_ref, q_ref, k_ref, v_ref, bias, acc, top, total):
    micro = pl.program_id(0)
    low, high = bounds[micro, 0], bounds[micro, 1]
    floats, halves = jnp.float32, jnp.bfloat16
    width = wq_ref.shape[-1]
    heads = width // HEAD_DIM
    rows = own_ref.shape[1]

    @pl.when(pl.program_id(1) == 0)
    def _():
        same = segk_ref[0] == segq_ref[0, 0:1]
        bias[...] = jnp.where(same, 0.0, MASK_VALUE)

    queries = jnp.dot(own_ref[0], wq_ref[0], preferred_element_type=floats) + bq_ref[0]
    queries = queries.astype(halves) * jnp.asarray(HEAD_DIM ** -0.5, halves)
    q_ref[0, 0] = queries
    lane = lax.broadcasted_iota(jnp.int32, (rows, width), 1) // HEAD_DIM
    query_heads = [jnp.where(lane == h, queries, jnp.zeros_like(queries)) for h in range(heads)]
    acc[...] = jnp.zeros_like(acc)
    total[...] = jnp.zeros_like(total)
    top[...] = jnp.full_like(top, 2 * MASK_VALUE)

    def step(block, carry):
        at = pl.ds(pl.multiple_of(block * KEY_BLOCK, KEY_BLOCK), KEY_BLOCK)
        x = all_ref[0, at, :]
        keys = jnp.dot(x, wk_ref[0], preferred_element_type=floats).astype(halves)
        k_ref[0, 0, at, :] = keys
        values = (jnp.dot(x, wv_ref[0], preferred_element_type=floats) + bv_ref[0]).astype(halves)
        v_ref[0, 0, at, :] = values
        values_t = values.T
        mask = bias[at, :]
        for h in range(heads):
            s = contract_cols(keys, query_heads[h]) + mask
            old = top[h : h + 1]
            new = jnp.maximum(old, jnp.max(s, 0, keepdims=True))
            p = jnp.exp(s - new)
            shrink = jnp.exp(old - new)
            top[h : h + 1] = new
            total[h : h + 1] = total[h : h + 1] * shrink + jnp.sum(p, 0, keepdims=True)
            part = pl.ds(h * HEAD_DIM, HEAD_DIM)
            acc[part, :] = acc[part, :] * shrink + jnp.dot(
                values_t[h * HEAD_DIM : (h + 1) * HEAD_DIM], p.astype(halves), preferred_element_type=floats
            )
        return carry

    lax.fori_loop(low, high, step, 0)
    for h in range(heads):
        part = pl.ds(h * HEAD_DIM, HEAD_DIM)
        acc[part, :] = acc[part, :] / total[h : h + 1]
    mixed_ref[0, 0] = acc[...].T.astype(halves)
    lse_ref[0, 0] = top[...] + jnp.log(jnp.maximum(total[...], 1e-30))


def attend(bounds, own, everything, wq, wk, wv, bq, bv, seg_own, seg_all):
    micro, rows, model = own.shape
    length = everything.shape[1]
    cols, _, width = wq.shape
    halves = jnp.bfloat16
    weight = pl.BlockSpec((1, model, width), lambda m, c, b: (c, 0, 0))
    per = lambda a, b_: pl.BlockSpec((1, 1, a, b_), lambda m, c, b: (c, m, 0, 0))
    spec = pltpu.PrefetchScalarGridSpec(
        num_scalar_prefetch=1,
        grid=(micro, cols),
        in_specs=[
            pl.BlockSpec((1, rows, model), lambda m, c, b: (m, 0, 0)),
            pl.BlockSpec((1, length, model), lambda m, c, b: (m, 0, 0)),
            weight, weight, weight,
            pl.BlockSpec((1, 1, width), lambda m, c, b: (c, 0, 0)),
            pl.BlockSpec((1, 1, width), lambda m, c, b: (c, 0, 0)),
            pl.BlockSpec((1, 1, rows), lambda m, c, b: (m, 0, 0)),
            pl.BlockSpec((1, length, 1), lambda m, c, b: (m, 0, 0)),
        ],
        out_specs=[per(rows, width), per(8, rows), per(rows, width), per(length, width), per(length, width)],
        scratch_shapes=[
            pltpu.VMEM((length, rows), jnp.float32),
            pltpu.VMEM((width, rows), jnp.float32),
            pltpu.VMEM((8, rows), jnp.float32),
            pltpu.VMEM((8, rows), jnp.float32),
        ],
    )
    shape = lambda a, b_, d=halves: jax.ShapeDtypeStruct((cols, micro, a, b_), d)
    return pl.pallas_call(
        attend_kernel,
        grid_spec=spec,
        out_shape=[shape(rows, width), shape(8, rows, jnp.float32), shape(rows, width), shape(length, width), shape(length, width)],
        compiler_params=pltpu.CompilerParams(vmem_limit_bytes=48 << 20),
        name="attend",
    )(bounds, own, everything, wq, wk, wv, bq[:, None], bv[:, None],
      seg_own[:, None], seg_all[:, :, None])


def attend_back_kernel(bounds, grad_ref, wot_ref, mixed_ref, lse_ref, q_ref, k_ref, v_ref, segq_ref, segk_ref,
                       dq_ref, dk_ref, dv_ref, bias, acc):
    micro = pl.program_id(0)
    low, high = bounds[micro, 0], bounds[micro, 1]
    floats, halves = jnp.float32, jnp.bfloat16
    rows, width = q_ref.shape[2:]
    heads = width // HEAD_DIM

    @pl.when(pl.program_id(1) == 0)
    def _():
        same = segk_ref[0] == segq_ref[0, 0:1]
        bias[...] = jnp.where(same, 0.0, MASK_VALUE)

    mixed_grad = jnp.dot(grad_ref[0], wot_ref[0], preferred_element_type=floats).astype(halves)
    product = mixed_grad.astype(floats) * mixed_ref[0, 0].astype(floats)
    product_high = product.astype(halves)
    product_low = (product - product_high.astype(floats)).astype(halves)
    pick = (
        lax.broadcasted_iota(jnp.int32, (8, width), 1) // HEAD_DIM == lax.broadcasted_iota(jnp.int32, (8, width), 0)
    ).astype(halves)
    inner = contract_cols(pick, product_high) + contract_cols(pick, product_low)
    lane = lax.broadcasted_iota(jnp.int32, (rows, width), 1) // HEAD_DIM
    queries = q_ref[0, 0]
    query_heads = [jnp.where(lane == h, queries, jnp.zeros_like(queries)) for h in range(heads)]
    grad_heads = [jnp.where(lane == h, mixed_grad, jnp.zeros_like(mixed_grad)) for h in range(heads)]
    acc[...] = jnp.zeros_like(acc)
    dk_ref[...] = jnp.zeros_like(dk_ref)
    dv_ref[...] = jnp.zeros_like(dv_ref)

    def step(block, carry):
        at = pl.ds(pl.multiple_of(block * KEY_BLOCK, KEY_BLOCK), KEY_BLOCK)
        keys = k_ref[0, 0, at, :]
        values = v_ref[0, 0, at, :]
        keys_t = keys.T
        mask = bias[at, :]
        key_grad = jnp.zeros((KEY_BLOCK, width), floats)
        value_grad = jnp.zeros((KEY_BLOCK, width), floats)
        for h in range(heads):
            s = contract_cols(keys, query_heads[h]) + mask
            p = jnp.exp(s - lse_ref[0, 0, h : h + 1])
            prob_grad = contract_cols(values, grad_heads[h])
            score_grad = (p * (prob_grad - inner[h : h + 1])).astype(halves)
            value_grad = value_grad + jnp.dot(p.astype(halves), grad_heads[h], preferred_element_type=floats)
            key_grad = key_grad + jnp.dot(score_grad, query_heads[h], preferred_element_type=floats)
            part = pl.ds(h * HEAD_DIM, HEAD_DIM)
            acc[part, :] += jnp.dot(keys_t[h * HEAD_DIM : (h + 1) * HEAD_DIM], score_grad, preferred_element_type=floats)
        dk_ref[0, 0, at, :] = key_grad.astype(halves)
        dv_ref[0, 0, at, :] = value_grad.astype(halves)
        return carry

    lax.fori_loop(low, high, step, 0)
    dq_ref[0, 0] = (acc[...].T * HEAD_DIM ** -0.5).astype(halves)


def attend_back(bounds, grad, wot, mixed, lse, q, k, v, seg_own, seg_all):
    micro, rows, model = grad.shape
    cols, _, length, width = k.shape
    halves = jnp.bfloat16
    per = lambda a, b_: pl.BlockSpec((1, 1, a, b_), lambda m, c, b: (c, m, 0, 0))
    spec = pltpu.PrefetchScalarGridSpec(
        num_scalar_prefetch=1,
        grid=(micro, cols),
        in_specs=[
            pl.BlockSpec((1, rows, model), lambda m, c, b: (m, 0, 0)),
            pl.BlockSpec((1, model, width), lambda m, c, b: (c, 0, 0)),
            per(rows, width), per(8, rows), per(rows, width), per(length, width), per(length, width),
            pl.BlockSpec((1, 1, rows), lambda m, c, b: (m, 0, 0)),
            pl.BlockSpec((1, length, 1), lambda m, c, b: (m, 0, 0)),
        ],
        out_specs=[per(rows, width), per(length, width), per(length, width)],
        scratch_shapes=[pltpu.VMEM((length, rows), jnp.float32), pltpu.VMEM((width, rows), jnp.float32)],
    )
    shape = lambda a, b_, d=halves: jax.ShapeDtypeStruct((cols, micro, a, b_), d)
    return pl.pallas_call(
        attend_back_kernel,
        grid_spec=spec,
        out_shape=[shape(rows, width), shape(length, width), shape(length, width)],
        compiler_params=pltpu.CompilerParams(vmem_limit_bytes=48 << 20),
        name="attend_back",
    )(bounds, grad, wot, mixed, lse, q, k, v, seg_own[:, None], seg_all[:, :, None])


def place(sizes):
    seq, row, col = (lax.axis_index(name) for name in ("seq", "row", "col"))
    lines = {"x": (seq, sizes[0]), "y": (row // 2, sizes[1] // 2), "k": (lax.rem(row, 2), 2), "z": (col, sizes[2])}

    def device(axis, index):
        if axis == "x":
            return (index, row, col)
        if axis == "y":
            return (seq, index * 2 + lax.rem(row, 2), col)
        if axis == "k":
            return (seq, row // 2 * 2 + index, col)
        return (seq, row, index)

    return lines, device


def greet(lines, device):
    barrier = pltpu.get_barrier_semaphore()
    count = 0
    for axis, (mine, size) in lines.items():
        for t in range(1, size):
            pl.semaphore_signal(barrier, inc=1, device_id=device(axis, lax.rem(mine + t, size)), device_id_type=MESH)
            count += 1
    pl.semaphore_wait(barrier, count)


class Post:
    def __init__(self, device, send_sems, recv_sems):
        self.device, self.send_sems, self.recv_sems = device, send_sems, recv_sems
        self.slots, self.sent = {}, []

    def slot(self, key):
        return self.slots.setdefault(key, len(self.slots))

    def copy(self, key, axis, index, source, target):
        n = self.slot(key)
        return pltpu.make_async_remote_copy(
            src_ref=source, dst_ref=target, send_sem=self.send_sems.at[n], recv_sem=self.recv_sems.at[n],
            device_id=self.device(axis, index), device_id_type=MESH,
        )

    def send(self, key, make):
        def run(act):
            axis, index, source, target, when = make()

            def go():
                act(self.copy(key, axis, index, source, target))

            if when is None:
                go()
            else:
                pl.when(when)(go)

        run(lambda copy: copy.start())
        self.sent.append(run)

    def wait(self, key, axis, index, target, when=None):
        def go():
            self.copy(key, axis, index, target, target).wait_recv()

        if when is None:
            go()
        else:
            pl.when(when)(go)

    def close(self):
        for run in self.sent:
            run(lambda copy: copy.wait_send())


def clip(index, size):
    return jnp.clip(index, 0, size - 1)


class LineGather:
    def __init__(self, post, name, axis, line, region, reach=None):
        self.post, self.name, self.axis, self.region = post, name, axis, region
        self.mine, self.size = line
        self.reach = min(self.size - 1, reach or self.size)

    def hop(self, way, t):
        mine, size = self.mine, self.size

        def make():
            origin, target = mine - way * t, mine + way
            ok = (origin >= 0) & (origin < size) & (target >= 0) & (target < size)
            here = self.region(clip(origin, size))
            return self.axis, clip(target, size), here, here, ok

        self.post.send((self.name, way, t + 1), make)

    def start(self):
        for way in (1, -1):
            if self.reach >= 1:
                self.hop(way, 0)

    def step(self, t):
        if t > self.reach:
            return
        for way in (1, -1):
            origin = self.mine - way * t
            ok = (origin >= 0) & (origin < self.size)
            self.post.wait((self.name, way, t), self.axis, clip(self.mine - way, self.size), self.region(clip(origin, self.size)), ok)
            if t < self.reach:
                self.hop(way, t)

    def finish(self, first=1):
        for t in range(first, self.reach + 1):
            self.step(t)


def gather_kernel(sizes, micro, own_ref, shard_ref, every_ref, full_ref, send_sems, recv_sems, local_sems):
    lines, device = place(sizes)
    (x, _), (y, _), (k, _), (z, cols) = (lines[a] for a in "xykz")
    half = shard_ref.shape[-1] // 2
    rows = own_ref.shape[1]
    reach = -(-(DOC_MOST - 1) // rows)
    parts = [pl.ds(p * half, half) for p in (0, 1)]
    local = [pltpu.make_async_copy(shard_ref.at[j], full_ref.at[j, z, x, y, k], local_sems.at[j]) for j in range(3)]
    local += [pltpu.make_async_copy(own_ref.at[m], every_ref.at[m, z], local_sems.at[3 + m]) for m in range(micro)]
    for copy in local:
        copy.start()
    greet(lines, device)
    post = Post(device, send_sems, recv_sems)
    for copy in local:
        copy.wait()
    zs = [LineGather(post, ("z", j), "z", lines["z"], lambda i, j=j: full_ref.at[j, i, x, y, k]) for j in range(3)]
    tokens = [LineGather(post, ("t", m), "z", lines["z"], lambda i, m=m: every_ref.at[m, i], reach) for m in range(micro)]
    second, third = {}, {}
    for j in range(3):
        second[j] = [
            LineGather(post, ("a", j), "y", lines["y"], lambda i, j=j: full_ref.at[j, :, x, i, k, :, parts[0]]),
            LineGather(post, ("b", j), "x", lines["x"], lambda i, j=j: full_ref.at[j, :, i, y, k, :, parts[1]]),
        ]
        third[j] = [
            LineGather(post, ("c", j), "x", lines["x"], lambda i, j=j: full_ref.at[j, :, i, :, k, :, parts[0]]),
            LineGather(post, ("d", j), "y", lines["y"], lambda i, j=j: full_ref.at[j, :, :, i, k, :, parts[1]]),
        ]

    def start(group):
        for line in group:
            line.start()

    def finish(group):
        for line in group:
            line.finish()

    def swap(j):
        plane = full_ref.at[j, :, :, :, k]
        post.send(("k", j), lambda: ("k", 1 - k, plane, plane, None))

    start(zs[:1])
    finish(zs[:1])
    start(second[0] + zs[1:2])
    finish(second[0])
    start(third[0])
    finish(zs[1:2])
    start(second[1] + tokens[:1])
    finish(third[0])
    swap(0)
    finish(second[1])
    start(third[1])
    finish(tokens[:1])
    start(zs[2:])
    finish(zs[2:])
    start(second[2] + tokens[1:])
    finish(third[1])
    swap(1)
    finish(second[2])
    start(third[2])
    finish(tokens[1:])
    finish(third[2])
    swap(2)
    for i in range(cols):
        far = (z - i > reach) | (i - z > reach)
        for m in range(micro):
            def fill(m=m, i=i):
                copy = pltpu.make_async_copy(own_ref.at[m], every_ref.at[m, i], local_sems.at[3 + m])
                copy.start()
                copy.wait()

            if i > reach or cols - 1 - i > reach:
                pl.when(far)(fill)
    for j in range(3):
        post.wait(("k", j), "k", 1 - k, full_ref.at[j, :, :, :, 1 - k])
    post.close()


def gather(sizes, own, shard):
    ns, nr, nc = sizes
    ny = nr // 2
    micro, rows, model = own.shape
    _, rb, w = shard.shape
    count = 3 * 2 * (nc - 1) + micro * 2 * (nc - 1) + 3 * (4 * (ny - 1) + 4 * (ns - 1) + 1)
    anywhere = pl.BlockSpec(memory_space=pl.ANY)
    every, full = pl.pallas_call(
        functools.partial(gather_kernel, sizes, micro),
        out_shape=[
            jax.ShapeDtypeStruct((micro, nc, rows, model), own.dtype),
            jax.ShapeDtypeStruct((3, nc, ns, ny, 2, rb, w), shard.dtype),
        ],
        in_specs=[pl.BlockSpec(memory_space=pltpu.VMEM)] * 2,
        out_specs=[anywhere] * 2,
        scratch_shapes=[pltpu.SemaphoreType.DMA((count,)), pltpu.SemaphoreType.DMA((count,)), pltpu.SemaphoreType.DMA((3 + micro,))],
        compiler_params=pltpu.CompilerParams(collective_id=0, has_side_effects=True),
        name="gather",
    )(own, shard)
    return every, full.reshape(3, nc, ns * nr * rb, w)


class LineReduce:
    def __init__(self, post, name, axis, line, region, inbox, add, reach=None):
        self.post, self.name, self.axis, self.region, self.inbox, self.add = post, name, axis, region, inbox, add
        self.mine, self.size = line
        self.reach = min(self.size - 1, reach or self.size)

    def arrived(self, way, e):
        behind, goal = self.mine - way, self.mine + way * e
        return (behind >= 0) & (behind < self.size) & (goal >= 0) & (goal < self.size)

    def take(self, way, e):
        ok = self.arrived(way, e)
        inbox = self.inbox(way, e)
        self.post.wait((self.name, way, e), self.axis, clip(self.mine - way, self.size), inbox, ok)

        @pl.when(ok)
        def _():
            self.add(self.region(clip(self.mine + way * e, self.size)), inbox)

    def forward(self, way, e):
        def make():
            goal = self.mine + way * e
            ok = (goal >= 0) & (goal < self.size)
            return self.axis, clip(self.mine + way, self.size), self.region(clip(goal, self.size)), self.inbox(way, e - 1), ok

        self.post.send((self.name, way, e - 1), make)

    def start(self):
        for way in (1, -1):
            if self.reach >= 1:
                self.forward(way, self.reach)

    def forward_from(self, nearest):
        for e in range(self.reach - 1, nearest - 1, -1):
            for way in (1, -1):
                self.take(way, e)
                self.forward(way, e)

    def finish(self, last=True):
        self.forward_from(1)
        if last:
            for way in (1, -1):
                if self.reach >= 1:
                    self.take(way, 0)


def reduce_to(post, name, axis, line, goal, e, region, inbox, add):
    mine, size = line
    for way in (1, -1):
        behind = mine - way
        arrives = (way * (goal - mine) == e) & (behind >= 0) & (behind < size)
        slot = inbox(way, min(e, size - 2))
        post.wait((name, way), axis, clip(behind, size), slot, arrives)

        @pl.when(arrives)
        def _():
            add(region, slot)

        def make(way=way):
            return axis, clip(mine + way, size), region, inbox(way, e - 1), way * (goal - mine) == e

        if e:
            post.send((name, way), make)


def reduce_kernel(sizes, micro, own_ref, spread_ref, part_ref, vec_ref, back_ref, block_ref, sums_ref,
                  mine_buf, core_buf, in_a, in_b, in_c, in_d, in_z, tok_buf, tok_in, vec_buf, send_sems, recv_sems, local_sems):
    floats, halves = jnp.float32, jnp.bfloat16
    lines, device = place(sizes)
    (x, ns), (y, ny), (k, _), (z, nc) = (lines[a] for a in "xykz")
    half = part_ref.shape[-1] // 2
    rows = own_ref.shape[1]
    reach = -(-(DOC_MOST - 1) // rows)
    parts = [pl.ds(p * half, half) for p in (0, 1)]
    local = [pltpu.make_async_copy(part_ref.at[j, :, :, :, k], mine_buf.at[j], local_sems.at[j]) for j in range(3)]
    local += [pltpu.make_async_copy(spread_ref.at[m], tok_buf.at[m], local_sems.at[3 + m]) for m in range(micro)]
    for copy in local:
        copy.start()
    greet(lines, device)
    post = Post(device, send_sems, recv_sems)
    for j in range(3):
        post.send(("k", j), lambda j=j: ("k", 1 - k, part_ref.at[j, :, :, :, 1 - k], core_buf.at[j], None))

    def plus(target, source):
        target[...] = (target[...].astype(floats) + source[...].astype(floats)).astype(halves)

    def plus_grid(target, source, first, second):
        @pl.loop(0, first * second)
        def _(n):
            plus(target.at[n // second, lax.rem(n, second)], source.at[n // second, lax.rem(n, second)])

    def plus_row(target, source, first):
        @pl.loop(0, first)
        def _(n):
            plus(target.at[n], source.at[n])

    vec_buf[0, 0] = vec_ref[...]

    def vector_start(stage, axis):
        mine, size = lines[axis]
        vec_buf[stage, 1 + mine] = vec_buf[stage, 0]
        for t in range(1, size):
            post.send(("v", stage, t), lambda t=t: (
                axis, lax.rem(mine + t, size), vec_buf.at[stage, 0], vec_buf.at[stage, 1 + mine], None))

    def vector_finish(stage, axis, out):
        mine, size = lines[axis]
        for t in range(1, size):
            origin = lax.rem(mine + size - t, size)
            post.wait(("v", stage, t), axis, origin, vec_buf.at[stage, 1 + origin])
        total = vec_buf[stage, 1]
        for i in range(1, size):
            total = total + vec_buf[stage, 1 + i]
        out[...] = total

    tokens = [
        LineReduce(post, ("t", m), "z", lines["z"], lambda i, m=m: tok_buf.at[m, i],
                   lambda way, e, m=m: tok_in.at[m, (1 - way) // 2, e], plus, reach)
        for m in range(micro)
    ]
    box = lambda way: (1 - way) // 2
    second, third, last = {}, {}, {}
    for j in range(3):
        second[j] = [
            LineReduce(post, ("a", j), "x", lines["x"], lambda i, j=j: mine_buf.at[j, :, i, :, :, parts[0]],
                       lambda way, e, j=j: in_a.at[j, box(way), e], lambda t, s: plus_grid(t, s, nc, ny)),
            LineReduce(post, ("b", j), "y", lines["y"], lambda i, j=j: mine_buf.at[j, :, :, i, :, parts[1]],
                       lambda way, e, j=j: in_b.at[j, box(way), e], lambda t, s: plus_grid(t, s, nc, ns)),
        ]
        third[j] = [
            LineReduce(post, ("c", j), "y", lines["y"], lambda i, j=j: mine_buf.at[j, :, x, i, :, parts[0]],
                       lambda way, e, j=j: in_c.at[j, box(way), e], lambda t, s: plus_row(t, s, nc)),
            LineReduce(post, ("d", j), "x", lines["x"], lambda i, j=j: mine_buf.at[j, :, i, y, :, parts[1]],
                       lambda way, e, j=j: in_d.at[j, box(way), e], lambda t, s: plus_row(t, s, nc)),
        ]
        last[j] = [
            LineReduce(post, ("z", j), "z", lines["z"], lambda i, j=j: mine_buf.at[j, i, x, y],
                       lambda way, e, j=j: in_z.at[j, box(way), e], plus)
        ]

    def start(group):
        for line in group:
            line.start()

    def finish(group):
        for line in group:
            line.finish()

    def core(j):
        local[j].wait()
        post.wait(("k", j), "k", 1 - k, core_buf.at[j])

        @pl.loop(0, nc * ns * ny)
        def _(n):
            at = (n // (ns * ny), lax.rem(n // ny, ns), lax.rem(n, ny))
            plus(mine_buf.at[(j, *at)], core_buf.at[(j, *at)])

    for m in range(micro):
        local[3 + m].wait()
    start(tokens)
    core(0)
    start(second[0])
    vector_start(0, "k")
    core(1)
    start(second[1])
    vector_finish(0, "k", vec_buf.at[1, 0])
    vector_start(1, "y")
    core(2)
    finish(second[0])
    start(third[0])
    start(second[2])
    vector_finish(1, "y", vec_buf.at[2, 0])
    vector_start(2, "x")
    finish(tokens)
    vector_finish(2, "x", vec_buf.at[3, 0])
    vector_start(3, "z")
    finish(second[1])
    start(third[1])
    finish(third[0])
    start(last[0])
    finish(second[2])
    start(third[2])
    finish(third[1])
    start(last[1])
    finish(last[0])
    finish(third[2])
    start(last[2])
    vector_finish(3, "z", sums_ref)
    for m in range(micro):
        back_ref[m] = own_ref[m] + tok_buf[m, z].astype(floats)
    finish(last[1])
    finish(last[2])
    for j in range(3):
        block_ref[j] = mine_buf[j, z, x, y].astype(floats)
    post.close()


def reduce(sizes, own_share, spread, partial, vectors):
    ns, nr, nc = sizes
    ny = nr // 2
    micro, rows, model = own_share.shape
    w = partial.shape[-1]
    rb = partial.shape[2] // (ns * nr)
    halves, floats = jnp.bfloat16, jnp.float32
    reach = min(nc - 1, -(-(DOC_MOST - 1) // rows))
    count = 3 + 2 * (ny - 1 + ns - 1) * 6 + 3 * 2 * (nc - 1) + micro * 2 * reach + (1 + ny - 1 + ns - 1 + nc - 1)
    widest = max(ns, ny, nc, 2)
    extra = -vectors.shape[0] % 8
    vectors = jnp.pad(vectors, ((0, extra), (0, 0)))
    vmem = pl.BlockSpec(memory_space=pltpu.VMEM)
    anywhere = pl.BlockSpec(memory_space=pl.ANY)
    back, blocks, sums = pl.pallas_call(
        functools.partial(reduce_kernel, sizes, micro),
        out_shape=[
            jax.ShapeDtypeStruct((micro, rows, model), floats),
            jax.ShapeDtypeStruct((3, rb, w), floats),
            jax.ShapeDtypeStruct(vectors.shape, floats),
        ],
        in_specs=[vmem, anywhere, anywhere, vmem],
        out_specs=[vmem] * 3,
        scratch_shapes=[
            pltpu.VMEM((3, nc, ns, ny, rb, w), halves),
            pltpu.VMEM((3, nc, ns, ny, rb, w), halves),
            pltpu.VMEM((3, 2, max(ns - 1, 1), nc, ny, rb, w // 2), halves),
            pltpu.VMEM((3, 2, max(ny - 1, 1), nc, ns, rb, w // 2), halves),
            pltpu.VMEM((3, 2, max(ny - 1, 1), nc, rb, w // 2), halves),
            pltpu.VMEM((3, 2, max(ns - 1, 1), nc, rb, w // 2), halves),
            pltpu.VMEM((3, 2, max(nc - 1, 1), rb, w), halves),
            pltpu.VMEM((micro, nc, rows, model), halves),
            pltpu.VMEM((micro, 2, max(reach, 1), rows, model), halves),
            pltpu.VMEM((4, 1 + widest, *vectors.shape), floats),
            pltpu.SemaphoreType.DMA((count,)),
            pltpu.SemaphoreType.DMA((count,)),
            pltpu.SemaphoreType.DMA((3 + micro,)),
        ],
        compiler_params=pltpu.CompilerParams(collective_id=1, has_side_effects=True, vmem_limit_bytes=60 << 20),
        name="reduce",
    )(own_share, spread, partial.reshape(3, nc, ns, ny, 2, rb, w), vectors)
    return back, blocks, sums


Q_AT, K_AT, V_AT, O_AT, WINDOW = 0, 128, 384, 512, 256


def plane(full_ref, c, at, size=WINDOW):
    value = full_ref[c, :, :, :, :, at : at + size]
    return value.reshape(-1, size)


def split_plan(plan):
    parts, order = [[]], []
    for task in plan:
        if task[0] == "U":
            order.append(task[1:])
            parts.append([])
        else:
            parts[-1].append(task)
    return parts[0], parts[1:], order


def pick(step, values):
    value = values[0]
    for i, other in enumerate(values[1:], 1):
        value = jnp.where(step == i, other, value)
    return value


def place_of(rows):
    return lax.broadcasted_iota(jnp.int32, (rows, WINDOW), 1) // HEAD_DIM


def keep(value, places, wanted):
    return jnp.where(places == wanted, value, jnp.zeros_like(value))


def forward_kernel(sizes, micro, own_ref, shard_ref, hidden_bias_ref, query_bias_ref, value_bias_ref, seg_ref,
                   rest_ref, first_ref, turned_ref, mask_ref, biases_ref, mixed_ref, lse_ref, q_ref, k_ref, v_ref,
                   weights, turned, bias_buf, mask, mixed_buf, lse_buf, q_buf, k_buf, v_buf, tokens_buf, acc, top, total,
                   send_sems, recv_sems, local_sems):
    floats, halves = jnp.float32, jnp.bfloat16
    lines, device = place(sizes)
    (x, _), (y, _), (k, _), (z, cols) = (lines[a] for a in "xykz")
    half = shard_ref.shape[-1] // 2
    rows = own_ref.shape[1]
    reach = -(-(DOC_MOST - 1) // rows)
    parts = [pl.ds(p * half, half) for p in (0, 1)]
    low, high = jnp.maximum(z - reach, 0), jnp.minimum(z + reach + 1, cols)
    used = [0]

    def local(source, target):
        copy = pltpu.make_async_copy(source, target, local_sems.at[used[0]])
        used[0] += 1
        copy.start()
        return copy

    targets = [weights.at[0], rest_ref.at[0], rest_ref.at[1]]
    begin = [local(shard_ref.at[j], targets[j].at[z, x, y, k]) for j in range(3)]
    begin += [local(own_ref.at[m], tokens_buf.at[m, z]) for m in range(micro)]
    for i, ref in enumerate((hidden_bias_ref, query_bias_ref, value_bias_ref)):
        bias_buf[z, i : i + 1, 0 : ref.shape[0]] = ref[...].astype(floats).reshape(1, -1)
        if ref.shape[0] < WINDOW:
            bias_buf[z, i : i + 1, ref.shape[0] : WINDOW] = jnp.zeros((1, WINDOW - ref.shape[0]), floats)
    greet(lines, device)
    post = Post(device, send_sems, recv_sems)
    for copy in begin:
        copy.wait()
    tokens = [
        LineGather(post, ("t", q), "z", lines["z"],
                   lambda i, q=q: tokens_buf.at[q // 2, i, pl.ds(q % 2 * (rows // 2), rows // 2)], reach)
        for q in range(2 * micro)
    ]
    small = LineGather(post, "bias", "z", lines["z"], lambda i: bias_buf.at[i])
    rb = shard_ref.shape[1]
    zs, second, third = {}, {}, {}
    for n in range(6):
        j, r = n // 2, pl.ds(n % 2 * (rb // 2), rb // 2)
        zs[n] = LineGather(post, ("z", n), "z", lines["z"], lambda i, j=j, r=r: targets[j].at[i, x, y, k, r])
        second[n] = [
            LineGather(post, ("a", n), "y", lines["y"], lambda i, j=j, r=r: targets[j].at[:, x, i, k, r, parts[0]]),
            LineGather(post, ("b", n), "x", lines["x"], lambda i, j=j, r=r: targets[j].at[:, i, y, k, r, parts[1]]),
        ]
        third[n] = [
            LineGather(post, ("c", n), "x", lines["x"], lambda i, j=j, r=r: targets[j].at[:, i, :, k, r, parts[0]]),
            LineGather(post, ("d", n), "y", lines["y"], lambda i, j=j, r=r: targets[j].at[:, :, i, k, r, parts[1]]),
        ]

    def start(*group):
        for line in group:
            line.start()

    def finish(*group):
        for line in group:
            line.finish()

    def side(n, which):
        return targets[n // 2].at[:, :, :, which, pl.ds(n % 2 * (rb // 2), rb // 2)]

    def swap(n):
        post.send(("k", n), lambda: ("k", 1 - k, side(n, k), side(n, k), None))

    def swapped(n):
        post.wait(("k", n), "k", 1 - k, side(n, 1 - k))

    places = place_of(rows)

    def unit(m, c):
        queries = jnp.dot(own_ref[m], plane(weights.at[0], c, Q_AT), preferred_element_type=floats) + bias_buf[c, 1:2, 0:WINDOW]
        queries = pltpu.roll(queries.astype(halves).astype(floats) * HEAD_DIM ** -0.5, HEAD_DIM, 1)
        queries = jnp.where(places > 0, queries, 0.0).astype(halves)
        q_buf[m, c] = queries
        heads = [keep(queries, places, h + 1) for h in range(3)]
        acc[...] = jnp.zeros_like(acc)
        total[...] = jnp.zeros_like(total)
        top[...] = jnp.full_like(top, 2 * MASK_VALUE)
        key_weight = plane(weights.at[0], c, K_AT)
        value_weight = plane(weights.at[0], c, V_AT)
        value_bias = bias_buf[c, 2:3, 0:WINDOW]

        def step(block):
            rows_at = tokens_buf[m, block]
            keys = jnp.dot(rows_at, key_weight, preferred_element_type=floats).astype(halves)
            values = (jnp.dot(rows_at, value_weight, preferred_element_type=floats) + value_bias).astype(halves)
            k_buf[m, c, block] = keys
            v_buf[m, c, block] = values
            values_t = values.T
            hidden = mask[m, block].astype(floats)
            for h in range(3):
                s = contract_cols(keys, heads[h]) + hidden
                old = top[h : h + 1]
                new = jnp.maximum(old, jnp.max(s, 0, keepdims=True))
                p = jnp.exp(s - new)
                shrink = jnp.exp(old - new)
                top[h : h + 1] = new
                total[h : h + 1] = total[h : h + 1] * shrink + jnp.sum(p, 0, keepdims=True)
                at = pl.ds((h + 1) * HEAD_DIM, HEAD_DIM)
                acc[at, :] = acc[at, :] * shrink + jnp.dot(
                    values_t[h * HEAD_DIM : (h + 1) * HEAD_DIM], p.astype(halves), preferred_element_type=floats
                )

        for block in range(cols):
            step(block)
        for h in range(3):
            at = pl.ds((h + 1) * HEAD_DIM, HEAD_DIM)
            acc[at, :] = acc[at, :] / total[h : h + 1]
        mixed_buf[c, m] = acc[...].T.astype(halves)
        lse_buf[m, c] = top[...] + jnp.log(jnp.maximum(total[...], 1e-30))

    def units(m, first, last):
        @pl.loop(first, last)
        def _(c):
            unit(m, c)

    def masks(m):
        asking = seg_ref[m, 0:1, pl.ds(pl.multiple_of(z * rows, 128), rows)].astype(floats)
        for block in range(cols):
            asked = seg_ref[m, 0:1, block * rows : (block + 1) * rows].astype(floats)
            same = jnp.broadcast_to(asked, (rows, rows)).T == asking
            mask[m, block] = jnp.where(same, 0.0, MASK_VALUE).astype(halves)

    def turn(m):
        for block in range(cols):
            turned[:, (m * cols + block) * rows : (m * cols + block + 1) * rows] = tokens_buf[m, block].T

    done = []
    keeps = ((q_buf, q_ref), (k_buf, k_ref), (v_buf, v_ref), (lse_buf, lse_ref))

    def take_z(n, t):
        zs[n].step(t)
        if n == 0:
            small.step(t)
        if t == cols - 1:
            start(*second[n])

    def take_second(n):
        finish(*second[n])
        start(*third[n])

    def take_third(n):
        finish(*third[n])
        swap(n)

    swaps = set()

    def take_core(n):
        swapped(n)
        swaps.add(n)
        if n < 2 and swaps >= {0, 1}:
            done.append(local(weights.at[0], first_ref))

    act = {
        "Zs": lambda n: zs[n].start(), "Z": take_z, "Ts": lambda q: tokens[q].start(), "T": lambda q, t: tokens[q].step(t),
        "B": take_second, "C": take_third, "K": take_core, "R": turn,
    }
    small.start()
    head, tail, order = split_plan(FORWARD_PLAN)
    act[head[0][0]](*head[0][1:])
    for block in range(cols):
        if block > reach or cols - 1 - block > reach:
            @pl.when(jnp.logical_not((low <= block) & (block < high)))
            def _(block=block):
                for m in range(micro):
                    tokens_buf[m, block] = jnp.zeros(own_ref.shape[1:], halves)
    for m in range(micro):
        masks(m)
    for task in head[1:]:
        act[task[0]](*task[1:])

    @pl.loop(0, len(order))
    def _(step):
        unit(pick(step, [m for m, _ in order]), pick(step, [c for _, c in order]))
        for i, tasks in enumerate(tail[:-1]):
            if tasks:
                @pl.when(step == i)
                def _(tasks=tasks):
                    for task in tasks:
                        act[task[0]](*task[1:])

    for source, target in (*keeps, (bias_buf, biases_ref), (mixed_buf, mixed_ref), (turned, turned_ref), (mask, mask_ref)):
        done.append(local(source, target))
    for task in tail[-1]:
        act[task[0]](*task[1:])
    for copy in done:
        copy.wait()
    post.close()


def forward(sizes, own, shard, hidden_bias, query_bias, value_bias, segments):
    ns, nr, nc = sizes
    ny = nr // 2
    micro, rows, model = own.shape
    _, rb, w = shard.shape
    halves, floats = own.dtype, jnp.float32
    reach = min(nc - 1, -(-(DOC_MOST - 1) // rows))
    count = (6 + 1) * 2 * (nc - 1) + micro * 4 * reach + 6 * (4 * (ny - 1) + 4 * (ns - 1) + 1)
    anywhere = pl.BlockSpec(memory_space=pl.ANY)
    vmem = pl.BlockSpec(memory_space=pltpu.VMEM)
    length = nc * rows
    arrays = [
        ((2, nc, ns, ny, 2, rb, w), halves), ((nc, ns, ny, 2, rb, w), halves), ((model, micro * length), halves), ((micro, nc, rows, rows), halves),
        ((nc, 8, model), floats), ((nc, micro, rows, WINDOW), halves), ((micro, nc, 8, rows), floats),
        ((micro, nc, rows, WINDOW), halves), ((micro, nc, nc, rows, WINDOW), halves), ((micro, nc, nc, rows, WINDOW), halves),
    ]
    shapes = [pltpu.VMEM(shape, kind) for shape, kind in arrays]
    return pl.pallas_call(
        functools.partial(forward_kernel, sizes, micro),
        out_shape=[jax.ShapeDtypeStruct(shape, kind) for shape, kind in arrays],
        in_specs=[vmem] * 6,
        out_specs=[anywhere] * len(arrays),
        scratch_shapes=[
            pltpu.VMEM((1, nc, ns, ny, 2, rb, w), halves),
            shapes[2], shapes[4], shapes[3], *shapes[5:],
            pltpu.VMEM((micro, nc, rows, model), halves), pltpu.VMEM((WINDOW, rows), floats), pltpu.VMEM((8, rows), floats), pltpu.VMEM((8, rows), floats),
            pltpu.SemaphoreType.DMA((count,)), pltpu.SemaphoreType.DMA((count,)), pltpu.SemaphoreType.DMA((20,)),
        ],
        compiler_params=pltpu.CompilerParams(collective_id=2, has_side_effects=True, vmem_limit_bytes=60 << 20),
        name="forward",
    )(own, shard, hidden_bias, query_bias, value_bias, segments)


def middle_kernel(cols, own_ref, mixed_ref, out_ref, hidden_ref, down_ref, bias_ref, *refs):
    vector_refs = refs[:6]
    (cot_ref, outputs_ref, first_grad_ref, attn_grad_ref, part_ref, sums_ref,
     normal, scale, normed, normed_low, normed_t, grad_low, grad_t, act_buf, slope_buf, total) = refs[6:]
    floats, halves = jnp.float32, jnp.bfloat16
    step = pl.program_id(0)
    rows, model = own_ref.shape
    chunks = [pl.ds(r * 256, 256) for r in range(rows // 256)]
    whole_rows = [pl.ds(0, rows)]
    bands = [pl.ds(n * 256, 256) for n in range(model // 256)]
    vector = lambda i: vector_refs[i][...].astype(floats).reshape(1, -1)

    @pl.when(step == 0)
    def _():
        sums_ref[...] = jnp.zeros_like(sums_ref)
        for chunk in chunks:
            first_sum = own_ref[chunk].astype(floats) + vector(0)
            for c in range(cols):
                first_sum = first_sum + contract_cols(mixed_ref[c, chunk], out_ref[c])
            normal_one, scale_one = norm_parts(first_sum)
            normal[chunk] = normal_one
            scale[chunk] = jnp.broadcast_to(scale_one, (256, 128))
            norm_one = normal_one * vector(1) + vector(2)
            total[chunk] = norm_one + vector(3)
            normed_low[chunk] = norm_one.astype(halves)
            normed_t[:, chunk] = norm_one.astype(halves).T

    @pl.when(step < cols)
    def _():
        for chunk in chunks:
            for band in bands:
                hidden = jnp.dot(normed_low[chunk], hidden_ref[0, 0, :, band], preferred_element_type=floats) + bias_ref[0, 0:1, band]
                half_erf = 0.5 * lax.erf(hidden * 0.7071067811865476) + 0.5
                act_buf[step, chunk, band] = (hidden * half_erf).astype(halves)
                slope_buf[step, chunk, band] = (half_erf + hidden * (jnp.exp(-0.5 * hidden * hidden) * 0.3989422804014327)).astype(halves)
        for chunk in chunks:
            for band in bands:
                total[chunk, band] += contract_cols(act_buf[step, chunk], down_ref[0, 0, band, :])

    @pl.when(step == cols - 1)
    def _():
        for chunk in chunks:
            normal_two, scale_two = norm_parts(total[chunk])
            outputs_ref[chunk] = (normal_two * vector(4) + vector(5)).astype(halves)
            cot = cot_ref[chunk].astype(floats)
            second_grad = norm_back(cot * vector(4), normal_two, scale_two)
            total[chunk] = second_grad
            grad_low[chunk] = second_grad.astype(halves)
            grad_t[:, chunk] = second_grad.astype(halves).T
            sums_ref[3:4] += jnp.sum(second_grad, 0, keepdims=True)
            sums_ref[4:5] += jnp.sum(cot * normal_two, 0, keepdims=True)
            sums_ref[5:6] += jnp.sum(cot, 0, keepdims=True)

    @pl.when(step >= cols)
    def _():
        c = step - cols
        bias_total = [jnp.zeros((1, 256), floats) for _ in bands]
        for chunk in chunks:
            for n, band in enumerate(bands):
                pre = jnp.dot(grad_low[chunk], down_ref[0, 0, :, band], preferred_element_type=floats)
                pre = (pre * slope_buf[c, chunk, band].astype(floats)).astype(halves)
                slope_buf[c, chunk, band] = pre
                bias_total[n] = bias_total[n] + jnp.sum(pre.astype(floats), 0, keepdims=True)
        for n, band in enumerate(bands):
            sums_ref[pl.ds(8 + c, 1), band] = bias_total[n]
        for band in bands:
            for side in [pl.ds(0, model)]:
                part_ref[0, 0, side, band] = jnp.dot(normed_t[side, :], slope_buf[c, :, band], preferred_element_type=floats).astype(halves)
                part_ref[1, 0, side, band] = jnp.dot(grad_t[side, :], act_buf[c, :, band], preferred_element_type=floats).astype(halves)
        for chunk in chunks:
            for band in bands:
                total[chunk, band] += contract_cols(slope_buf[c, chunk], hidden_ref[0, 0, band, :])

    @pl.when(step == 2 * cols - 1)
    def _():
        for chunk in chunks:
            normed_grad, normal_one = total[chunk], normal[chunk]
            first_grad = norm_back(normed_grad * vector(1), normal_one, scale[chunk, 0:1])
            first_grad_ref[chunk] = first_grad
            attn_grad_ref[chunk] = first_grad.astype(halves)
            sums_ref[0:1] += jnp.sum(first_grad, 0, keepdims=True)
            sums_ref[1:2] += jnp.sum(normed_grad * normal_one, 0, keepdims=True)
            sums_ref[2:3] += jnp.sum(normed_grad, 0, keepdims=True)


def middle(own, mixed, first, rest, biases, vectors, cot):
    rows, model = own.shape
    cols = first.shape[0]
    halves, floats = jnp.bfloat16, jnp.float32
    whole = lambda shape: pl.BlockSpec(shape, lambda i: (0,) * len(shape))
    wide = lambda kind: pltpu.VMEM((rows, model), kind)
    return pl.pallas_call(
        functools.partial(middle_kernel, cols),
        grid=(2 * cols,),
        in_specs=[
            whole((rows, model)), whole(mixed.shape),
            pl.BlockSpec((cols, model, WINDOW), lambda i: (0, 0, O_AT // WINDOW)),
            pl.BlockSpec((1, 1, model, rest.shape[-1]), lambda i: (0, lax.rem(i, cols), 0, 0)),
            pl.BlockSpec((1, 1, model, rest.shape[-1]), lambda i: (1, lax.rem(i, cols), 0, 0)),
            pl.BlockSpec((1, *biases.shape[1:]), lambda i: (lax.rem(i, cols), 0, 0)),
            *[whole((model,))] * 6, whole((rows, model)),
        ],
        out_specs=[
            whole((rows, model)), whole((rows, model)), whole((rows, model)),
            pl.BlockSpec((2, 1, model, rest.shape[-1]), lambda i: (0, jnp.maximum(i - cols, 0), 0, 0)),
            whole((8 + cols + -cols % 8, model)),
        ],
        out_shape=[
            jax.ShapeDtypeStruct((rows, model), halves), jax.ShapeDtypeStruct((rows, model), floats),
            jax.ShapeDtypeStruct((rows, model), halves), jax.ShapeDtypeStruct(rest.shape, halves),
            jax.ShapeDtypeStruct((8 + cols + -cols % 8, model), floats),
        ],
        scratch_shapes=[
            wide(floats), pltpu.VMEM((rows, 128), floats), wide(floats), wide(halves), pltpu.VMEM((model, rows), halves), wide(halves),
            pltpu.VMEM((model, rows), halves), pltpu.VMEM((cols, rows, rest.shape[-1]), halves),
            pltpu.VMEM((cols, rows, rest.shape[-1]), halves), wide(floats),
        ],
        compiler_params=pltpu.CompilerParams(vmem_limit_bytes=56 << 20),
        name="middle",
    )(own, mixed, first, rest, rest, biases, *vectors, cot)


class Inbox:
    def __init__(self, ref, size):
        self.ref, self.size = ref, size

    def __call__(self, way, e):
        return self.ref.at[0 if self.size == 2 else (1 - way) // 2, e]


def backward_kernel(sizes, micro, grad_ref, share_ref, first_ref, turned_ref, mixed_ref, lse_ref, q_ref, k_ref, v_ref,
                    mask_ref, part_ref, vec_ref,
                    back_ref, block_ref, sums_ref,
                    mine_buf, core_buf, stage_buf, in_a, in_b, in_c, in_d, in_z, tok_buf, tok_in, vec_buf,
                    weights, mixed_buf, q_buf, k_buf, v_buf, every_t, grad_t, mask, acc, spread, block_sum,
                    send_sems, recv_sems, local_sems, free_sem):
    floats, halves = jnp.float32, jnp.bfloat16
    lines, device = place(sizes)
    (x, ns), (y, ny), (k, _), (z, cols) = (lines[a] for a in "xykz")
    model = first_ref.shape[1]
    half = part_ref.shape[-1] // 2
    rb = part_ref.shape[-2]
    rows = grad_ref.shape[1]
    reach = -(-(DOC_MOST - 1) // rows)
    parts = [pl.ds(p * half, half) for p in (0, 1)]
    used = [0]

    def local(source, target):
        copy = pltpu.make_async_copy(source, target, local_sems.at[used[0]])
        used[0] += 1
        copy.start()
        return copy

    def rows_of(n):
        return pl.ds(n % 2 * (rb // 2), rb // 2)

    planes = [local(part_ref.at[n // 2, :, :, :, k, rows_of(n)], mine_buf.at[n // 2 + 1, :, :, :, rows_of(n)]) for n in range(4)]
    loads = [local(*pair) for pair in ((first_ref, weights), (mixed_ref, mixed_buf), (q_ref, q_buf), (share_ref, back_ref))]
    loads += [local(k_ref, k_buf), local(v_ref, v_buf)]
    loads += [local(mask_ref, mask)]
    late = [local(turned_ref, every_t)]
    greet(lines, device)
    post = Post(device, send_sems, recv_sems)

    def give(n):
        post.send(("k", n), lambda: (
            "k", 1 - k, part_ref.at[n // 2, :, :, :, 1 - k, rows_of(n)], core_buf.at[n // 2, :, :, :, rows_of(n)], None))

    def plus(target, source):
        target[...] = target[...] + source[...]

    def plus_grid(target, source, first, second):
        @pl.loop(0, first * second)
        def _(n):
            at = (n // second, lax.rem(n, second))
            plus(target.at[at], source.at[at])

    def plus_row(target, source, first):
        @pl.loop(0, first)
        def _(n):
            plus(target.at[n], source.at[n])

    class Stream:
        def __init__(self, name, j, begin, size, r):
            cs = pl.ds(begin, size)
            self.second = [
                LineReduce(post, (name, "a"), "x", lines["x"], lambda i: mine_buf.at[j, cs, i, :, r, parts[0]],
                           lambda way, e: Inbox(in_a.at[j], ns)(way, e).at[cs, :, r], lambda t, s: plus_grid(t, s, size, ny)),
                LineReduce(post, (name, "b"), "y", lines["y"], lambda i: mine_buf.at[j, cs, :, i, r, parts[1]],
                           lambda way, e: Inbox(in_b.at[j], ny)(way, e).at[cs, :, r], lambda t, s: plus_grid(t, s, size, ns)),
            ]
            self.third = [
                LineReduce(post, (name, "c"), "y", lines["y"], lambda i: mine_buf.at[j, cs, x, i, r, parts[0]],
                           lambda way, e: Inbox(in_c.at[j], ny)(way, e).at[cs, r], lambda t, s: plus_row(t, s, size)),
                LineReduce(post, (name, "d"), "x", lines["x"], lambda i: mine_buf.at[j, cs, i, y, r, parts[1]],
                           lambda way, e: Inbox(in_d.at[j], ns)(way, e).at[cs, r], lambda t, s: plus_row(t, s, size)),
            ]

    def line_z(name, j, r):
        return LineReduce(post, ("z", name), "z", lines["z"], lambda i: mine_buf.at[j, i, x, y, r],
                          lambda way, e: in_z.at[j, (1 - way) // 2, e, r], plus)

    ffn = [Stream(("s", n), n // 2 + 1, 0, cols, rows_of(n)) for n in range(4)]
    ffn_z = [line_z(n, n // 2 + 1, rows_of(n)) for n in range(4)]
    attn = [Stream(("u", c), 0, c, 1, pl.ds(0, rb)) for c in range(cols)]

    def take_y(c, e):
        reduce_to(post, ("y", c), "z", lines["z"], c, e, mine_buf.at[0, c, x, y], lambda way, e: in_z.at[0, (1 - way) // 2, e], plus)

    def half_of(h):
        return pl.ds(h * (rows // 2), rows // 2)

    def line_tokens(m, h):
        at = half_of(h)
        return LineReduce(post, ("t", m, h), "z", lines["z"], lambda i: tok_buf.at[m, i, at],
                          lambda way, e: tok_in.at[m, (1 - way) // 2, e, at], plus, reach)

    tokens = [[line_tokens(m, h) for h in range(2)] for m in range(micro)]

    def start(*group):
        for line in group:
            line.start()

    def finish(*group):
        for line in group:
            line.finish()

    def core(n):
        planes[n].wait()
        r = rows_of(n)
        post.wait(("k", n), "k", 1 - k, core_buf.at[n // 2, :, :, :, r])

        @pl.loop(0, cols * ns * ny)
        def _(i):
            at = (i // (ns * ny), lax.rem(i // ny, ns), lax.rem(i, ny), r)
            plus(mine_buf.at[(n // 2 + 1, *at)], core_buf.at[(n // 2, *at)])

    def vector_start(stage, axis):
        mine, size = lines[axis]
        vec_buf[stage, 1 + mine] = vec_buf[stage, 0]
        for t in range(1, size):
            post.send(("v", stage, t), lambda t=t: (
                axis, lax.rem(mine + t, size), vec_buf.at[stage, 0], vec_buf.at[stage, 1 + mine], None))

    def vector_finish(stage, axis, out):
        mine, size = lines[axis]
        for t in range(1, size):
            origin = lax.rem(mine + size - t, size)
            post.wait(("v", stage, t), axis, origin, vec_buf.at[stage, 1 + origin])
        total = vec_buf[stage, 1]
        for i in range(1, size):
            total = total + vec_buf[stage, 1 + i]
        out[...] = total

    places = place_of(rows)
    small = vec_ref.shape[0]
    vec_buf[0, 0] = jnp.zeros_like(vec_buf[0, 0])
    vec_buf[0, 0, 0:small] = vec_ref[...]

    def unit(m, c):
        mixed_grad = jnp.dot(grad_ref[m], weights[c, :, O_AT : O_AT + WINDOW], preferred_element_type=floats).astype(halves)
        mixed_grad = jnp.where(places > 0, mixed_grad.astype(floats), 0.0)
        product = mixed_grad * mixed_buf[c, m].astype(floats)
        product_high = product.astype(halves)
        product_low = (product - product_high.astype(floats)).astype(halves)
        pick = (
            lax.broadcasted_iota(jnp.int32, (8, WINDOW), 1) // HEAD_DIM == lax.broadcasted_iota(jnp.int32, (8, WINDOW), 0) + 1
        ).astype(floats).astype(halves)
        inner = contract_cols(pick, product_high) + contract_cols(pick, product_low)
        value_side = pltpu.roll(mixed_grad, WINDOW - HEAD_DIM, 1).astype(halves)
        queries = q_buf[m, c]
        query_heads = [keep(queries, places, h + 1) for h in range(3)]
        grad_heads = [keep(value_side, places, h) for h in range(3)]
        acc[...] = jnp.zeros_like(acc)
        key_weight = weights[c, :, K_AT : K_AT + WINDOW]
        value_weight = weights[c, :, V_AT : V_AT + WINDOW]

        def step(block, value_bias):
            keys = k_buf[m, c, block]
            values = v_buf[m, c, block]
            keys_t = keys.T
            hidden = mask[m, block].astype(floats)
            key_grad = jnp.zeros((rows, WINDOW), floats)
            value_grad = jnp.zeros((rows, WINDOW), floats)
            for h in range(3):
                p = jnp.exp(contract_cols(keys, query_heads[h]) + hidden - lse_ref[m, c, h : h + 1])
                prob_grad = contract_cols(values, grad_heads[h])
                score_grad = (p * (prob_grad - inner[h : h + 1])).astype(halves)
                value_grad = value_grad + jnp.dot(p.astype(halves), grad_heads[h], preferred_element_type=floats)
                key_grad = key_grad + jnp.dot(score_grad, query_heads[h], preferred_element_type=floats)
                at = pl.ds(h * HEAD_DIM, HEAD_DIM)
                acc[at, :] += jnp.dot(keys_t[(h + 1) * HEAD_DIM : (h + 2) * HEAD_DIM], score_grad, preferred_element_type=floats)
            key_low, value_low = key_grad.astype(halves), value_grad.astype(halves)
            k_buf[m, c, block] = key_low
            v_buf[m, c, block] = value_low
            spread[m, block] += contract_cols(key_low, key_weight) + contract_cols(value_low, value_weight)
            return value_bias + jnp.sum(value_low.astype(floats), 0, keepdims=True)

        value_bias = jnp.zeros((1, WINDOW), floats)
        for block in range(cols):
            value_bias = step(block, value_bias)
        query_low = (acc[...].T * HEAD_DIM ** -0.5).astype(halves)
        q_buf[m, c] = query_low
        vec_buf[0, 0, pl.ds(small + c, 1), 0:WINDOW] += jnp.sum(query_low.astype(floats), 0, keepdims=True)
        vec_buf[0, 0, pl.ds(small + c, 1), WINDOW : 2 * WINDOW] += value_bias
        back_ref[m] += contract_cols(query_low, weights[c, :, Q_AT : Q_AT + WINDOW])

    def send_tokens(m):
        back_ref[m] += spread[m, z]

        @pl.loop(0, cols)
        def _(block):
            tok_buf[m, block] = spread[m, block].astype(halves)

        start(*tokens[m])

    def weight_grads(c):
        strip = block_sum.shape[0]

        @pl.loop(0, model // strip)
        def _(part):
            base = pl.multiple_of(part * strip, strip)
            side = pl.ds(base, strip)
            block_sum[...] = jnp.zeros_like(block_sum)
            for m in range(micro):
                mine_at = pl.ds(pl.multiple_of((m * cols + z) * rows, rows), rows)
                block_sum[:, Q_AT : Q_AT + WINDOW] += jnp.dot(every_t[side, mine_at], q_buf[m, c], preferred_element_type=floats)
                all_at = pl.ds(m * cols * rows, cols * rows)
                block_sum[:, K_AT : K_AT + WINDOW] += jnp.dot(
                    every_t[side, all_at], k_buf[m, c].reshape(-1, WINDOW), preferred_element_type=floats)
                block_sum[:, V_AT : V_AT + WINDOW] += jnp.dot(
                    every_t[side, all_at], v_buf[m, c].reshape(-1, WINDOW), preferred_element_type=floats)
                block_sum[:, O_AT : O_AT + WINDOW] += jnp.dot(
                    grad_t[side, m * rows : (m + 1) * rows], mixed_buf[c, m], preferred_element_type=floats)
            for i in range(strip // (2 * rb)):
                ours = pl.ds(pl.multiple_of((2 * i + k) * rb, 16), rb)
                theirs = pl.ds(pl.multiple_of((2 * i + 1 - k) * rb, 16), rb)
                chip = part * (strip // (2 * rb)) + i
                mine_buf[0, c, chip // ny, lax.rem(chip, ny)] = block_sum[ours].astype(halves)
                stage_buf[c, chip // ny, lax.rem(chip, ny)] = block_sum[theirs].astype(halves)

    waited = []

    def attn_give(c):
        if not waited:
            pl.semaphore_wait(free_sem, 1)
            waited.append(c)
        post.send(("g", c), lambda: ("k", 1 - k, stage_buf.at[c], core_buf.at[0, c], None))

    def attn_add(c):
        post.wait(("g", c), "k", 1 - k, core_buf.at[0, c])

        @pl.loop(0, ns * ny)
        def _(n):
            at = (c, n // ny, lax.rem(n, ny))
            plus(mine_buf.at[(0, *at)], core_buf.at[(0, *at)])

    streams = ffn + attn
    added = set()

    def take_core(n):
        if n < 4:
            core(n)
            added.add(n)
            if added >= {0, 1} and n in (0, 1):
                pl.semaphore_signal(free_sem, 1, device_id=device("k", 1 - k), device_id_type=MESH)
        else:
            attn_add(n - 4)
        start(*streams[n].second)

    def take_second(n):
        finish(*streams[n].second)
        start(*streams[n].third)

    def take_third(n):
        finish(*streams[n].third)
        if n < 4:
            start(ffn_z[n])

    def along(line, e):
        for way in (1, -1):
            line.take(way, e)
            if e:
                line.forward(way, e)

    def take_tokens(m, h, e):
        line = tokens[m][h]
        if e == 0:
            at = half_of(h)

            def add(target, source):
                back_ref[m, at] += source[...].astype(floats)

            line.add = add
        along(line, e)

    def vectors(stage):
        if stage:
            vector_finish(stage - 1, "kyxz"[stage - 1], vec_buf.at[stage, 0] if stage < 4 else sums_ref)
        if stage < 4:
            vector_start(stage, "kyxz"[stage])

    def load():
        for copy in loads:
            copy.wait()

    act = {
        "L": load, "G": lambda n: give(n) if n < 4 else attn_give(n - 4), "A": take_core, "B": take_second, "C": take_third,
        "Z": lambda n, e: along(ffn_z[n], e), "S": send_tokens, "T": take_tokens, "Y": take_y, "V": vectors,
    }
    head, tail, order = split_plan([("U", "W", task[1], 0) if task[0] == "W" else task for task in BACKWARD_PLAN])
    kinds = [item[0] == "W" for item in order]
    heads = [item[1] if item[0] == "W" else item[0] for item in order]
    micros = [0 if item[0] == "W" else item[1] for item in order]
    act[head[0][0]](*head[0][1:])
    spread[...] = jnp.zeros_like(spread)
    for m in range(micro):
        grad_t[:, m * rows : (m + 1) * rows] = grad_ref[m].T
    for task in head[1:]:
        act[task[0]](*task[1:])

    @pl.loop(0, len(order))
    def _(step):
        c, m, kind = pick(step, heads), pick(step, micros), pick(step, [int(k_) for k_ in kinds])

        @pl.when(kind == 0)
        def _():
            unit(m, c)

        @pl.when(kind == 1)
        def _():
            @pl.when(step == kinds.index(True))
            def _():
                for copy in late:
                    copy.wait()

            weight_grads(c)

        for i, tasks in enumerate(tail[:-1]):
            if tasks:
                @pl.when(step == i)
                def _(tasks=tasks):
                    for task in tasks:
                        act[task[0]](*task[1:])

    for task in tail[-1]:
        act[task[0]](*task[1:])
    for j in range(3):
        block_ref[j] = mine_buf[j, z, x, y].astype(floats)
    post.close()


def backward(sizes, grad, share, first, turned, mixed, lse, q, k, v, mask, part, vectors):
    ns, nr, nc = sizes
    ny = nr // 2
    micro, rows, model = grad.shape
    w = part.shape[-1]
    rb = model // (ns * nr)
    halves, floats = jnp.bfloat16, jnp.float32
    reach = min(nc - 1, -(-(DOC_MOST - 1) // rows))
    streams = 4 + nc
    count = 4 + nc + 4 * (ny - 1 + ns - 1) * streams + 4 * 2 * (nc - 1) + 2 * nc * 2 + micro * 4 * reach + (1 + ny - 1 + ns - 1 + nc - 1)
    widest = max(ns, ny, nc, 2)
    ways = lambda n: 1 if n == 2 else 2
    vec_shape = (vectors.shape[0] + nc + -nc % 8, model)
    vmem = pl.BlockSpec(memory_space=pltpu.VMEM)
    anywhere = pl.BlockSpec(memory_space=pl.ANY)
    buf = lambda *shape, kind=halves: pltpu.VMEM(shape, kind)
    return pl.pallas_call(
        functools.partial(backward_kernel, sizes, micro),
        out_shape=[
            jax.ShapeDtypeStruct((micro, rows, model), floats),
            jax.ShapeDtypeStruct((3, rb, w), floats),
            jax.ShapeDtypeStruct(vec_shape, floats),
        ],
        in_specs=[vmem, anywhere, anywhere, anywhere, anywhere, vmem, anywhere, anywhere, anywhere, anywhere, anywhere, vmem],
        out_specs=[vmem] * 3,
        scratch_shapes=[
            buf(3, nc, ns, ny, rb, w), buf(2, nc, ns, ny, rb, w), buf(nc, ns, ny, rb, w),
            buf(3, ways(ns), max(ns - 1, 1), nc, ny, rb, w // 2), buf(3, ways(ny), max(ny - 1, 1), nc, ns, rb, w // 2),
            buf(3, ways(ny), max(ny - 1, 1), nc, rb, w // 2), buf(3, ways(ns), max(ns - 1, 1), nc, rb, w // 2),
            buf(3, 2, max(nc - 1, 1), rb, w), buf(micro, nc, rows, model), buf(micro, 2, max(reach, 1), rows, model),
            buf(4, 1 + widest, *vec_shape, kind=floats),
            buf(nc, model, w), buf(nc, micro, rows, WINDOW), buf(micro, nc, rows, WINDOW),
            buf(micro, nc, nc, rows, WINDOW), buf(micro, nc, nc, rows, WINDOW),
            buf(model, micro * nc * rows), buf(model, micro * rows),
            buf(micro, nc, rows, rows), buf(WINDOW, rows, kind=floats), buf(micro, nc, rows, model, kind=floats), buf(model // 2, w, kind=floats),
            pltpu.SemaphoreType.DMA((count,)), pltpu.SemaphoreType.DMA((count,)), pltpu.SemaphoreType.DMA((24,)), pltpu.SemaphoreType.REGULAR,
        ],
        compiler_params=pltpu.CompilerParams(collective_id=3, has_side_effects=True, vmem_limit_bytes=62 << 20),
        name="backward",
    )(grad, share, first, turned, mixed, lse, q, k, v, mask,
      part.reshape(2, nc, ns, ny, 2, rb, w), vectors)


def per_device_plain(sizes, inputs, segment_ids, query_weight, key_weight, value_weight, query_bias, value_bias,
               output_weight, output_bias, first_gain, first_shift, hidden_weight, hidden_bias, down_weight,
               down_bias, second_gain, second_shift, cotangent):
    floats, halves = jnp.float32, jnp.bfloat16
    cols = sizes[2]
    micro, _, rows, model = inputs.shape
    length = segment_ids.shape[-1]
    width = query_weight.shape[1]
    here = lax.axis_index("col")
    own = inputs[:, 0]
    shard = jnp.stack([
        jnp.concatenate([query_weight, key_weight, value_weight, output_weight.T], 1),
        hidden_weight,
        down_weight.T,
    ])
    biases = lax.all_gather(jnp.concatenate([query_bias, value_bias, hidden_bias]), "col", axis=0)
    everything, gathered = gather(sizes, own, shard)
    everything = everything.reshape(micro, length, model)
    attn_weights = gathered[0]
    wq, wk, wv, wot = (attn_weights[:, :, i * width : (i + 1) * width] for i in range(4))
    hidden_full, down_full = gathered[1], gathered[2]
    bq, bv, bh = biases[:, :width], biases[:, width : 2 * width], biases[:, 2 * width :]
    seg_all = segment_ids[:, 0]
    seg_own = lax.dynamic_slice_in_dim(seg_all, here * rows, rows, 1)
    first_key = jnp.sum((seg_all < seg_own[:, :1]).astype(jnp.int32), 1)
    last_key = jnp.sum((seg_all <= seg_own[:, -1:]).astype(jnp.int32), 1)
    bounds = jnp.stack([first_key // KEY_BLOCK, (last_key + KEY_BLOCK - 1) // KEY_BLOCK], 1)

    mixed, lse, q, k, v = attend(bounds, own, everything, wq, wk, wv, bq.astype(floats), bv.astype(floats), seg_own, seg_all)
    total = micro * rows
    flat = lambda a: a.reshape(total, -1)
    mixed_flat = mixed.reshape(cols, total, width)
    attn = sum(contract_cols(mixed_flat[c], wot[c]) for c in range(cols))
    first_sum = flat(own).astype(floats) + attn + output_bias.astype(floats)
    normal_one, scale_one = norm_parts(first_sum)
    gain_one = first_gain.astype(floats)
    normed = normal_one * gain_one + first_shift.astype(floats)
    normed_low = normed.astype(halves)
    ffn = 0
    activated, slopes = [], []
    for c in range(cols):
        hidden = jnp.dot(normed_low, hidden_full[c], preferred_element_type=floats) + bh[c].astype(floats)
        half_erf = 0.5 * lax.erf(hidden * 0.7071067811865476) + 0.5
        act = (hidden * half_erf).astype(halves)
        slope = half_erf + hidden * (jnp.exp(-0.5 * hidden * hidden) * 0.3989422804014327)
        activated.append(act)
        slopes.append(slope.astype(halves))
        ffn = ffn + contract_cols(act, down_full[c])
    second_sum = normed + ffn + down_bias.astype(floats)
    normal_two, scale_two = norm_parts(second_sum)
    gain_two = second_gain.astype(floats)
    outputs = (normal_two * gain_two + second_shift.astype(floats)).astype(halves)
    cot = flat(cotangent[:, 0]).astype(floats)
    second_grad = norm_back(cot * gain_two, normal_two, scale_two)
    ffn_grad = second_grad.astype(halves)
    hidden_grads, down_grads, hidden_bias_grads = [], [], []
    normed_grad = second_grad
    for c in range(cols):
        pre = (jnp.dot(ffn_grad, down_full[c], preferred_element_type=floats) * slopes[c].astype(floats)).astype(halves)
        hidden_grads.append(contract_rows(normed_low, pre).astype(halves))
        down_grads.append(contract_rows(ffn_grad, activated[c]).astype(halves))
        hidden_bias_grads.append(jnp.sum(pre.astype(floats), 0))
        normed_grad = normed_grad + contract_cols(pre, hidden_full[c])
    first_grad = norm_back(normed_grad * gain_one, normal_one, scale_one)
    attn_grad = first_grad.astype(halves)
    dq, dk, dv = attend_back(bounds, attn_grad.reshape(micro, rows, model), wot, mixed, lse, q, k, v, seg_own, seg_all)
    every_flat = everything.reshape(micro * length, model)
    attn_grads = []
    own_share = first_grad
    spread = 0
    for c in range(cols):
        dq_c, dk_c, dv_c = dq[c].reshape(total, width), dk[c].reshape(micro * length, width), dv[c].reshape(micro * length, width)
        attn_grads.append(jnp.concatenate([
            contract_rows(flat(own), dq_c), contract_rows(every_flat, dk_c), contract_rows(every_flat, dv_c),
            contract_rows(attn_grad, mixed_flat[c]),
        ], 1).astype(halves))
        own_share = own_share + contract_cols(dq_c, wq[c])
        spread = spread + contract_cols(dk_c, wk[c]) + contract_cols(dv_c, wv[c])
    bias_q = jnp.sum(dq.astype(floats), (1, 2)).reshape(-1)
    bias_v = jnp.sum(dv.astype(floats), (1, 2)).reshape(-1)
    vectors = jnp.concatenate([
        jnp.sum(first_grad, 0), jnp.sum(normed_grad * normal_one, 0), jnp.sum(normed_grad, 0), jnp.sum(second_grad, 0),
        jnp.sum(cot * normal_two, 0), jnp.sum(cot, 0), bias_q, bias_v, *hidden_bias_grads,
    ]).reshape(-1, model)
    partial = jnp.stack([jnp.stack(attn_grads), jnp.stack(hidden_grads), jnp.stack(down_grads)])
    input_grad, reduced, sums = reduce(sizes, own_share.reshape(micro, rows, model),
                                       spread.astype(halves).reshape(micro, cols, rows, model), partial, vectors)
    attn_block = reduced[0]
    piece = lambda i: attn_block[:, i * width : (i + 1) * width]
    mine = lambda vector, size: lax.dynamic_slice_in_dim(vector.reshape(-1), here * size, size, 0)
    return (
        outputs.reshape(micro, 1, rows, model), input_grad[:, None],
        piece(0), piece(1), piece(2), mine(sums[6], width), mine(sums[7], width), piece(3).T,
        sums[0], sums[1], sums[2], reduced[1], mine(sums[8:], hidden_bias.shape[0]), reduced[2].T,
        sums[3], sums[4], sums[5],
    )


def per_device_fused(sizes, inputs, segment_ids, query_weight, key_weight, value_weight, query_bias, value_bias,
               output_weight, output_bias, first_gain, first_shift, hidden_weight, hidden_bias, down_weight,
               down_bias, second_gain, second_shift, cotangent):
    floats, halves = jnp.float32, jnp.bfloat16
    cols = sizes[2]
    micro, _, rows, model = inputs.shape
    length = segment_ids.shape[-1]
    width = query_weight.shape[1]
    here = lax.axis_index("col")
    own = inputs[:, 0]
    shard = jnp.stack([
        jnp.concatenate([query_weight, key_weight, value_weight, output_weight.T], 1),
        hidden_weight,
        down_weight.T,
    ])
    rest, first, turned, mask, biases, mixed, lse, q, k, v = forward(sizes, own, shard, hidden_bias, query_bias, value_bias, segment_ids)
    first = first.reshape(cols, model, 4 * width)
    total = micro * rows
    flat = lambda a: a.reshape(total, -1)
    outputs, first_grad, attn_grad, part, sums = middle(
        flat(own), mixed.reshape(cols, total, WINDOW), first, rest.reshape(2, cols, model, -1), biases,
        (output_bias, first_gain, first_shift, down_bias, second_gain, second_shift), flat(cotangent[:, 0]))
    parted = lambda a: a.reshape(micro, rows, model)
    input_grad, reduced, sums = backward(sizes, parted(attn_grad), parted(first_grad), first, turned, mixed, lse, q, k, v,
                                         mask, part, sums)
    piece = lambda i: reduced[0, :, i * width : (i + 1) * width]
    mine = lambda first_row, at, size: lax.dynamic_slice(sums, (first_row + here, at), (1, size))[0]
    heads_at = sums.shape[0] - (cols + -cols % 8)
    return (
        outputs.reshape(micro, 1, rows, model), input_grad[:, None],
        piece(0), piece(1), piece(2), mine(heads_at, 0, width), mine(heads_at, WINDOW, width), piece(3).T,
        sums[0], sums[1], sums[2], reduced[1], mine(8, 0, hidden_bias.shape[0]), reduced[2].T,
        sums[3], sums[4], sums[5],
    )


def per_device(sizes, inputs, segment_ids, query_weight, *rest):
    micro, _, rows, _ = inputs.shape
    fits = (query_weight.shape == (query_weight.shape[0] // 32 * 32, 3 * HEAD_DIM) and micro == 2 and sizes[2] == 4
            and DOC_MOST // 2 == rows)
    return (per_device_fused if fits else per_device_plain)(sizes, inputs, segment_ids, query_weight, *rest)


def solution(mesh):
    sizes = tuple(mesh.shape[name] for name in ("seq", "row", "col"))
    block, line = P(("seq", "row"), "col"), P("col", ("seq", "row"))
    tokens = P(None, ("seq", "row"), "col", None)
    placed = (tokens, P(None, ("seq", "row"), None), block, block, block, P("col"), P("col"), line, P(), P(), P(),
              block, P("col"), line, P(), P(), P(), tokens)
    given = (tokens, tokens, block, block, block, P("col"), P("col"), line, P(), P(), P(), block, P("col"), line,
             P(), P(), P())
    return jax.shard_map(functools.partial(per_device, sizes), mesh=mesh, in_specs=placed, out_specs=given, check_vma=False)
```

```python
import functools

import jax
import jax.numpy as jnp
from jax import lax
from jax.experimental import pallas as pl
from jax.experimental.pallas import tpu as pltpu
from jax.sharding import PartitionSpec as P

HEAD_DIM = 64
NORM_EPS = 1e-05
MASK_VALUE = -1000000000.0
DOC_MOST = 512
KEY_BLOCK = 256
MESH = pl.DeviceIdType.MESH


def contract_rows(left, right):
    return lax.dot_general(
        left, right, (((0,), (0,)), ((), ())), preferred_element_type=jnp.float32
    )


def contract_cols(left, right):
    return lax.dot_general(
        left, right, (((1,), (1,)), ((), ())), preferred_element_type=jnp.float32
    )


def norm_parts(summed):
    deviation = summed - jnp.mean(summed, -1, keepdims=True)
    scale = lax.rsqrt(jnp.mean(deviation * deviation, -1, keepdims=True) + NORM_EPS)
    return deviation * scale, scale


def norm_back(pull, normal, scale):
    return scale * (
        pull - jnp.mean(pull, -1, keepdims=True) - normal * jnp.mean(pull * normal, -1, keepdims=True)
    )

FORWARD_PLAN = (
    ("Zs", 1), ("Zs", 0), ("Zs", 3), ("Z", 1, 1), ("Z", 0, 1), ("Zs", 2), ("Z", 1, 2), ("Zs", 4), ("Z", 1, 3),
    ("Z", 0, 2), ("Z", 0, 3), ("Z", 2, 1), ("Z", 4, 1), ("Ts", 1), ("Z", 2, 2), ("B", 1), ("Z", 3, 1), ("Ts", 0),
    ("Z", 4, 2), ("B", 0), ("T", 1, 1), ("T", 0, 1), ("Z", 2, 3), ("Z", 3, 2), ("Ts", 3), ("C", 1), ("C", 0),
    ("Ts", 2), ("Z", 4, 3), ("K", 0), ("B", 2), ("T", 1, 2), ("T", 0, 2), ("R", 0), ("Zs", 5), ("K", 1), ("Z", 3, 3),
    ("B", 4), ("U", 0, 0), ("T", 3, 1), ("U", 0, 1), ("B", 3), ("U", 0, 2), ("T", 2, 1), ("C", 2), ("T", 3, 2),
    ("Z", 5, 1), ("C", 4), ("U", 0, 3), ("T", 2, 2), ("R", 1), ("C", 3), ("Z", 5, 2), ("K", 2), ("Z", 5, 3),
    ("U", 1, 0), ("K", 3), ("K", 4), ("B", 5), ("U", 1, 1), ("U", 1, 2), ("C", 5), ("U", 1, 3), ("K", 5),
)
BACKWARD_PLAN = (
    ("L",), ("G", 2), ("G", 1), ("G", 0), ("U", 0, 0), ("U", 1, 0), ("G", 3), ("A", 0), ("A", 2), ("U", 3, 0),
    ("U", 2, 0), ("S", 0), ("B", 0), ("U", 2, 1), ("B", 2), ("A", 1), ("T", 0, 0, 1), ("U", 0, 1), ("C", 0), ("A", 3),
    ("C", 2), ("T", 0, 1, 1), ("U", 1, 1), ("Z", 2, 2), ("U", 3, 1), ("S", 1), ("B", 1), ("V", 0), ("B", 3), ("W", 2),
    ("G", 6), ("W", 0), ("C", 1), ("V", 1), ("A", 6), ("G", 4), ("Z", 0, 2), ("W", 3), ("A", 4), ("V", 2), ("G", 7),
    ("T", 1, 0, 1), ("W", 1), ("C", 3), ("G", 5), ("A", 7), ("T", 1, 1, 1), ("A", 5), ("Z", 0, 1), ("B", 4), ("B", 7),
    ("Z", 1, 2), ("Z", 2, 1), ("V", 3), ("B", 5), ("C", 4), ("Z", 1, 1), ("B", 6), ("Z", 2, 0), ("T", 0, 0, 0),
    ("C", 7), ("Y", 3, 3), ("Y", 0, 3), ("Z", 3, 2), ("C", 5), ("T", 1, 0, 0), ("C", 6), ("Y", 2, 2), ("Y", 1, 2),
    ("V", 4), ("Y", 0, 2), ("Y", 3, 2), ("Z", 3, 1), ("Z", 1, 0), ("T", 1, 1, 0), ("Y", 1, 1), ("Y", 3, 1),
    ("Y", 2, 1), ("Y", 0, 1), ("Z", 3, 0), ("Z", 0, 0), ("T", 0, 1, 0), ("Y", 2, 0), ("Y", 0, 0), ("Y", 3, 0),
    ("Y", 1, 0),
)
def attend_kernel(bounds, own_ref, all_ref, wq_ref, wk_ref, wv_ref, bq_ref, bv_ref,
                  segq_ref, segk_ref, mixed_ref, lse_ref, q_ref, k_ref, v_ref, bias, acc, top, total):
    micro = pl.program_id(0)
    low, high = bounds[micro, 0], bounds[micro, 1]
    floats, halves = jnp.float32, jnp.bfloat16
    width = wq_ref.shape[-1]
    heads = width // HEAD_DIM
    rows = own_ref.shape[1]

    @pl.when(pl.program_id(1) == 0)
    def _():
        same = segk_ref[0] == segq_ref[0, 0:1]
        bias[...] = jnp.where(same, 0.0, MASK_VALUE)

    queries = jnp.dot(own_ref[0], wq_ref[0], preferred_element_type=floats) + bq_ref[0]
    queries = queries.astype(halves) * jnp.asarray(HEAD_DIM ** -0.5, halves)
    q_ref[0, 0] = queries
    lane = lax.broadcasted_iota(jnp.int32, (rows, width), 1) // HEAD_DIM
    query_heads = [jnp.where(lane == h, queries, jnp.zeros_like(queries)) for h in range(heads)]
    acc[...] = jnp.zeros_like(acc)
    total[...] = jnp.zeros_like(total)
    top[...] = jnp.full_like(top, 2 * MASK_VALUE)

    def step(block, carry):
        at = pl.ds(pl.multiple_of(block * KEY_BLOCK, KEY_BLOCK), KEY_BLOCK)
        x = all_ref[0, at, :]
        keys = jnp.dot(x, wk_ref[0], preferred_element_type=floats).astype(halves)
        k_ref[0, 0, at, :] = keys
        values = (jnp.dot(x, wv_ref[0], preferred_element_type=floats) + bv_ref[0]).astype(halves)
        v_ref[0, 0, at, :] = values
        values_t = values.T
        mask = bias[at, :]
        for h in range(heads):
            s = contract_cols(keys, query_heads[h]) + mask
            old = top[h : h + 1]
            new = jnp.maximum(old, jnp.max(s, 0, keepdims=True))
            p = jnp.exp(s - new)
            shrink = jnp.exp(old - new)
            top[h : h + 1] = new
            total[h : h + 1] = total[h : h + 1] * shrink + jnp.sum(p, 0, keepdims=True)
            part = pl.ds(h * HEAD_DIM, HEAD_DIM)
            acc[part, :] = acc[part, :] * shrink + jnp.dot(
                values_t[h * HEAD_DIM : (h + 1) * HEAD_DIM], p.astype(halves), preferred_element_type=floats
            )
        return carry

    lax.fori_loop(low, high, step, 0)
    for h in range(heads):
        part = pl.ds(h * HEAD_DIM, HEAD_DIM)
        acc[part, :] = acc[part, :] / total[h : h + 1]
    mixed_ref[0, 0] = acc[...].T.astype(halves)
    lse_ref[0, 0] = top[...] + jnp.log(jnp.maximum(total[...], 1e-30))


def attend(bounds, own, everything, wq, wk, wv, bq, bv, seg_own, seg_all):
    micro, rows, model = own.shape
    length = everything.shape[1]
    cols, _, width = wq.shape
    halves = jnp.bfloat16
    weight = pl.BlockSpec((1, model, width), lambda m, c, b: (c, 0, 0))
    per = lambda a, b_: pl.BlockSpec((1, 1, a, b_), lambda m, c, b: (c, m, 0, 0))
    spec = pltpu.PrefetchScalarGridSpec(
        num_scalar_prefetch=1,
        grid=(micro, cols),
        in_specs=[
            pl.BlockSpec((1, rows, model), lambda m, c, b: (m, 0, 0)),
            pl.BlockSpec((1, length, model), lambda m, c, b: (m, 0, 0)),
            weight, weight, weight,
            pl.BlockSpec((1, 1, width), lambda m, c, b: (c, 0, 0)),
            pl.BlockSpec((1, 1, width), lambda m, c, b: (c, 0, 0)),
            pl.BlockSpec((1, 1, rows), lambda m, c, b: (m, 0, 0)),
            pl.BlockSpec((1, length, 1), lambda m, c, b: (m, 0, 0)),
        ],
        out_specs=[per(rows, width), per(8, rows), per(rows, width), per(length, width), per(length, width)],
        scratch_shapes=[
            pltpu.VMEM((length, rows), jnp.float32),
            pltpu.VMEM((width, rows), jnp.float32),
            pltpu.VMEM((8, rows), jnp.float32),
            pltpu.VMEM((8, rows), jnp.float32),
        ],
    )
    shape = lambda a, b_, d=halves: jax.ShapeDtypeStruct((cols, micro, a, b_), d)
    return pl.pallas_call(
        attend_kernel,
        grid_spec=spec,
        out_shape=[shape(rows, width), shape(8, rows, jnp.float32), shape(rows, width), shape(length, width), shape(length, width)],
        compiler_params=pltpu.CompilerParams(vmem_limit_bytes=48 << 20),
        name="attend",
    )(bounds, own, everything, wq, wk, wv, bq[:, None], bv[:, None],
      seg_own[:, None], seg_all[:, :, None])


def attend_back_kernel(bounds, grad_ref, wot_ref, mixed_ref, lse_ref, q_ref, k_ref, v_ref, segq_ref, segk_ref,
                       dq_ref, dk_ref, dv_ref, bias, acc):
    micro = pl.program_id(0)
    low, high = bounds[micro, 0], bounds[micro, 1]
    floats, halves = jnp.float32, jnp.bfloat16
    rows, width = q_ref.shape[2:]
    heads = width // HEAD_DIM

    @pl.when(pl.program_id(1) == 0)
    def _():
        same = segk_ref[0] == segq_ref[0, 0:1]
        bias[...] = jnp.where(same, 0.0, MASK_VALUE)

    mixed_grad = jnp.dot(grad_ref[0], wot_ref[0], preferred_element_type=floats).astype(halves)
    product = mixed_grad.astype(floats) * mixed_ref[0, 0].astype(floats)
    product_high = product.astype(halves)
    product_low = (product - product_high.astype(floats)).astype(halves)
    pick = (
        lax.broadcasted_iota(jnp.int32, (8, width), 1) // HEAD_DIM == lax.broadcasted_iota(jnp.int32, (8, width), 0)
    ).astype(halves)
    inner = contract_cols(pick, product_high) + contract_cols(pick, product_low)
    lane = lax.broadcasted_iota(jnp.int32, (rows, width), 1) // HEAD_DIM
    queries = q_ref[0, 0]
    query_heads = [jnp.where(lane == h, queries, jnp.zeros_like(queries)) for h in range(heads)]
    grad_heads = [jnp.where(lane == h, mixed_grad, jnp.zeros_like(mixed_grad)) for h in range(heads)]
    acc[...] = jnp.zeros_like(acc)
    dk_ref[...] = jnp.zeros_like(dk_ref)
    dv_ref[...] = jnp.zeros_like(dv_ref)

    def step(block, carry):
        at = pl.ds(pl.multiple_of(block * KEY_BLOCK, KEY_BLOCK), KEY_BLOCK)
        keys = k_ref[0, 0, at, :]
        values = v_ref[0, 0, at, :]
        keys_t = keys.T
        mask = bias[at, :]
        key_grad = jnp.zeros((KEY_BLOCK, width), floats)
        value_grad = jnp.zeros((KEY_BLOCK, width), floats)
        for h in range(heads):
            s = contract_cols(keys, query_heads[h]) + mask
            p = jnp.exp(s - lse_ref[0, 0, h : h + 1])
            prob_grad = contract_cols(values, grad_heads[h])
            score_grad = (p * (prob_grad - inner[h : h + 1])).astype(halves)
            value_grad = value_grad + jnp.dot(p.astype(halves), grad_heads[h], preferred_element_type=floats)
            key_grad = key_grad + jnp.dot(score_grad, query_heads[h], preferred_element_type=floats)
            part = pl.ds(h * HEAD_DIM, HEAD_DIM)
            acc[part, :] += jnp.dot(keys_t[h * HEAD_DIM : (h + 1) * HEAD_DIM], score_grad, preferred_element_type=floats)
        dk_ref[0, 0, at, :] = key_grad.astype(halves)
        dv_ref[0, 0, at, :] = value_grad.astype(halves)
        return carry

    lax.fori_loop(low, high, step, 0)
    dq_ref[0, 0] = (acc[...].T * HEAD_DIM ** -0.5).astype(halves)


def attend_back(bounds, grad, wot, mixed, lse, q, k, v, seg_own, seg_all):
    micro, rows, model = grad.shape
    cols, _, length, width = k.shape
    halves = jnp.bfloat16
    per = lambda a, b_: pl.BlockSpec((1, 1, a, b_), lambda m, c, b: (c, m, 0, 0))
    spec = pltpu.PrefetchScalarGridSpec(
        num_scalar_prefetch=1,
        grid=(micro, cols),
        in_specs=[
            pl.BlockSpec((1, rows, model), lambda m, c, b: (m, 0, 0)),
            pl.BlockSpec((1, model, width), lambda m, c, b: (c, 0, 0)),
            per(rows, width), per(8, rows), per(rows, width), per(length, width), per(length, width),
            pl.BlockSpec((1, 1, rows), lambda m, c, b: (m, 0, 0)),
            pl.BlockSpec((1, length, 1), lambda m, c, b: (m, 0, 0)),
        ],
        out_specs=[per(rows, width), per(length, width), per(length, width)],
        scratch_shapes=[pltpu.VMEM((length, rows), jnp.float32), pltpu.VMEM((width, rows), jnp.float32)],
    )
    shape = lambda a, b_, d=halves: jax.ShapeDtypeStruct((cols, micro, a, b_), d)
    return pl.pallas_call(
        attend_back_kernel,
        grid_spec=spec,
        out_shape=[shape(rows, width), shape(length, width), shape(length, width)],
        compiler_params=pltpu.CompilerParams(vmem_limit_bytes=48 << 20),
        name="attend_back",
    )(bounds, grad, wot, mixed, lse, q, k, v, seg_own[:, None], seg_all[:, :, None])


def place(sizes):
    seq, row, col = (lax.axis_index(name) for name in ("seq", "row", "col"))
    lines = {"x": (seq, sizes[0]), "y": (row // 2, sizes[1] // 2), "k": (lax.rem(row, 2), 2), "z": (col, sizes[2])}

    def device(axis, index):
        if axis == "x":
            return (index, row, col)
        if axis == "y":
            return (seq, index * 2 + lax.rem(row, 2), col)
        if axis == "k":
            return (seq, row // 2 * 2 + index, col)
        return (seq, row, index)

    return lines, device


def greet(lines, device):
    barrier = pltpu.get_barrier_semaphore()
    count = 0
    for axis, (mine, size) in lines.items():
        for t in range(1, size):
            pl.semaphore_signal(barrier, inc=1, device_id=device(axis, lax.rem(mine + t, size)), device_id_type=MESH)
            count += 1
    pl.semaphore_wait(barrier, count)


class Post:
    def __init__(self, device, send_sems, recv_sems):
        self.device, self.send_sems, self.recv_sems = device, send_sems, recv_sems
        self.slots, self.sent = {}, []

    def slot(self, key):
        return self.slots.setdefault(key, len(self.slots))

    def copy(self, key, axis, index, source, target):
        n = self.slot(key)
        return pltpu.make_async_remote_copy(
            src_ref=source, dst_ref=target, send_sem=self.send_sems.at[n], recv_sem=self.recv_sems.at[n],
            device_id=self.device(axis, index), device_id_type=MESH,
        )

    def send(self, key, make):
        def run(act):
            axis, index, source, target, when = make()

            def go():
                act(self.copy(key, axis, index, source, target))

            if when is None:
                go()
            else:
                pl.when(when)(go)

        run(lambda copy: copy.start())
        self.sent.append(run)

    def wait(self, key, axis, index, target, when=None):
        def go():
            self.copy(key, axis, index, target, target).wait_recv()

        if when is None:
            go()
        else:
            pl.when(when)(go)

    def close(self):
        for run in self.sent:
            run(lambda copy: copy.wait_send())


def clip(index, size):
    return jnp.clip(index, 0, size - 1)


class LineGather:
    def __init__(self, post, name, axis, line, region, reach=None):
        self.post, self.name, self.axis, self.region = post, name, axis, region
        self.mine, self.size = line
        self.reach = min(self.size - 1, reach or self.size)

    def hop(self, way, t):
        mine, size = self.mine, self.size

        def make():
            origin, target = mine - way * t, mine + way
            ok = (origin >= 0) & (origin < size) & (target >= 0) & (target < size)
            here = self.region(clip(origin, size))
            return self.axis, clip(target, size), here, here, ok

        self.post.send((self.name, way, t + 1), make)

    def start(self):
        for way in (1, -1):
            if self.reach >= 1:
                self.hop(way, 0)

    def step(self, t):
        if t > self.reach:
            return
        for way in (1, -1):
            origin = self.mine - way * t
            ok = (origin >= 0) & (origin < self.size)
            self.post.wait((self.name, way, t), self.axis, clip(self.mine - way, self.size), self.region(clip(origin, self.size)), ok)
            if t < self.reach:
                self.hop(way, t)

    def finish(self, first=1):
        for t in range(first, self.reach + 1):
            self.step(t)


def gather_kernel(sizes, micro, own_ref, shard_ref, every_ref, full_ref, send_sems, recv_sems, local_sems):
    lines, device = place(sizes)
    (x, _), (y, _), (k, _), (z, cols) = (lines[a] for a in "xykz")
    half = shard_ref.shape[-1] // 2
    rows = own_ref.shape[1]
    reach = -(-(DOC_MOST - 1) // rows)
    parts = [pl.ds(p * half, half) for p in (0, 1)]
    local = [pltpu.make_async_copy(shard_ref.at[j], full_ref.at[j, z, x, y, k], local_sems.at[j]) for j in range(3)]
    local += [pltpu.make_async_copy(own_ref.at[m], every_ref.at[m, z], local_sems.at[3 + m]) for m in range(micro)]
    for copy in local:
        copy.start()
    greet(lines, device)
    post = Post(device, send_sems, recv_sems)
    for copy in local:
        copy.wait()
    zs = [LineGather(post, ("z", j), "z", lines["z"], lambda i, j=j: full_ref.at[j, i, x, y, k]) for j in range(3)]
    tokens = [LineGather(post, ("t", m), "z", lines["z"], lambda i, m=m: every_ref.at[m, i], reach) for m in range(micro)]
    second, third = {}, {}
    for j in range(3):
        second[j] = [
            LineGather(post, ("a", j), "y", lines["y"], lambda i, j=j: full_ref.at[j, :, x, i, k, :, parts[0]]),
            LineGather(post, ("b", j), "x", lines["x"], lambda i, j=j: full_ref.at[j, :, i, y, k, :, parts[1]]),
        ]
        third[j] = [
            LineGather(post, ("c", j), "x", lines["x"], lambda i, j=j: full_ref.at[j, :, i, :, k, :, parts[0]]),
            LineGather(post, ("d", j), "y", lines["y"], lambda i, j=j: full_ref.at[j, :, :, i, k, :, parts[1]]),
        ]

    def start(group):
        for line in group:
            line.start()

    def finish(group):
        for line in group:
            line.finish()

    def swap(j):
        plane = full_ref.at[j, :, :, :, k]
        post.send(("k", j), lambda: ("k", 1 - k, plane, plane, None))

    start(zs[:1])
    finish(zs[:1])
    start(second[0] + zs[1:2])
    finish(second[0])
    start(third[0])
    finish(zs[1:2])
    start(second[1] + tokens[:1])
    finish(third[0])
    swap(0)
    finish(second[1])
    start(third[1])
    finish(tokens[:1])
    start(zs[2:])
    finish(zs[2:])
    start(second[2] + tokens[1:])
    finish(third[1])
    swap(1)
    finish(second[2])
    start(third[2])
    finish(tokens[1:])
    finish(third[2])
    swap(2)
    for i in range(cols):
        far = (z - i > reach) | (i - z > reach)
        for m in range(micro):
            def fill(m=m, i=i):
                copy = pltpu.make_async_copy(own_ref.at[m], every_ref.at[m, i], local_sems.at[3 + m])
                copy.start()
                copy.wait()

            if i > reach or cols - 1 - i > reach:
                pl.when(far)(fill)
    for j in range(3):
        post.wait(("k", j), "k", 1 - k, full_ref.at[j, :, :, :, 1 - k])
    post.close()


def gather(sizes, own, shard):
    ns, nr, nc = sizes
    ny = nr // 2
    micro, rows, model = own.shape
    _, rb, w = shard.shape
    count = 3 * 2 * (nc - 1) + micro * 2 * (nc - 1) + 3 * (4 * (ny - 1) + 4 * (ns - 1) + 1)
    anywhere = pl.BlockSpec(memory_space=pl.ANY)
    every, full = pl.pallas_call(
        functools.partial(gather_kernel, sizes, micro),
        out_shape=[
            jax.ShapeDtypeStruct((micro, nc, rows, model), own.dtype),
            jax.ShapeDtypeStruct((3, nc, ns, ny, 2, rb, w), shard.dtype),
        ],
        in_specs=[pl.BlockSpec(memory_space=pltpu.VMEM)] * 2,
        out_specs=[anywhere] * 2,
        scratch_shapes=[pltpu.SemaphoreType.DMA((count,)), pltpu.SemaphoreType.DMA((count,)), pltpu.SemaphoreType.DMA((3 + micro,))],
        compiler_params=pltpu.CompilerParams(collective_id=0, has_side_effects=True),
        name="gather",
    )(own, shard)
    return every, full.reshape(3, nc, ns * nr * rb, w)


class LineReduce:
    def __init__(self, post, name, axis, line, region, inbox, add, reach=None):
        self.post, self.name, self.axis, self.region, self.inbox, self.add = post, name, axis, region, inbox, add
        self.mine, self.size = line
        self.reach = min(self.size - 1, reach or self.size)

    def arrived(self, way, e):
        behind, goal = self.mine - way, self.mine + way * e
        return (behind >= 0) & (behind < self.size) & (goal >= 0) & (goal < self.size)

    def take(self, way, e):
        ok = self.arrived(way, e)
        inbox = self.inbox(way, e)
        self.post.wait((self.name, way, e), self.axis, clip(self.mine - way, self.size), inbox, ok)

        @pl.when(ok)
        def _():
            self.add(self.region(clip(self.mine + way * e, self.size)), inbox)

    def forward(self, way, e):
        def make():
            goal = self.mine + way * e
            ok = (goal >= 0) & (goal < self.size)
            return self.axis, clip(self.mine + way, self.size), self.region(clip(goal, self.size)), self.inbox(way, e - 1), ok

        self.post.send((self.name, way, e - 1), make)

    def start(self):
        for way in (1, -1):
            if self.reach >= 1:
                self.forward(way, self.reach)

    def forward_from(self, nearest):
        for e in range(self.reach - 1, nearest - 1, -1):
            for way in (1, -1):
                self.take(way, e)
                self.forward(way, e)

    def finish(self, last=True):
        self.forward_from(1)
        if last:
            for way in (1, -1):
                if self.reach >= 1:
                    self.take(way, 0)


def reduce_to(post, name, axis, line, goal, e, region, inbox, add):
    mine, size = line
    for way in (1, -1):
        behind = mine - way
        arrives = (way * (goal - mine) == e) & (behind >= 0) & (behind < size)
        slot = inbox(way, min(e, size - 2))
        post.wait((name, way), axis, clip(behind, size), slot, arrives)

        @pl.when(arrives)
        def _():
            add(region, slot)

        def make(way=way):
            return axis, clip(mine + way, size), region, inbox(way, e - 1), way * (goal - mine) == e

        if e:
            post.send((name, way), make)


def reduce_kernel(sizes, micro, own_ref, spread_ref, part_ref, vec_ref, back_ref, block_ref, sums_ref,
                  mine_buf, core_buf, in_a, in_b, in_c, in_d, in_z, tok_buf, tok_in, vec_buf, send_sems, recv_sems, local_sems):
    floats, halves = jnp.float32, jnp.bfloat16
    lines, device = place(sizes)
    (x, ns), (y, ny), (k, _), (z, nc) = (lines[a] for a in "xykz")
    half = part_ref.shape[-1] // 2
    rows = own_ref.shape[1]
    reach = -(-(DOC_MOST - 1) // rows)
    parts = [pl.ds(p * half, half) for p in (0, 1)]
    local = [pltpu.make_async_copy(part_ref.at[j, :, :, :, k], mine_buf.at[j], local_sems.at[j]) for j in range(3)]
    local += [pltpu.make_async_copy(spread_ref.at[m], tok_buf.at[m], local_sems.at[3 + m]) for m in range(micro)]
    for copy in local:
        copy.start()
    greet(lines, device)
    post = Post(device, send_sems, recv_sems)
    for j in range(3):
        post.send(("k", j), lambda j=j: ("k", 1 - k, part_ref.at[j, :, :, :, 1 - k], core_buf.at[j], None))

    def plus(target, source):
        target[...] = (target[...].astype(floats) + source[...].astype(floats)).astype(halves)

    def plus_grid(target, source, first, second):
        @pl.loop(0, first * second)
        def _(n):
            plus(target.at[n // second, lax.rem(n, second)], source.at[n // second, lax.rem(n, second)])

    def plus_row(target, source, first):
        @pl.loop(0, first)
        def _(n):
            plus(target.at[n], source.at[n])

    vec_buf[0, 0] = vec_ref[...]

    def vector_start(stage, axis):
        mine, size = lines[axis]
        vec_buf[stage, 1 + mine] = vec_buf[stage, 0]
        for t in range(1, size):
            post.send(("v", stage, t), lambda t=t: (
                axis, lax.rem(mine + t, size), vec_buf.at[stage, 0], vec_buf.at[stage, 1 + mine], None))

    def vector_finish(stage, axis, out):
        mine, size = lines[axis]
        for t in range(1, size):
            origin = lax.rem(mine + size - t, size)
            post.wait(("v", stage, t), axis, origin, vec_buf.at[stage, 1 + origin])
        total = vec_buf[stage, 1]
        for i in range(1, size):
            total = total + vec_buf[stage, 1 + i]
        out[...] = total

    tokens = [
        LineReduce(post, ("t", m), "z", lines["z"], lambda i, m=m: tok_buf.at[m, i],
                   lambda way, e, m=m: tok_in.at[m, (1 - way) // 2, e], plus, reach)
        for m in range(micro)
    ]
    box = lambda way: (1 - way) // 2
    second, third, last = {}, {}, {}
    for j in range(3):
        second[j] = [
            LineReduce(post, ("a", j), "x", lines["x"], lambda i, j=j: mine_buf.at[j, :, i, :, :, parts[0]],
                       lambda way, e, j=j: in_a.at[j, box(way), e], lambda t, s: plus_grid(t, s, nc, ny)),
            LineReduce(post, ("b", j), "y", lines["y"], lambda i, j=j: mine_buf.at[j, :, :, i, :, parts[1]],
                       lambda way, e, j=j: in_b.at[j, box(way), e], lambda t, s: plus_grid(t, s, nc, ns)),
        ]
        third[j] = [
            LineReduce(post, ("c", j), "y", lines["y"], lambda i, j=j: mine_buf.at[j, :, x, i, :, parts[0]],
                       lambda way, e, j=j: in_c.at[j, box(way), e], lambda t, s: plus_row(t, s, nc)),
            LineReduce(post, ("d", j), "x", lines["x"], lambda i, j=j: mine_buf.at[j, :, i, y, :, parts[1]],
                       lambda way, e, j=j: in_d.at[j, box(way), e], lambda t, s: plus_row(t, s, nc)),
        ]
        last[j] = [
            LineReduce(post, ("z", j), "z", lines["z"], lambda i, j=j: mine_buf.at[j, i, x, y],
                       lambda way, e, j=j: in_z.at[j, box(way), e], plus)
        ]

    def start(group):
        for line in group:
            line.start()

    def finish(group):
        for line in group:
            line.finish()

    def core(j):
        local[j].wait()
        post.wait(("k", j), "k", 1 - k, core_buf.at[j])

        @pl.loop(0, nc * ns * ny)
        def _(n):
            at = (n // (ns * ny), lax.rem(n // ny, ns), lax.rem(n, ny))
            plus(mine_buf.at[(j, *at)], core_buf.at[(j, *at)])

    for m in range(micro):
        local[3 + m].wait()
    start(tokens)
    core(0)
    start(second[0])
    vector_start(0, "k")
    core(1)
    start(second[1])
    vector_finish(0, "k", vec_buf.at[1, 0])
    vector_start(1, "y")
    core(2)
    finish(second[0])
    start(third[0])
    start(second[2])
    vector_finish(1, "y", vec_buf.at[2, 0])
    vector_start(2, "x")
    finish(tokens)
    vector_finish(2, "x", vec_buf.at[3, 0])
    vector_start(3, "z")
    finish(second[1])
    start(third[1])
    finish(third[0])
    start(last[0])
    finish(second[2])
    start(third[2])
    finish(third[1])
    start(last[1])
    finish(last[0])
    finish(third[2])
    start(last[2])
    vector_finish(3, "z", sums_ref)
    for m in range(micro):
        back_ref[m] = own_ref[m] + tok_buf[m, z].astype(floats)
    finish(last[1])
    finish(last[2])
    for j in range(3):
        block_ref[j] = mine_buf[j, z, x, y].astype(floats)
    post.close()


def reduce(sizes, own_share, spread, partial, vectors):
    ns, nr, nc = sizes
    ny = nr // 2
    micro, rows, model = own_share.shape
    w = partial.shape[-1]
    rb = partial.shape[2] // (ns * nr)
    halves, floats = jnp.bfloat16, jnp.float32
    reach = min(nc - 1, -(-(DOC_MOST - 1) // rows))
    count = 3 + 2 * (ny - 1 + ns - 1) * 6 + 3 * 2 * (nc - 1) + micro * 2 * reach + (1 + ny - 1 + ns - 1 + nc - 1)
    widest = max(ns, ny, nc, 2)
    extra = -vectors.shape[0] % 8
    vectors = jnp.pad(vectors, ((0, extra), (0, 0)))
    vmem = pl.BlockSpec(memory_space=pltpu.VMEM)
    anywhere = pl.BlockSpec(memory_space=pl.ANY)
    back, blocks, sums = pl.pallas_call(
        functools.partial(reduce_kernel, sizes, micro),
        out_shape=[
            jax.ShapeDtypeStruct((micro, rows, model), floats),
            jax.ShapeDtypeStruct((3, rb, w), floats),
            jax.ShapeDtypeStruct(vectors.shape, floats),
        ],
        in_specs=[vmem, anywhere, anywhere, vmem],
        out_specs=[vmem] * 3,
        scratch_shapes=[
            pltpu.VMEM((3, nc, ns, ny, rb, w), halves),
            pltpu.VMEM((3, nc, ns, ny, rb, w), halves),
            pltpu.VMEM((3, 2, max(ns - 1, 1), nc, ny, rb, w // 2), halves),
            pltpu.VMEM((3, 2, max(ny - 1, 1), nc, ns, rb, w // 2), halves),
            pltpu.VMEM((3, 2, max(ny - 1, 1), nc, rb, w // 2), halves),
            pltpu.VMEM((3, 2, max(ns - 1, 1), nc, rb, w // 2), halves),
            pltpu.VMEM((3, 2, max(nc - 1, 1), rb, w), halves),
            pltpu.VMEM((micro, nc, rows, model), halves),
            pltpu.VMEM((micro, 2, max(reach, 1), rows, model), halves),
            pltpu.VMEM((4, 1 + widest, *vectors.shape), floats),
            pltpu.SemaphoreType.DMA((count,)),
            pltpu.SemaphoreType.DMA((count,)),
            pltpu.SemaphoreType.DMA((3 + micro,)),
        ],
        compiler_params=pltpu.CompilerParams(collective_id=1, has_side_effects=True, vmem_limit_bytes=60 << 20),
        name="reduce",
    )(own_share, spread, partial.reshape(3, nc, ns, ny, 2, rb, w), vectors)
    return back, blocks, sums


Q_AT, K_AT, V_AT, O_AT, WINDOW = 0, 128, 384, 512, 256


def plane(full_ref, c, at, size=WINDOW):
    value = full_ref[c, :, :, :, :, at : at + size]
    return value.reshape(-1, size)


def split_plan(plan):
    parts, order = [[]], []
    for task in plan:
        if task[0] == "U":
            order.append(task[1:])
            parts.append([])
        else:
            parts[-1].append(task)
    return parts[0], parts[1:], order


def pick(step, values):
    value = values[0]
    for i, other in enumerate(values[1:], 1):
        value = jnp.where(step == i, other, value)
    return value


def place_of(rows):
    return lax.broadcasted_iota(jnp.int32, (rows, WINDOW), 1) // HEAD_DIM


def keep(value, places, wanted):
    return jnp.where(places == wanted, value, jnp.zeros_like(value))


def forward_kernel(sizes, micro, own_ref, wq_ref, wk_ref, wv_ref, wo_ref, wh_ref, wd_ref, hidden_bias_ref, query_bias_ref, value_bias_ref, seg_ref,
                   rest_ref, first_ref, turned_ref, mask_ref, biases_ref, mixed_ref, lse_ref, q_ref, k_ref, v_ref,
                   weights, turned, bias_buf, mask, mixed_buf, lse_buf, q_buf, k_buf, v_buf, tokens_buf, acc, top, total,
                   send_sems, recv_sems, local_sems, unit_sems, turn_buf):
    floats, halves = jnp.float32, jnp.bfloat16
    lines, device = place(sizes)
    (x, _), (y, _), (k, _), (z, cols) = (lines[a] for a in "xykz")
    half = wh_ref.shape[-1] // 2
    rows = own_ref.shape[1]
    reach = -(-(DOC_MOST - 1) // rows)
    parts = [pl.ds(p * half, half) for p in (0, 1)]
    low, high = jnp.maximum(z - reach, 0), jnp.minimum(z + reach + 1, cols)
    used = [0]

    class Local:
        def __init__(self, source, target):
            self.source, self.target, self.n = source, target, used[0]
            used[0] += 1
            self.describe().start()

        def describe(self):
            source = self.source() if callable(self.source) else self.source
            return pltpu.make_async_copy(source, self.target, local_sems.at[self.n])

        def wait(self):
            self.describe().wait()

    local = Local
    targets = [weights.at[0], rest_ref.at[0], rest_ref.at[1]]
    packed = [wq_ref[...], wk_ref[...], wv_ref[...], wo_ref[...].astype(floats).T.astype(halves)]
    weights[0, z, x, y, k] = jnp.concatenate(packed, 1)
    turn_buf[...] = wd_ref[...].astype(floats).T.astype(halves)
    begin = [local(wh_ref, targets[1].at[z, x, y, k]), local(turn_buf, targets[2].at[z, x, y, k])]
    begin += [local(own_ref.at[m], tokens_buf.at[m, z]) for m in range(micro)]
    for i, ref in enumerate((hidden_bias_ref, query_bias_ref, value_bias_ref)):
        bias_buf[z, i : i + 1, 0 : ref.shape[0]] = ref[...].astype(floats).reshape(1, -1)
        if ref.shape[0] < WINDOW:
            bias_buf[z, i : i + 1, ref.shape[0] : WINDOW] = jnp.zeros((1, WINDOW - ref.shape[0]), floats)
    greet(lines, device)
    post = Post(device, send_sems, recv_sems)
    for copy in begin:
        copy.wait()
    tokens = [
        LineGather(post, ("t", q), "z", lines["z"],
                   lambda i, q=q: tokens_buf.at[q // 2, i, pl.ds(q % 2 * (rows // 2), rows // 2)], reach)
        for q in range(2 * micro)
    ]
    small = LineGather(post, "bias", "z", lines["z"], lambda i: bias_buf.at[i])
    rb = wh_ref.shape[0]
    zs, second, third = {}, {}, {}
    for n in range(6):
        j, r = n // 2, pl.ds(n % 2 * (rb // 2), rb // 2)
        zs[n] = LineGather(post, ("z", n), "z", lines["z"], lambda i, j=j, r=r: targets[j].at[i, x, y, k, r])
        second[n] = [
            LineGather(post, ("a", n), "y", lines["y"], lambda i, j=j, r=r: targets[j].at[:, x, i, k, r, parts[0]]),
            LineGather(post, ("b", n), "x", lines["x"], lambda i, j=j, r=r: targets[j].at[:, i, y, k, r, parts[1]]),
        ]
        third[n] = [
            LineGather(post, ("c", n), "x", lines["x"], lambda i, j=j, r=r: targets[j].at[:, i, :, k, r, parts[0]]),
            LineGather(post, ("d", n), "y", lines["y"], lambda i, j=j, r=r: targets[j].at[:, :, i, k, r, parts[1]]),
        ]

    def start(*group):
        for line in group:
            line.start()

    def finish(*group):
        for line in group:
            line.finish()

    def side(n, which):
        return targets[n // 2].at[:, :, :, which, pl.ds(n % 2 * (rb // 2), rb // 2)]

    def swap(n):
        post.send(("k", n), lambda: ("k", 1 - k, side(n, k), side(n, k), None))

    def swapped(n):
        post.wait(("k", n), "k", 1 - k, side(n, 1 - k))

    places = place_of(rows)

    def unit(m, c):
        queries = jnp.dot(own_ref[m], plane(weights.at[0], c, Q_AT), preferred_element_type=floats) + bias_buf[c, 1:2, 0:WINDOW]
        queries = pltpu.roll(queries.astype(halves).astype(floats) * HEAD_DIM ** -0.5, HEAD_DIM, 1)
        queries = jnp.where(places > 0, queries, 0.0).astype(halves)
        q_buf[m, c] = queries
        heads = [keep(queries, places, h + 1) for h in range(3)]
        acc[...] = jnp.zeros_like(acc)
        total[...] = jnp.zeros_like(total)
        top[...] = jnp.full_like(top, 2 * MASK_VALUE)
        key_weight = plane(weights.at[0], c, K_AT)
        value_weight = plane(weights.at[0], c, V_AT)
        value_bias = bias_buf[c, 2:3, 0:WINDOW]

        def step(block):
            rows_at = tokens_buf[m, block]
            keys = jnp.dot(rows_at, key_weight, preferred_element_type=floats).astype(halves)
            values = (jnp.dot(rows_at, value_weight, preferred_element_type=floats) + value_bias).astype(halves)
            k_buf[m, c, block] = keys
            v_buf[m, c, block] = values
            values_t = values.T
            hidden = mask[m, block].astype(floats)
            for h in range(3):
                s = contract_cols(keys, heads[h]) + hidden
                old = top[h : h + 1]
                new = jnp.maximum(old, jnp.max(s, 0, keepdims=True))
                p = jnp.exp(s - new)
                shrink = jnp.exp(old - new)
                top[h : h + 1] = new
                total[h : h + 1] = total[h : h + 1] * shrink + jnp.sum(p, 0, keepdims=True)
                at = pl.ds((h + 1) * HEAD_DIM, HEAD_DIM)
                acc[at, :] = acc[at, :] * shrink + jnp.dot(
                    values_t[h * HEAD_DIM : (h + 1) * HEAD_DIM], p.astype(halves), preferred_element_type=floats
                )

        for block in range(cols):
            step(block)
        for h in range(3):
            at = pl.ds((h + 1) * HEAD_DIM, HEAD_DIM)
            acc[at, :] = acc[at, :] / total[h : h + 1]
        mixed_buf[c, m] = acc[...].T.astype(halves)
        lse_buf[m, c] = top[...] + jnp.log(jnp.maximum(total[...], 1e-30))

    def units(m, first, last):
        @pl.loop(first, last)
        def _(c):
            unit(m, c)

    def masks(m):
        asking = seg_ref[m, 0:1, pl.ds(pl.multiple_of(z * rows, 128), rows)].astype(floats)
        for block in range(cols):
            asked = seg_ref[m, 0:1, block * rows : (block + 1) * rows].astype(floats)
            same = jnp.broadcast_to(asked, (rows, rows)).T == asking
            mask[m, block] = jnp.where(same, 0.0, MASK_VALUE).astype(halves)

    done = []

    def turn(m):
        for block in range(cols):
            turned[:, (m * cols + block) * rows : (m * cols + block + 1) * rows] = tokens_buf[m, block].T
        if m == micro - 1:
            done.append(local(turned, turned_ref))

    keeps = ((q_buf, q_ref), (k_buf, k_ref), (v_buf, v_ref), (lse_buf, lse_ref))

    def take_z(n, t):
        zs[n].step(t)
        if n == 0:
            small.step(t)
        if t == cols - 1:
            start(*second[n])

    def take_second(n):
        finish(*second[n])
        start(*third[n])

    def take_third(n):
        finish(*third[n])
        swap(n)

    swaps = set()

    def take_core(n):
        swapped(n)
        swaps.add(n)
        if n < 2 and swaps >= {0, 1}:
            done.append(local(lambda: weights.at[0], first_ref))

    act = {
        "Zs": lambda n: zs[n].start(), "Z": take_z, "Ts": lambda q: tokens[q].start(), "T": lambda q, t: tokens[q].step(t),
        "B": take_second, "C": take_third, "K": take_core, "R": turn,
    }
    small.start()
    head, tail, order = split_plan(FORWARD_PLAN)
    act[head[0][0]](*head[0][1:])
    for block in range(cols):
        if block > reach or cols - 1 - block > reach:
            @pl.when(jnp.logical_not((low <= block) & (block < high)))
            def _(block=block):
                for m in range(micro):
                    tokens_buf[m, block] = jnp.zeros(own_ref.shape[1:], halves)
    for m in range(micro):
        masks(m)
    for task in head[1:]:
        act[task[0]](*task[1:])

    def leave(m, c, step, go):
        for i, (source, target) in enumerate(keeps):
            go(pltpu.make_async_copy(source.at[m, c], target.at[m, c], unit_sems.at[i, step]))

    @pl.loop(0, len(order))
    def _(step):
        m, c = pick(step, [m for m, _ in order]), pick(step, [c for _, c in order])
        unit(m, c)
        leave(m, c, step, lambda copy: copy.start())
        for i, tasks in enumerate(tail[:-1]):
            if tasks:
                @pl.when(step == i)
                def _(tasks=tasks):
                    for task in tasks:
                        act[task[0]](*task[1:])

    for source, target in ((bias_buf, biases_ref), (mixed_buf, mixed_ref), (mask, mask_ref)):
        done.append(local(source, target))
    for task in tail[-1]:
        act[task[0]](*task[1:])
    for step, (m, c) in enumerate(order):
        leave(m, c, step, lambda copy: copy.wait())
    for copy in done:
        copy.wait()
    post.close()


def forward(sizes, own, shards, hidden_bias, query_bias, value_bias, segments):
    ns, nr, nc = sizes
    ny = nr // 2
    micro, rows, model = own.shape
    rb, w = shards[4].shape
    halves, floats = own.dtype, jnp.float32
    reach = min(nc - 1, -(-(DOC_MOST - 1) // rows))
    count = (6 + 1) * 2 * (nc - 1) + micro * 4 * reach + 6 * (4 * (ny - 1) + 4 * (ns - 1) + 1)
    anywhere = pl.BlockSpec(memory_space=pl.ANY)
    vmem = pl.BlockSpec(memory_space=pltpu.VMEM)
    length = nc * rows
    arrays = [
        ((2, nc, ns, ny, 2, rb, w), halves), ((nc, ns, ny, 2, rb, w), halves), ((model, micro * length), halves), ((micro, nc, rows, rows), halves),
        ((nc, 8, model), floats), ((nc, micro, rows, WINDOW), halves), ((micro, nc, 8, rows), floats),
        ((micro, nc, rows, WINDOW), halves), ((micro, nc, nc, rows, WINDOW), halves), ((micro, nc, nc, rows, WINDOW), halves),
    ]
    shapes = [pltpu.VMEM(shape, kind) for shape, kind in arrays]
    return pl.pallas_call(
        functools.partial(forward_kernel, sizes, micro),
        out_shape=[jax.ShapeDtypeStruct(shape, kind) for shape, kind in arrays],
        in_specs=[vmem] * 11,
        out_specs=[anywhere] * len(arrays),
        scratch_shapes=[
            pltpu.VMEM((1, nc, ns, ny, 2, rb, w), halves),
            shapes[2], shapes[4], shapes[3], *shapes[5:],
            pltpu.VMEM((micro, nc, rows, model), halves), pltpu.VMEM((WINDOW, rows), floats), pltpu.VMEM((8, rows), floats), pltpu.VMEM((8, rows), floats),
            pltpu.SemaphoreType.DMA((count,)), pltpu.SemaphoreType.DMA((count,)), pltpu.SemaphoreType.DMA((20,)), pltpu.SemaphoreType.DMA((4, micro * nc)), pltpu.VMEM((rb, w), halves),
        ],
        compiler_params=pltpu.CompilerParams(collective_id=2, has_side_effects=True, vmem_limit_bytes=60 << 20),
        name="forward",
    )(own, *shards, hidden_bias, query_bias, value_bias, segments)


def middle_kernel(cols, own_ref, mixed_ref, out_ref, hidden_ref, down_ref, bias_ref, *refs):
    vector_refs = refs[:6]
    (cot_ref, outputs_ref, first_grad_ref, attn_grad_ref, part_ref, sums_ref,
     normal, scale, normed, normed_low, normed_t, grad_low, grad_t, act_buf, slope_buf, total) = refs[6:]
    floats, halves = jnp.float32, jnp.bfloat16
    step = pl.program_id(0)
    rows, model = own_ref.shape
    chunks = [pl.ds(r * 256, 256) for r in range(rows // 256)]
    whole_rows = [pl.ds(0, rows)]
    bands = [pl.ds(n * 256, 256) for n in range(model // 256)]
    vector = lambda i: vector_refs[i][...].astype(floats).reshape(1, -1)

    @pl.when(step == 0)
    def _():
        sums_ref[...] = jnp.zeros_like(sums_ref)
        for chunk in chunks:
            first_sum = own_ref[chunk].astype(floats) + vector(0)
            for c in range(cols):
                first_sum = first_sum + contract_cols(mixed_ref[c, chunk], out_ref[c])
            normal_one, scale_one = norm_parts(first_sum)
            normal[chunk] = normal_one
            scale[chunk] = jnp.broadcast_to(scale_one, (256, 128))
            norm_one = normal_one * vector(1) + vector(2)
            total[chunk] = norm_one + vector(3)
            normed_low[chunk] = norm_one.astype(halves)
            normed_t[:, chunk] = norm_one.astype(halves).T

    @pl.when(step < cols)
    def _():
        for chunk in chunks:
            for band in bands:
                hidden = jnp.dot(normed_low[chunk], hidden_ref[0, 0, :, band], preferred_element_type=floats) + bias_ref[0, 0:1, band]
                half_erf = 0.5 * lax.erf(hidden * 0.7071067811865476) + 0.5
                act_buf[step, chunk, band] = (hidden * half_erf).astype(halves)
                slope_buf[step, chunk, band] = (half_erf + hidden * (jnp.exp(-0.5 * hidden * hidden) * 0.3989422804014327)).astype(halves)
        for chunk in chunks:
            for band in bands:
                total[chunk, band] += contract_cols(act_buf[step, chunk], down_ref[0, 0, band, :])

    @pl.when(step == cols - 1)
    def _():
        for chunk in chunks:
            normal_two, scale_two = norm_parts(total[chunk])
            outputs_ref[chunk] = (normal_two * vector(4) + vector(5)).astype(halves)
            cot = cot_ref[chunk].astype(floats)
            second_grad = norm_back(cot * vector(4), normal_two, scale_two)
            total[chunk] = second_grad
            grad_low[chunk] = second_grad.astype(halves)
            grad_t[:, chunk] = second_grad.astype(halves).T
            sums_ref[3:4] += jnp.sum(second_grad, 0, keepdims=True)
            sums_ref[4:5] += jnp.sum(cot * normal_two, 0, keepdims=True)
            sums_ref[5:6] += jnp.sum(cot, 0, keepdims=True)

    @pl.when(step >= cols)
    def _():
        c = step - cols
        bias_total = [jnp.zeros((1, 256), floats) for _ in bands]
        for chunk in chunks:
            for n, band in enumerate(bands):
                pre = jnp.dot(grad_low[chunk], down_ref[0, 0, :, band], preferred_element_type=floats)
                pre = (pre * slope_buf[c, chunk, band].astype(floats)).astype(halves)
                slope_buf[c, chunk, band] = pre
                bias_total[n] = bias_total[n] + jnp.sum(pre.astype(floats), 0, keepdims=True)
        for n, band in enumerate(bands):
            sums_ref[pl.ds(8 + c, 1), band] = bias_total[n]
        for band in bands:
            for side in [pl.ds(0, model)]:
                part_ref[0, 0, side, band] = jnp.dot(normed_t[side, :], slope_buf[c, :, band], preferred_element_type=floats).astype(halves)
                part_ref[1, 0, side, band] = jnp.dot(grad_t[side, :], act_buf[c, :, band], preferred_element_type=floats).astype(halves)
        for chunk in chunks:
            for band in bands:
                total[chunk, band] += contract_cols(slope_buf[c, chunk], hidden_ref[0, 0, band, :])

    @pl.when(step == 2 * cols - 1)
    def _():
        for chunk in chunks:
            normed_grad, normal_one = total[chunk], normal[chunk]
            first_grad = norm_back(normed_grad * vector(1), normal_one, scale[chunk, 0:1])
            first_grad_ref[chunk] = first_grad
            attn_grad_ref[chunk] = first_grad.astype(halves)
            sums_ref[0:1] += jnp.sum(first_grad, 0, keepdims=True)
            sums_ref[1:2] += jnp.sum(normed_grad * normal_one, 0, keepdims=True)
            sums_ref[2:3] += jnp.sum(normed_grad, 0, keepdims=True)


def middle(own, mixed, first, rest, biases, vectors, cot):
    rows, model = own.shape
    cols = first.shape[0]
    halves, floats = jnp.bfloat16, jnp.float32
    whole = lambda shape: pl.BlockSpec(shape, lambda i: (0,) * len(shape))
    wide = lambda kind: pltpu.VMEM((rows, model), kind)
    return pl.pallas_call(
        functools.partial(middle_kernel, cols),
        grid=(2 * cols,),
        in_specs=[
            whole((rows, model)), whole(mixed.shape),
            pl.BlockSpec((cols, model, WINDOW), lambda i: (0, 0, O_AT // WINDOW)),
            pl.BlockSpec((1, 1, model, rest.shape[-1]), lambda i: (0, lax.rem(i, cols), 0, 0)),
            pl.BlockSpec((1, 1, model, rest.shape[-1]), lambda i: (1, lax.rem(i, cols), 0, 0)),
            pl.BlockSpec((1, *biases.shape[1:]), lambda i: (lax.rem(i, cols), 0, 0)),
            *[whole((model,))] * 6, whole((rows, model)),
        ],
        out_specs=[
            whole((rows, model)), whole((rows, model)), whole((rows, model)),
            pl.BlockSpec((2, 1, model, rest.shape[-1]), lambda i: (0, jnp.maximum(i - cols, 0), 0, 0)),
            whole((8 + cols + -cols % 8, model)),
        ],
        out_shape=[
            jax.ShapeDtypeStruct((rows, model), halves), jax.ShapeDtypeStruct((rows, model), floats),
            jax.ShapeDtypeStruct((rows, model), halves), jax.ShapeDtypeStruct(rest.shape, halves),
            jax.ShapeDtypeStruct((8 + cols + -cols % 8, model), floats),
        ],
        scratch_shapes=[
            wide(floats), pltpu.VMEM((rows, 128), floats), wide(floats), wide(halves), pltpu.VMEM((model, rows), halves), wide(halves),
            pltpu.VMEM((model, rows), halves), pltpu.VMEM((cols, rows, rest.shape[-1]), halves),
            pltpu.VMEM((cols, rows, rest.shape[-1]), halves), wide(floats),
        ],
        compiler_params=pltpu.CompilerParams(vmem_limit_bytes=56 << 20),
        name="middle",
    )(own, mixed, first, rest, rest, biases, *vectors, cot)


class Inbox:
    def __init__(self, ref, size):
        self.ref, self.size = ref, size

    def __call__(self, way, e):
        return self.ref.at[0 if self.size == 2 else (1 - way) // 2, e]


def backward_kernel(sizes, micro, grad_ref, share_ref, first_ref, turned_ref, mixed_ref, lse_ref, q_ref, k_ref, v_ref,
                    mask_ref, part_ref, vec_ref,
                    back_ref, block_ref, sums_ref,
                    mine_buf, core_buf, stage_buf, in_a, in_b, in_c, in_d, in_z, tok_buf, tok_in, vec_buf,
                    weights, mixed_buf, q_buf, k_buf, v_buf, every_t, grad_t, mask, acc, spread, block_sum,
                    send_sems, recv_sems, local_sems, free_sem):
    floats, halves = jnp.float32, jnp.bfloat16
    lines, device = place(sizes)
    (x, ns), (y, ny), (k, _), (z, cols) = (lines[a] for a in "xykz")
    model = first_ref.shape[1]
    half = part_ref.shape[-1] // 2
    rb = part_ref.shape[-2]
    rows = grad_ref.shape[1]
    reach = -(-(DOC_MOST - 1) // rows)
    parts = [pl.ds(p * half, half) for p in (0, 1)]
    used = [0]

    def local(source, target):
        copy = pltpu.make_async_copy(source, target, local_sems.at[used[0]])
        used[0] += 1
        copy.start()
        return copy

    def rows_of(n):
        return pl.ds(n % 2 * (rb // 2), rb // 2)

    planes = [local(part_ref.at[n // 2, :, :, :, k, rows_of(n)], mine_buf.at[n // 2 + 1, :, :, :, rows_of(n)]) for n in range(4)]
    loads = [local(*pair) for pair in ((first_ref, weights), (mixed_ref, mixed_buf), (q_ref, q_buf), (share_ref, back_ref))]
    loads += [local(k_ref, k_buf), local(v_ref, v_buf)]
    loads += [local(mask_ref, mask)]
    late = [local(turned_ref, every_t)]
    greet(lines, device)
    post = Post(device, send_sems, recv_sems)

    def give(n):
        post.send(("k", n), lambda: (
            "k", 1 - k, part_ref.at[n // 2, :, :, :, 1 - k, rows_of(n)], core_buf.at[n // 2, :, :, :, rows_of(n)], None))

    def plus(target, source):
        target[...] = target[...] + source[...]

    def plus_grid(target, source, first, second):
        @pl.loop(0, first * second)
        def _(n):
            at = (n // second, lax.rem(n, second))
            plus(target.at[at], source.at[at])

    def plus_row(target, source, first):
        @pl.loop(0, first)
        def _(n):
            plus(target.at[n], source.at[n])

    class Stream:
        def __init__(self, name, j, begin, size, r):
            cs = pl.ds(begin, size)
            self.second = [
                LineReduce(post, (name, "a"), "x", lines["x"], lambda i: mine_buf.at[j, cs, i, :, r, parts[0]],
                           lambda way, e: Inbox(in_a.at[j], ns)(way, e).at[cs, :, r], lambda t, s: plus_grid(t, s, size, ny)),
                LineReduce(post, (name, "b"), "y", lines["y"], lambda i: mine_buf.at[j, cs, :, i, r, parts[1]],
                           lambda way, e: Inbox(in_b.at[j], ny)(way, e).at[cs, :, r], lambda t, s: plus_grid(t, s, size, ns)),
            ]
            self.third = [
                LineReduce(post, (name, "c"), "y", lines["y"], lambda i: mine_buf.at[j, cs, x, i, r, parts[0]],
                           lambda way, e: Inbox(in_c.at[j], ny)(way, e).at[cs, r], lambda t, s: plus_row(t, s, size)),
                LineReduce(post, (name, "d"), "x", lines["x"], lambda i: mine_buf.at[j, cs, i, y, r, parts[1]],
                           lambda way, e: Inbox(in_d.at[j], ns)(way, e).at[cs, r], lambda t, s: plus_row(t, s, size)),
            ]

    def line_z(name, j, r):
        return LineReduce(post, ("z", name), "z", lines["z"], lambda i: mine_buf.at[j, i, x, y, r],
                          lambda way, e: in_z.at[j, (1 - way) // 2, e, r], plus)

    ffn = [Stream(("s", n), n // 2 + 1, 0, cols, rows_of(n)) for n in range(4)]
    ffn_z = [line_z(n, n // 2 + 1, rows_of(n)) for n in range(4)]
    attn = [Stream(("u", c), 0, c, 1, pl.ds(0, rb)) for c in range(cols)]

    def take_y(c, e):
        reduce_to(post, ("y", c), "z", lines["z"], c, e, mine_buf.at[0, c, x, y], lambda way, e: in_z.at[0, (1 - way) // 2, e], plus)

    def half_of(h):
        return pl.ds(h * (rows // 2), rows // 2)

    def line_tokens(m, h):
        at = half_of(h)
        return LineReduce(post, ("t", m, h), "z", lines["z"], lambda i: tok_buf.at[m, i, at],
                          lambda way, e: tok_in.at[m, (1 - way) // 2, e, at], plus, reach)

    tokens = [[line_tokens(m, h) for h in range(2)] for m in range(micro)]

    def start(*group):
        for line in group:
            line.start()

    def finish(*group):
        for line in group:
            line.finish()

    def core(n):
        planes[n].wait()
        r = rows_of(n)
        post.wait(("k", n), "k", 1 - k, core_buf.at[n // 2, :, :, :, r])

        @pl.loop(0, cols * ns * ny)
        def _(i):
            at = (i // (ns * ny), lax.rem(i // ny, ns), lax.rem(i, ny), r)
            plus(mine_buf.at[(n // 2 + 1, *at)], core_buf.at[(n // 2, *at)])

    def vector_start(stage, axis):
        mine, size = lines[axis]
        vec_buf[stage, 1 + mine] = vec_buf[stage, 0]
        for t in range(1, size):
            post.send(("v", stage, t), lambda t=t: (
                axis, lax.rem(mine + t, size), vec_buf.at[stage, 0], vec_buf.at[stage, 1 + mine], None))

    def vector_finish(stage, axis, out):
        mine, size = lines[axis]
        for t in range(1, size):
            origin = lax.rem(mine + size - t, size)
            post.wait(("v", stage, t), axis, origin, vec_buf.at[stage, 1 + origin])
        total = vec_buf[stage, 1]
        for i in range(1, size):
            total = total + vec_buf[stage, 1 + i]
        out[...] = total

    places = place_of(rows)
    small = vec_ref.shape[0]
    vec_buf[0, 0] = jnp.zeros_like(vec_buf[0, 0])
    vec_buf[0, 0, 0:small] = vec_ref[...]

    def unit(m, c):
        mixed_grad = jnp.dot(grad_ref[m], weights[c, :, O_AT : O_AT + WINDOW], preferred_element_type=floats).astype(halves)
        mixed_grad = jnp.where(places > 0, mixed_grad.astype(floats), 0.0)
        product = mixed_grad * mixed_buf[c, m].astype(floats)
        product_high = product.astype(halves)
        product_low = (product - product_high.astype(floats)).astype(halves)
        pick = (
            lax.broadcasted_iota(jnp.int32, (8, WINDOW), 1) // HEAD_DIM == lax.broadcasted_iota(jnp.int32, (8, WINDOW), 0) + 1
        ).astype(floats).astype(halves)
        inner = contract_cols(pick, product_high) + contract_cols(pick, product_low)
        value_side = pltpu.roll(mixed_grad, WINDOW - HEAD_DIM, 1).astype(halves)
        queries = q_buf[m, c]
        query_heads = [keep(queries, places, h + 1) for h in range(3)]
        grad_heads = [keep(value_side, places, h) for h in range(3)]
        acc[...] = jnp.zeros_like(acc)
        key_weight = weights[c, :, K_AT : K_AT + WINDOW]
        value_weight = weights[c, :, V_AT : V_AT + WINDOW]

        def step(block, value_bias):
            keys = k_buf[m, c, block]
            values = v_buf[m, c, block]
            keys_t = keys.T
            hidden = mask[m, block].astype(floats)
            key_grad = jnp.zeros((rows, WINDOW), floats)
            value_grad = jnp.zeros((rows, WINDOW), floats)
            for h in range(3):
                p = jnp.exp(contract_cols(keys, query_heads[h]) + hidden - lse_ref[m, c, h : h + 1])
                prob_grad = contract_cols(values, grad_heads[h])
                score_grad = (p * (prob_grad - inner[h : h + 1])).astype(halves)
                value_grad = value_grad + jnp.dot(p.astype(halves), grad_heads[h], preferred_element_type=floats)
                key_grad = key_grad + jnp.dot(score_grad, query_heads[h], preferred_element_type=floats)
                at = pl.ds(h * HEAD_DIM, HEAD_DIM)
                acc[at, :] += jnp.dot(keys_t[(h + 1) * HEAD_DIM : (h + 2) * HEAD_DIM], score_grad, preferred_element_type=floats)
            key_low, value_low = key_grad.astype(halves), value_grad.astype(halves)
            k_buf[m, c, block] = key_low
            v_buf[m, c, block] = value_low
            spread[m, block] += contract_cols(key_low, key_weight) + contract_cols(value_low, value_weight)
            return value_bias + jnp.sum(value_low.astype(floats), 0, keepdims=True)

        value_bias = jnp.zeros((1, WINDOW), floats)
        for block in range(cols):
            value_bias = step(block, value_bias)
        query_low = (acc[...].T * HEAD_DIM ** -0.5).astype(halves)
        q_buf[m, c] = query_low
        vec_buf[0, 0, pl.ds(small + c, 1), 0:WINDOW] += jnp.sum(query_low.astype(floats), 0, keepdims=True)
        vec_buf[0, 0, pl.ds(small + c, 1), WINDOW : 2 * WINDOW] += value_bias
        back_ref[m] += contract_cols(query_low, weights[c, :, Q_AT : Q_AT + WINDOW])

    def send_tokens(m):
        back_ref[m] += spread[m, z]

        @pl.loop(0, cols)
        def _(block):
            tok_buf[m, block] = spread[m, block].astype(halves)

        start(*tokens[m])

    def weight_grads(c):
        strip = block_sum.shape[0]

        @pl.loop(0, model // strip)
        def _(part):
            base = pl.multiple_of(part * strip, strip)
            side = pl.ds(base, strip)
            block_sum[...] = jnp.zeros_like(block_sum)
            for m in range(micro):
                mine_at = pl.ds(pl.multiple_of((m * cols + z) * rows, rows), rows)
                block_sum[:, Q_AT : Q_AT + WINDOW] += jnp.dot(every_t[side, mine_at], q_buf[m, c], preferred_element_type=floats)
                all_at = pl.ds(m * cols * rows, cols * rows)
                block_sum[:, K_AT : K_AT + WINDOW] += jnp.dot(
                    every_t[side, all_at], k_buf[m, c].reshape(-1, WINDOW), preferred_element_type=floats)
                block_sum[:, V_AT : V_AT + WINDOW] += jnp.dot(
                    every_t[side, all_at], v_buf[m, c].reshape(-1, WINDOW), preferred_element_type=floats)
                block_sum[:, O_AT : O_AT + WINDOW] += jnp.dot(
                    grad_t[side, m * rows : (m + 1) * rows], mixed_buf[c, m], preferred_element_type=floats)
            for i in range(strip // (2 * rb)):
                ours = pl.ds(pl.multiple_of((2 * i + k) * rb, 16), rb)
                theirs = pl.ds(pl.multiple_of((2 * i + 1 - k) * rb, 16), rb)
                chip = part * (strip // (2 * rb)) + i
                mine_buf[0, c, chip // ny, lax.rem(chip, ny)] = block_sum[ours].astype(halves)
                stage_buf[c, chip // ny, lax.rem(chip, ny)] = block_sum[theirs].astype(halves)

    waited = []

    def attn_give(c):
        if not waited:
            pl.semaphore_wait(free_sem, 1)
            waited.append(c)
        post.send(("g", c), lambda: ("k", 1 - k, stage_buf.at[c], core_buf.at[0, c], None))

    def attn_add(c):
        post.wait(("g", c), "k", 1 - k, core_buf.at[0, c])

        @pl.loop(0, ns * ny)
        def _(n):
            at = (c, n // ny, lax.rem(n, ny))
            plus(mine_buf.at[(0, *at)], core_buf.at[(0, *at)])

    streams = ffn + attn
    added = set()

    def take_core(n):
        if n < 4:
            core(n)
            added.add(n)
            if added >= {0, 1} and n in (0, 1):
                pl.semaphore_signal(free_sem, 1, device_id=device("k", 1 - k), device_id_type=MESH)
        else:
            attn_add(n - 4)
        start(*streams[n].second)

    def take_second(n):
        finish(*streams[n].second)
        start(*streams[n].third)

    def take_third(n):
        finish(*streams[n].third)
        if n < 4:
            start(ffn_z[n])

    def along(line, e):
        for way in (1, -1):
            line.take(way, e)
            if e:
                line.forward(way, e)

    def take_tokens(m, h, e):
        line = tokens[m][h]
        if e == 0:
            at = half_of(h)

            def add(target, source):
                back_ref[m, at] += source[...].astype(floats)

            line.add = add
        along(line, e)

    def vectors(stage):
        if stage:
            vector_finish(stage - 1, "kyxz"[stage - 1], vec_buf.at[stage, 0] if stage < 4 else sums_ref)
        if stage < 4:
            vector_start(stage, "kyxz"[stage])

    def load():
        for copy in loads:
            copy.wait()

    act = {
        "L": load, "G": lambda n: give(n) if n < 4 else attn_give(n - 4), "A": take_core, "B": take_second, "C": take_third,
        "Z": lambda n, e: along(ffn_z[n], e), "S": send_tokens, "T": take_tokens, "Y": take_y, "V": vectors,
    }
    head, tail, order = split_plan([("U", "W", task[1], 0) if task[0] == "W" else task for task in BACKWARD_PLAN])
    kinds = [item[0] == "W" for item in order]
    heads = [item[1] if item[0] == "W" else item[0] for item in order]
    micros = [0 if item[0] == "W" else item[1] for item in order]
    act[head[0][0]](*head[0][1:])
    spread[...] = jnp.zeros_like(spread)
    for m in range(micro):
        grad_t[:, m * rows : (m + 1) * rows] = grad_ref[m].T
    for task in head[1:]:
        act[task[0]](*task[1:])

    @pl.loop(0, len(order))
    def _(step):
        c, m, kind = pick(step, heads), pick(step, micros), pick(step, [int(k_) for k_ in kinds])

        @pl.when(kind == 0)
        def _():
            unit(m, c)

        @pl.when(kind == 1)
        def _():
            @pl.when(step == kinds.index(True))
            def _():
                for copy in late:
                    copy.wait()

            weight_grads(c)

        for i, tasks in enumerate(tail[:-1]):
            if tasks:
                @pl.when(step == i)
                def _(tasks=tasks):
                    for task in tasks:
                        act[task[0]](*task[1:])

    for task in tail[-1]:
        act[task[0]](*task[1:])
    for j in range(3):
        block_ref[j] = mine_buf[j, z, x, y].astype(floats)
    post.close()


def backward(sizes, grad, share, first, turned, mixed, lse, q, k, v, mask, part, vectors):
    ns, nr, nc = sizes
    ny = nr // 2
    micro, rows, model = grad.shape
    w = part.shape[-1]
    rb = model // (ns * nr)
    halves, floats = jnp.bfloat16, jnp.float32
    reach = min(nc - 1, -(-(DOC_MOST - 1) // rows))
    streams = 4 + nc
    count = 4 + nc + 4 * (ny - 1 + ns - 1) * streams + 4 * 2 * (nc - 1) + 2 * nc * 2 + micro * 4 * reach + (1 + ny - 1 + ns - 1 + nc - 1)
    widest = max(ns, ny, nc, 2)
    ways = lambda n: 1 if n == 2 else 2
    vec_shape = (vectors.shape[0] + nc + -nc % 8, model)
    vmem = pl.BlockSpec(memory_space=pltpu.VMEM)
    anywhere = pl.BlockSpec(memory_space=pl.ANY)
    buf = lambda *shape, kind=halves: pltpu.VMEM(shape, kind)
    return pl.pallas_call(
        functools.partial(backward_kernel, sizes, micro),
        out_shape=[
            jax.ShapeDtypeStruct((micro, rows, model), floats),
            jax.ShapeDtypeStruct((3, rb, w), floats),
            jax.ShapeDtypeStruct(vec_shape, floats),
        ],
        in_specs=[vmem, anywhere, anywhere, anywhere, anywhere, vmem, anywhere, anywhere, anywhere, anywhere, anywhere, vmem],
        out_specs=[vmem] * 3,
        scratch_shapes=[
            buf(3, nc, ns, ny, rb, w), buf(2, nc, ns, ny, rb, w), buf(nc, ns, ny, rb, w),
            buf(3, ways(ns), max(ns - 1, 1), nc, ny, rb, w // 2), buf(3, ways(ny), max(ny - 1, 1), nc, ns, rb, w // 2),
            buf(3, ways(ny), max(ny - 1, 1), nc, rb, w // 2), buf(3, ways(ns), max(ns - 1, 1), nc, rb, w // 2),
            buf(3, 2, max(nc - 1, 1), rb, w), buf(micro, nc, rows, model), buf(micro, 2, max(reach, 1), rows, model),
            buf(4, 1 + widest, *vec_shape, kind=floats),
            buf(nc, model, w), buf(nc, micro, rows, WINDOW), buf(micro, nc, rows, WINDOW),
            buf(micro, nc, nc, rows, WINDOW), buf(micro, nc, nc, rows, WINDOW),
            buf(model, micro * nc * rows), buf(model, micro * rows),
            buf(micro, nc, rows, rows), buf(WINDOW, rows, kind=floats), buf(micro, nc, rows, model, kind=floats), buf(model // 2, w, kind=floats),
            pltpu.SemaphoreType.DMA((count,)), pltpu.SemaphoreType.DMA((count,)), pltpu.SemaphoreType.DMA((24,)), pltpu.SemaphoreType.REGULAR,
        ],
        compiler_params=pltpu.CompilerParams(collective_id=3, has_side_effects=True, vmem_limit_bytes=62 << 20),
        name="backward",
    )(grad, share, first, turned, mixed, lse, q, k, v, mask,
      part.reshape(2, nc, ns, ny, 2, rb, w), vectors)


def per_device_plain(sizes, inputs, segment_ids, query_weight, key_weight, value_weight, query_bias, value_bias,
               output_weight, output_bias, first_gain, first_shift, hidden_weight, hidden_bias, down_weight,
               down_bias, second_gain, second_shift, cotangent):
    floats, halves = jnp.float32, jnp.bfloat16
    cols = sizes[2]
    micro, _, rows, model = inputs.shape
    length = segment_ids.shape[-1]
    width = query_weight.shape[1]
    here = lax.axis_index("col")
    own = inputs[:, 0]
    shard = jnp.stack([
        jnp.concatenate([query_weight, key_weight, value_weight, output_weight.T], 1),
        hidden_weight,
        down_weight.T,
    ])
    biases = lax.all_gather(jnp.concatenate([query_bias, value_bias, hidden_bias]), "col", axis=0)
    everything, gathered = gather(sizes, own, shard)
    everything = everything.reshape(micro, length, model)
    attn_weights = gathered[0]
    wq, wk, wv, wot = (attn_weights[:, :, i * width : (i + 1) * width] for i in range(4))
    hidden_full, down_full = gathered[1], gathered[2]
    bq, bv, bh = biases[:, :width], biases[:, width : 2 * width], biases[:, 2 * width :]
    seg_all = segment_ids[:, 0]
    seg_own = lax.dynamic_slice_in_dim(seg_all, here * rows, rows, 1)
    first_key = jnp.sum((seg_all < seg_own[:, :1]).astype(jnp.int32), 1)
    last_key = jnp.sum((seg_all <= seg_own[:, -1:]).astype(jnp.int32), 1)
    bounds = jnp.stack([first_key // KEY_BLOCK, (last_key + KEY_BLOCK - 1) // KEY_BLOCK], 1)

    mixed, lse, q, k, v = attend(bounds, own, everything, wq, wk, wv, bq.astype(floats), bv.astype(floats), seg_own, seg_all)
    total = micro * rows
    flat = lambda a: a.reshape(total, -1)
    mixed_flat = mixed.reshape(cols, total, width)
    attn = sum(contract_cols(mixed_flat[c], wot[c]) for c in range(cols))
    first_sum = flat(own).astype(floats) + attn + output_bias.astype(floats)
    normal_one, scale_one = norm_parts(first_sum)
    gain_one = first_gain.astype(floats)
    normed = normal_one * gain_one + first_shift.astype(floats)
    normed_low = normed.astype(halves)
    ffn = 0
    activated, slopes = [], []
    for c in range(cols):
        hidden = jnp.dot(normed_low, hidden_full[c], preferred_element_type=floats) + bh[c].astype(floats)
        half_erf = 0.5 * lax.erf(hidden * 0.7071067811865476) + 0.5
        act = (hidden * half_erf).astype(halves)
        slope = half_erf + hidden * (jnp.exp(-0.5 * hidden * hidden) * 0.3989422804014327)
        activated.append(act)
        slopes.append(slope.astype(halves))
        ffn = ffn + contract_cols(act, down_full[c])
    second_sum = normed + ffn + down_bias.astype(floats)
    normal_two, scale_two = norm_parts(second_sum)
    gain_two = second_gain.astype(floats)
    outputs = (normal_two * gain_two + second_shift.astype(floats)).astype(halves)
    cot = flat(cotangent[:, 0]).astype(floats)
    second_grad = norm_back(cot * gain_two, normal_two, scale_two)
    ffn_grad = second_grad.astype(halves)
    hidden_grads, down_grads, hidden_bias_grads = [], [], []
    normed_grad = second_grad
    for c in range(cols):
        pre = (jnp.dot(ffn_grad, down_full[c], preferred_element_type=floats) * slopes[c].astype(floats)).astype(halves)
        hidden_grads.append(contract_rows(normed_low, pre).astype(halves))
        down_grads.append(contract_rows(ffn_grad, activated[c]).astype(halves))
        hidden_bias_grads.append(jnp.sum(pre.astype(floats), 0))
        normed_grad = normed_grad + contract_cols(pre, hidden_full[c])
    first_grad = norm_back(normed_grad * gain_one, normal_one, scale_one)
    attn_grad = first_grad.astype(halves)
    dq, dk, dv = attend_back(bounds, attn_grad.reshape(micro, rows, model), wot, mixed, lse, q, k, v, seg_own, seg_all)
    every_flat = everything.reshape(micro * length, model)
    attn_grads = []
    own_share = first_grad
    spread = 0
    for c in range(cols):
        dq_c, dk_c, dv_c = dq[c].reshape(total, width), dk[c].reshape(micro * length, width), dv[c].reshape(micro * length, width)
        attn_grads.append(jnp.concatenate([
            contract_rows(flat(own), dq_c), contract_rows(every_flat, dk_c), contract_rows(every_flat, dv_c),
            contract_rows(attn_grad, mixed_flat[c]),
        ], 1).astype(halves))
        own_share = own_share + contract_cols(dq_c, wq[c])
        spread = spread + contract_cols(dk_c, wk[c]) + contract_cols(dv_c, wv[c])
    bias_q = jnp.sum(dq.astype(floats), (1, 2)).reshape(-1)
    bias_v = jnp.sum(dv.astype(floats), (1, 2)).reshape(-1)
    vectors = jnp.concatenate([
        jnp.sum(first_grad, 0), jnp.sum(normed_grad * normal_one, 0), jnp.sum(normed_grad, 0), jnp.sum(second_grad, 0),
        jnp.sum(cot * normal_two, 0), jnp.sum(cot, 0), bias_q, bias_v, *hidden_bias_grads,
    ]).reshape(-1, model)
    partial = jnp.stack([jnp.stack(attn_grads), jnp.stack(hidden_grads), jnp.stack(down_grads)])
    input_grad, reduced, sums = reduce(sizes, own_share.reshape(micro, rows, model),
                                       spread.astype(halves).reshape(micro, cols, rows, model), partial, vectors)
    attn_block = reduced[0]
    piece = lambda i: attn_block[:, i * width : (i + 1) * width]
    mine = lambda vector, size: lax.dynamic_slice_in_dim(vector.reshape(-1), here * size, size, 0)
    return (
        outputs.reshape(micro, 1, rows, model), input_grad[:, None],
        piece(0), piece(1), piece(2), mine(sums[6], width), mine(sums[7], width), piece(3).T,
        sums[0], sums[1], sums[2], reduced[1], mine(sums[8:], hidden_bias.shape[0]), reduced[2].T,
        sums[3], sums[4], sums[5],
    )


def deliver_kernel(sizes, width, back_ref, block_ref, sums_ref, *outs):
    (input_grad, query, key, value, query_bias, value_bias, output, output_bias, first_gain, first_shift, hidden, hidden_bias, down,
     down_bias, second_gain, second_shift) = outs
    here = lax.axis_index("col")
    input_grad[...] = back_ref[...]
    for i, ref in enumerate((query, key, value)):
        ref[...] = block_ref[0, :, i * width : (i + 1) * width]
    output[...] = block_ref[0, :, 3 * width : 4 * width].T
    hidden[...] = block_ref[1]
    down[...] = block_ref[2].T
    for i, ref in enumerate((output_bias, first_gain, first_shift, down_bias, second_gain, second_shift)):
        ref[...] = sums_ref[i : i + 1].reshape(-1)
    hidden_bias[...] = sums_ref[pl.ds(8 + here, 1)].reshape(-1)
    heads_at = sums_ref.shape[0] - (sizes[2] + -sizes[2] % 8)
    row = sums_ref[pl.ds(heads_at + here, 1)]
    query_bias[...] = row[:, 0:width].reshape(-1)
    value_bias[...] = row[:, WINDOW : WINDOW + width].reshape(-1)


def deliver(sizes, width, back, blocks, sums):
    model = sums.shape[1]
    _, rb, w = blocks.shape
    vmem = pl.BlockSpec(memory_space=pltpu.VMEM)
    square, vector = (rb, width), (model,)
    shapes = [back.shape, square, square, square, (width,), (width,), (width, rb), vector, vector, vector, (rb, w), (w,), (w, rb),
              vector, vector, vector]
    return pl.pallas_call(
        functools.partial(deliver_kernel, sizes, width),
        out_shape=[jax.ShapeDtypeStruct(shape, jnp.float32) for shape in shapes],
        in_specs=[vmem] * 3,
        out_specs=[vmem] * len(shapes),
        compiler_params=pltpu.CompilerParams(vmem_limit_bytes=32 << 20),
        name="deliver",
    )(back, blocks, sums)


def per_device_fused(sizes, inputs, segment_ids, query_weight, key_weight, value_weight, query_bias, value_bias,
               output_weight, output_bias, first_gain, first_shift, hidden_weight, hidden_bias, down_weight,
               down_bias, second_gain, second_shift, cotangent):
    floats, halves = jnp.float32, jnp.bfloat16
    cols = sizes[2]
    micro, _, rows, model = inputs.shape
    length = segment_ids.shape[-1]
    width = query_weight.shape[1]
    here = lax.axis_index("col")
    own = inputs[:, 0]
    rest, first, turned, mask, biases, mixed, lse, q, k, v = forward(
        sizes, own, (query_weight, key_weight, value_weight, output_weight, hidden_weight, down_weight), hidden_bias, query_bias, value_bias, segment_ids)
    first = first.reshape(cols, model, 4 * width)
    total = micro * rows
    flat = lambda a: a.reshape(total, -1)
    outputs, first_grad, attn_grad, part, sums = middle(
        flat(own), mixed.reshape(cols, total, WINDOW), first, rest.reshape(2, cols, model, -1), biases,
        (output_bias, first_gain, first_shift, down_bias, second_gain, second_shift), flat(cotangent[:, 0]))
    parted = lambda a: a.reshape(micro, rows, model)
    input_grad, reduced, sums = backward(sizes, parted(attn_grad), parted(first_grad), first, turned, mixed, lse, q, k, v,
                                         mask, part, sums)
    grads = deliver(sizes, width, input_grad, reduced, sums)
    return (outputs.reshape(micro, 1, rows, model), grads[0][:, None], *grads[1:])


def per_device(sizes, inputs, segment_ids, query_weight, *rest):
    micro, _, rows, _ = inputs.shape
    fits = (query_weight.shape == (query_weight.shape[0] // 32 * 32, 3 * HEAD_DIM) and micro == 2 and sizes[2] == 4
            and DOC_MOST // 2 == rows)
    return (per_device_fused if fits else per_device_plain)(sizes, inputs, segment_ids, query_weight, *rest)


def solution(mesh):
    sizes = tuple(mesh.shape[name] for name in ("seq", "row", "col"))
    block, line = P(("seq", "row"), "col"), P("col", ("seq", "row"))
    tokens = P(None, ("seq", "row"), "col", None)
    placed = (tokens, P(None, ("seq", "row"), None), block, block, block, P("col"), P("col"), line, P(), P(), P(),
              block, P("col"), line, P(), P(), P(), tokens)
    given = (tokens, tokens, block, block, block, P("col"), P("col"), line, P(), P(), P(), block, P("col"), line,
             P(), P(), P())
    return jax.shard_map(functools.partial(per_device, sizes), mesh=mesh, in_specs=placed, out_specs=given, check_vma=False)
```

```python
import functools

import jax
import jax.numpy as jnp
from jax import lax
from jax.experimental import pallas as pl
from jax.experimental.pallas import tpu as pltpu
from jax.sharding import PartitionSpec as P

HEAD_DIM = 64
NORM_EPS = 1e-05
MASK_VALUE = -1000000000.0
DOC_MOST = 512
KEY_BLOCK = 256
MESH = pl.DeviceIdType.MESH


def contract_rows(left, right):
    return lax.dot_general(
        left, right, (((0,), (0,)), ((), ())), preferred_element_type=jnp.float32
    )


def contract_cols(left, right):
    return lax.dot_general(
        left, right, (((1,), (1,)), ((), ())), preferred_element_type=jnp.float32
    )


def norm_parts(summed):
    deviation = summed - jnp.mean(summed, -1, keepdims=True)
    scale = lax.rsqrt(jnp.mean(deviation * deviation, -1, keepdims=True) + NORM_EPS)
    return deviation * scale, scale


def norm_back(pull, normal, scale):
    return scale * (
        pull - jnp.mean(pull, -1, keepdims=True) - normal * jnp.mean(pull * normal, -1, keepdims=True)
    )

FORWARD_PLAN = (
    ("Zs", 1), ("Zs", 3), ("Zs", 0), ("Z", 1, 1), ("Z", 3, 1), ("Z", 1, 2), ("Z", 1, 3), ("Zs", 2), ("Z", 3, 2),
    ("Zs", 5), ("Z", 3, 3), ("Z", 0, 1), ("B", 1), ("Z", 0, 2), ("Z", 0, 3), ("Z", 2, 1), ("Zs", 4), ("Ts", 0),
    ("Z", 2, 2), ("Z", 5, 1), ("B", 3), ("Z", 5, 2), ("Ts", 1), ("B", 0), ("Z", 2, 3), ("Z", 4, 1), ("T", 0, 1),
    ("T", 0, 2), ("Z", 4, 2), ("T", 1, 1), ("Z", 5, 3), ("Ts", 2), ("Z", 4, 3), ("C", 1), ("C", 0), ("C", 3),
    ("B", 5), ("Ts", 3), ("K", 1), ("T", 1, 2), ("R", 0), ("K", 0), ("U", 0, 0), ("B", 2), ("T", 2, 1), ("U", 0, 1),
    ("C", 5), ("T", 3, 1), ("U", 0, 2), ("K", 3), ("B", 4), ("U", 0, 3), ("T", 2, 2), ("K", 5), ("C", 2), ("T", 3, 2),
    ("R", 1), ("U", 1, 0), ("U", 1, 1), ("C", 4), ("U", 1, 2), ("U", 1, 3), ("K", 2), ("K", 4),
)
BACKWARD_PLAN = (
    ("G", 1), ("G", 3), ("L",), ("U", 2, 0), ("A", 1), ("G", 0), ("U", 0, 0), ("A", 3), ("U", 1, 0), ("U", 3, 0),
    ("S", 0), ("G", 2), ("B", 1), ("A", 0), ("U", 0, 1), ("A", 2), ("B", 3), ("T", 0, 0, 1), ("C", 1), ("U", 2, 1),
    ("U", 1, 1), ("T", 0, 1, 1), ("U", 3, 1), ("S", 1), ("B", 2), ("W", 2), ("V", 0), ("G", 6), ("B", 0), ("W", 3),
    ("V", 1), ("Z", 1, 2), ("A", 6), ("G", 7), ("C", 3), ("W", 0), ("C", 2), ("G", 4), ("A", 7), ("T", 1, 1, 1),
    ("W", 1), ("Z", 3, 2), ("V", 2), ("G", 5), ("C", 0), ("A", 4), ("B", 7), ("V", 3), ("A", 5), ("Z", 1, 1),
    ("B", 4), ("Z", 2, 2), ("C", 7), ("T", 1, 0, 1), ("B", 6), ("Y", 3, 3), ("B", 5), ("T", 1, 1, 0), ("Z", 3, 1),
    ("C", 4), ("C", 6), ("Y", 0, 3), ("Z", 0, 2), ("Y", 2, 2), ("T", 0, 1, 0), ("C", 5), ("Y", 1, 2), ("V", 4),
    ("Y", 3, 2), ("Y", 0, 2), ("Z", 0, 1), ("Z", 1, 0), ("T", 1, 0, 0), ("Z", 2, 1), ("Z", 3, 0), ("Y", 3, 1),
    ("Y", 2, 1), ("Y", 1, 1), ("T", 0, 0, 0), ("Y", 0, 1), ("Z", 0, 0), ("Z", 2, 0), ("Y", 2, 0), ("Y", 3, 0),
    ("Y", 1, 0), ("Y", 0, 0),
)
def attend_kernel(bounds, own_ref, all_ref, wq_ref, wk_ref, wv_ref, bq_ref, bv_ref,
                  segq_ref, segk_ref, mixed_ref, lse_ref, q_ref, k_ref, v_ref, bias, acc, top, total):
    micro = pl.program_id(0)
    low, high = bounds[micro, 0], bounds[micro, 1]
    floats, halves = jnp.float32, jnp.bfloat16
    width = wq_ref.shape[-1]
    heads = width // HEAD_DIM
    rows = own_ref.shape[1]

    @pl.when(pl.program_id(1) == 0)
    def _():
        same = segk_ref[0] == segq_ref[0, 0:1]
        bias[...] = jnp.where(same, 0.0, MASK_VALUE)

    queries = jnp.dot(own_ref[0], wq_ref[0], preferred_element_type=floats) + bq_ref[0]
    queries = queries.astype(halves) * jnp.asarray(HEAD_DIM ** -0.5, halves)
    q_ref[0, 0] = queries
    lane = lax.broadcasted_iota(jnp.int32, (rows, width), 1) // HEAD_DIM
    query_heads = [jnp.where(lane == h, queries, jnp.zeros_like(queries)) for h in range(heads)]
    acc[...] = jnp.zeros_like(acc)
    total[...] = jnp.zeros_like(total)
    top[...] = jnp.full_like(top, 2 * MASK_VALUE)

    def step(block, carry):
        at = pl.ds(pl.multiple_of(block * KEY_BLOCK, KEY_BLOCK), KEY_BLOCK)
        x = all_ref[0, at, :]
        keys = jnp.dot(x, wk_ref[0], preferred_element_type=floats).astype(halves)
        k_ref[0, 0, at, :] = keys
        values = (jnp.dot(x, wv_ref[0], preferred_element_type=floats) + bv_ref[0]).astype(halves)
        v_ref[0, 0, at, :] = values
        values_t = values.T
        mask = bias[at, :]
        for h in range(heads):
            s = contract_cols(keys, query_heads[h]) + mask
            old = top[h : h + 1]
            new = jnp.maximum(old, jnp.max(s, 0, keepdims=True))
            p = jnp.exp(s - new)
            shrink = jnp.exp(old - new)
            top[h : h + 1] = new
            total[h : h + 1] = total[h : h + 1] * shrink + jnp.sum(p, 0, keepdims=True)
            part = pl.ds(h * HEAD_DIM, HEAD_DIM)
            acc[part, :] = acc[part, :] * shrink + jnp.dot(
                values_t[h * HEAD_DIM : (h + 1) * HEAD_DIM], p.astype(halves), preferred_element_type=floats
            )
        return carry

    lax.fori_loop(low, high, step, 0)
    for h in range(heads):
        part = pl.ds(h * HEAD_DIM, HEAD_DIM)
        acc[part, :] = acc[part, :] / total[h : h + 1]
    mixed_ref[0, 0] = acc[...].T.astype(halves)
    lse_ref[0, 0] = top[...] + jnp.log(jnp.maximum(total[...], 1e-30))


def attend(bounds, own, everything, wq, wk, wv, bq, bv, seg_own, seg_all):
    micro, rows, model = own.shape
    length = everything.shape[1]
    cols, _, width = wq.shape
    halves = jnp.bfloat16
    weight = pl.BlockSpec((1, model, width), lambda m, c, b: (c, 0, 0))
    per = lambda a, b_: pl.BlockSpec((1, 1, a, b_), lambda m, c, b: (c, m, 0, 0))
    spec = pltpu.PrefetchScalarGridSpec(
        num_scalar_prefetch=1,
        grid=(micro, cols),
        in_specs=[
            pl.BlockSpec((1, rows, model), lambda m, c, b: (m, 0, 0)),
            pl.BlockSpec((1, length, model), lambda m, c, b: (m, 0, 0)),
            weight, weight, weight,
            pl.BlockSpec((1, 1, width), lambda m, c, b: (c, 0, 0)),
            pl.BlockSpec((1, 1, width), lambda m, c, b: (c, 0, 0)),
            pl.BlockSpec((1, 1, rows), lambda m, c, b: (m, 0, 0)),
            pl.BlockSpec((1, length, 1), lambda m, c, b: (m, 0, 0)),
        ],
        out_specs=[per(rows, width), per(8, rows), per(rows, width), per(length, width), per(length, width)],
        scratch_shapes=[
            pltpu.VMEM((length, rows), jnp.float32),
            pltpu.VMEM((width, rows), jnp.float32),
            pltpu.VMEM((8, rows), jnp.float32),
            pltpu.VMEM((8, rows), jnp.float32),
        ],
    )
    shape = lambda a, b_, d=halves: jax.ShapeDtypeStruct((cols, micro, a, b_), d)
    return pl.pallas_call(
        attend_kernel,
        grid_spec=spec,
        out_shape=[shape(rows, width), shape(8, rows, jnp.float32), shape(rows, width), shape(length, width), shape(length, width)],
        compiler_params=pltpu.CompilerParams(vmem_limit_bytes=48 << 20),
        name="attend",
    )(bounds, own, everything, wq, wk, wv, bq[:, None], bv[:, None],
      seg_own[:, None], seg_all[:, :, None])


def attend_back_kernel(bounds, grad_ref, wot_ref, mixed_ref, lse_ref, q_ref, k_ref, v_ref, segq_ref, segk_ref,
                       dq_ref, dk_ref, dv_ref, bias, acc):
    micro = pl.program_id(0)
    low, high = bounds[micro, 0], bounds[micro, 1]
    floats, halves = jnp.float32, jnp.bfloat16
    rows, width = q_ref.shape[2:]
    heads = width // HEAD_DIM

    @pl.when(pl.program_id(1) == 0)
    def _():
        same = segk_ref[0] == segq_ref[0, 0:1]
        bias[...] = jnp.where(same, 0.0, MASK_VALUE)

    mixed_grad = jnp.dot(grad_ref[0], wot_ref[0], preferred_element_type=floats).astype(halves)
    product = mixed_grad.astype(floats) * mixed_ref[0, 0].astype(floats)
    product_high = product.astype(halves)
    product_low = (product - product_high.astype(floats)).astype(halves)
    pick = (
        lax.broadcasted_iota(jnp.int32, (8, width), 1) // HEAD_DIM == lax.broadcasted_iota(jnp.int32, (8, width), 0)
    ).astype(halves)
    inner = contract_cols(pick, product_high) + contract_cols(pick, product_low)
    lane = lax.broadcasted_iota(jnp.int32, (rows, width), 1) // HEAD_DIM
    queries = q_ref[0, 0]
    query_heads = [jnp.where(lane == h, queries, jnp.zeros_like(queries)) for h in range(heads)]
    grad_heads = [jnp.where(lane == h, mixed_grad, jnp.zeros_like(mixed_grad)) for h in range(heads)]
    acc[...] = jnp.zeros_like(acc)
    dk_ref[...] = jnp.zeros_like(dk_ref)
    dv_ref[...] = jnp.zeros_like(dv_ref)

    def step(block, carry):
        at = pl.ds(pl.multiple_of(block * KEY_BLOCK, KEY_BLOCK), KEY_BLOCK)
        keys = k_ref[0, 0, at, :]
        values = v_ref[0, 0, at, :]
        keys_t = keys.T
        mask = bias[at, :]
        key_grad = jnp.zeros((KEY_BLOCK, width), floats)
        value_grad = jnp.zeros((KEY_BLOCK, width), floats)
        for h in range(heads):
            s = contract_cols(keys, query_heads[h]) + mask
            p = jnp.exp(s - lse_ref[0, 0, h : h + 1])
            prob_grad = contract_cols(values, grad_heads[h])
            score_grad = (p * (prob_grad - inner[h : h + 1])).astype(halves)
            value_grad = value_grad + jnp.dot(p.astype(halves), grad_heads[h], preferred_element_type=floats)
            key_grad = key_grad + jnp.dot(score_grad, query_heads[h], preferred_element_type=floats)
            part = pl.ds(h * HEAD_DIM, HEAD_DIM)
            acc[part, :] += jnp.dot(keys_t[h * HEAD_DIM : (h + 1) * HEAD_DIM], score_grad, preferred_element_type=floats)
        dk_ref[0, 0, at, :] = key_grad.astype(halves)
        dv_ref[0, 0, at, :] = value_grad.astype(halves)
        return carry

    lax.fori_loop(low, high, step, 0)
    dq_ref[0, 0] = (acc[...].T * HEAD_DIM ** -0.5).astype(halves)


def attend_back(bounds, grad, wot, mixed, lse, q, k, v, seg_own, seg_all):
    micro, rows, model = grad.shape
    cols, _, length, width = k.shape
    halves = jnp.bfloat16
    per = lambda a, b_: pl.BlockSpec((1, 1, a, b_), lambda m, c, b: (c, m, 0, 0))
    spec = pltpu.PrefetchScalarGridSpec(
        num_scalar_prefetch=1,
        grid=(micro, cols),
        in_specs=[
            pl.BlockSpec((1, rows, model), lambda m, c, b: (m, 0, 0)),
            pl.BlockSpec((1, model, width), lambda m, c, b: (c, 0, 0)),
            per(rows, width), per(8, rows), per(rows, width), per(length, width), per(length, width),
            pl.BlockSpec((1, 1, rows), lambda m, c, b: (m, 0, 0)),
            pl.BlockSpec((1, length, 1), lambda m, c, b: (m, 0, 0)),
        ],
        out_specs=[per(rows, width), per(length, width), per(length, width)],
        scratch_shapes=[pltpu.VMEM((length, rows), jnp.float32), pltpu.VMEM((width, rows), jnp.float32)],
    )
    shape = lambda a, b_, d=halves: jax.ShapeDtypeStruct((cols, micro, a, b_), d)
    return pl.pallas_call(
        attend_back_kernel,
        grid_spec=spec,
        out_shape=[shape(rows, width), shape(length, width), shape(length, width)],
        compiler_params=pltpu.CompilerParams(vmem_limit_bytes=48 << 20),
        name="attend_back",
    )(bounds, grad, wot, mixed, lse, q, k, v, seg_own[:, None], seg_all[:, :, None])


def place(sizes):
    seq, row, col = (lax.axis_index(name) for name in ("seq", "row", "col"))
    lines = {"x": (seq, sizes[0]), "y": (row // 2, sizes[1] // 2), "k": (lax.rem(row, 2), 2), "z": (col, sizes[2])}

    def device(axis, index):
        if axis == "x":
            return (index, row, col)
        if axis == "y":
            return (seq, index * 2 + lax.rem(row, 2), col)
        if axis == "k":
            return (seq, row // 2 * 2 + index, col)
        return (seq, row, index)

    return lines, device


def greet(lines, device):
    barrier = pltpu.get_barrier_semaphore()
    count = 0
    for axis, (mine, size) in lines.items():
        for t in range(1, size):
            pl.semaphore_signal(barrier, inc=1, device_id=device(axis, lax.rem(mine + t, size)), device_id_type=MESH)
            count += 1
    pl.semaphore_wait(barrier, count)


class Post:
    def __init__(self, device, send_sems, recv_sems):
        self.device, self.send_sems, self.recv_sems = device, send_sems, recv_sems
        self.slots, self.sent = {}, []

    def slot(self, key):
        return self.slots.setdefault(key, len(self.slots))

    def copy(self, key, axis, index, source, target):
        n = self.slot(key)
        return pltpu.make_async_remote_copy(
            src_ref=source, dst_ref=target, send_sem=self.send_sems.at[n], recv_sem=self.recv_sems.at[n],
            device_id=self.device(axis, index), device_id_type=MESH,
        )

    def send(self, key, make):
        def run(act):
            axis, index, source, target, when = make()

            def go():
                act(self.copy(key, axis, index, source, target))

            if when is None:
                go()
            else:
                pl.when(when)(go)

        run(lambda copy: copy.start())
        self.sent.append(run)

    def wait(self, key, axis, index, target, when=None):
        def go():
            self.copy(key, axis, index, target, target).wait_recv()

        if when is None:
            go()
        else:
            pl.when(when)(go)

    def close(self):
        for run in self.sent:
            run(lambda copy: copy.wait_send())


def clip(index, size):
    return jnp.clip(index, 0, size - 1)


class LineGather:
    def __init__(self, post, name, axis, line, region, reach=None):
        self.post, self.name, self.axis, self.region = post, name, axis, region
        self.mine, self.size = line
        self.reach = min(self.size - 1, reach or self.size)

    def hop(self, way, t):
        mine, size = self.mine, self.size

        def make():
            origin, target = mine - way * t, mine + way
            ok = (origin >= 0) & (origin < size) & (target >= 0) & (target < size)
            here = self.region(clip(origin, size))
            return self.axis, clip(target, size), here, here, ok

        self.post.send((self.name, way, t + 1), make)

    def start(self):
        for way in (1, -1):
            if self.reach >= 1:
                self.hop(way, 0)

    def step(self, t):
        if t > self.reach:
            return
        for way in (1, -1):
            origin = self.mine - way * t
            ok = (origin >= 0) & (origin < self.size)
            self.post.wait((self.name, way, t), self.axis, clip(self.mine - way, self.size), self.region(clip(origin, self.size)), ok)
            if t < self.reach:
                self.hop(way, t)

    def finish(self, first=1):
        for t in range(first, self.reach + 1):
            self.step(t)


def gather_kernel(sizes, micro, own_ref, shard_ref, every_ref, full_ref, send_sems, recv_sems, local_sems):
    lines, device = place(sizes)
    (x, _), (y, _), (k, _), (z, cols) = (lines[a] for a in "xykz")
    half = shard_ref.shape[-1] // 2
    rows = own_ref.shape[1]
    reach = -(-(DOC_MOST - 1) // rows)
    parts = [pl.ds(p * half, half) for p in (0, 1)]
    local = [pltpu.make_async_copy(shard_ref.at[j], full_ref.at[j, z, x, y, k], local_sems.at[j]) for j in range(3)]
    local += [pltpu.make_async_copy(own_ref.at[m], every_ref.at[m, z], local_sems.at[3 + m]) for m in range(micro)]
    for copy in local:
        copy.start()
    greet(lines, device)
    post = Post(device, send_sems, recv_sems)
    for copy in local:
        copy.wait()
    zs = [LineGather(post, ("z", j), "z", lines["z"], lambda i, j=j: full_ref.at[j, i, x, y, k]) for j in range(3)]
    tokens = [LineGather(post, ("t", m), "z", lines["z"], lambda i, m=m: every_ref.at[m, i], reach) for m in range(micro)]
    second, third = {}, {}
    for j in range(3):
        second[j] = [
            LineGather(post, ("a", j), "y", lines["y"], lambda i, j=j: full_ref.at[j, :, x, i, k, :, parts[0]]),
            LineGather(post, ("b", j), "x", lines["x"], lambda i, j=j: full_ref.at[j, :, i, y, k, :, parts[1]]),
        ]
        third[j] = [
            LineGather(post, ("c", j), "x", lines["x"], lambda i, j=j: full_ref.at[j, :, i, :, k, :, parts[0]]),
            LineGather(post, ("d", j), "y", lines["y"], lambda i, j=j: full_ref.at[j, :, :, i, k, :, parts[1]]),
        ]

    def start(group):
        for line in group:
            line.start()

    def finish(group):
        for line in group:
            line.finish()

    def swap(j):
        plane = full_ref.at[j, :, :, :, k]
        post.send(("k", j), lambda: ("k", 1 - k, plane, plane, None))

    start(zs[:1])
    finish(zs[:1])
    start(second[0] + zs[1:2])
    finish(second[0])
    start(third[0])
    finish(zs[1:2])
    start(second[1] + tokens[:1])
    finish(third[0])
    swap(0)
    finish(second[1])
    start(third[1])
    finish(tokens[:1])
    start(zs[2:])
    finish(zs[2:])
    start(second[2] + tokens[1:])
    finish(third[1])
    swap(1)
    finish(second[2])
    start(third[2])
    finish(tokens[1:])
    finish(third[2])
    swap(2)
    for i in range(cols):
        far = (z - i > reach) | (i - z > reach)
        for m in range(micro):
            def fill(m=m, i=i):
                copy = pltpu.make_async_copy(own_ref.at[m], every_ref.at[m, i], local_sems.at[3 + m])
                copy.start()
                copy.wait()

            if i > reach or cols - 1 - i > reach:
                pl.when(far)(fill)
    for j in range(3):
        post.wait(("k", j), "k", 1 - k, full_ref.at[j, :, :, :, 1 - k])
    post.close()


def gather(sizes, own, shard):
    ns, nr, nc = sizes
    ny = nr // 2
    micro, rows, model = own.shape
    _, rb, w = shard.shape
    count = 3 * 2 * (nc - 1) + micro * 2 * (nc - 1) + 3 * (4 * (ny - 1) + 4 * (ns - 1) + 1)
    anywhere = pl.BlockSpec(memory_space=pl.ANY)
    every, full = pl.pallas_call(
        functools.partial(gather_kernel, sizes, micro),
        out_shape=[
            jax.ShapeDtypeStruct((micro, nc, rows, model), own.dtype),
            jax.ShapeDtypeStruct((3, nc, ns, ny, 2, rb, w), shard.dtype),
        ],
        in_specs=[pl.BlockSpec(memory_space=pltpu.VMEM)] * 2,
        out_specs=[anywhere] * 2,
        scratch_shapes=[pltpu.SemaphoreType.DMA((count,)), pltpu.SemaphoreType.DMA((count,)), pltpu.SemaphoreType.DMA((3 + micro,))],
        compiler_params=pltpu.CompilerParams(collective_id=0, has_side_effects=True),
        name="gather",
    )(own, shard)
    return every, full.reshape(3, nc, ns * nr * rb, w)


class LineReduce:
    def __init__(self, post, name, axis, line, region, inbox, add, reach=None):
        self.post, self.name, self.axis, self.region, self.inbox, self.add = post, name, axis, region, inbox, add
        self.mine, self.size = line
        self.reach = min(self.size - 1, reach or self.size)

    def arrived(self, way, e):
        behind, goal = self.mine - way, self.mine + way * e
        return (behind >= 0) & (behind < self.size) & (goal >= 0) & (goal < self.size)

    def take(self, way, e):
        ok = self.arrived(way, e)
        inbox = self.inbox(way, e)
        self.post.wait((self.name, way, e), self.axis, clip(self.mine - way, self.size), inbox, ok)

        @pl.when(ok)
        def _():
            self.add(self.region(clip(self.mine + way * e, self.size)), inbox)

    def forward(self, way, e):
        def make():
            goal = self.mine + way * e
            ok = (goal >= 0) & (goal < self.size)
            return self.axis, clip(self.mine + way, self.size), self.region(clip(goal, self.size)), self.inbox(way, e - 1), ok

        self.post.send((self.name, way, e - 1), make)

    def start(self):
        for way in (1, -1):
            if self.reach >= 1:
                self.forward(way, self.reach)

    def forward_from(self, nearest):
        for e in range(self.reach - 1, nearest - 1, -1):
            for way in (1, -1):
                self.take(way, e)
                self.forward(way, e)

    def finish(self, last=True):
        self.forward_from(1)
        if last:
            for way in (1, -1):
                if self.reach >= 1:
                    self.take(way, 0)


def reduce_to(post, name, axis, line, goal, e, region, inbox, add):
    mine, size = line
    for way in (1, -1):
        behind = mine - way
        arrives = (way * (goal - mine) == e) & (behind >= 0) & (behind < size)
        slot = inbox(way, min(e, size - 2))
        post.wait((name, way), axis, clip(behind, size), slot, arrives)

        @pl.when(arrives)
        def _():
            add(region, slot)

        def make(way=way):
            return axis, clip(mine + way, size), region, inbox(way, e - 1), way * (goal - mine) == e

        if e:
            post.send((name, way), make)


def reduce_kernel(sizes, micro, own_ref, spread_ref, part_ref, vec_ref, back_ref, block_ref, sums_ref,
                  mine_buf, core_buf, in_a, in_b, in_c, in_d, in_z, tok_buf, tok_in, vec_buf, send_sems, recv_sems, local_sems):
    floats, halves = jnp.float32, jnp.bfloat16
    lines, device = place(sizes)
    (x, ns), (y, ny), (k, _), (z, nc) = (lines[a] for a in "xykz")
    half = part_ref.shape[-1] // 2
    rows = own_ref.shape[1]
    reach = -(-(DOC_MOST - 1) // rows)
    parts = [pl.ds(p * half, half) for p in (0, 1)]
    local = [pltpu.make_async_copy(part_ref.at[j, :, :, :, k], mine_buf.at[j], local_sems.at[j]) for j in range(3)]
    local += [pltpu.make_async_copy(spread_ref.at[m], tok_buf.at[m], local_sems.at[3 + m]) for m in range(micro)]
    for copy in local:
        copy.start()
    greet(lines, device)
    post = Post(device, send_sems, recv_sems)
    for j in range(3):
        post.send(("k", j), lambda j=j: ("k", 1 - k, part_ref.at[j, :, :, :, 1 - k], core_buf.at[j], None))

    def plus(target, source):
        target[...] = (target[...].astype(floats) + source[...].astype(floats)).astype(halves)

    def plus_grid(target, source, first, second):
        @pl.loop(0, first * second)
        def _(n):
            plus(target.at[n // second, lax.rem(n, second)], source.at[n // second, lax.rem(n, second)])

    def plus_row(target, source, first):
        @pl.loop(0, first)
        def _(n):
            plus(target.at[n], source.at[n])

    vec_buf[0, 0] = vec_ref[...]

    def vector_start(stage, axis):
        mine, size = lines[axis]
        vec_buf[stage, 1 + mine] = vec_buf[stage, 0]
        for t in range(1, size):
            post.send(("v", stage, t), lambda t=t: (
                axis, lax.rem(mine + t, size), vec_buf.at[stage, 0], vec_buf.at[stage, 1 + mine], None))

    def vector_finish(stage, axis, out):
        mine, size = lines[axis]
        for t in range(1, size):
            origin = lax.rem(mine + size - t, size)
            post.wait(("v", stage, t), axis, origin, vec_buf.at[stage, 1 + origin])
        total = vec_buf[stage, 1]
        for i in range(1, size):
            total = total + vec_buf[stage, 1 + i]
        out[...] = total

    tokens = [
        LineReduce(post, ("t", m), "z", lines["z"], lambda i, m=m: tok_buf.at[m, i],
                   lambda way, e, m=m: tok_in.at[m, (1 - way) // 2, e], plus, reach)
        for m in range(micro)
    ]
    box = lambda way: (1 - way) // 2
    second, third, last = {}, {}, {}
    for j in range(3):
        second[j] = [
            LineReduce(post, ("a", j), "x", lines["x"], lambda i, j=j: mine_buf.at[j, :, i, :, :, parts[0]],
                       lambda way, e, j=j: in_a.at[j, box(way), e], lambda t, s: plus_grid(t, s, nc, ny)),
            LineReduce(post, ("b", j), "y", lines["y"], lambda i, j=j: mine_buf.at[j, :, :, i, :, parts[1]],
                       lambda way, e, j=j: in_b.at[j, box(way), e], lambda t, s: plus_grid(t, s, nc, ns)),
        ]
        third[j] = [
            LineReduce(post, ("c", j), "y", lines["y"], lambda i, j=j: mine_buf.at[j, :, x, i, :, parts[0]],
                       lambda way, e, j=j: in_c.at[j, box(way), e], lambda t, s: plus_row(t, s, nc)),
            LineReduce(post, ("d", j), "x", lines["x"], lambda i, j=j: mine_buf.at[j, :, i, y, :, parts[1]],
                       lambda way, e, j=j: in_d.at[j, box(way), e], lambda t, s: plus_row(t, s, nc)),
        ]
        last[j] = [
            LineReduce(post, ("z", j), "z", lines["z"], lambda i, j=j: mine_buf.at[j, i, x, y],
                       lambda way, e, j=j: in_z.at[j, box(way), e], plus)
        ]

    def start(group):
        for line in group:
            line.start()

    def finish(group):
        for line in group:
            line.finish()

    def core(j):
        local[j].wait()
        post.wait(("k", j), "k", 1 - k, core_buf.at[j])

        @pl.loop(0, nc * ns * ny)
        def _(n):
            at = (n // (ns * ny), lax.rem(n // ny, ns), lax.rem(n, ny))
            plus(mine_buf.at[(j, *at)], core_buf.at[(j, *at)])

    for m in range(micro):
        local[3 + m].wait()
    start(tokens)
    core(0)
    start(second[0])
    vector_start(0, "k")
    core(1)
    start(second[1])
    vector_finish(0, "k", vec_buf.at[1, 0])
    vector_start(1, "y")
    core(2)
    finish(second[0])
    start(third[0])
    start(second[2])
    vector_finish(1, "y", vec_buf.at[2, 0])
    vector_start(2, "x")
    finish(tokens)
    vector_finish(2, "x", vec_buf.at[3, 0])
    vector_start(3, "z")
    finish(second[1])
    start(third[1])
    finish(third[0])
    start(last[0])
    finish(second[2])
    start(third[2])
    finish(third[1])
    start(last[1])
    finish(last[0])
    finish(third[2])
    start(last[2])
    vector_finish(3, "z", sums_ref)
    for m in range(micro):
        back_ref[m] = own_ref[m] + tok_buf[m, z].astype(floats)
    finish(last[1])
    finish(last[2])
    for j in range(3):
        block_ref[j] = mine_buf[j, z, x, y].astype(floats)
    post.close()


def reduce(sizes, own_share, spread, partial, vectors):
    ns, nr, nc = sizes
    ny = nr // 2
    micro, rows, model = own_share.shape
    w = partial.shape[-1]
    rb = partial.shape[2] // (ns * nr)
    halves, floats = jnp.bfloat16, jnp.float32
    reach = min(nc - 1, -(-(DOC_MOST - 1) // rows))
    count = 3 + 2 * (ny - 1 + ns - 1) * 6 + 3 * 2 * (nc - 1) + micro * 2 * reach + (1 + ny - 1 + ns - 1 + nc - 1)
    widest = max(ns, ny, nc, 2)
    extra = -vectors.shape[0] % 8
    vectors = jnp.pad(vectors, ((0, extra), (0, 0)))
    vmem = pl.BlockSpec(memory_space=pltpu.VMEM)
    anywhere = pl.BlockSpec(memory_space=pl.ANY)
    back, blocks, sums = pl.pallas_call(
        functools.partial(reduce_kernel, sizes, micro),
        out_shape=[
            jax.ShapeDtypeStruct((micro, rows, model), floats),
            jax.ShapeDtypeStruct((3, rb, w), floats),
            jax.ShapeDtypeStruct(vectors.shape, floats),
        ],
        in_specs=[vmem, anywhere, anywhere, vmem],
        out_specs=[vmem] * 3,
        scratch_shapes=[
            pltpu.VMEM((3, nc, ns, ny, rb, w), halves),
            pltpu.VMEM((3, nc, ns, ny, rb, w), halves),
            pltpu.VMEM((3, 2, max(ns - 1, 1), nc, ny, rb, w // 2), halves),
            pltpu.VMEM((3, 2, max(ny - 1, 1), nc, ns, rb, w // 2), halves),
            pltpu.VMEM((3, 2, max(ny - 1, 1), nc, rb, w // 2), halves),
            pltpu.VMEM((3, 2, max(ns - 1, 1), nc, rb, w // 2), halves),
            pltpu.VMEM((3, 2, max(nc - 1, 1), rb, w), halves),
            pltpu.VMEM((micro, nc, rows, model), halves),
            pltpu.VMEM((micro, 2, max(reach, 1), rows, model), halves),
            pltpu.VMEM((4, 1 + widest, *vectors.shape), floats),
            pltpu.SemaphoreType.DMA((count,)),
            pltpu.SemaphoreType.DMA((count,)),
            pltpu.SemaphoreType.DMA((3 + micro,)),
        ],
        compiler_params=pltpu.CompilerParams(collective_id=1, has_side_effects=True, vmem_limit_bytes=60 << 20),
        name="reduce",
    )(own_share, spread, partial.reshape(3, nc, ns, ny, 2, rb, w), vectors)
    return back, blocks, sums


Q_AT, K_AT, V_AT, O_AT, WINDOW = 0, 128, 384, 512, 256


def plane(full_ref, c, at, size=WINDOW):
    value = full_ref[c, :, :, :, :, at : at + size]
    return value.reshape(-1, size)


def split_plan(plan):
    parts, order = [[]], []
    for task in plan:
        if task[0] == "U":
            order.append(task[1:])
            parts.append([])
        else:
            parts[-1].append(task)
    return parts[0], parts[1:], order


def pick(step, values):
    value = values[0]
    for i, other in enumerate(values[1:], 1):
        value = jnp.where(step == i, other, value)
    return value


def place_of(rows):
    return lax.broadcasted_iota(jnp.int32, (rows, WINDOW), 1) // HEAD_DIM


def keep(value, places, wanted):
    return jnp.where(places == wanted, value, jnp.zeros_like(value))


def forward_kernel(sizes, micro, own_ref, wq_ref, wk_ref, wv_ref, wo_ref, wh_ref, wd_ref, hidden_bias_ref, query_bias_ref, value_bias_ref, seg_ref,
                   rest_ref, first_ref, turned_ref, mask_ref, biases_ref, mixed_ref, lse_ref, q_ref, k_ref, v_ref,
                   weights, turned, bias_buf, mask, mixed_buf, lse_buf, q_buf, k_buf, v_buf, tokens_buf, acc, score_buf, prob_buf, values_t,
                   send_sems, recv_sems, local_sems, unit_sems):
    floats, halves = jnp.float32, jnp.bfloat16
    lines, device = place(sizes)
    (x, _), (y, _), (k, _), (z, cols) = (lines[a] for a in "xykz")
    half = wh_ref.shape[-1] // 2
    rows = own_ref.shape[1]
    reach = -(-(DOC_MOST - 1) // rows)
    parts = [pl.ds(p * half, half) for p in (0, 1)]
    low, high = jnp.maximum(z - reach, 0), jnp.minimum(z + reach + 1, cols)
    used = [0]

    class Local:
        def __init__(self, source, target):
            self.source, self.target, self.n = source, target, used[0]
            used[0] += 1
            self.describe().start()

        def describe(self):
            source = self.source() if callable(self.source) else self.source
            return pltpu.make_async_copy(source, self.target, local_sems.at[self.n])

        def wait(self):
            self.describe().wait()

    local = Local
    targets = [weights.at[0], rest_ref.at[0], rest_ref.at[1]]
    packed = [wq_ref[...], wk_ref[...], wv_ref[...], wo_ref[...].astype(floats).T.astype(halves)]
    weights[0, z, x, y, k] = jnp.concatenate(packed, 1)
    begin = [local(wh_ref, targets[1].at[z, x, y, k]), local(wd_ref, targets[2].at[z, x, y, k])]
    begin += [local(own_ref.at[m], tokens_buf.at[m, z]) for m in range(micro)]
    for i, ref in enumerate((hidden_bias_ref, query_bias_ref, value_bias_ref)):
        bias_buf[z, i : i + 1, 0 : ref.shape[0]] = ref[...].astype(floats).reshape(1, -1)
        if ref.shape[0] < WINDOW:
            bias_buf[z, i : i + 1, ref.shape[0] : WINDOW] = jnp.zeros((1, WINDOW - ref.shape[0]), floats)
    greet(lines, device)
    post = Post(device, send_sems, recv_sems)
    for copy in begin:
        copy.wait()
    tokens = [
        LineGather(post, ("t", q), "z", lines["z"],
                   lambda i, q=q: tokens_buf.at[q // 2, i, pl.ds(q % 2 * (rows // 2), rows // 2)], reach)
        for q in range(2 * micro)
    ]
    small = LineGather(post, "bias", "z", lines["z"], lambda i: bias_buf.at[i])
    rb = wh_ref.shape[0]
    zs, second, third = {}, {}, {}
    for n in range(6):
        j, r = n // 2, pl.ds(n % 2 * (rb // 2), rb // 2)
        zs[n] = LineGather(post, ("z", n), "z", lines["z"], lambda i, j=j, r=r: targets[j].at[i, x, y, k, r])
        second[n] = [
            LineGather(post, ("a", n), "y", lines["y"], lambda i, j=j, r=r: targets[j].at[:, x, i, k, r, parts[0]]),
            LineGather(post, ("b", n), "x", lines["x"], lambda i, j=j, r=r: targets[j].at[:, i, y, k, r, parts[1]]),
        ]
        third[n] = [
            LineGather(post, ("c", n), "x", lines["x"], lambda i, j=j, r=r: targets[j].at[:, i, :, k, r, parts[0]]),
            LineGather(post, ("d", n), "y", lines["y"], lambda i, j=j, r=r: targets[j].at[:, :, i, k, r, parts[1]]),
        ]

    def start(*group):
        for line in group:
            line.start()

    def finish(*group):
        for line in group:
            line.finish()

    def side(n, which):
        return targets[n // 2].at[:, :, :, which, pl.ds(n % 2 * (rb // 2), rb // 2)]

    def swap(n):
        post.send(("k", n), lambda: ("k", 1 - k, side(n, k), side(n, k), None))

    def swapped(n):
        post.wait(("k", n), "k", 1 - k, side(n, 1 - k))

    places = place_of(rows)

    def unit(m, c):
        queries = jnp.dot(own_ref[m], plane(weights.at[0], c, Q_AT), preferred_element_type=floats) + bias_buf[c, 1:2, 0:WINDOW]
        queries = pltpu.roll(queries.astype(halves).astype(floats) * HEAD_DIM ** -0.5, HEAD_DIM, 1)
        queries = jnp.where(places > 0, queries, 0.0).astype(halves)
        q_buf[m, c] = queries
        heads = jnp.concatenate([keep(queries, places, h + 1) for h in range(3)], 0)
        key_weight = plane(weights.at[0], c, K_AT)
        value_weight = plane(weights.at[0], c, V_AT)
        value_bias = bias_buf[c, 2:3, 0:WINDOW]
        largest = jnp.full((1, 3 * rows), 2 * MASK_VALUE, floats)
        for block in range(cols):
            rows_at = tokens_buf[m, block]
            keys = jnp.dot(rows_at, key_weight, preferred_element_type=floats).astype(halves)
            values = (jnp.dot(rows_at, value_weight, preferred_element_type=floats) + value_bias).astype(halves)
            k_buf[m, c, block] = keys
            v_buf[m, c, block] = values
            values_t[:, block * rows : (block + 1) * rows] = values.T
            hidden = mask[m, block].astype(floats)
            s = contract_cols(keys, heads) + jnp.concatenate([hidden] * 3, 1)
            score_buf[block] = s
            largest = jnp.maximum(largest, jnp.max(s, 0, keepdims=True))
        row_total = jnp.zeros((1, 3 * rows), floats)
        for block in range(cols):
            p = jnp.exp(score_buf[block] - largest)
            row_total = row_total + jnp.sum(p, 0, keepdims=True)
            prob_buf[block * rows : (block + 1) * rows] = p.astype(halves)
        log_total = largest + jnp.log(row_total)
        acc[0:HEAD_DIM] = jnp.zeros((HEAD_DIM, rows), floats)
        for h in range(3):
            lanes = slice(h * rows, (h + 1) * rows)
            product = jnp.dot(values_t[h * HEAD_DIM : (h + 1) * HEAD_DIM], prob_buf[:, lanes], preferred_element_type=floats)
            acc[pl.ds((h + 1) * HEAD_DIM, HEAD_DIM), :] = product / row_total[:, lanes]
            lse_buf[m, c, h : h + 1] = log_total[:, lanes]
        mixed_buf[c, m] = acc[...].T.astype(halves)

    def units(m, first, last):
        @pl.loop(first, last)
        def _(c):
            unit(m, c)

    def masks(m):
        asking = seg_ref[m, 0:1, pl.ds(pl.multiple_of(z * rows, 128), rows)].astype(floats)
        for block in range(cols):
            asked = seg_ref[m, 0:1, block * rows : (block + 1) * rows].astype(floats)
            same = jnp.broadcast_to(asked, (rows, rows)).T == asking
            mask[m, block] = jnp.where(same, 0.0, MASK_VALUE).astype(halves)

    done = []

    def turn(m):
        for block in range(cols):
            turned[:, (m * cols + block) * rows : (m * cols + block + 1) * rows] = tokens_buf[m, block].T
        if m == micro - 1:
            done.append(local(turned, turned_ref))

    keeps = ((q_buf, q_ref), (k_buf, k_ref), (v_buf, v_ref), (lse_buf, lse_ref))

    def take_z(n, t):
        zs[n].step(t)
        if n == 0:
            small.step(t)
        if t == cols - 1:
            start(*second[n])

    def take_second(n):
        finish(*second[n])
        start(*third[n])

    def take_third(n):
        finish(*third[n])
        swap(n)

    swaps = set()

    def take_core(n):
        swapped(n)
        swaps.add(n)
        if n < 2 and swaps >= {0, 1}:
            done.append(local(lambda: weights.at[0], first_ref))

    act = {
        "Zs": lambda n: zs[n].start(), "Z": take_z, "Ts": lambda q: tokens[q].start(), "T": lambda q, t: tokens[q].step(t),
        "B": take_second, "C": take_third, "K": take_core, "R": turn,
    }
    small.start()
    head, tail, order = split_plan(FORWARD_PLAN)
    act[head[0][0]](*head[0][1:])
    for block in range(cols):
        if block > reach or cols - 1 - block > reach:
            @pl.when(jnp.logical_not((low <= block) & (block < high)))
            def _(block=block):
                for m in range(micro):
                    tokens_buf[m, block] = jnp.zeros(own_ref.shape[1:], halves)
    for m in range(micro):
        masks(m)
    for task in head[1:]:
        act[task[0]](*task[1:])

    def leave(m, c, step, go):
        for i, (source, target) in enumerate(keeps):
            go(pltpu.make_async_copy(source.at[m, c], target.at[m, c], unit_sems.at[i, step]))

    @pl.loop(0, len(order))
    def _(step):
        m, c = pick(step, [m for m, _ in order]), pick(step, [c for _, c in order])
        unit(m, c)
        leave(m, c, step, lambda copy: copy.start())
        for i, tasks in enumerate(tail[:-1]):
            if tasks:
                @pl.when(step == i)
                def _(tasks=tasks):
                    for task in tasks:
                        act[task[0]](*task[1:])

    for source, target in ((bias_buf, biases_ref), (mixed_buf, mixed_ref), (mask, mask_ref)):
        done.append(local(source, target))
    for task in tail[-1]:
        act[task[0]](*task[1:])
    for step, (m, c) in enumerate(order):
        leave(m, c, step, lambda copy: copy.wait())
    for copy in done:
        copy.wait()
    post.close()


def forward(sizes, own, shards, hidden_bias, query_bias, value_bias, segments):
    ns, nr, nc = sizes
    ny = nr // 2
    micro, rows, model = own.shape
    rb, w = shards[4].shape
    halves, floats = own.dtype, jnp.float32
    reach = min(nc - 1, -(-(DOC_MOST - 1) // rows))
    count = (6 + 1) * 2 * (nc - 1) + micro * 4 * reach + 6 * (4 * (ny - 1) + 4 * (ns - 1) + 1)
    anywhere = pl.BlockSpec(memory_space=pl.ANY)
    vmem = pl.BlockSpec(memory_space=pltpu.VMEM)
    length = nc * rows
    arrays = [
        ((2, nc, ns, ny, 2, rb, w), halves), ((nc, ns, ny, 2, rb, w), halves), ((model, micro * length), halves), ((micro, nc, rows, rows), halves),
        ((nc, 8, model), floats), ((nc, micro, rows, WINDOW), halves), ((micro, nc, 8, rows), floats),
        ((micro, nc, rows, WINDOW), halves), ((micro, nc, nc, rows, WINDOW), halves), ((micro, nc, nc, rows, WINDOW), halves),
    ]
    shapes = [pltpu.VMEM(shape, kind) for shape, kind in arrays]
    return pl.pallas_call(
        functools.partial(forward_kernel, sizes, micro),
        out_shape=[jax.ShapeDtypeStruct(shape, kind) for shape, kind in arrays],
        in_specs=[vmem] * 11,
        out_specs=[anywhere] * len(arrays),
        scratch_shapes=[
            pltpu.VMEM((1, nc, ns, ny, 2, rb, w), halves),
            shapes[2], shapes[4], shapes[3], *shapes[5:],
            pltpu.VMEM((micro, nc, rows, model), halves), pltpu.VMEM((WINDOW, rows), floats), pltpu.VMEM((nc, rows, 3 * rows), floats), pltpu.VMEM((length, 3 * rows), halves), pltpu.VMEM((WINDOW, length), halves),
            pltpu.SemaphoreType.DMA((count,)), pltpu.SemaphoreType.DMA((count,)), pltpu.SemaphoreType.DMA((20,)), pltpu.SemaphoreType.DMA((4, micro * nc)),
        ],
        compiler_params=pltpu.CompilerParams(collective_id=2, has_side_effects=True, vmem_limit_bytes=60 << 20),
        name="forward",
    )(own, *shards, hidden_bias, query_bias, value_bias, segments)


def middle_kernel(cols, own_ref, mixed_ref, out_ref, hidden_ref, down_ref, bias_ref, *refs):
    vector_refs = refs[:6]
    (cot_ref, outputs_ref, first_grad_ref, attn_grad_ref, part_ref, sums_ref,
     normal, scale, normed, normed_low, normed_t, grad_low, grad_t, act_buf, slope_buf, total) = refs[6:]
    floats, halves = jnp.float32, jnp.bfloat16
    step = pl.program_id(0)
    rows, model = own_ref.shape
    chunks = [pl.ds(r * 256, 256) for r in range(rows // 256)]
    whole_rows = [pl.ds(0, rows)]
    bands = [pl.ds(n * 256, 256) for n in range(model // 256)]
    vector = lambda i: vector_refs[i][...].astype(floats).reshape(1, -1)

    @pl.when(step == 0)
    def _():
        sums_ref[...] = jnp.zeros_like(sums_ref)
        for chunk in chunks:
            first_sum = own_ref[chunk].astype(floats) + vector(0)
            for c in range(cols):
                first_sum = first_sum + contract_cols(mixed_ref[c, chunk], out_ref[c])
            normal_one, scale_one = norm_parts(first_sum)
            normal[chunk] = normal_one
            scale[chunk] = jnp.broadcast_to(scale_one, (256, 128))
            norm_one = normal_one * vector(1) + vector(2)
            total[chunk] = norm_one + vector(3)
            normed_low[chunk] = norm_one.astype(halves)
            normed_t[:, chunk] = norm_one.astype(halves).T

    @pl.when(step < cols)
    def _():
        for chunk in chunks:
            for band in bands:
                hidden = jnp.dot(normed_low[chunk], hidden_ref[0, 0, :, band], preferred_element_type=floats) + bias_ref[0, 0:1, band]
                half_erf = 0.5 * lax.erf(hidden * 0.7071067811865476) + 0.5
                act_buf[step, chunk, band] = (hidden * half_erf).astype(halves)
                slope_buf[step, chunk, band] = (half_erf + hidden * (jnp.exp(-0.5 * hidden * hidden) * 0.3989422804014327)).astype(halves)
        for chunk in chunks:
            for band in bands:
                total[chunk, band] += contract_cols(act_buf[step, chunk], down_ref[0, 0, band, :])

    @pl.when(step == cols - 1)
    def _():
        for chunk in chunks:
            normal_two, scale_two = norm_parts(total[chunk])
            outputs_ref[chunk] = (normal_two * vector(4) + vector(5)).astype(halves)
            cot = cot_ref[chunk].astype(floats)
            second_grad = norm_back(cot * vector(4), normal_two, scale_two)
            total[chunk] = second_grad
            grad_low[chunk] = second_grad.astype(halves)
            grad_t[:, chunk] = second_grad.astype(halves).T
            sums_ref[3:4] += jnp.sum(second_grad, 0, keepdims=True)
            sums_ref[4:5] += jnp.sum(cot * normal_two, 0, keepdims=True)
            sums_ref[5:6] += jnp.sum(cot, 0, keepdims=True)

    @pl.when(step >= cols)
    def _():
        c = step - cols
        bias_total = [jnp.zeros((1, 256), floats) for _ in bands]
        for chunk in chunks:
            for n, band in enumerate(bands):
                pre = jnp.dot(grad_low[chunk], down_ref[0, 0, :, band], preferred_element_type=floats)
                pre = (pre * slope_buf[c, chunk, band].astype(floats)).astype(halves)
                slope_buf[c, chunk, band] = pre
                bias_total[n] = bias_total[n] + jnp.sum(pre.astype(floats), 0, keepdims=True)
        for n, band in enumerate(bands):
            sums_ref[pl.ds(8 + c, 1), band] = bias_total[n]
        for band in bands:
            for side in [pl.ds(0, model)]:
                part_ref[0, 0, side, band] = jnp.dot(normed_t[side, :], slope_buf[c, :, band], preferred_element_type=floats).astype(halves)
                part_ref[1, 0, side, band] = jnp.dot(grad_t[side, :], act_buf[c, :, band], preferred_element_type=floats).astype(halves)
        for chunk in chunks:
            for band in bands:
                total[chunk, band] += contract_cols(slope_buf[c, chunk], hidden_ref[0, 0, band, :])

    @pl.when(step == 2 * cols - 1)
    def _():
        for chunk in chunks:
            normed_grad, normal_one = total[chunk], normal[chunk]
            first_grad = norm_back(normed_grad * vector(1), normal_one, scale[chunk, 0:1])
            first_grad_ref[chunk] = first_grad
            attn_grad_ref[chunk] = first_grad.astype(halves)
            sums_ref[0:1] += jnp.sum(first_grad, 0, keepdims=True)
            sums_ref[1:2] += jnp.sum(normed_grad * normal_one, 0, keepdims=True)
            sums_ref[2:3] += jnp.sum(normed_grad, 0, keepdims=True)


def middle(own, mixed, first, rest, biases, vectors, cot):
    rows, model = own.shape
    cols = first.shape[0]
    halves, floats = jnp.bfloat16, jnp.float32
    whole = lambda shape: pl.BlockSpec(shape, lambda i: (0,) * len(shape))
    wide = lambda kind: pltpu.VMEM((rows, model), kind)
    return pl.pallas_call(
        functools.partial(middle_kernel, cols),
        grid=(2 * cols,),
        in_specs=[
            whole((rows, model)), whole(mixed.shape),
            pl.BlockSpec((cols, model, WINDOW), lambda i: (0, 0, O_AT // WINDOW)),
            pl.BlockSpec((1, 1, model, rest.shape[-1]), lambda i: (0, lax.rem(i, cols), 0, 0)),
            pl.BlockSpec((1, 1, model, rest.shape[-1]), lambda i: (1, lax.rem(i, cols), 0, 0)),
            pl.BlockSpec((1, *biases.shape[1:]), lambda i: (lax.rem(i, cols), 0, 0)),
            *[whole((model,))] * 6, whole((rows, model)),
        ],
        out_specs=[
            whole((rows, model)), whole((rows, model)), whole((rows, model)),
            pl.BlockSpec((2, 1, model, rest.shape[-1]), lambda i: (0, jnp.maximum(i - cols, 0), 0, 0)),
            whole((8 + cols + -cols % 8, model)),
        ],
        out_shape=[
            jax.ShapeDtypeStruct((rows, model), halves), jax.ShapeDtypeStruct((rows, model), floats),
            jax.ShapeDtypeStruct((rows, model), halves), jax.ShapeDtypeStruct(rest.shape, halves),
            jax.ShapeDtypeStruct((8 + cols + -cols % 8, model), floats),
        ],
        scratch_shapes=[
            wide(floats), pltpu.VMEM((rows, 128), floats), wide(floats), wide(halves), pltpu.VMEM((model, rows), halves), wide(halves),
            pltpu.VMEM((model, rows), halves), pltpu.VMEM((cols, rows, rest.shape[-1]), halves),
            pltpu.VMEM((cols, rows, rest.shape[-1]), halves), wide(floats),
        ],
        compiler_params=pltpu.CompilerParams(vmem_limit_bytes=56 << 20),
        name="middle",
    )(own, mixed, first, rest, rest, biases, *vectors, cot)


class Inbox:
    def __init__(self, ref, size):
        self.ref, self.size = ref, size

    def __call__(self, way, e):
        return self.ref.at[0 if self.size == 2 else (1 - way) // 2, e]


def backward_kernel(sizes, micro, grad_ref, share_ref, first_ref, turned_ref, mixed_ref, lse_ref, q_ref, k_ref, v_ref,
                    mask_ref, part_ref, vec_ref,
                    back_ref, block_ref, sums_ref,
                    mine_buf, core_buf, stage_buf, in_a, in_b, in_c, in_d, in_z, tok_buf, tok_in, vec_buf,
                    weights, mixed_buf, q_buf, k_buf, v_buf, every_t, grad_t, mask, acc, spread, block_sum,
                    send_sems, recv_sems, local_sems, free_sem):
    floats, halves = jnp.float32, jnp.bfloat16
    lines, device = place(sizes)
    (x, ns), (y, ny), (k, _), (z, cols) = (lines[a] for a in "xykz")
    model = first_ref.shape[1]
    half = part_ref.shape[-1] // 2
    rb = part_ref.shape[-2]
    rows = grad_ref.shape[1]
    reach = -(-(DOC_MOST - 1) // rows)
    parts = [pl.ds(p * half, half) for p in (0, 1)]
    used = [0]

    def local(source, target):
        copy = pltpu.make_async_copy(source, target, local_sems.at[used[0]])
        used[0] += 1
        copy.start()
        return copy

    def rows_of(n):
        return pl.ds(n % 2 * (rb // 2), rb // 2)

    planes = [local(part_ref.at[n // 2, :, :, :, k, rows_of(n)], mine_buf.at[n // 2 + 1, :, :, :, rows_of(n)]) for n in range(4)]
    loads = [local(*pair) for pair in ((first_ref, weights), (mixed_ref, mixed_buf), (q_ref, q_buf), (share_ref, back_ref))]
    loads += [local(k_ref, k_buf), local(v_ref, v_buf)]
    loads += [local(mask_ref, mask)]
    late = [local(turned_ref, every_t)]
    greet(lines, device)
    post = Post(device, send_sems, recv_sems)

    def give(n):
        post.send(("k", n), lambda: (
            "k", 1 - k, part_ref.at[n // 2, :, :, :, 1 - k, rows_of(n)], core_buf.at[n // 2, :, :, :, rows_of(n)], None))

    def plus(target, source):
        target[...] = target[...] + source[...]

    def plus_grid(target, source, first, second):
        @pl.loop(0, first * second)
        def _(n):
            at = (n // second, lax.rem(n, second))
            plus(target.at[at], source.at[at])

    def plus_row(target, source, first):
        @pl.loop(0, first)
        def _(n):
            plus(target.at[n], source.at[n])

    class Stream:
        def __init__(self, name, j, begin, size, r):
            cs = pl.ds(begin, size)
            self.second = [
                LineReduce(post, (name, "a"), "x", lines["x"], lambda i: mine_buf.at[j, cs, i, :, r, parts[0]],
                           lambda way, e: Inbox(in_a.at[j], ns)(way, e).at[cs, :, r], lambda t, s: plus_grid(t, s, size, ny)),
                LineReduce(post, (name, "b"), "y", lines["y"], lambda i: mine_buf.at[j, cs, :, i, r, parts[1]],
                           lambda way, e: Inbox(in_b.at[j], ny)(way, e).at[cs, :, r], lambda t, s: plus_grid(t, s, size, ns)),
            ]
            self.third = [
                LineReduce(post, (name, "c"), "y", lines["y"], lambda i: mine_buf.at[j, cs, x, i, r, parts[0]],
                           lambda way, e: Inbox(in_c.at[j], ny)(way, e).at[cs, r], lambda t, s: plus_row(t, s, size)),
                LineReduce(post, (name, "d"), "x", lines["x"], lambda i: mine_buf.at[j, cs, i, y, r, parts[1]],
                           lambda way, e: Inbox(in_d.at[j], ns)(way, e).at[cs, r], lambda t, s: plus_row(t, s, size)),
            ]

    def line_z(name, j, r):
        return LineReduce(post, ("z", name), "z", lines["z"], lambda i: mine_buf.at[j, i, x, y, r],
                          lambda way, e: in_z.at[j, (1 - way) // 2, e, r], plus)

    ffn = [Stream(("s", n), n // 2 + 1, 0, cols, rows_of(n)) for n in range(4)]
    ffn_z = [line_z(n, n // 2 + 1, rows_of(n)) for n in range(4)]
    attn = [Stream(("u", c), 0, c, 1, pl.ds(0, rb)) for c in range(cols)]

    def take_y(c, e):
        reduce_to(post, ("y", c), "z", lines["z"], c, e, mine_buf.at[0, c, x, y], lambda way, e: in_z.at[0, (1 - way) // 2, e], plus)

    def half_of(h):
        return pl.ds(h * (rows // 2), rows // 2)

    def line_tokens(m, h):
        at = half_of(h)
        return LineReduce(post, ("t", m, h), "z", lines["z"], lambda i: tok_buf.at[m, i, at],
                          lambda way, e: tok_in.at[m, (1 - way) // 2, e, at], plus, reach)

    tokens = [[line_tokens(m, h) for h in range(2)] for m in range(micro)]

    def start(*group):
        for line in group:
            line.start()

    def finish(*group):
        for line in group:
            line.finish()

    def core(n):
        planes[n].wait()
        r = rows_of(n)
        post.wait(("k", n), "k", 1 - k, core_buf.at[n // 2, :, :, :, r])

        @pl.loop(0, cols * ns * ny)
        def _(i):
            at = (i // (ns * ny), lax.rem(i // ny, ns), lax.rem(i, ny), r)
            plus(mine_buf.at[(n // 2 + 1, *at)], core_buf.at[(n // 2, *at)])

    def vector_start(stage, axis):
        mine, size = lines[axis]
        vec_buf[stage, 1 + mine] = vec_buf[stage, 0]
        for t in range(1, size):
            post.send(("v", stage, t), lambda t=t: (
                axis, lax.rem(mine + t, size), vec_buf.at[stage, 0], vec_buf.at[stage, 1 + mine], None))

    def vector_finish(stage, axis, out):
        mine, size = lines[axis]
        for t in range(1, size):
            origin = lax.rem(mine + size - t, size)
            post.wait(("v", stage, t), axis, origin, vec_buf.at[stage, 1 + origin])
        total = vec_buf[stage, 1]
        for i in range(1, size):
            total = total + vec_buf[stage, 1 + i]
        out[...] = total

    places = place_of(rows)
    small = vec_ref.shape[0]
    vec_buf[0, 0] = jnp.zeros_like(vec_buf[0, 0])
    vec_buf[0, 0, 0:small] = vec_ref[...]

    def unit(m, c):
        mixed_grad = jnp.dot(grad_ref[m], weights[c, :, O_AT : O_AT + WINDOW], preferred_element_type=floats).astype(halves)
        mixed_grad = jnp.where(places > 0, mixed_grad.astype(floats), 0.0)
        product = mixed_grad * mixed_buf[c, m].astype(floats)
        product_high = product.astype(halves)
        product_low = (product - product_high.astype(floats)).astype(halves)
        pick = (
            lax.broadcasted_iota(jnp.int32, (8, WINDOW), 1) // HEAD_DIM == lax.broadcasted_iota(jnp.int32, (8, WINDOW), 0) + 1
        ).astype(floats).astype(halves)
        inner = contract_cols(pick, product_high) + contract_cols(pick, product_low)
        value_side = pltpu.roll(mixed_grad, WINDOW - HEAD_DIM, 1).astype(halves)
        queries = q_buf[m, c]
        query_heads = jnp.concatenate([keep(queries, places, h + 1) for h in range(3)], 0)
        grad_heads = jnp.concatenate([keep(value_side, places, h) for h in range(3)], 0)
        side_by_side = lambda ref_rows: jnp.concatenate([ref_rows(h) for h in range(3)], 1)
        log_total = side_by_side(lambda h: lse_ref[m, c, h : h + 1])
        inner_row = side_by_side(lambda h: inner[h : h + 1])
        acc[...] = jnp.zeros_like(acc)
        key_weight = weights[c, :, K_AT : K_AT + WINDOW]
        value_weight = weights[c, :, V_AT : V_AT + WINDOW]

        def step(block, value_bias):
            keys = k_buf[m, c, block]
            values = v_buf[m, c, block]
            keys_t = keys.T
            hidden = mask[m, block].astype(floats)
            hidden = jnp.concatenate([hidden] * 3, 1)
            p = jnp.exp(contract_cols(keys, query_heads) + hidden - log_total)
            prob_grad = contract_cols(values, grad_heads)
            score_grad = (p * (prob_grad - inner_row)).astype(halves)
            value_grad = jnp.dot(p.astype(halves), grad_heads, preferred_element_type=floats)
            key_grad = jnp.dot(score_grad, query_heads, preferred_element_type=floats)
            for h in range(3):
                acc[pl.ds(h * HEAD_DIM, HEAD_DIM), :] += jnp.dot(
                    keys_t[(h + 1) * HEAD_DIM : (h + 2) * HEAD_DIM], score_grad[:, h * rows : (h + 1) * rows], preferred_element_type=floats)
            key_low, value_low = key_grad.astype(halves), value_grad.astype(halves)
            k_buf[m, c, block] = key_low
            v_buf[m, c, block] = value_low
            spread[m, block] += contract_cols(key_low, key_weight) + contract_cols(value_low, value_weight)
            return value_bias + jnp.sum(value_low.astype(floats), 0, keepdims=True)

        value_bias = jnp.zeros((1, WINDOW), floats)
        for block in range(cols):
            value_bias = step(block, value_bias)
        query_low = (acc[...].T * HEAD_DIM ** -0.5).astype(halves)
        q_buf[m, c] = query_low
        vec_buf[0, 0, pl.ds(small + c, 1), 0:WINDOW] += jnp.sum(query_low.astype(floats), 0, keepdims=True)
        vec_buf[0, 0, pl.ds(small + c, 1), WINDOW : 2 * WINDOW] += value_bias
        back_ref[m] += contract_cols(query_low, weights[c, :, Q_AT : Q_AT + WINDOW])

    def send_tokens(m):
        back_ref[m] += spread[m, z]

        @pl.loop(0, cols)
        def _(block):
            tok_buf[m, block] = spread[m, block].astype(halves)

        start(*tokens[m])

    def weight_grads(c):
        strip = block_sum.shape[0]

        @pl.loop(0, model // strip)
        def _(part):
            base = pl.multiple_of(part * strip, strip)
            side = pl.ds(base, strip)
            block_sum[...] = jnp.zeros_like(block_sum)
            for m in range(micro):
                mine_at = pl.ds(pl.multiple_of((m * cols + z) * rows, rows), rows)
                block_sum[:, Q_AT : Q_AT + WINDOW] += jnp.dot(every_t[side, mine_at], q_buf[m, c], preferred_element_type=floats)
                all_at = pl.ds(m * cols * rows, cols * rows)
                block_sum[:, K_AT : K_AT + WINDOW] += jnp.dot(
                    every_t[side, all_at], k_buf[m, c].reshape(-1, WINDOW), preferred_element_type=floats)
                block_sum[:, V_AT : V_AT + WINDOW] += jnp.dot(
                    every_t[side, all_at], v_buf[m, c].reshape(-1, WINDOW), preferred_element_type=floats)
                block_sum[:, O_AT : O_AT + WINDOW] += jnp.dot(
                    grad_t[side, m * rows : (m + 1) * rows], mixed_buf[c, m], preferred_element_type=floats)
            for i in range(strip // (2 * rb)):
                ours = pl.ds(pl.multiple_of((2 * i + k) * rb, 16), rb)
                theirs = pl.ds(pl.multiple_of((2 * i + 1 - k) * rb, 16), rb)
                chip = part * (strip // (2 * rb)) + i
                mine_buf[0, c, chip // ny, lax.rem(chip, ny)] = block_sum[ours].astype(halves)
                stage_buf[c, chip // ny, lax.rem(chip, ny)] = block_sum[theirs].astype(halves)

    waited = []

    def attn_give(c):
        if not waited:
            pl.semaphore_wait(free_sem, 1)
            waited.append(c)
        post.send(("g", c), lambda: ("k", 1 - k, stage_buf.at[c], core_buf.at[0, c], None))

    def attn_add(c):
        post.wait(("g", c), "k", 1 - k, core_buf.at[0, c])

        @pl.loop(0, ns * ny)
        def _(n):
            at = (c, n // ny, lax.rem(n, ny))
            plus(mine_buf.at[(0, *at)], core_buf.at[(0, *at)])

    streams = ffn + attn
    added = set()

    def take_core(n):
        if n < 4:
            core(n)
            added.add(n)
            if added >= {0, 1} and n in (0, 1):
                pl.semaphore_signal(free_sem, 1, device_id=device("k", 1 - k), device_id_type=MESH)
        else:
            attn_add(n - 4)
        start(*streams[n].second)

    def take_second(n):
        finish(*streams[n].second)
        start(*streams[n].third)

    def take_third(n):
        finish(*streams[n].third)
        if n < 4:
            start(ffn_z[n])

    def along(line, e):
        for way in (1, -1):
            line.take(way, e)
            if e:
                line.forward(way, e)

    def take_tokens(m, h, e):
        line = tokens[m][h]
        if e == 0:
            at = half_of(h)

            def add(target, source):
                back_ref[m, at] += source[...].astype(floats)

            line.add = add
        along(line, e)

    def vectors(stage):
        if stage:
            vector_finish(stage - 1, "kyxz"[stage - 1], vec_buf.at[stage, 0] if stage < 4 else sums_ref)
        if stage < 4:
            vector_start(stage, "kyxz"[stage])

    def load():
        for copy in loads:
            copy.wait()

    act = {
        "L": load, "G": lambda n: give(n) if n < 4 else attn_give(n - 4), "A": take_core, "B": take_second, "C": take_third,
        "Z": lambda n, e: along(ffn_z[n], e), "S": send_tokens, "T": take_tokens, "Y": take_y, "V": vectors,
    }
    head, tail, order = split_plan([("U", "W", task[1], 0) if task[0] == "W" else task for task in BACKWARD_PLAN])
    kinds = [item[0] == "W" for item in order]
    heads = [item[1] if item[0] == "W" else item[0] for item in order]
    micros = [0 if item[0] == "W" else item[1] for item in order]
    act[head[0][0]](*head[0][1:])
    spread[...] = jnp.zeros_like(spread)
    for m in range(micro):
        grad_t[:, m * rows : (m + 1) * rows] = grad_ref[m].T
    for task in head[1:]:
        act[task[0]](*task[1:])

    @pl.loop(0, len(order))
    def _(step):
        c, m, kind = pick(step, heads), pick(step, micros), pick(step, [int(k_) for k_ in kinds])

        @pl.when(kind == 0)
        def _():
            unit(m, c)

        @pl.when(kind == 1)
        def _():
            @pl.when(step == kinds.index(True))
            def _():
                for copy in late:
                    copy.wait()

            weight_grads(c)

        for i, tasks in enumerate(tail[:-1]):
            if tasks:
                @pl.when(step == i)
                def _(tasks=tasks):
                    for task in tasks:
                        act[task[0]](*task[1:])

    for task in tail[-1]:
        act[task[0]](*task[1:])
    for j in range(3):
        block_ref[j] = mine_buf[j, z, x, y].astype(floats)
    post.close()


def backward(sizes, grad, share, first, turned, mixed, lse, q, k, v, mask, part, vectors):
    ns, nr, nc = sizes
    ny = nr // 2
    micro, rows, model = grad.shape
    w = part.shape[-1]
    rb = model // (ns * nr)
    halves, floats = jnp.bfloat16, jnp.float32
    reach = min(nc - 1, -(-(DOC_MOST - 1) // rows))
    streams = 4 + nc
    count = 4 + nc + 4 * (ny - 1 + ns - 1) * streams + 4 * 2 * (nc - 1) + 2 * nc * 2 + micro * 4 * reach + (1 + ny - 1 + ns - 1 + nc - 1)
    widest = max(ns, ny, nc, 2)
    ways = lambda n: 1 if n == 2 else 2
    vec_shape = (vectors.shape[0] + nc + -nc % 8, model)
    vmem = pl.BlockSpec(memory_space=pltpu.VMEM)
    anywhere = pl.BlockSpec(memory_space=pl.ANY)
    buf = lambda *shape, kind=halves: pltpu.VMEM(shape, kind)
    return pl.pallas_call(
        functools.partial(backward_kernel, sizes, micro),
        out_shape=[
            jax.ShapeDtypeStruct((micro, rows, model), floats),
            jax.ShapeDtypeStruct((3, rb, w), floats),
            jax.ShapeDtypeStruct(vec_shape, floats),
        ],
        in_specs=[vmem, anywhere, anywhere, anywhere, anywhere, vmem, anywhere, anywhere, anywhere, anywhere, anywhere, vmem],
        out_specs=[vmem] * 3,
        scratch_shapes=[
            buf(3, nc, ns, ny, rb, w), buf(2, nc, ns, ny, rb, w), buf(nc, ns, ny, rb, w),
            buf(3, ways(ns), max(ns - 1, 1), nc, ny, rb, w // 2), buf(3, ways(ny), max(ny - 1, 1), nc, ns, rb, w // 2),
            buf(3, ways(ny), max(ny - 1, 1), nc, rb, w // 2), buf(3, ways(ns), max(ns - 1, 1), nc, rb, w // 2),
            buf(3, 2, max(nc - 1, 1), rb, w), buf(micro, nc, rows, model), buf(micro, 2, max(reach, 1), rows, model),
            buf(4, 1 + widest, *vec_shape, kind=floats),
            buf(nc, model, w), buf(nc, micro, rows, WINDOW), buf(micro, nc, rows, WINDOW),
            buf(micro, nc, nc, rows, WINDOW), buf(micro, nc, nc, rows, WINDOW),
            buf(model, micro * nc * rows), buf(model, micro * rows),
            buf(micro, nc, rows, rows), buf(WINDOW, rows, kind=floats), buf(micro, nc, rows, model, kind=floats), buf(model // 2, w, kind=floats),
            pltpu.SemaphoreType.DMA((count,)), pltpu.SemaphoreType.DMA((count,)), pltpu.SemaphoreType.DMA((24,)), pltpu.SemaphoreType.REGULAR,
        ],
        compiler_params=pltpu.CompilerParams(collective_id=3, has_side_effects=True, vmem_limit_bytes=62 << 20),
        name="backward",
    )(grad, share, first, turned, mixed, lse, q, k, v, mask,
      part.reshape(2, nc, ns, ny, 2, rb, w), vectors)


def per_device_plain(sizes, inputs, segment_ids, query_weight, key_weight, value_weight, query_bias, value_bias,
               output_weight, output_bias, first_gain, first_shift, hidden_weight, hidden_bias, down_weight,
               down_bias, second_gain, second_shift, cotangent):
    floats, halves = jnp.float32, jnp.bfloat16
    cols = sizes[2]
    micro, _, rows, model = inputs.shape
    length = segment_ids.shape[-1]
    width = query_weight.shape[1]
    here = lax.axis_index("col")
    own = inputs[:, 0]
    shard = jnp.stack([
        jnp.concatenate([query_weight, key_weight, value_weight, output_weight.T], 1),
        hidden_weight,
        down_weight.T,
    ])
    biases = lax.all_gather(jnp.concatenate([query_bias, value_bias, hidden_bias]), "col", axis=0)
    everything, gathered = gather(sizes, own, shard)
    everything = everything.reshape(micro, length, model)
    attn_weights = gathered[0]
    wq, wk, wv, wot = (attn_weights[:, :, i * width : (i + 1) * width] for i in range(4))
    hidden_full, down_full = gathered[1], gathered[2]
    bq, bv, bh = biases[:, :width], biases[:, width : 2 * width], biases[:, 2 * width :]
    seg_all = segment_ids[:, 0]
    seg_own = lax.dynamic_slice_in_dim(seg_all, here * rows, rows, 1)
    first_key = jnp.sum((seg_all < seg_own[:, :1]).astype(jnp.int32), 1)
    last_key = jnp.sum((seg_all <= seg_own[:, -1:]).astype(jnp.int32), 1)
    bounds = jnp.stack([first_key // KEY_BLOCK, (last_key + KEY_BLOCK - 1) // KEY_BLOCK], 1)

    mixed, lse, q, k, v = attend(bounds, own, everything, wq, wk, wv, bq.astype(floats), bv.astype(floats), seg_own, seg_all)
    total = micro * rows
    flat = lambda a: a.reshape(total, -1)
    mixed_flat = mixed.reshape(cols, total, width)
    attn = sum(contract_cols(mixed_flat[c], wot[c]) for c in range(cols))
    first_sum = flat(own).astype(floats) + attn + output_bias.astype(floats)
    normal_one, scale_one = norm_parts(first_sum)
    gain_one = first_gain.astype(floats)
    normed = normal_one * gain_one + first_shift.astype(floats)
    normed_low = normed.astype(halves)
    ffn = 0
    activated, slopes = [], []
    for c in range(cols):
        hidden = jnp.dot(normed_low, hidden_full[c], preferred_element_type=floats) + bh[c].astype(floats)
        half_erf = 0.5 * lax.erf(hidden * 0.7071067811865476) + 0.5
        act = (hidden * half_erf).astype(halves)
        slope = half_erf + hidden * (jnp.exp(-0.5 * hidden * hidden) * 0.3989422804014327)
        activated.append(act)
        slopes.append(slope.astype(halves))
        ffn = ffn + contract_cols(act, down_full[c])
    second_sum = normed + ffn + down_bias.astype(floats)
    normal_two, scale_two = norm_parts(second_sum)
    gain_two = second_gain.astype(floats)
    outputs = (normal_two * gain_two + second_shift.astype(floats)).astype(halves)
    cot = flat(cotangent[:, 0]).astype(floats)
    second_grad = norm_back(cot * gain_two, normal_two, scale_two)
    ffn_grad = second_grad.astype(halves)
    hidden_grads, down_grads, hidden_bias_grads = [], [], []
    normed_grad = second_grad
    for c in range(cols):
        pre = (jnp.dot(ffn_grad, down_full[c], preferred_element_type=floats) * slopes[c].astype(floats)).astype(halves)
        hidden_grads.append(contract_rows(normed_low, pre).astype(halves))
        down_grads.append(contract_rows(ffn_grad, activated[c]).astype(halves))
        hidden_bias_grads.append(jnp.sum(pre.astype(floats), 0))
        normed_grad = normed_grad + contract_cols(pre, hidden_full[c])
    first_grad = norm_back(normed_grad * gain_one, normal_one, scale_one)
    attn_grad = first_grad.astype(halves)
    dq, dk, dv = attend_back(bounds, attn_grad.reshape(micro, rows, model), wot, mixed, lse, q, k, v, seg_own, seg_all)
    every_flat = everything.reshape(micro * length, model)
    attn_grads = []
    own_share = first_grad
    spread = 0
    for c in range(cols):
        dq_c, dk_c, dv_c = dq[c].reshape(total, width), dk[c].reshape(micro * length, width), dv[c].reshape(micro * length, width)
        attn_grads.append(jnp.concatenate([
            contract_rows(flat(own), dq_c), contract_rows(every_flat, dk_c), contract_rows(every_flat, dv_c),
            contract_rows(attn_grad, mixed_flat[c]),
        ], 1).astype(halves))
        own_share = own_share + contract_cols(dq_c, wq[c])
        spread = spread + contract_cols(dk_c, wk[c]) + contract_cols(dv_c, wv[c])
    bias_q = jnp.sum(dq.astype(floats), (1, 2)).reshape(-1)
    bias_v = jnp.sum(dv.astype(floats), (1, 2)).reshape(-1)
    vectors = jnp.concatenate([
        jnp.sum(first_grad, 0), jnp.sum(normed_grad * normal_one, 0), jnp.sum(normed_grad, 0), jnp.sum(second_grad, 0),
        jnp.sum(cot * normal_two, 0), jnp.sum(cot, 0), bias_q, bias_v, *hidden_bias_grads,
    ]).reshape(-1, model)
    partial = jnp.stack([jnp.stack(attn_grads), jnp.stack(hidden_grads), jnp.stack(down_grads)])
    input_grad, reduced, sums = reduce(sizes, own_share.reshape(micro, rows, model),
                                       spread.astype(halves).reshape(micro, cols, rows, model), partial, vectors)
    attn_block = reduced[0]
    piece = lambda i: attn_block[:, i * width : (i + 1) * width]
    mine = lambda vector, size: lax.dynamic_slice_in_dim(vector.reshape(-1), here * size, size, 0)
    return (
        outputs.reshape(micro, 1, rows, model), input_grad[:, None],
        piece(0), piece(1), piece(2), mine(sums[6], width), mine(sums[7], width), piece(3).T,
        sums[0], sums[1], sums[2], reduced[1], mine(sums[8:], hidden_bias.shape[0]), reduced[2].T,
        sums[3], sums[4], sums[5],
    )


def deliver_kernel(sizes, width, back_hbm, block_hbm, sums_hbm, *refs):
    *outs, back_ref, block_ref, sums_ref, sems = refs
    copies = [
        pltpu.make_async_copy(source, target, sems.at[i])
        for i, (source, target) in enumerate(((block_hbm, block_ref), (sums_hbm, sums_ref), (back_hbm, back_ref)))
    ]
    for copy in copies:
        copy.start()
    (input_grad, query, key, value, query_bias, value_bias, output, output_bias, first_gain, first_shift, hidden, hidden_bias, down,
     down_bias, second_gain, second_shift) = outs
    here = lax.axis_index("col")
    for copy in copies[:2]:
        copy.wait()
    for i, ref in enumerate((query, key, value)):
        ref[...] = block_ref[0, :, i * width : (i + 1) * width]
    output[...] = block_ref[0, :, 3 * width : 4 * width].T
    hidden[...] = block_ref[1]
    down[...] = block_ref[2]
    for i, ref in enumerate((output_bias, first_gain, first_shift, down_bias, second_gain, second_shift)):
        ref[...] = sums_ref[i : i + 1].reshape(-1)
    hidden_bias[...] = sums_ref[pl.ds(8 + here, 1)].reshape(-1)
    heads_at = sums_ref.shape[0] - (sizes[2] + -sizes[2] % 8)
    row = sums_ref[pl.ds(heads_at + here, 1)]
    query_bias[...] = row[:, 0:width].reshape(-1)
    value_bias[...] = row[:, WINDOW : WINDOW + width].reshape(-1)
    copies[2].wait()
    input_grad[...] = back_ref[...]


def deliver(sizes, width, back, blocks, sums):
    model = sums.shape[1]
    _, rb, w = blocks.shape
    vmem = pl.BlockSpec(memory_space=pltpu.VMEM)
    square, vector = (rb, width), (model,)
    shapes = [back.shape, square, square, square, (width,), (width,), (width, rb), vector, vector, vector, (rb, w), (w,), (rb, w),
              vector, vector, vector]
    return pl.pallas_call(
        functools.partial(deliver_kernel, sizes, width),
        out_shape=[jax.ShapeDtypeStruct(shape, jnp.float32) for shape in shapes],
        in_specs=[pl.BlockSpec(memory_space=pltpu.MemorySpace.HBM)] * 3,
        out_specs=[vmem] * len(shapes),
        scratch_shapes=[pltpu.VMEM(a.shape, jnp.float32) for a in (back, blocks, sums)] + [pltpu.SemaphoreType.DMA((3,))],
        compiler_params=pltpu.CompilerParams(vmem_limit_bytes=32 << 20),
        name="deliver",
    )(back, blocks, sums)


def per_device_fused(sizes, inputs, segment_ids, query_weight, key_weight, value_weight, query_bias, value_bias,
               output_weight, output_bias, first_gain, first_shift, hidden_weight, hidden_bias, down_weight,
               down_bias, second_gain, second_shift, cotangent):
    floats, halves = jnp.float32, jnp.bfloat16
    cols = sizes[2]
    micro, _, rows, model = inputs.shape
    length = segment_ids.shape[-1]
    width = query_weight.shape[1]
    here = lax.axis_index("col")
    own = inputs[:, 0]
    rest, first, turned, mask, biases, mixed, lse, q, k, v = forward(
        sizes, own, (query_weight, key_weight, value_weight, output_weight, hidden_weight, down_weight.T), hidden_bias, query_bias, value_bias, segment_ids)
    first = first.reshape(cols, model, 4 * width)
    total = micro * rows
    flat = lambda a: a.reshape(total, -1)
    outputs, first_grad, attn_grad, part, sums = middle(
        flat(own), mixed.reshape(cols, total, WINDOW), first, rest.reshape(2, cols, model, -1), biases,
        (output_bias, first_gain, first_shift, down_bias, second_gain, second_shift), flat(cotangent[:, 0]))
    parted = lambda a: a.reshape(micro, rows, model)
    input_grad, reduced, sums = backward(sizes, parted(attn_grad), parted(first_grad), first, turned, mixed, lse, q, k, v,
                                         mask, part, sums)
    grads = deliver(sizes, width, input_grad, reduced, sums)
    return (outputs.reshape(micro, 1, rows, model), grads[0][:, None], *grads[1:12], grads[12].T, *grads[13:])


def per_device(sizes, inputs, segment_ids, query_weight, *rest):
    micro, _, rows, _ = inputs.shape
    fits = (query_weight.shape == (query_weight.shape[0] // 32 * 32, 3 * HEAD_DIM) and micro == 2 and sizes[2] == 4
            and DOC_MOST // 2 == rows)
    return (per_device_fused if fits else per_device_plain)(sizes, inputs, segment_ids, query_weight, *rest)


def solution(mesh):
    sizes = tuple(mesh.shape[name] for name in ("seq", "row", "col"))
    block, line = P(("seq", "row"), "col"), P("col", ("seq", "row"))
    tokens = P(None, ("seq", "row"), "col", None)
    placed = (tokens, P(None, ("seq", "row"), None), block, block, block, P("col"), P("col"), line, P(), P(), P(),
              block, P("col"), line, P(), P(), P(), tokens)
    given = (tokens, tokens, block, block, block, P("col"), P("col"), line, P(), P(), P(), block, P("col"), line,
             P(), P(), P())
    return jax.shard_map(functools.partial(per_device, sizes), mesh=mesh, in_specs=placed, out_specs=given, check_vma=False)
```

```python
import functools

import jax
import jax.numpy as jnp
from jax import lax
from jax.experimental import pallas as pl
from jax.experimental.pallas import tpu as pltpu
from jax.sharding import PartitionSpec as P

HEAD_DIM = 64
NORM_EPS = 1e-05
MASK_VALUE = -1000000000.0
DOC_MOST = 512
KEY_BLOCK = 256
MESH = pl.DeviceIdType.MESH


def contract_rows(left, right):
    return lax.dot_general(
        left, right, (((0,), (0,)), ((), ())), preferred_element_type=jnp.float32
    )


def contract_cols(left, right):
    return lax.dot_general(
        left, right, (((1,), (1,)), ((), ())), preferred_element_type=jnp.float32
    )


def norm_parts(summed):
    deviation = summed - jnp.mean(summed, -1, keepdims=True)
    scale = lax.rsqrt(jnp.mean(deviation * deviation, -1, keepdims=True) + NORM_EPS)
    return deviation * scale, scale


def norm_back(pull, normal, scale):
    return scale * (
        pull - jnp.mean(pull, -1, keepdims=True) - normal * jnp.mean(pull * normal, -1, keepdims=True)
    )

FORWARD_PLAN = (
    ("Zs", 1), ("Zs", 0), ("Z", 1, 1), ("Z", 0, 1), ("Z", 1, 2), ("Z", 1, 3), ("Zs", 4), ("Z", 0, 2), ("Ts", 1),
    ("Zs", 2), ("Z", 0, 3), ("Zs", 5), ("B", 1), ("B", 0), ("Z", 4, 1), ("Z", 2, 1), ("Zs", 3), ("Z", 5, 1),
    ("Z", 4, 2), ("Z", 4, 3), ("Z", 3, 1), ("Z", 2, 2), ("Z", 2, 3), ("T", 1, 1), ("C", 0), ("Ts", 0), ("B", 4),
    ("C", 1), ("Z", 3, 2), ("Z", 5, 2), ("K", 1), ("Z", 3, 3), ("Z", 5, 3), ("T", 0, 1), ("K", 0), ("C", 4),
    ("Ts", 3), ("T", 1, 2), ("B", 2), ("P", 0, 0), ("P", 0, 1), ("Ts", 2), ("T", 0, 2), ("R", 0), ("U", 0, 0),
    ("P", 0, 2), ("U", 0, 1), ("T", 3, 1), ("B", 3), ("U", 0, 2), ("P", 0, 3), ("T", 2, 1), ("P", 1, 0), ("P", 1, 1),
    ("P", 1, 2), ("K", 4), ("C", 2), ("B", 5), ("P", 1, 3), ("C", 3), ("U", 0, 3), ("T", 3, 2), ("T", 2, 2), ("R", 1),
    ("U", 1, 0), ("U", 1, 1), ("C", 5), ("U", 1, 2), ("K", 2), ("K", 3), ("U", 1, 3), ("K", 5),
)
BACKWARD_PLAN = (
    ("G", 1), ("G", 3), ("L",), ("U", 2, 0), ("A", 1), ("G", 0), ("U", 0, 0), ("A", 3), ("U", 1, 0), ("U", 3, 0),
    ("S", 0), ("G", 2), ("B", 1), ("A", 0), ("U", 0, 1), ("A", 2), ("B", 3), ("T", 0, 0, 1), ("C", 1), ("U", 2, 1),
    ("U", 1, 1), ("T", 0, 1, 1), ("U", 3, 1), ("S", 1), ("B", 2), ("W", 2), ("V", 0), ("G", 6), ("B", 0), ("W", 3),
    ("V", 1), ("Z", 1, 2), ("A", 6), ("G", 7), ("C", 3), ("W", 0), ("C", 2), ("G", 4), ("A", 7), ("T", 1, 1, 1),
    ("W", 1), ("Z", 3, 2), ("V", 2), ("G", 5), ("C", 0), ("A", 4), ("B", 7), ("V", 3), ("A", 5), ("Z", 1, 1),
    ("B", 4), ("Z", 2, 2), ("C", 7), ("T", 1, 0, 1), ("B", 6), ("Y", 3, 3), ("B", 5), ("T", 1, 1, 0), ("Z", 3, 1),
    ("C", 4), ("C", 6), ("Y", 0, 3), ("Z", 0, 2), ("Y", 2, 2), ("T", 0, 1, 0), ("C", 5), ("Y", 1, 2), ("V", 4),
    ("Y", 3, 2), ("Y", 0, 2), ("Z", 0, 1), ("Z", 1, 0), ("T", 1, 0, 0), ("Z", 2, 1), ("Z", 3, 0), ("Y", 3, 1),
    ("Y", 2, 1), ("Y", 1, 1), ("T", 0, 0, 0), ("Y", 0, 1), ("Z", 0, 0), ("Z", 2, 0), ("Y", 2, 0), ("Y", 3, 0),
    ("Y", 1, 0), ("Y", 0, 0),
)
def attend_kernel(bounds, own_ref, all_ref, wq_ref, wk_ref, wv_ref, bq_ref, bv_ref,
                  segq_ref, segk_ref, mixed_ref, lse_ref, q_ref, k_ref, v_ref, bias, acc, top, total):
    micro = pl.program_id(0)
    low, high = bounds[micro, 0], bounds[micro, 1]
    floats, halves = jnp.float32, jnp.bfloat16
    width = wq_ref.shape[-1]
    heads = width // HEAD_DIM
    rows = own_ref.shape[1]

    @pl.when(pl.program_id(1) == 0)
    def _():
        same = segk_ref[0] == segq_ref[0, 0:1]
        bias[...] = jnp.where(same, 0.0, MASK_VALUE)

    queries = jnp.dot(own_ref[0], wq_ref[0], preferred_element_type=floats) + bq_ref[0]
    queries = queries.astype(halves) * jnp.asarray(HEAD_DIM ** -0.5, halves)
    q_ref[0, 0] = queries
    lane = lax.broadcasted_iota(jnp.int32, (rows, width), 1) // HEAD_DIM
    query_heads = [jnp.where(lane == h, queries, jnp.zeros_like(queries)) for h in range(heads)]
    acc[...] = jnp.zeros_like(acc)
    total[...] = jnp.zeros_like(total)
    top[...] = jnp.full_like(top, 2 * MASK_VALUE)

    def step(block, carry):
        at = pl.ds(pl.multiple_of(block * KEY_BLOCK, KEY_BLOCK), KEY_BLOCK)
        x = all_ref[0, at, :]
        keys = jnp.dot(x, wk_ref[0], preferred_element_type=floats).astype(halves)
        k_ref[0, 0, at, :] = keys
        values = (jnp.dot(x, wv_ref[0], preferred_element_type=floats) + bv_ref[0]).astype(halves)
        v_ref[0, 0, at, :] = values
        values_t = values.T
        mask = bias[at, :]
        for h in range(heads):
            s = contract_cols(keys, query_heads[h]) + mask
            old = top[h : h + 1]
            new = jnp.maximum(old, jnp.max(s, 0, keepdims=True))
            p = jnp.exp(s - new)
            shrink = jnp.exp(old - new)
            top[h : h + 1] = new
            total[h : h + 1] = total[h : h + 1] * shrink + jnp.sum(p, 0, keepdims=True)
            part = pl.ds(h * HEAD_DIM, HEAD_DIM)
            acc[part, :] = acc[part, :] * shrink + jnp.dot(
                values_t[h * HEAD_DIM : (h + 1) * HEAD_DIM], p.astype(halves), preferred_element_type=floats
            )
        return carry

    lax.fori_loop(low, high, step, 0)
    for h in range(heads):
        part = pl.ds(h * HEAD_DIM, HEAD_DIM)
        acc[part, :] = acc[part, :] / total[h : h + 1]
    mixed_ref[0, 0] = acc[...].T.astype(halves)
    lse_ref[0, 0] = top[...] + jnp.log(jnp.maximum(total[...], 1e-30))


def attend(bounds, own, everything, wq, wk, wv, bq, bv, seg_own, seg_all):
    micro, rows, model = own.shape
    length = everything.shape[1]
    cols, _, width = wq.shape
    halves = jnp.bfloat16
    weight = pl.BlockSpec((1, model, width), lambda m, c, b: (c, 0, 0))
    per = lambda a, b_: pl.BlockSpec((1, 1, a, b_), lambda m, c, b: (c, m, 0, 0))
    spec = pltpu.PrefetchScalarGridSpec(
        num_scalar_prefetch=1,
        grid=(micro, cols),
        in_specs=[
            pl.BlockSpec((1, rows, model), lambda m, c, b: (m, 0, 0)),
            pl.BlockSpec((1, length, model), lambda m, c, b: (m, 0, 0)),
            weight, weight, weight,
            pl.BlockSpec((1, 1, width), lambda m, c, b: (c, 0, 0)),
            pl.BlockSpec((1, 1, width), lambda m, c, b: (c, 0, 0)),
            pl.BlockSpec((1, 1, rows), lambda m, c, b: (m, 0, 0)),
            pl.BlockSpec((1, length, 1), lambda m, c, b: (m, 0, 0)),
        ],
        out_specs=[per(rows, width), per(8, rows), per(rows, width), per(length, width), per(length, width)],
        scratch_shapes=[
            pltpu.VMEM((length, rows), jnp.float32),
            pltpu.VMEM((width, rows), jnp.float32),
            pltpu.VMEM((8, rows), jnp.float32),
            pltpu.VMEM((8, rows), jnp.float32),
        ],
    )
    shape = lambda a, b_, d=halves: jax.ShapeDtypeStruct((cols, micro, a, b_), d)
    return pl.pallas_call(
        attend_kernel,
        grid_spec=spec,
        out_shape=[shape(rows, width), shape(8, rows, jnp.float32), shape(rows, width), shape(length, width), shape(length, width)],
        compiler_params=pltpu.CompilerParams(vmem_limit_bytes=48 << 20),
        name="attend",
    )(bounds, own, everything, wq, wk, wv, bq[:, None], bv[:, None],
      seg_own[:, None], seg_all[:, :, None])


def attend_back_kernel(bounds, grad_ref, wot_ref, mixed_ref, lse_ref, q_ref, k_ref, v_ref, segq_ref, segk_ref,
                       dq_ref, dk_ref, dv_ref, bias, acc):
    micro = pl.program_id(0)
    low, high = bounds[micro, 0], bounds[micro, 1]
    floats, halves = jnp.float32, jnp.bfloat16
    rows, width = q_ref.shape[2:]
    heads = width // HEAD_DIM

    @pl.when(pl.program_id(1) == 0)
    def _():
        same = segk_ref[0] == segq_ref[0, 0:1]
        bias[...] = jnp.where(same, 0.0, MASK_VALUE)

    mixed_grad = jnp.dot(grad_ref[0], wot_ref[0], preferred_element_type=floats).astype(halves)
    product = mixed_grad.astype(floats) * mixed_ref[0, 0].astype(floats)
    product_high = product.astype(halves)
    product_low = (product - product_high.astype(floats)).astype(halves)
    pick = (
        lax.broadcasted_iota(jnp.int32, (8, width), 1) // HEAD_DIM == lax.broadcasted_iota(jnp.int32, (8, width), 0)
    ).astype(halves)
    inner = contract_cols(pick, product_high) + contract_cols(pick, product_low)
    lane = lax.broadcasted_iota(jnp.int32, (rows, width), 1) // HEAD_DIM
    queries = q_ref[0, 0]
    query_heads = [jnp.where(lane == h, queries, jnp.zeros_like(queries)) for h in range(heads)]
    grad_heads = [jnp.where(lane == h, mixed_grad, jnp.zeros_like(mixed_grad)) for h in range(heads)]
    acc[...] = jnp.zeros_like(acc)
    dk_ref[...] = jnp.zeros_like(dk_ref)
    dv_ref[...] = jnp.zeros_like(dv_ref)

    def step(block, carry):
        at = pl.ds(pl.multiple_of(block * KEY_BLOCK, KEY_BLOCK), KEY_BLOCK)
        keys = k_ref[0, 0, at, :]
        values = v_ref[0, 0, at, :]
        keys_t = keys.T
        mask = bias[at, :]
        key_grad = jnp.zeros((KEY_BLOCK, width), floats)
        value_grad = jnp.zeros((KEY_BLOCK, width), floats)
        for h in range(heads):
            s = contract_cols(keys, query_heads[h]) + mask
            p = jnp.exp(s - lse_ref[0, 0, h : h + 1])
            prob_grad = contract_cols(values, grad_heads[h])
            score_grad = (p * (prob_grad - inner[h : h + 1])).astype(halves)
            value_grad = value_grad + jnp.dot(p.astype(halves), grad_heads[h], preferred_element_type=floats)
            key_grad = key_grad + jnp.dot(score_grad, query_heads[h], preferred_element_type=floats)
            part = pl.ds(h * HEAD_DIM, HEAD_DIM)
            acc[part, :] += jnp.dot(keys_t[h * HEAD_DIM : (h + 1) * HEAD_DIM], score_grad, preferred_element_type=floats)
        dk_ref[0, 0, at, :] = key_grad.astype(halves)
        dv_ref[0, 0, at, :] = value_grad.astype(halves)
        return carry

    lax.fori_loop(low, high, step, 0)
    dq_ref[0, 0] = (acc[...].T * HEAD_DIM ** -0.5).astype(halves)


def attend_back(bounds, grad, wot, mixed, lse, q, k, v, seg_own, seg_all):
    micro, rows, model = grad.shape
    cols, _, length, width = k.shape
    halves = jnp.bfloat16
    per = lambda a, b_: pl.BlockSpec((1, 1, a, b_), lambda m, c, b: (c, m, 0, 0))
    spec = pltpu.PrefetchScalarGridSpec(
        num_scalar_prefetch=1,
        grid=(micro, cols),
        in_specs=[
            pl.BlockSpec((1, rows, model), lambda m, c, b: (m, 0, 0)),
            pl.BlockSpec((1, model, width), lambda m, c, b: (c, 0, 0)),
            per(rows, width), per(8, rows), per(rows, width), per(length, width), per(length, width),
            pl.BlockSpec((1, 1, rows), lambda m, c, b: (m, 0, 0)),
            pl.BlockSpec((1, length, 1), lambda m, c, b: (m, 0, 0)),
        ],
        out_specs=[per(rows, width), per(length, width), per(length, width)],
        scratch_shapes=[pltpu.VMEM((length, rows), jnp.float32), pltpu.VMEM((width, rows), jnp.float32)],
    )
    shape = lambda a, b_, d=halves: jax.ShapeDtypeStruct((cols, micro, a, b_), d)
    return pl.pallas_call(
        attend_back_kernel,
        grid_spec=spec,
        out_shape=[shape(rows, width), shape(length, width), shape(length, width)],
        compiler_params=pltpu.CompilerParams(vmem_limit_bytes=48 << 20),
        name="attend_back",
    )(bounds, grad, wot, mixed, lse, q, k, v, seg_own[:, None], seg_all[:, :, None])


def place(sizes):
    seq, row, col = (lax.axis_index(name) for name in ("seq", "row", "col"))
    lines = {"x": (seq, sizes[0]), "y": (row // 2, sizes[1] // 2), "k": (lax.rem(row, 2), 2), "z": (col, sizes[2])}

    def device(axis, index):
        if axis == "x":
            return (index, row, col)
        if axis == "y":
            return (seq, index * 2 + lax.rem(row, 2), col)
        if axis == "k":
            return (seq, row // 2 * 2 + index, col)
        return (seq, row, index)

    return lines, device


def greet(lines, device):
    barrier = pltpu.get_barrier_semaphore()
    count = 0
    for axis, (mine, size) in lines.items():
        for t in range(1, size):
            pl.semaphore_signal(barrier, inc=1, device_id=device(axis, lax.rem(mine + t, size)), device_id_type=MESH)
            count += 1
    pl.semaphore_wait(barrier, count)


class Post:
    def __init__(self, device, send_sems, recv_sems):
        self.device, self.send_sems, self.recv_sems = device, send_sems, recv_sems
        self.slots, self.sent = {}, []

    def slot(self, key):
        return self.slots.setdefault(key, len(self.slots))

    def copy(self, key, axis, index, source, target):
        n = self.slot(key)
        return pltpu.make_async_remote_copy(
            src_ref=source, dst_ref=target, send_sem=self.send_sems.at[n], recv_sem=self.recv_sems.at[n],
            device_id=self.device(axis, index), device_id_type=MESH,
        )

    def send(self, key, make):
        def run(act):
            axis, index, source, target, when = make()

            def go():
                act(self.copy(key, axis, index, source, target))

            if when is None:
                go()
            else:
                pl.when(when)(go)

        run(lambda copy: copy.start())
        self.sent.append(run)

    def wait(self, key, axis, index, target, when=None):
        def go():
            self.copy(key, axis, index, target, target).wait_recv()

        if when is None:
            go()
        else:
            pl.when(when)(go)

    def close(self):
        for run in self.sent:
            run(lambda copy: copy.wait_send())


def clip(index, size):
    return jnp.clip(index, 0, size - 1)


class LineGather:
    def __init__(self, post, name, axis, line, region, reach=None):
        self.post, self.name, self.axis, self.region = post, name, axis, region
        self.mine, self.size = line
        self.reach = min(self.size - 1, reach or self.size)

    def hop(self, way, t):
        mine, size = self.mine, self.size

        def make():
            origin, target = mine - way * t, mine + way
            ok = (origin >= 0) & (origin < size) & (target >= 0) & (target < size)
            here = self.region(clip(origin, size))
            return self.axis, clip(target, size), here, here, ok

        self.post.send((self.name, way, t + 1), make)

    def start(self):
        for way in (1, -1):
            if self.reach >= 1:
                self.hop(way, 0)

    def step(self, t):
        if t > self.reach:
            return
        for way in (1, -1):
            origin = self.mine - way * t
            ok = (origin >= 0) & (origin < self.size)
            self.post.wait((self.name, way, t), self.axis, clip(self.mine - way, self.size), self.region(clip(origin, self.size)), ok)
            if t < self.reach:
                self.hop(way, t)

    def finish(self, first=1):
        for t in range(first, self.reach + 1):
            self.step(t)


def gather_kernel(sizes, micro, own_ref, shard_ref, every_ref, full_ref, send_sems, recv_sems, local_sems):
    lines, device = place(sizes)
    (x, _), (y, _), (k, _), (z, cols) = (lines[a] for a in "xykz")
    half = shard_ref.shape[-1] // 2
    rows = own_ref.shape[1]
    reach = -(-(DOC_MOST - 1) // rows)
    parts = [pl.ds(p * half, half) for p in (0, 1)]
    local = [pltpu.make_async_copy(shard_ref.at[j], full_ref.at[j, z, x, y, k], local_sems.at[j]) for j in range(3)]
    local += [pltpu.make_async_copy(own_ref.at[m], every_ref.at[m, z], local_sems.at[3 + m]) for m in range(micro)]
    for copy in local:
        copy.start()
    greet(lines, device)
    post = Post(device, send_sems, recv_sems)
    for copy in local:
        copy.wait()
    zs = [LineGather(post, ("z", j), "z", lines["z"], lambda i, j=j: full_ref.at[j, i, x, y, k]) for j in range(3)]
    tokens = [LineGather(post, ("t", m), "z", lines["z"], lambda i, m=m: every_ref.at[m, i], reach) for m in range(micro)]
    second, third = {}, {}
    for j in range(3):
        second[j] = [
            LineGather(post, ("a", j), "y", lines["y"], lambda i, j=j: full_ref.at[j, :, x, i, k, :, parts[0]]),
            LineGather(post, ("b", j), "x", lines["x"], lambda i, j=j: full_ref.at[j, :, i, y, k, :, parts[1]]),
        ]
        third[j] = [
            LineGather(post, ("c", j), "x", lines["x"], lambda i, j=j: full_ref.at[j, :, i, :, k, :, parts[0]]),
            LineGather(post, ("d", j), "y", lines["y"], lambda i, j=j: full_ref.at[j, :, :, i, k, :, parts[1]]),
        ]

    def start(group):
        for line in group:
            line.start()

    def finish(group):
        for line in group:
            line.finish()

    def swap(j):
        plane = full_ref.at[j, :, :, :, k]
        post.send(("k", j), lambda: ("k", 1 - k, plane, plane, None))

    start(zs[:1])
    finish(zs[:1])
    start(second[0] + zs[1:2])
    finish(second[0])
    start(third[0])
    finish(zs[1:2])
    start(second[1] + tokens[:1])
    finish(third[0])
    swap(0)
    finish(second[1])
    start(third[1])
    finish(tokens[:1])
    start(zs[2:])
    finish(zs[2:])
    start(second[2] + tokens[1:])
    finish(third[1])
    swap(1)
    finish(second[2])
    start(third[2])
    finish(tokens[1:])
    finish(third[2])
    swap(2)
    for i in range(cols):
        far = (z - i > reach) | (i - z > reach)
        for m in range(micro):
            def fill(m=m, i=i):
                copy = pltpu.make_async_copy(own_ref.at[m], every_ref.at[m, i], local_sems.at[3 + m])
                copy.start()
                copy.wait()

            if i > reach or cols - 1 - i > reach:
                pl.when(far)(fill)
    for j in range(3):
        post.wait(("k", j), "k", 1 - k, full_ref.at[j, :, :, :, 1 - k])
    post.close()


def gather(sizes, own, shard):
    ns, nr, nc = sizes
    ny = nr // 2
    micro, rows, model = own.shape
    _, rb, w = shard.shape
    count = 3 * 2 * (nc - 1) + micro * 2 * (nc - 1) + 3 * (4 * (ny - 1) + 4 * (ns - 1) + 1)
    anywhere = pl.BlockSpec(memory_space=pl.ANY)
    every, full = pl.pallas_call(
        functools.partial(gather_kernel, sizes, micro),
        out_shape=[
            jax.ShapeDtypeStruct((micro, nc, rows, model), own.dtype),
            jax.ShapeDtypeStruct((3, nc, ns, ny, 2, rb, w), shard.dtype),
        ],
        in_specs=[pl.BlockSpec(memory_space=pltpu.VMEM)] * 2,
        out_specs=[anywhere] * 2,
        scratch_shapes=[pltpu.SemaphoreType.DMA((count,)), pltpu.SemaphoreType.DMA((count,)), pltpu.SemaphoreType.DMA((3 + micro,))],
        compiler_params=pltpu.CompilerParams(collective_id=0, has_side_effects=True),
        name="gather",
    )(own, shard)
    return every, full.reshape(3, nc, ns * nr * rb, w)


class LineReduce:
    def __init__(self, post, name, axis, line, region, inbox, add, reach=None):
        self.post, self.name, self.axis, self.region, self.inbox, self.add = post, name, axis, region, inbox, add
        self.mine, self.size = line
        self.reach = min(self.size - 1, reach or self.size)

    def arrived(self, way, e):
        behind, goal = self.mine - way, self.mine + way * e
        return (behind >= 0) & (behind < self.size) & (goal >= 0) & (goal < self.size)

    def take(self, way, e):
        ok = self.arrived(way, e)
        inbox = self.inbox(way, e)
        self.post.wait((self.name, way, e), self.axis, clip(self.mine - way, self.size), inbox, ok)

        @pl.when(ok)
        def _():
            self.add(self.region(clip(self.mine + way * e, self.size)), inbox)

    def forward(self, way, e):
        def make():
            goal = self.mine + way * e
            ok = (goal >= 0) & (goal < self.size)
            return self.axis, clip(self.mine + way, self.size), self.region(clip(goal, self.size)), self.inbox(way, e - 1), ok

        self.post.send((self.name, way, e - 1), make)

    def start(self):
        for way in (1, -1):
            if self.reach >= 1:
                self.forward(way, self.reach)

    def forward_from(self, nearest):
        for e in range(self.reach - 1, nearest - 1, -1):
            for way in (1, -1):
                self.take(way, e)
                self.forward(way, e)

    def finish(self, last=True):
        self.forward_from(1)
        if last:
            for way in (1, -1):
                if self.reach >= 1:
                    self.take(way, 0)


def reduce_to(post, name, axis, line, goal, e, region, inbox, add):
    mine, size = line
    for way in (1, -1):
        behind = mine - way
        arrives = (way * (goal - mine) == e) & (behind >= 0) & (behind < size)
        slot = inbox(way, min(e, size - 2))
        post.wait((name, way), axis, clip(behind, size), slot, arrives)

        @pl.when(arrives)
        def _():
            add(region, slot)

        def make(way=way):
            return axis, clip(mine + way, size), region, inbox(way, e - 1), way * (goal - mine) == e

        if e:
            post.send((name, way), make)


def reduce_kernel(sizes, micro, own_ref, spread_ref, part_ref, vec_ref, back_ref, block_ref, sums_ref,
                  mine_buf, core_buf, in_a, in_b, in_c, in_d, in_z, tok_buf, tok_in, vec_buf, send_sems, recv_sems, local_sems):
    floats, halves = jnp.float32, jnp.bfloat16
    lines, device = place(sizes)
    (x, ns), (y, ny), (k, _), (z, nc) = (lines[a] for a in "xykz")
    half = part_ref.shape[-1] // 2
    rows = own_ref.shape[1]
    reach = -(-(DOC_MOST - 1) // rows)
    parts = [pl.ds(p * half, half) for p in (0, 1)]
    local = [pltpu.make_async_copy(part_ref.at[j, :, :, :, k], mine_buf.at[j], local_sems.at[j]) for j in range(3)]
    local += [pltpu.make_async_copy(spread_ref.at[m], tok_buf.at[m], local_sems.at[3 + m]) for m in range(micro)]
    for copy in local:
        copy.start()
    greet(lines, device)
    post = Post(device, send_sems, recv_sems)
    for j in range(3):
        post.send(("k", j), lambda j=j: ("k", 1 - k, part_ref.at[j, :, :, :, 1 - k], core_buf.at[j], None))

    def plus(target, source):
        target[...] = (target[...].astype(floats) + source[...].astype(floats)).astype(halves)

    def plus_grid(target, source, first, second):
        @pl.loop(0, first * second)
        def _(n):
            plus(target.at[n // second, lax.rem(n, second)], source.at[n // second, lax.rem(n, second)])

    def plus_row(target, source, first):
        @pl.loop(0, first)
        def _(n):
            plus(target.at[n], source.at[n])

    vec_buf[0, 0] = vec_ref[...]

    def vector_start(stage, axis):
        mine, size = lines[axis]
        vec_buf[stage, 1 + mine] = vec_buf[stage, 0]
        for t in range(1, size):
            post.send(("v", stage, t), lambda t=t: (
                axis, lax.rem(mine + t, size), vec_buf.at[stage, 0], vec_buf.at[stage, 1 + mine], None))

    def vector_finish(stage, axis, out):
        mine, size = lines[axis]
        for t in range(1, size):
            origin = lax.rem(mine + size - t, size)
            post.wait(("v", stage, t), axis, origin, vec_buf.at[stage, 1 + origin])
        total = vec_buf[stage, 1]
        for i in range(1, size):
            total = total + vec_buf[stage, 1 + i]
        out[...] = total

    tokens = [
        LineReduce(post, ("t", m), "z", lines["z"], lambda i, m=m: tok_buf.at[m, i],
                   lambda way, e, m=m: tok_in.at[m, (1 - way) // 2, e], plus, reach)
        for m in range(micro)
    ]
    box = lambda way: (1 - way) // 2
    second, third, last = {}, {}, {}
    for j in range(3):
        second[j] = [
            LineReduce(post, ("a", j), "x", lines["x"], lambda i, j=j: mine_buf.at[j, :, i, :, :, parts[0]],
                       lambda way, e, j=j: in_a.at[j, box(way), e], lambda t, s: plus_grid(t, s, nc, ny)),
            LineReduce(post, ("b", j), "y", lines["y"], lambda i, j=j: mine_buf.at[j, :, :, i, :, parts[1]],
                       lambda way, e, j=j: in_b.at[j, box(way), e], lambda t, s: plus_grid(t, s, nc, ns)),
        ]
        third[j] = [
            LineReduce(post, ("c", j), "y", lines["y"], lambda i, j=j: mine_buf.at[j, :, x, i, :, parts[0]],
                       lambda way, e, j=j: in_c.at[j, box(way), e], lambda t, s: plus_row(t, s, nc)),
            LineReduce(post, ("d", j), "x", lines["x"], lambda i, j=j: mine_buf.at[j, :, i, y, :, parts[1]],
                       lambda way, e, j=j: in_d.at[j, box(way), e], lambda t, s: plus_row(t, s, nc)),
        ]
        last[j] = [
            LineReduce(post, ("z", j), "z", lines["z"], lambda i, j=j: mine_buf.at[j, i, x, y],
                       lambda way, e, j=j: in_z.at[j, box(way), e], plus)
        ]

    def start(group):
        for line in group:
            line.start()

    def finish(group):
        for line in group:
            line.finish()

    def core(j):
        local[j].wait()
        post.wait(("k", j), "k", 1 - k, core_buf.at[j])

        @pl.loop(0, nc * ns * ny)
        def _(n):
            at = (n // (ns * ny), lax.rem(n // ny, ns), lax.rem(n, ny))
            plus(mine_buf.at[(j, *at)], core_buf.at[(j, *at)])

    for m in range(micro):
        local[3 + m].wait()
    start(tokens)
    core(0)
    start(second[0])
    vector_start(0, "k")
    core(1)
    start(second[1])
    vector_finish(0, "k", vec_buf.at[1, 0])
    vector_start(1, "y")
    core(2)
    finish(second[0])
    start(third[0])
    start(second[2])
    vector_finish(1, "y", vec_buf.at[2, 0])
    vector_start(2, "x")
    finish(tokens)
    vector_finish(2, "x", vec_buf.at[3, 0])
    vector_start(3, "z")
    finish(second[1])
    start(third[1])
    finish(third[0])
    start(last[0])
    finish(second[2])
    start(third[2])
    finish(third[1])
    start(last[1])
    finish(last[0])
    finish(third[2])
    start(last[2])
    vector_finish(3, "z", sums_ref)
    for m in range(micro):
        back_ref[m] = own_ref[m] + tok_buf[m, z].astype(floats)
    finish(last[1])
    finish(last[2])
    for j in range(3):
        block_ref[j] = mine_buf[j, z, x, y].astype(floats)
    post.close()


def reduce(sizes, own_share, spread, partial, vectors):
    ns, nr, nc = sizes
    ny = nr // 2
    micro, rows, model = own_share.shape
    w = partial.shape[-1]
    rb = partial.shape[2] // (ns * nr)
    halves, floats = jnp.bfloat16, jnp.float32
    reach = min(nc - 1, -(-(DOC_MOST - 1) // rows))
    count = 3 + 2 * (ny - 1 + ns - 1) * 6 + 3 * 2 * (nc - 1) + micro * 2 * reach + (1 + ny - 1 + ns - 1 + nc - 1)
    widest = max(ns, ny, nc, 2)
    extra = -vectors.shape[0] % 8
    vectors = jnp.pad(vectors, ((0, extra), (0, 0)))
    vmem = pl.BlockSpec(memory_space=pltpu.VMEM)
    anywhere = pl.BlockSpec(memory_space=pl.ANY)
    back, blocks, sums = pl.pallas_call(
        functools.partial(reduce_kernel, sizes, micro),
        out_shape=[
            jax.ShapeDtypeStruct((micro, rows, model), floats),
            jax.ShapeDtypeStruct((3, rb, w), floats),
            jax.ShapeDtypeStruct(vectors.shape, floats),
        ],
        in_specs=[vmem, anywhere, anywhere, vmem],
        out_specs=[vmem] * 3,
        scratch_shapes=[
            pltpu.VMEM((3, nc, ns, ny, rb, w), halves),
            pltpu.VMEM((3, nc, ns, ny, rb, w), halves),
            pltpu.VMEM((3, 2, max(ns - 1, 1), nc, ny, rb, w // 2), halves),
            pltpu.VMEM((3, 2, max(ny - 1, 1), nc, ns, rb, w // 2), halves),
            pltpu.VMEM((3, 2, max(ny - 1, 1), nc, rb, w // 2), halves),
            pltpu.VMEM((3, 2, max(ns - 1, 1), nc, rb, w // 2), halves),
            pltpu.VMEM((3, 2, max(nc - 1, 1), rb, w), halves),
            pltpu.VMEM((micro, nc, rows, model), halves),
            pltpu.VMEM((micro, 2, max(reach, 1), rows, model), halves),
            pltpu.VMEM((4, 1 + widest, *vectors.shape), floats),
            pltpu.SemaphoreType.DMA((count,)),
            pltpu.SemaphoreType.DMA((count,)),
            pltpu.SemaphoreType.DMA((3 + micro,)),
        ],
        compiler_params=pltpu.CompilerParams(collective_id=1, has_side_effects=True, vmem_limit_bytes=60 << 20),
        name="reduce",
    )(own_share, spread, partial.reshape(3, nc, ns, ny, 2, rb, w), vectors)
    return back, blocks, sums


Q_AT, K_AT, V_AT, O_AT, WINDOW = 0, 128, 384, 512, 256


def plane(full_ref, c, at, size=WINDOW):
    value = full_ref[c, :, :, :, :, at : at + size]
    return value.reshape(-1, size)


def split_plan(plan):
    parts, order = [[]], []
    for task in plan:
        if task[0] == "U":
            order.append(task[1:])
            parts.append([])
        else:
            parts[-1].append(task)
    return parts[0], parts[1:], order


def pick(step, values):
    value = values[0]
    for i, other in enumerate(values[1:], 1):
        value = jnp.where(step == i, other, value)
    return value


def place_of(rows):
    return lax.broadcasted_iota(jnp.int32, (rows, WINDOW), 1) // HEAD_DIM


def keep(value, places, wanted):
    return jnp.where(places == wanted, value, jnp.zeros_like(value))


def forward_kernel(sizes, micro, own_ref, wq_ref, wk_ref, wv_ref, wo_ref, wh_ref, wd_ref, hidden_bias_ref, query_bias_ref, value_bias_ref, seg_ref,
                   rest_ref, first_ref, turned_ref, mask_ref, biases_ref, mixed_ref, lse_ref, q_ref, k_ref, v_ref,
                   weights, turned, bias_buf, mask, mixed_buf, lse_buf, q_buf, k_buf, v_buf, tokens_buf, acc, score_buf, prob_buf, values_t,
                   send_sems, recv_sems, local_sems, unit_sems):
    floats, halves = jnp.float32, jnp.bfloat16
    lines, device = place(sizes)
    (x, _), (y, _), (k, _), (z, cols) = (lines[a] for a in "xykz")
    half = wh_ref.shape[-1] // 2
    rows = own_ref.shape[1]
    reach = -(-(DOC_MOST - 1) // rows)
    parts = [pl.ds(p * half, half) for p in (0, 1)]
    low, high = jnp.maximum(z - reach, 0), jnp.minimum(z + reach + 1, cols)
    used = [0]

    class Local:
        def __init__(self, source, target):
            self.source, self.target, self.n = source, target, used[0]
            used[0] += 1
            self.describe().start()

        def describe(self):
            source = self.source() if callable(self.source) else self.source
            return pltpu.make_async_copy(source, self.target, local_sems.at[self.n])

        def wait(self):
            self.describe().wait()

    local = Local
    targets = [weights.at[0], rest_ref.at[0], rest_ref.at[1]]
    packed = [wq_ref[...], wk_ref[...], wv_ref[...], wo_ref[...].astype(floats).T.astype(halves)]
    weights[0, z, x, y, k] = jnp.concatenate(packed, 1)
    begin = [local(wh_ref, targets[1].at[z, x, y, k]), local(wd_ref, targets[2].at[z, x, y, k])]
    begin += [local(own_ref.at[m], tokens_buf.at[m, z]) for m in range(micro)]
    for i, ref in enumerate((hidden_bias_ref, query_bias_ref, value_bias_ref)):
        bias_buf[z, i : i + 1, 0 : ref.shape[0]] = ref[...].astype(floats).reshape(1, -1)
        if ref.shape[0] < WINDOW:
            bias_buf[z, i : i + 1, ref.shape[0] : WINDOW] = jnp.zeros((1, WINDOW - ref.shape[0]), floats)
    greet(lines, device)
    post = Post(device, send_sems, recv_sems)
    for copy in begin:
        copy.wait()
    tokens = [
        LineGather(post, ("t", q), "z", lines["z"],
                   lambda i, q=q: tokens_buf.at[q // 2, i, pl.ds(q % 2 * (rows // 2), rows // 2)], reach)
        for q in range(2 * micro)
    ]
    small = LineGather(post, "bias", "z", lines["z"], lambda i: bias_buf.at[i])
    rb = wh_ref.shape[0]
    zs, second, third = {}, {}, {}
    for n in range(6):
        j, r = n // 2, pl.ds(n % 2 * (rb // 2), rb // 2)
        zs[n] = LineGather(post, ("z", n), "z", lines["z"], lambda i, j=j, r=r: targets[j].at[i, x, y, k, r])
        second[n] = [
            LineGather(post, ("a", n), "y", lines["y"], lambda i, j=j, r=r: targets[j].at[:, x, i, k, r, parts[0]]),
            LineGather(post, ("b", n), "x", lines["x"], lambda i, j=j, r=r: targets[j].at[:, i, y, k, r, parts[1]]),
        ]
        third[n] = [
            LineGather(post, ("c", n), "x", lines["x"], lambda i, j=j, r=r: targets[j].at[:, i, :, k, r, parts[0]]),
            LineGather(post, ("d", n), "y", lines["y"], lambda i, j=j, r=r: targets[j].at[:, :, i, k, r, parts[1]]),
        ]

    def start(*group):
        for line in group:
            line.start()

    def finish(*group):
        for line in group:
            line.finish()

    def side(n, which):
        return targets[n // 2].at[:, :, :, which, pl.ds(n % 2 * (rb // 2), rb // 2)]

    def swap(n):
        post.send(("k", n), lambda: ("k", 1 - k, side(n, k), side(n, k), None))

    def swapped(n):
        post.wait(("k", n), "k", 1 - k, side(n, 1 - k))

    places = place_of(rows)

    def project(m, c, block):
        rows_at = tokens_buf[m, block]
        k_buf[m, c, block] = jnp.dot(rows_at, plane(weights.at[0], c, K_AT), preferred_element_type=floats).astype(halves)
        values = jnp.dot(rows_at, plane(weights.at[0], c, V_AT), preferred_element_type=floats) + bias_buf[c, 2:3, 0:WINDOW]
        v_buf[m, c, block] = values.astype(halves)

    def prepare(m, c):
        queries = jnp.dot(own_ref[m], plane(weights.at[0], c, Q_AT), preferred_element_type=floats) + bias_buf[c, 1:2, 0:WINDOW]
        queries = pltpu.roll(queries.astype(halves).astype(floats) * HEAD_DIM ** -0.5, HEAD_DIM, 1)
        q_buf[m, c] = jnp.where(places > 0, queries, 0.0).astype(halves)
        for way in (0, 1, 3):
            project(m, c, lax.rem(z + way, cols))

    def unit(m, c):
        project(m, c, lax.rem(z + 2, cols))
        queries = q_buf[m, c]
        heads = jnp.concatenate([keep(queries, places, h + 1) for h in range(3)], 0)
        largest = jnp.full((1, 3 * rows), 2 * MASK_VALUE, floats)
        for block in range(cols):
            keys = k_buf[m, c, block]
            values_t[:, block * rows : (block + 1) * rows] = v_buf[m, c, block].T
            hidden = mask[m, block].astype(floats)
            s = contract_cols(keys, heads) + jnp.concatenate([hidden] * 3, 1)
            score_buf[block] = s
            largest = jnp.maximum(largest, jnp.max(s, 0, keepdims=True))
        row_total = jnp.zeros((1, 3 * rows), floats)
        for block in range(cols):
            p = jnp.exp(score_buf[block] - largest)
            row_total = row_total + jnp.sum(p, 0, keepdims=True)
            prob_buf[block * rows : (block + 1) * rows] = p.astype(halves)
        log_total = largest + jnp.log(row_total)
        acc[0:HEAD_DIM] = jnp.zeros((HEAD_DIM, rows), floats)
        for h in range(3):
            lanes = slice(h * rows, (h + 1) * rows)
            product = jnp.dot(values_t[h * HEAD_DIM : (h + 1) * HEAD_DIM], prob_buf[:, lanes], preferred_element_type=floats)
            acc[pl.ds((h + 1) * HEAD_DIM, HEAD_DIM), :] = product / row_total[:, lanes]
            lse_buf[m, c, h : h + 1] = log_total[:, lanes]
        mixed_buf[c, m] = acc[...].T.astype(halves)

    def units(m, first, last):
        @pl.loop(first, last)
        def _(c):
            unit(m, c)

    def masks(m):
        asking = seg_ref[m, 0:1, pl.ds(pl.multiple_of(z * rows, 128), rows)].astype(floats)
        for block in range(cols):
            asked = seg_ref[m, 0:1, block * rows : (block + 1) * rows].astype(floats)
            same = jnp.broadcast_to(asked, (rows, rows)).T == asking
            mask[m, block] = jnp.where(same, 0.0, MASK_VALUE).astype(halves)

    done = []

    def turn(m):
        for block in range(cols):
            turned[:, (m * cols + block) * rows : (m * cols + block + 1) * rows] = tokens_buf[m, block].T
        if m == micro - 1:
            done.append(local(turned, turned_ref))

    keeps = ((q_buf, q_ref), (k_buf, k_ref), (v_buf, v_ref), (lse_buf, lse_ref))

    def take_z(n, t):
        zs[n].step(t)
        if n == 0:
            small.step(t)
        if t == cols - 1:
            start(*second[n])

    def take_second(n):
        finish(*second[n])
        start(*third[n])

    def take_third(n):
        finish(*third[n])
        swap(n)

    swaps = set()

    def take_core(n):
        swapped(n)
        swaps.add(n)
        if n < 2 and swaps >= {0, 1}:
            done.append(local(lambda: weights.at[0], first_ref))

    act = {
        "Zs": lambda n: zs[n].start(), "Z": take_z, "Ts": lambda q: tokens[q].start(), "T": lambda q, t: tokens[q].step(t),
        "B": take_second, "C": take_third, "K": take_core, "R": turn,
    }
    small.start()
    head, tail, order = split_plan([("U", *task) if task[0] == "P" else task for task in FORWARD_PLAN])
    kinds = [int(item[0] == "P") for item in order]
    micros, heads_of = [item[-2] for item in order], [item[-1] for item in order]
    act[head[0][0]](*head[0][1:])
    for block in range(cols):
        if block > reach or cols - 1 - block > reach:
            @pl.when(jnp.logical_not((low <= block) & (block < high)))
            def _(block=block):
                for m in range(micro):
                    tokens_buf[m, block] = jnp.zeros(own_ref.shape[1:], halves)
    for m in range(micro):
        masks(m)
    for task in head[1:]:
        act[task[0]](*task[1:])

    def leave(m, c, go):
        for i, (source, target) in enumerate(keeps):
            go(pltpu.make_async_copy(source.at[m, c], target.at[m, c], unit_sems.at[i, m * cols + c]))

    @pl.loop(0, len(order))
    def _(step):
        m, c, kind = pick(step, micros), pick(step, heads_of), pick(step, kinds)

        @pl.when(kind == 1)
        def _():
            prepare(m, c)

        @pl.when(kind == 0)
        def _():
            unit(m, c)
            leave(m, c, lambda copy: copy.start())

        for i, tasks in enumerate(tail[:-1]):
            if tasks:
                @pl.when(step == i)
                def _(tasks=tasks):
                    for task in tasks:
                        act[task[0]](*task[1:])

    for source, target in ((bias_buf, biases_ref), (mixed_buf, mixed_ref), (mask, mask_ref)):
        done.append(local(source, target))
    for task in tail[-1]:
        act[task[0]](*task[1:])
    for m in range(micro):
        for c in range(cols):
            leave(m, c, lambda copy: copy.wait())
    for copy in done:
        copy.wait()
    post.close()


def forward(sizes, own, shards, hidden_bias, query_bias, value_bias, segments):
    ns, nr, nc = sizes
    ny = nr // 2
    micro, rows, model = own.shape
    rb, w = shards[4].shape
    halves, floats = own.dtype, jnp.float32
    reach = min(nc - 1, -(-(DOC_MOST - 1) // rows))
    count = (6 + 1) * 2 * (nc - 1) + micro * 4 * reach + 6 * (4 * (ny - 1) + 4 * (ns - 1) + 1)
    anywhere = pl.BlockSpec(memory_space=pl.ANY)
    vmem = pl.BlockSpec(memory_space=pltpu.VMEM)
    length = nc * rows
    arrays = [
        ((2, nc, ns, ny, 2, rb, w), halves), ((nc, ns, ny, 2, rb, w), halves), ((model, micro * length), halves), ((micro, nc, rows, rows), halves),
        ((nc, 8, model), floats), ((nc, micro, rows, WINDOW), halves), ((micro, nc, 8, rows), floats),
        ((micro, nc, rows, WINDOW), halves), ((micro, nc, nc, rows, WINDOW), halves), ((micro, nc, nc, rows, WINDOW), halves),
    ]
    shapes = [pltpu.VMEM(shape, kind) for shape, kind in arrays]
    return pl.pallas_call(
        functools.partial(forward_kernel, sizes, micro),
        out_shape=[jax.ShapeDtypeStruct(shape, kind) for shape, kind in arrays],
        in_specs=[vmem] * 11,
        out_specs=[anywhere] * len(arrays),
        scratch_shapes=[
            pltpu.VMEM((1, nc, ns, ny, 2, rb, w), halves),
            shapes[2], shapes[4], shapes[3], *shapes[5:],
            pltpu.VMEM((micro, nc, rows, model), halves), pltpu.VMEM((WINDOW, rows), floats), pltpu.VMEM((nc, rows, 3 * rows), floats), pltpu.VMEM((length, 3 * rows), halves), pltpu.VMEM((WINDOW, length), halves),
            pltpu.SemaphoreType.DMA((count,)), pltpu.SemaphoreType.DMA((count,)), pltpu.SemaphoreType.DMA((20,)), pltpu.SemaphoreType.DMA((4, micro * nc)),
        ],
        compiler_params=pltpu.CompilerParams(collective_id=2, has_side_effects=True, vmem_limit_bytes=60 << 20),
        name="forward",
    )(own, *shards, hidden_bias, query_bias, value_bias, segments)


def middle_kernel(cols, own_ref, mixed_ref, out_ref, rest_ref, bias_ref, *refs):
    vector_refs = refs[:6]
    (cot_ref, outputs_ref, first_grad_ref, attn_grad_ref, part_ref, sums_ref,
     normal, scale, normed, normed_low, normed_t, grad_low, grad_t, act_buf, slope_buf, total, cot_buf, weight_buf, sems) = refs[6:]
    floats, halves = jnp.float32, jnp.bfloat16
    step = pl.program_id(0)
    rows, model = own_ref.shape
    chunks = [pl.ds(r * 256, 256) for r in range(rows // 256)]
    whole_rows = [pl.ds(0, rows)]
    bands = [pl.ds(n * 256, 256) for n in range(model // 256)]
    loads = [[pltpu.make_async_copy(rest_ref.at[j, c], weight_buf.at[j, c], sems.at[j, c]) for j in range(2)] for c in range(cols)]
    load_cot = pltpu.make_async_copy(cot_ref, cot_buf, sems.at[0, cols])
    vector = lambda i: vector_refs[i][...].astype(floats).reshape(1, -1)

    @pl.when(step == 0)
    def _():
        for pair in loads:
            for copy in pair:
                copy.start()
        load_cot.start()
        sums_ref[...] = jnp.zeros_like(sums_ref)
        for chunk in chunks:
            first_sum = own_ref[chunk].astype(floats) + vector(0)
            for c in range(cols):
                first_sum = first_sum + contract_cols(mixed_ref[c, chunk], out_ref[c])
            normal_one, scale_one = norm_parts(first_sum)
            normal[chunk] = normal_one
            scale[chunk] = jnp.broadcast_to(scale_one, (256, 128))
            norm_one = normal_one * vector(1) + vector(2)
            total[chunk] = norm_one + vector(3)
            normed_low[chunk] = norm_one.astype(halves)
            normed_t[:, chunk] = norm_one.astype(halves).T

    for c in range(cols):
        @pl.when(step == c)
        def _(c=c):
            for copy in loads[c]:
                copy.wait()

    @pl.when(step < cols)
    def _():
        for chunk in chunks:
            for band in bands:
                hidden = jnp.dot(normed_low[chunk], weight_buf[0, step, :, band], preferred_element_type=floats) + bias_ref[0, 0:1, band]
                half_erf = 0.5 * lax.erf(hidden * 0.7071067811865476) + 0.5
                act_buf[step, chunk, band] = (hidden * half_erf).astype(halves)
                slope_buf[step, chunk, band] = (half_erf + hidden * (jnp.exp(-0.5 * hidden * hidden) * 0.3989422804014327)).astype(halves)
        for chunk in chunks:
            for band in bands:
                total[chunk, band] += contract_cols(act_buf[step, chunk], weight_buf[1, step, band, :])

    @pl.when(step == cols - 1)
    def _():
        load_cot.wait()
        for chunk in chunks:
            normal_two, scale_two = norm_parts(total[chunk])
            outputs_ref[chunk] = (normal_two * vector(4) + vector(5)).astype(halves)
            cot = cot_buf[chunk].astype(floats)
            second_grad = norm_back(cot * vector(4), normal_two, scale_two)
            total[chunk] = second_grad
            grad_low[chunk] = second_grad.astype(halves)
            grad_t[:, chunk] = second_grad.astype(halves).T
            sums_ref[3:4] += jnp.sum(second_grad, 0, keepdims=True)
            sums_ref[4:5] += jnp.sum(cot * normal_two, 0, keepdims=True)
            sums_ref[5:6] += jnp.sum(cot, 0, keepdims=True)

    @pl.when(step >= cols)
    def _():
        c = step - cols
        bias_total = [jnp.zeros((1, 256), floats) for _ in bands]
        for chunk in chunks:
            for n, band in enumerate(bands):
                pre = jnp.dot(grad_low[chunk], weight_buf[1, c, :, band], preferred_element_type=floats)
                pre = (pre * slope_buf[c, chunk, band].astype(floats)).astype(halves)
                slope_buf[c, chunk, band] = pre
                bias_total[n] = bias_total[n] + jnp.sum(pre.astype(floats), 0, keepdims=True)
        for n, band in enumerate(bands):
            sums_ref[pl.ds(8 + c, 1), band] = bias_total[n]
        for band in bands:
            for side in [pl.ds(0, model)]:
                part_ref[0, 0, side, band] = jnp.dot(normed_t[side, :], slope_buf[c, :, band], preferred_element_type=floats).astype(halves)
                part_ref[1, 0, side, band] = jnp.dot(grad_t[side, :], act_buf[c, :, band], preferred_element_type=floats).astype(halves)
        for chunk in chunks:
            for band in bands:
                total[chunk, band] += contract_cols(slope_buf[c, chunk], weight_buf[0, c, band, :])

    @pl.when(step == 2 * cols - 1)
    def _():
        for chunk in chunks:
            normed_grad, normal_one = total[chunk], normal[chunk]
            first_grad = norm_back(normed_grad * vector(1), normal_one, scale[chunk, 0:1])
            first_grad_ref[chunk] = first_grad
            attn_grad_ref[chunk] = first_grad.astype(halves)
            sums_ref[0:1] += jnp.sum(first_grad, 0, keepdims=True)
            sums_ref[1:2] += jnp.sum(normed_grad * normal_one, 0, keepdims=True)
            sums_ref[2:3] += jnp.sum(normed_grad, 0, keepdims=True)


def middle(own, mixed, first, rest, biases, vectors, cot):
    rows, model = own.shape
    cols = first.shape[0]
    halves, floats = jnp.bfloat16, jnp.float32
    whole = lambda shape: pl.BlockSpec(shape, lambda i: (0,) * len(shape))
    wide = lambda kind: pltpu.VMEM((rows, model), kind)
    return pl.pallas_call(
        functools.partial(middle_kernel, cols),
        grid=(2 * cols,),
        in_specs=[
            whole((rows, model)), whole(mixed.shape),
            pl.BlockSpec((cols, model, WINDOW), lambda i: (0, 0, O_AT // WINDOW)),
            pl.BlockSpec(memory_space=pl.ANY),
            pl.BlockSpec((1, *biases.shape[1:]), lambda i: (lax.rem(i, cols), 0, 0)),
            *[whole((model,))] * 6, pl.BlockSpec(memory_space=pl.ANY),
        ],
        out_specs=[
            whole((rows, model)), whole((rows, model)), whole((rows, model)),
            pl.BlockSpec((2, 1, model, rest.shape[-1]), lambda i: (0, jnp.maximum(i - cols, 0), 0, 0)),
            whole((8 + cols + -cols % 8, model)),
        ],
        out_shape=[
            jax.ShapeDtypeStruct((rows, model), halves), jax.ShapeDtypeStruct((rows, model), floats),
            jax.ShapeDtypeStruct((rows, model), halves), jax.ShapeDtypeStruct(rest.shape, halves),
            jax.ShapeDtypeStruct((8 + cols + -cols % 8, model), floats),
        ],
        scratch_shapes=[
            wide(floats), pltpu.VMEM((rows, 128), floats), wide(floats), wide(halves), pltpu.VMEM((model, rows), halves), wide(halves),
            pltpu.VMEM((model, rows), halves), pltpu.VMEM((cols, rows, rest.shape[-1]), halves),
            pltpu.VMEM((cols, rows, rest.shape[-1]), halves), wide(floats), wide(halves),
            pltpu.VMEM(rest.shape, halves), pltpu.SemaphoreType.DMA((2, cols + 1)),
        ],
        compiler_params=pltpu.CompilerParams(vmem_limit_bytes=56 << 20),
        name="middle",
    )(own, mixed, first, rest, biases, *vectors, cot)


class Inbox:
    def __init__(self, ref, size):
        self.ref, self.size = ref, size

    def __call__(self, way, e):
        return self.ref.at[0 if self.size == 2 else (1 - way) // 2, e]


def backward_kernel(sizes, micro, grad_ref, share_ref, first_ref, turned_ref, mixed_ref, lse_ref, q_ref, k_ref, v_ref,
                    mask_ref, part_ref, vec_ref,
                    back_ref, block_ref, sums_ref,
                    mine_buf, core_buf, stage_buf, in_a, in_b, in_c, in_d, in_z, tok_buf, tok_in, vec_buf,
                    weights, mixed_buf, q_buf, k_buf, v_buf, every_t, grad_t, mask, acc, spread, block_sum,
                    send_sems, recv_sems, local_sems, free_sem):
    floats, halves = jnp.float32, jnp.bfloat16
    lines, device = place(sizes)
    (x, ns), (y, ny), (k, _), (z, cols) = (lines[a] for a in "xykz")
    model = first_ref.shape[1]
    half = part_ref.shape[-1] // 2
    rb = part_ref.shape[-2]
    rows = grad_ref.shape[1]
    reach = -(-(DOC_MOST - 1) // rows)
    parts = [pl.ds(p * half, half) for p in (0, 1)]
    used = [0]

    def local(source, target):
        copy = pltpu.make_async_copy(source, target, local_sems.at[used[0]])
        used[0] += 1
        copy.start()
        return copy

    def rows_of(n):
        return pl.ds(n % 2 * (rb // 2), rb // 2)

    planes = [local(part_ref.at[n // 2, :, :, :, k, rows_of(n)], mine_buf.at[n // 2 + 1, :, :, :, rows_of(n)]) for n in range(4)]
    loads = [local(*pair) for pair in ((first_ref, weights), (mixed_ref, mixed_buf), (q_ref, q_buf), (share_ref, back_ref))]
    loads += [local(k_ref, k_buf), local(v_ref, v_buf)]
    loads += [local(mask_ref, mask)]
    late = [local(turned_ref, every_t)]
    greet(lines, device)
    post = Post(device, send_sems, recv_sems)

    def give(n):
        post.send(("k", n), lambda: (
            "k", 1 - k, part_ref.at[n // 2, :, :, :, 1 - k, rows_of(n)], core_buf.at[n // 2, :, :, :, rows_of(n)], None))

    def plus(target, source):
        target[...] = target[...] + source[...]

    def plus_grid(target, source, first, second):
        @pl.loop(0, first * second)
        def _(n):
            at = (n // second, lax.rem(n, second))
            plus(target.at[at], source.at[at])

    def plus_row(target, source, first):
        @pl.loop(0, first)
        def _(n):
            plus(target.at[n], source.at[n])

    class Stream:
        def __init__(self, name, j, begin, size, r):
            cs = pl.ds(begin, size)
            self.second = [
                LineReduce(post, (name, "a"), "x", lines["x"], lambda i: mine_buf.at[j, cs, i, :, r, parts[0]],
                           lambda way, e: Inbox(in_a.at[j], ns)(way, e).at[cs, :, r], lambda t, s: plus_grid(t, s, size, ny)),
                LineReduce(post, (name, "b"), "y", lines["y"], lambda i: mine_buf.at[j, cs, :, i, r, parts[1]],
                           lambda way, e: Inbox(in_b.at[j], ny)(way, e).at[cs, :, r], lambda t, s: plus_grid(t, s, size, ns)),
            ]
            self.third = [
                LineReduce(post, (name, "c"), "y", lines["y"], lambda i: mine_buf.at[j, cs, x, i, r, parts[0]],
                           lambda way, e: Inbox(in_c.at[j], ny)(way, e).at[cs, r], lambda t, s: plus_row(t, s, size)),
                LineReduce(post, (name, "d"), "x", lines["x"], lambda i: mine_buf.at[j, cs, i, y, r, parts[1]],
                           lambda way, e: Inbox(in_d.at[j], ns)(way, e).at[cs, r], lambda t, s: plus_row(t, s, size)),
            ]

    def line_z(name, j, r):
        return LineReduce(post, ("z", name), "z", lines["z"], lambda i: mine_buf.at[j, i, x, y, r],
                          lambda way, e: in_z.at[j, (1 - way) // 2, e, r], plus)

    ffn = [Stream(("s", n), n // 2 + 1, 0, cols, rows_of(n)) for n in range(4)]
    ffn_z = [line_z(n, n // 2 + 1, rows_of(n)) for n in range(4)]
    attn = [Stream(("u", c), 0, c, 1, pl.ds(0, rb)) for c in range(cols)]

    def take_y(c, e):
        reduce_to(post, ("y", c), "z", lines["z"], c, e, mine_buf.at[0, c, x, y], lambda way, e: in_z.at[0, (1 - way) // 2, e], plus)

    def half_of(h):
        return pl.ds(h * (rows // 2), rows // 2)

    def line_tokens(m, h):
        at = half_of(h)
        return LineReduce(post, ("t", m, h), "z", lines["z"], lambda i: tok_buf.at[m, i, at],
                          lambda way, e: tok_in.at[m, (1 - way) // 2, e, at], plus, reach)

    tokens = [[line_tokens(m, h) for h in range(2)] for m in range(micro)]

    def start(*group):
        for line in group:
            line.start()

    def finish(*group):
        for line in group:
            line.finish()

    def core(n):
        planes[n].wait()
        r = rows_of(n)
        post.wait(("k", n), "k", 1 - k, core_buf.at[n // 2, :, :, :, r])

        @pl.loop(0, cols * ns * ny)
        def _(i):
            at = (i // (ns * ny), lax.rem(i // ny, ns), lax.rem(i, ny), r)
            plus(mine_buf.at[(n // 2 + 1, *at)], core_buf.at[(n // 2, *at)])

    def vector_start(stage, axis):
        mine, size = lines[axis]
        vec_buf[stage, 1 + mine] = vec_buf[stage, 0]
        for t in range(1, size):
            post.send(("v", stage, t), lambda t=t: (
                axis, lax.rem(mine + t, size), vec_buf.at[stage, 0], vec_buf.at[stage, 1 + mine], None))

    def vector_finish(stage, axis, out):
        mine, size = lines[axis]
        for t in range(1, size):
            origin = lax.rem(mine + size - t, size)
            post.wait(("v", stage, t), axis, origin, vec_buf.at[stage, 1 + origin])
        total = vec_buf[stage, 1]
        for i in range(1, size):
            total = total + vec_buf[stage, 1 + i]
        out[...] = total

    places = place_of(rows)
    small = vec_ref.shape[0]
    vec_buf[0, 0] = jnp.zeros_like(vec_buf[0, 0])
    vec_buf[0, 0, 0:small] = vec_ref[...]

    def unit(m, c):
        mixed_grad = jnp.dot(grad_ref[m], weights[c, :, O_AT : O_AT + WINDOW], preferred_element_type=floats).astype(halves)
        mixed_grad = jnp.where(places > 0, mixed_grad.astype(floats), 0.0)
        product = mixed_grad * mixed_buf[c, m].astype(floats)
        product_high = product.astype(halves)
        product_low = (product - product_high.astype(floats)).astype(halves)
        pick = (
            lax.broadcasted_iota(jnp.int32, (8, WINDOW), 1) // HEAD_DIM == lax.broadcasted_iota(jnp.int32, (8, WINDOW), 0) + 1
        ).astype(floats).astype(halves)
        inner = contract_cols(pick, product_high) + contract_cols(pick, product_low)
        value_side = pltpu.roll(mixed_grad, WINDOW - HEAD_DIM, 1).astype(halves)
        queries = q_buf[m, c]
        query_heads = jnp.concatenate([keep(queries, places, h + 1) for h in range(3)], 0)
        grad_heads = jnp.concatenate([keep(value_side, places, h) for h in range(3)], 0)
        side_by_side = lambda ref_rows: jnp.concatenate([ref_rows(h) for h in range(3)], 1)
        log_total = side_by_side(lambda h: lse_ref[m, c, h : h + 1])
        inner_row = side_by_side(lambda h: inner[h : h + 1])
        acc[...] = jnp.zeros_like(acc)
        key_weight = weights[c, :, K_AT : K_AT + WINDOW]
        value_weight = weights[c, :, V_AT : V_AT + WINDOW]

        def step(block, value_bias):
            keys = k_buf[m, c, block]
            values = v_buf[m, c, block]
            keys_t = keys.T
            hidden = mask[m, block].astype(floats)
            hidden = jnp.concatenate([hidden] * 3, 1)
            p = jnp.exp(contract_cols(keys, query_heads) + hidden - log_total)
            prob_grad = contract_cols(values, grad_heads)
            score_grad = (p * (prob_grad - inner_row)).astype(halves)
            value_grad = jnp.dot(p.astype(halves), grad_heads, preferred_element_type=floats)
            key_grad = jnp.dot(score_grad, query_heads, preferred_element_type=floats)
            for h in range(3):
                acc[pl.ds(h * HEAD_DIM, HEAD_DIM), :] += jnp.dot(
                    keys_t[(h + 1) * HEAD_DIM : (h + 2) * HEAD_DIM], score_grad[:, h * rows : (h + 1) * rows], preferred_element_type=floats)
            key_low, value_low = key_grad.astype(halves), value_grad.astype(halves)
            k_buf[m, c, block] = key_low
            v_buf[m, c, block] = value_low
            spread[m, block] += contract_cols(key_low, key_weight) + contract_cols(value_low, value_weight)
            return value_bias + jnp.sum(value_low.astype(floats), 0, keepdims=True)

        value_bias = jnp.zeros((1, WINDOW), floats)
        for block in range(cols):
            value_bias = step(block, value_bias)
        query_low = (acc[...].T * HEAD_DIM ** -0.5).astype(halves)
        q_buf[m, c] = query_low
        vec_buf[0, 0, pl.ds(small + c, 1), 0:WINDOW] += jnp.sum(query_low.astype(floats), 0, keepdims=True)
        vec_buf[0, 0, pl.ds(small + c, 1), WINDOW : 2 * WINDOW] += value_bias
        back_ref[m] += contract_cols(query_low, weights[c, :, Q_AT : Q_AT + WINDOW])

    def send_tokens(m):
        back_ref[m] += spread[m, z]

        @pl.loop(0, cols)
        def _(block):
            tok_buf[m, block] = spread[m, block].astype(halves)

        start(*tokens[m])

    def weight_grads(c):
        strip = block_sum.shape[0]

        @pl.loop(0, model // strip)
        def _(part):
            base = pl.multiple_of(part * strip, strip)
            side = pl.ds(base, strip)
            block_sum[...] = jnp.zeros_like(block_sum)
            for m in range(micro):
                mine_at = pl.ds(pl.multiple_of((m * cols + z) * rows, rows), rows)
                block_sum[:, Q_AT : Q_AT + WINDOW] += jnp.dot(every_t[side, mine_at], q_buf[m, c], preferred_element_type=floats)
                all_at = pl.ds(m * cols * rows, cols * rows)
                block_sum[:, K_AT : K_AT + WINDOW] += jnp.dot(
                    every_t[side, all_at], k_buf[m, c].reshape(-1, WINDOW), preferred_element_type=floats)
                block_sum[:, V_AT : V_AT + WINDOW] += jnp.dot(
                    every_t[side, all_at], v_buf[m, c].reshape(-1, WINDOW), preferred_element_type=floats)
                block_sum[:, O_AT : O_AT + WINDOW] += jnp.dot(
                    grad_t[side, m * rows : (m + 1) * rows], mixed_buf[c, m], preferred_element_type=floats)
            for i in range(strip // (2 * rb)):
                ours = pl.ds(pl.multiple_of((2 * i + k) * rb, 16), rb)
                theirs = pl.ds(pl.multiple_of((2 * i + 1 - k) * rb, 16), rb)
                chip = part * (strip // (2 * rb)) + i
                mine_buf[0, c, chip // ny, lax.rem(chip, ny)] = block_sum[ours].astype(halves)
                stage_buf[c, chip // ny, lax.rem(chip, ny)] = block_sum[theirs].astype(halves)

    waited = []

    def attn_give(c):
        if not waited:
            pl.semaphore_wait(free_sem, 1)
            waited.append(c)
        post.send(("g", c), lambda: ("k", 1 - k, stage_buf.at[c], core_buf.at[0, c], None))

    def attn_add(c):
        post.wait(("g", c), "k", 1 - k, core_buf.at[0, c])

        @pl.loop(0, ns * ny)
        def _(n):
            at = (c, n // ny, lax.rem(n, ny))
            plus(mine_buf.at[(0, *at)], core_buf.at[(0, *at)])

    streams = ffn + attn
    added = set()

    def take_core(n):
        if n < 4:
            core(n)
            added.add(n)
            if added >= {0, 1} and n in (0, 1):
                pl.semaphore_signal(free_sem, 1, device_id=device("k", 1 - k), device_id_type=MESH)
        else:
            attn_add(n - 4)
        start(*streams[n].second)

    def take_second(n):
        finish(*streams[n].second)
        start(*streams[n].third)

    def take_third(n):
        finish(*streams[n].third)
        if n < 4:
            start(ffn_z[n])

    def along(line, e):
        for way in (1, -1):
            line.take(way, e)
            if e:
                line.forward(way, e)

    def take_tokens(m, h, e):
        line = tokens[m][h]
        if e == 0:
            at = half_of(h)

            def add(target, source):
                back_ref[m, at] += source[...].astype(floats)

            line.add = add
        along(line, e)

    def vectors(stage):
        if stage:
            vector_finish(stage - 1, "kyxz"[stage - 1], vec_buf.at[stage, 0] if stage < 4 else sums_ref)
        if stage < 4:
            vector_start(stage, "kyxz"[stage])

    def load():
        for copy in loads:
            copy.wait()

    act = {
        "L": load, "G": lambda n: give(n) if n < 4 else attn_give(n - 4), "A": take_core, "B": take_second, "C": take_third,
        "Z": lambda n, e: along(ffn_z[n], e), "S": send_tokens, "T": take_tokens, "Y": take_y, "V": vectors,
    }
    head, tail, order = split_plan([("U", "W", task[1], 0) if task[0] == "W" else task for task in BACKWARD_PLAN])
    kinds = [item[0] == "W" for item in order]
    heads = [item[1] if item[0] == "W" else item[0] for item in order]
    micros = [0 if item[0] == "W" else item[1] for item in order]
    act[head[0][0]](*head[0][1:])
    spread[...] = jnp.zeros_like(spread)
    for m in range(micro):
        grad_t[:, m * rows : (m + 1) * rows] = grad_ref[m].T
    for task in head[1:]:
        act[task[0]](*task[1:])

    @pl.loop(0, len(order))
    def _(step):
        c, m, kind = pick(step, heads), pick(step, micros), pick(step, [int(k_) for k_ in kinds])

        @pl.when(kind == 0)
        def _():
            unit(m, c)

        @pl.when(kind == 1)
        def _():
            @pl.when(step == kinds.index(True))
            def _():
                for copy in late:
                    copy.wait()

            weight_grads(c)

        for i, tasks in enumerate(tail[:-1]):
            if tasks:
                @pl.when(step == i)
                def _(tasks=tasks):
                    for task in tasks:
                        act[task[0]](*task[1:])

    for task in tail[-1]:
        act[task[0]](*task[1:])
    for j in range(3):
        block_ref[j] = mine_buf[j, z, x, y].astype(floats)
    post.close()


def backward(sizes, grad, share, first, turned, mixed, lse, q, k, v, mask, part, vectors):
    ns, nr, nc = sizes
    ny = nr // 2
    micro, rows, model = grad.shape
    w = part.shape[-1]
    rb = model // (ns * nr)
    halves, floats = jnp.bfloat16, jnp.float32
    reach = min(nc - 1, -(-(DOC_MOST - 1) // rows))
    streams = 4 + nc
    count = 4 + nc + 4 * (ny - 1 + ns - 1) * streams + 4 * 2 * (nc - 1) + 2 * nc * 2 + micro * 4 * reach + (1 + ny - 1 + ns - 1 + nc - 1)
    widest = max(ns, ny, nc, 2)
    ways = lambda n: 1 if n == 2 else 2
    vec_shape = (vectors.shape[0] + nc + -nc % 8, model)
    vmem = pl.BlockSpec(memory_space=pltpu.VMEM)
    anywhere = pl.BlockSpec(memory_space=pl.ANY)
    buf = lambda *shape, kind=halves: pltpu.VMEM(shape, kind)
    return pl.pallas_call(
        functools.partial(backward_kernel, sizes, micro),
        out_shape=[
            jax.ShapeDtypeStruct((micro, rows, model), floats),
            jax.ShapeDtypeStruct((3, rb, w), floats),
            jax.ShapeDtypeStruct(vec_shape, floats),
        ],
        in_specs=[vmem, anywhere, anywhere, anywhere, anywhere, vmem, anywhere, anywhere, anywhere, anywhere, anywhere, vmem],
        out_specs=[vmem] * 3,
        scratch_shapes=[
            buf(3, nc, ns, ny, rb, w), buf(2, nc, ns, ny, rb, w), buf(nc, ns, ny, rb, w),
            buf(3, ways(ns), max(ns - 1, 1), nc, ny, rb, w // 2), buf(3, ways(ny), max(ny - 1, 1), nc, ns, rb, w // 2),
            buf(3, ways(ny), max(ny - 1, 1), nc, rb, w // 2), buf(3, ways(ns), max(ns - 1, 1), nc, rb, w // 2),
            buf(3, 2, max(nc - 1, 1), rb, w), buf(micro, nc, rows, model), buf(micro, 2, max(reach, 1), rows, model),
            buf(4, 1 + widest, *vec_shape, kind=floats),
            buf(nc, model, w), buf(nc, micro, rows, WINDOW), buf(micro, nc, rows, WINDOW),
            buf(micro, nc, nc, rows, WINDOW), buf(micro, nc, nc, rows, WINDOW),
            buf(model, micro * nc * rows), buf(model, micro * rows),
            buf(micro, nc, rows, rows), buf(WINDOW, rows, kind=floats), buf(micro, nc, rows, model, kind=floats), buf(model // 2, w, kind=floats),
            pltpu.SemaphoreType.DMA((count,)), pltpu.SemaphoreType.DMA((count,)), pltpu.SemaphoreType.DMA((24,)), pltpu.SemaphoreType.REGULAR,
        ],
        compiler_params=pltpu.CompilerParams(collective_id=3, has_side_effects=True, vmem_limit_bytes=62 << 20),
        name="backward",
    )(grad, share, first, turned, mixed, lse, q, k, v, mask,
      part.reshape(2, nc, ns, ny, 2, rb, w), vectors)


def per_device_plain(sizes, inputs, segment_ids, query_weight, key_weight, value_weight, query_bias, value_bias,
               output_weight, output_bias, first_gain, first_shift, hidden_weight, hidden_bias, down_weight,
               down_bias, second_gain, second_shift, cotangent):
    floats, halves = jnp.float32, jnp.bfloat16
    cols = sizes[2]
    micro, _, rows, model = inputs.shape
    length = segment_ids.shape[-1]
    width = query_weight.shape[1]
    here = lax.axis_index("col")
    own = inputs[:, 0]
    shard = jnp.stack([
        jnp.concatenate([query_weight, key_weight, value_weight, output_weight.T], 1),
        hidden_weight,
        down_weight.T,
    ])
    biases = lax.all_gather(jnp.concatenate([query_bias, value_bias, hidden_bias]), "col", axis=0)
    everything, gathered = gather(sizes, own, shard)
    everything = everything.reshape(micro, length, model)
    attn_weights = gathered[0]
    wq, wk, wv, wot = (attn_weights[:, :, i * width : (i + 1) * width] for i in range(4))
    hidden_full, down_full = gathered[1], gathered[2]
    bq, bv, bh = biases[:, :width], biases[:, width : 2 * width], biases[:, 2 * width :]
    seg_all = segment_ids[:, 0]
    seg_own = lax.dynamic_slice_in_dim(seg_all, here * rows, rows, 1)
    first_key = jnp.sum((seg_all < seg_own[:, :1]).astype(jnp.int32), 1)
    last_key = jnp.sum((seg_all <= seg_own[:, -1:]).astype(jnp.int32), 1)
    bounds = jnp.stack([first_key // KEY_BLOCK, (last_key + KEY_BLOCK - 1) // KEY_BLOCK], 1)

    mixed, lse, q, k, v = attend(bounds, own, everything, wq, wk, wv, bq.astype(floats), bv.astype(floats), seg_own, seg_all)
    total = micro * rows
    flat = lambda a: a.reshape(total, -1)
    mixed_flat = mixed.reshape(cols, total, width)
    attn = sum(contract_cols(mixed_flat[c], wot[c]) for c in range(cols))
    first_sum = flat(own).astype(floats) + attn + output_bias.astype(floats)
    normal_one, scale_one = norm_parts(first_sum)
    gain_one = first_gain.astype(floats)
    normed = normal_one * gain_one + first_shift.astype(floats)
    normed_low = normed.astype(halves)
    ffn = 0
    activated, slopes = [], []
    for c in range(cols):
        hidden = jnp.dot(normed_low, hidden_full[c], preferred_element_type=floats) + bh[c].astype(floats)
        half_erf = 0.5 * lax.erf(hidden * 0.7071067811865476) + 0.5
        act = (hidden * half_erf).astype(halves)
        slope = half_erf + hidden * (jnp.exp(-0.5 * hidden * hidden) * 0.3989422804014327)
        activated.append(act)
        slopes.append(slope.astype(halves))
        ffn = ffn + contract_cols(act, down_full[c])
    second_sum = normed + ffn + down_bias.astype(floats)
    normal_two, scale_two = norm_parts(second_sum)
    gain_two = second_gain.astype(floats)
    outputs = (normal_two * gain_two + second_shift.astype(floats)).astype(halves)
    cot = flat(cotangent[:, 0]).astype(floats)
    second_grad = norm_back(cot * gain_two, normal_two, scale_two)
    ffn_grad = second_grad.astype(halves)
    hidden_grads, down_grads, hidden_bias_grads = [], [], []
    normed_grad = second_grad
    for c in range(cols):
        pre = (jnp.dot(ffn_grad, down_full[c], preferred_element_type=floats) * slopes[c].astype(floats)).astype(halves)
        hidden_grads.append(contract_rows(normed_low, pre).astype(halves))
        down_grads.append(contract_rows(ffn_grad, activated[c]).astype(halves))
        hidden_bias_grads.append(jnp.sum(pre.astype(floats), 0))
        normed_grad = normed_grad + contract_cols(pre, hidden_full[c])
    first_grad = norm_back(normed_grad * gain_one, normal_one, scale_one)
    attn_grad = first_grad.astype(halves)
    dq, dk, dv = attend_back(bounds, attn_grad.reshape(micro, rows, model), wot, mixed, lse, q, k, v, seg_own, seg_all)
    every_flat = everything.reshape(micro * length, model)
    attn_grads = []
    own_share = first_grad
    spread = 0
    for c in range(cols):
        dq_c, dk_c, dv_c = dq[c].reshape(total, width), dk[c].reshape(micro * length, width), dv[c].reshape(micro * length, width)
        attn_grads.append(jnp.concatenate([
            contract_rows(flat(own), dq_c), contract_rows(every_flat, dk_c), contract_rows(every_flat, dv_c),
            contract_rows(attn_grad, mixed_flat[c]),
        ], 1).astype(halves))
        own_share = own_share + contract_cols(dq_c, wq[c])
        spread = spread + contract_cols(dk_c, wk[c]) + contract_cols(dv_c, wv[c])
    bias_q = jnp.sum(dq.astype(floats), (1, 2)).reshape(-1)
    bias_v = jnp.sum(dv.astype(floats), (1, 2)).reshape(-1)
    vectors = jnp.concatenate([
        jnp.sum(first_grad, 0), jnp.sum(normed_grad * normal_one, 0), jnp.sum(normed_grad, 0), jnp.sum(second_grad, 0),
        jnp.sum(cot * normal_two, 0), jnp.sum(cot, 0), bias_q, bias_v, *hidden_bias_grads,
    ]).reshape(-1, model)
    partial = jnp.stack([jnp.stack(attn_grads), jnp.stack(hidden_grads), jnp.stack(down_grads)])
    input_grad, reduced, sums = reduce(sizes, own_share.reshape(micro, rows, model),
                                       spread.astype(halves).reshape(micro, cols, rows, model), partial, vectors)
    attn_block = reduced[0]
    piece = lambda i: attn_block[:, i * width : (i + 1) * width]
    mine = lambda vector, size: lax.dynamic_slice_in_dim(vector.reshape(-1), here * size, size, 0)
    return (
        outputs.reshape(micro, 1, rows, model), input_grad[:, None],
        piece(0), piece(1), piece(2), mine(sums[6], width), mine(sums[7], width), piece(3).T,
        sums[0], sums[1], sums[2], reduced[1], mine(sums[8:], hidden_bias.shape[0]), reduced[2].T,
        sums[3], sums[4], sums[5],
    )


def deliver_kernel(sizes, width, back_hbm, block_hbm, sums_hbm, *refs):
    *outs, back_ref, block_ref, sums_ref, sems = refs
    copies = [
        pltpu.make_async_copy(source, target, sems.at[i])
        for i, (source, target) in enumerate(((block_hbm, block_ref), (sums_hbm, sums_ref), (back_hbm, back_ref)))
    ]
    for copy in copies:
        copy.start()
    (input_grad, query, key, value, query_bias, value_bias, output, output_bias, first_gain, first_shift, hidden, hidden_bias, down,
     down_bias, second_gain, second_shift) = outs
    here = lax.axis_index("col")
    for copy in copies[:2]:
        copy.wait()
    for i, ref in enumerate((query, key, value)):
        ref[...] = block_ref[0, :, i * width : (i + 1) * width]
    output[...] = block_ref[0, :, 3 * width : 4 * width].T
    hidden[...] = block_ref[1]
    down[...] = block_ref[2]
    for i, ref in enumerate((output_bias, first_gain, first_shift, down_bias, second_gain, second_shift)):
        ref[...] = sums_ref[i : i + 1].reshape(-1)
    hidden_bias[...] = sums_ref[pl.ds(8 + here, 1)].reshape(-1)
    heads_at = sums_ref.shape[0] - (sizes[2] + -sizes[2] % 8)
    row = sums_ref[pl.ds(heads_at + here, 1)]
    query_bias[...] = row[:, 0:width].reshape(-1)
    value_bias[...] = row[:, WINDOW : WINDOW + width].reshape(-1)
    copies[2].wait()
    input_grad[...] = back_ref[...]


def deliver(sizes, width, back, blocks, sums):
    model = sums.shape[1]
    _, rb, w = blocks.shape
    vmem = pl.BlockSpec(memory_space=pltpu.VMEM)
    square, vector = (rb, width), (model,)
    shapes = [back.shape, square, square, square, (width,), (width,), (width, rb), vector, vector, vector, (rb, w), (w,), (rb, w),
              vector, vector, vector]
    return pl.pallas_call(
        functools.partial(deliver_kernel, sizes, width),
        out_shape=[jax.ShapeDtypeStruct(shape, jnp.float32) for shape in shapes],
        in_specs=[pl.BlockSpec(memory_space=pltpu.MemorySpace.HBM)] * 3,
        out_specs=[vmem] * len(shapes),
        scratch_shapes=[pltpu.VMEM(a.shape, jnp.float32) for a in (back, blocks, sums)] + [pltpu.SemaphoreType.DMA((3,))],
        compiler_params=pltpu.CompilerParams(vmem_limit_bytes=32 << 20),
        name="deliver",
    )(back, blocks, sums)


def per_device_fused(sizes, inputs, segment_ids, query_weight, key_weight, value_weight, query_bias, value_bias,
               output_weight, output_bias, first_gain, first_shift, hidden_weight, hidden_bias, down_weight,
               down_bias, second_gain, second_shift, cotangent):
    floats, halves = jnp.float32, jnp.bfloat16
    cols = sizes[2]
    micro, _, rows, model = inputs.shape
    length = segment_ids.shape[-1]
    width = query_weight.shape[1]
    here = lax.axis_index("col")
    own = inputs[:, 0]
    rest, first, turned, mask, biases, mixed, lse, q, k, v = forward(
        sizes, own, (query_weight, key_weight, value_weight, output_weight, hidden_weight, down_weight.T), hidden_bias, query_bias, value_bias, segment_ids)
    first = first.reshape(cols, model, 4 * width)
    total = micro * rows
    flat = lambda a: a.reshape(total, -1)
    outputs, first_grad, attn_grad, part, sums = middle(
        flat(own), mixed.reshape(cols, total, WINDOW), first, rest.reshape(2, cols, model, -1), biases,
        (output_bias, first_gain, first_shift, down_bias, second_gain, second_shift), flat(cotangent[:, 0]))
    parted = lambda a: a.reshape(micro, rows, model)
    input_grad, reduced, sums = backward(sizes, parted(attn_grad), parted(first_grad), first, turned, mixed, lse, q, k, v,
                                         mask, part, sums)
    grads = deliver(sizes, width, input_grad, reduced, sums)
    return (outputs.reshape(micro, 1, rows, model), grads[0][:, None], *grads[1:12], grads[12].T, *grads[13:])


def per_device(sizes, inputs, segment_ids, query_weight, *rest):
    micro, _, rows, _ = inputs.shape
    fits = (query_weight.shape == (query_weight.shape[0] // 32 * 32, 3 * HEAD_DIM) and micro == 2 and sizes[2] == 4
            and DOC_MOST // 2 == rows)
    return (per_device_fused if fits else per_device_plain)(sizes, inputs, segment_ids, query_weight, *rest)


def solution(mesh):
    sizes = tuple(mesh.shape[name] for name in ("seq", "row", "col"))
    block, line = P(("seq", "row"), "col"), P("col", ("seq", "row"))
    tokens = P(None, ("seq", "row"), "col", None)
    placed = (tokens, P(None, ("seq", "row"), None), block, block, block, P("col"), P("col"), line, P(), P(), P(),
              block, P("col"), line, P(), P(), P(), tokens)
    given = (tokens, tokens, block, block, block, P("col"), P("col"), line, P(), P(), P(), block, P("col"), line,
             P(), P(), P())
    return jax.shard_map(functools.partial(per_device, sizes), mesh=mesh, in_specs=placed, out_specs=given, check_vma=False)
```

```python
import functools

import jax
import jax.numpy as jnp
from jax import lax
from jax.experimental import pallas as pl
from jax.experimental.pallas import tpu as pltpu
from jax.sharding import PartitionSpec as P

HEAD_DIM = 64
NORM_EPS = 1e-05
MASK_VALUE = -1000000000.0
DOC_MOST = 512
KEY_BLOCK = 256
MESH = pl.DeviceIdType.MESH


def contract_rows(left, right):
    return lax.dot_general(
        left, right, (((0,), (0,)), ((), ())), preferred_element_type=jnp.float32
    )


def contract_cols(left, right):
    return lax.dot_general(
        left, right, (((1,), (1,)), ((), ())), preferred_element_type=jnp.float32
    )


def norm_parts(summed):
    deviation = summed - jnp.mean(summed, -1, keepdims=True)
    scale = lax.rsqrt(jnp.mean(deviation * deviation, -1, keepdims=True) + NORM_EPS)
    return deviation * scale, scale


def norm_back(pull, normal, scale):
    return scale * (
        pull - jnp.mean(pull, -1, keepdims=True) - normal * jnp.mean(pull * normal, -1, keepdims=True)
    )

FORWARD_PLAN = (
    ("Zs", 1), ("Zs", 0), ("Z", 1, 1), ("Z", 0, 1), ("Z", 1, 2), ("Z", 1, 3), ("Zs", 4), ("Z", 0, 2), ("Ts", 1),
    ("Zs", 2), ("Z", 0, 3), ("Zs", 5), ("B", 1), ("B", 0), ("Z", 4, 1), ("Z", 2, 1), ("Zs", 3), ("Z", 5, 1),
    ("Z", 4, 2), ("Z", 4, 3), ("Z", 3, 1), ("Z", 2, 2), ("Z", 2, 3), ("T", 1, 1), ("C", 0), ("Ts", 0), ("B", 4),
    ("C", 1), ("Z", 3, 2), ("Z", 5, 2), ("K", 1), ("Z", 3, 3), ("Z", 5, 3), ("T", 0, 1), ("K", 0), ("C", 4),
    ("Ts", 3), ("T", 1, 2), ("B", 2), ("P", 0, 0), ("P", 0, 1), ("Ts", 2), ("T", 0, 2), ("R", 0), ("U", 0, 0),
    ("P", 0, 2), ("U", 0, 1), ("T", 3, 1), ("B", 3), ("U", 0, 2), ("P", 0, 3), ("T", 2, 1), ("P", 1, 0), ("P", 1, 1),
    ("P", 1, 2), ("K", 4), ("C", 2), ("B", 5), ("P", 1, 3), ("C", 3), ("U", 0, 3), ("T", 3, 2), ("T", 2, 2), ("R", 1),
    ("U", 1, 0), ("U", 1, 1), ("C", 5), ("U", 1, 2), ("K", 2), ("K", 3), ("U", 1, 3), ("K", 5),
)
BACKWARD_PLAN = (
    ("G", 1), ("G", 3), ("L",), ("U", 2, 0), ("A", 1), ("G", 0), ("U", 0, 0), ("A", 3), ("U", 1, 0), ("U", 3, 0),
    ("S", 0), ("G", 2), ("B", 1), ("A", 0), ("U", 0, 1), ("A", 2), ("B", 3), ("T", 0, 0, 1), ("C", 1), ("U", 2, 1),
    ("U", 1, 1), ("T", 0, 1, 1), ("U", 3, 1), ("S", 1), ("B", 2), ("W", 2), ("V", 0), ("G", 6), ("B", 0), ("W", 3),
    ("V", 1), ("Z", 1, 2), ("A", 6), ("G", 7), ("C", 3), ("W", 0), ("C", 2), ("G", 4), ("A", 7), ("T", 1, 1, 1),
    ("W", 1), ("Z", 3, 2), ("V", 2), ("G", 5), ("C", 0), ("A", 4), ("B", 7), ("V", 3), ("A", 5), ("Z", 1, 1),
    ("B", 4), ("Z", 2, 2), ("C", 7), ("T", 1, 0, 1), ("B", 6), ("Y", 3, 3), ("B", 5), ("T", 1, 1, 0), ("Z", 3, 1),
    ("C", 4), ("C", 6), ("Y", 0, 3), ("Z", 0, 2), ("Y", 2, 2), ("T", 0, 1, 0), ("C", 5), ("Y", 1, 2), ("V", 4),
    ("Y", 3, 2), ("Y", 0, 2), ("Z", 0, 1), ("Z", 1, 0), ("T", 1, 0, 0), ("Z", 2, 1), ("Z", 3, 0), ("Y", 3, 1),
    ("Y", 2, 1), ("Y", 1, 1), ("T", 0, 0, 0), ("Y", 0, 1), ("Z", 0, 0), ("Z", 2, 0), ("Y", 2, 0), ("Y", 3, 0),
    ("Y", 1, 0), ("Y", 0, 0),
)
def attend_kernel(bounds, own_ref, all_ref, wq_ref, wk_ref, wv_ref, bq_ref, bv_ref,
                  segq_ref, segk_ref, mixed_ref, lse_ref, q_ref, k_ref, v_ref, bias, acc, top, total):
    micro = pl.program_id(0)
    low, high = bounds[micro, 0], bounds[micro, 1]
    floats, halves = jnp.float32, jnp.bfloat16
    width = wq_ref.shape[-1]
    heads = width // HEAD_DIM
    rows = own_ref.shape[1]

    @pl.when(pl.program_id(1) == 0)
    def _():
        same = segk_ref[0] == segq_ref[0, 0:1]
        bias[...] = jnp.where(same, 0.0, MASK_VALUE)

    queries = jnp.dot(own_ref[0], wq_ref[0], preferred_element_type=floats) + bq_ref[0]
    queries = queries.astype(halves) * jnp.asarray(HEAD_DIM ** -0.5, halves)
    q_ref[0, 0] = queries
    lane = lax.broadcasted_iota(jnp.int32, (rows, width), 1) // HEAD_DIM
    query_heads = [jnp.where(lane == h, queries, jnp.zeros_like(queries)) for h in range(heads)]
    acc[...] = jnp.zeros_like(acc)
    total[...] = jnp.zeros_like(total)
    top[...] = jnp.full_like(top, 2 * MASK_VALUE)

    def step(block, carry):
        at = pl.ds(pl.multiple_of(block * KEY_BLOCK, KEY_BLOCK), KEY_BLOCK)
        x = all_ref[0, at, :]
        keys = jnp.dot(x, wk_ref[0], preferred_element_type=floats).astype(halves)
        k_ref[0, 0, at, :] = keys
        values = (jnp.dot(x, wv_ref[0], preferred_element_type=floats) + bv_ref[0]).astype(halves)
        v_ref[0, 0, at, :] = values
        values_t = values.T
        mask = bias[at, :]
        for h in range(heads):
            s = contract_cols(keys, query_heads[h]) + mask
            old = top[h : h + 1]
            new = jnp.maximum(old, jnp.max(s, 0, keepdims=True))
            p = jnp.exp(s - new)
            shrink = jnp.exp(old - new)
            top[h : h + 1] = new
            total[h : h + 1] = total[h : h + 1] * shrink + jnp.sum(p, 0, keepdims=True)
            part = pl.ds(h * HEAD_DIM, HEAD_DIM)
            acc[part, :] = acc[part, :] * shrink + jnp.dot(
                values_t[h * HEAD_DIM : (h + 1) * HEAD_DIM], p.astype(halves), preferred_element_type=floats
            )
        return carry

    lax.fori_loop(low, high, step, 0)
    for h in range(heads):
        part = pl.ds(h * HEAD_DIM, HEAD_DIM)
        acc[part, :] = acc[part, :] / total[h : h + 1]
    mixed_ref[0, 0] = acc[...].T.astype(halves)
    lse_ref[0, 0] = top[...] + jnp.log(jnp.maximum(total[...], 1e-30))


def attend(bounds, own, everything, wq, wk, wv, bq, bv, seg_own, seg_all):
    micro, rows, model = own.shape
    length = everything.shape[1]
    cols, _, width = wq.shape
    halves = jnp.bfloat16
    weight = pl.BlockSpec((1, model, width), lambda m, c, b: (c, 0, 0))
    per = lambda a, b_: pl.BlockSpec((1, 1, a, b_), lambda m, c, b: (c, m, 0, 0))
    spec = pltpu.PrefetchScalarGridSpec(
        num_scalar_prefetch=1,
        grid=(micro, cols),
        in_specs=[
            pl.BlockSpec((1, rows, model), lambda m, c, b: (m, 0, 0)),
            pl.BlockSpec((1, length, model), lambda m, c, b: (m, 0, 0)),
            weight, weight, weight,
            pl.BlockSpec((1, 1, width), lambda m, c, b: (c, 0, 0)),
            pl.BlockSpec((1, 1, width), lambda m, c, b: (c, 0, 0)),
            pl.BlockSpec((1, 1, rows), lambda m, c, b: (m, 0, 0)),
            pl.BlockSpec((1, length, 1), lambda m, c, b: (m, 0, 0)),
        ],
        out_specs=[per(rows, width), per(8, rows), per(rows, width), per(length, width), per(length, width)],
        scratch_shapes=[
            pltpu.VMEM((length, rows), jnp.float32),
            pltpu.VMEM((width, rows), jnp.float32),
            pltpu.VMEM((8, rows), jnp.float32),
            pltpu.VMEM((8, rows), jnp.float32),
        ],
    )
    shape = lambda a, b_, d=halves: jax.ShapeDtypeStruct((cols, micro, a, b_), d)
    return pl.pallas_call(
        attend_kernel,
        grid_spec=spec,
        out_shape=[shape(rows, width), shape(8, rows, jnp.float32), shape(rows, width), shape(length, width), shape(length, width)],
        compiler_params=pltpu.CompilerParams(vmem_limit_bytes=48 << 20),
        name="attend",
    )(bounds, own, everything, wq, wk, wv, bq[:, None], bv[:, None],
      seg_own[:, None], seg_all[:, :, None])


def attend_back_kernel(bounds, grad_ref, wot_ref, mixed_ref, lse_ref, q_ref, k_ref, v_ref, segq_ref, segk_ref,
                       dq_ref, dk_ref, dv_ref, bias, acc):
    micro = pl.program_id(0)
    low, high = bounds[micro, 0], bounds[micro, 1]
    floats, halves = jnp.float32, jnp.bfloat16
    rows, width = q_ref.shape[2:]
    heads = width // HEAD_DIM

    @pl.when(pl.program_id(1) == 0)
    def _():
        same = segk_ref[0] == segq_ref[0, 0:1]
        bias[...] = jnp.where(same, 0.0, MASK_VALUE)

    mixed_grad = jnp.dot(grad_ref[0], wot_ref[0], preferred_element_type=floats).astype(halves)
    product = mixed_grad.astype(floats) * mixed_ref[0, 0].astype(floats)
    product_high = product.astype(halves)
    product_low = (product - product_high.astype(floats)).astype(halves)
    pick = (
        lax.broadcasted_iota(jnp.int32, (8, width), 1) // HEAD_DIM == lax.broadcasted_iota(jnp.int32, (8, width), 0)
    ).astype(halves)
    inner = contract_cols(pick, product_high) + contract_cols(pick, product_low)
    lane = lax.broadcasted_iota(jnp.int32, (rows, width), 1) // HEAD_DIM
    queries = q_ref[0, 0]
    query_heads = [jnp.where(lane == h, queries, jnp.zeros_like(queries)) for h in range(heads)]
    grad_heads = [jnp.where(lane == h, mixed_grad, jnp.zeros_like(mixed_grad)) for h in range(heads)]
    acc[...] = jnp.zeros_like(acc)
    dk_ref[...] = jnp.zeros_like(dk_ref)
    dv_ref[...] = jnp.zeros_like(dv_ref)

    def step(block, carry):
        at = pl.ds(pl.multiple_of(block * KEY_BLOCK, KEY_BLOCK), KEY_BLOCK)
        keys = k_ref[0, 0, at, :]
        values = v_ref[0, 0, at, :]
        keys_t = keys.T
        mask = bias[at, :]
        key_grad = jnp.zeros((KEY_BLOCK, width), floats)
        value_grad = jnp.zeros((KEY_BLOCK, width), floats)
        for h in range(heads):
            s = contract_cols(keys, query_heads[h]) + mask
            p = jnp.exp(s - lse_ref[0, 0, h : h + 1])
            prob_grad = contract_cols(values, grad_heads[h])
            score_grad = (p * (prob_grad - inner[h : h + 1])).astype(halves)
            value_grad = value_grad + jnp.dot(p.astype(halves), grad_heads[h], preferred_element_type=floats)
            key_grad = key_grad + jnp.dot(score_grad, query_heads[h], preferred_element_type=floats)
            part = pl.ds(h * HEAD_DIM, HEAD_DIM)
            acc[part, :] += jnp.dot(keys_t[h * HEAD_DIM : (h + 1) * HEAD_DIM], score_grad, preferred_element_type=floats)
        dk_ref[0, 0, at, :] = key_grad.astype(halves)
        dv_ref[0, 0, at, :] = value_grad.astype(halves)
        return carry

    lax.fori_loop(low, high, step, 0)
    dq_ref[0, 0] = (acc[...].T * HEAD_DIM ** -0.5).astype(halves)


def attend_back(bounds, grad, wot, mixed, lse, q, k, v, seg_own, seg_all):
    micro, rows, model = grad.shape
    cols, _, length, width = k.shape
    halves = jnp.bfloat16
    per = lambda a, b_: pl.BlockSpec((1, 1, a, b_), lambda m, c, b: (c, m, 0, 0))
    spec = pltpu.PrefetchScalarGridSpec(
        num_scalar_prefetch=1,
        grid=(micro, cols),
        in_specs=[
            pl.BlockSpec((1, rows, model), lambda m, c, b: (m, 0, 0)),
            pl.BlockSpec((1, model, width), lambda m, c, b: (c, 0, 0)),
            per(rows, width), per(8, rows), per(rows, width), per(length, width), per(length, width),
            pl.BlockSpec((1, 1, rows), lambda m, c, b: (m, 0, 0)),
            pl.BlockSpec((1, length, 1), lambda m, c, b: (m, 0, 0)),
        ],
        out_specs=[per(rows, width), per(length, width), per(length, width)],
        scratch_shapes=[pltpu.VMEM((length, rows), jnp.float32), pltpu.VMEM((width, rows), jnp.float32)],
    )
    shape = lambda a, b_, d=halves: jax.ShapeDtypeStruct((cols, micro, a, b_), d)
    return pl.pallas_call(
        attend_back_kernel,
        grid_spec=spec,
        out_shape=[shape(rows, width), shape(length, width), shape(length, width)],
        compiler_params=pltpu.CompilerParams(vmem_limit_bytes=48 << 20),
        name="attend_back",
    )(bounds, grad, wot, mixed, lse, q, k, v, seg_own[:, None], seg_all[:, :, None])


def place(sizes):
    seq, row, col = (lax.axis_index(name) for name in ("seq", "row", "col"))
    lines = {"x": (seq, sizes[0]), "y": (row // 2, sizes[1] // 2), "k": (lax.rem(row, 2), 2), "z": (col, sizes[2])}

    def device(axis, index):
        if axis == "x":
            return (index, row, col)
        if axis == "y":
            return (seq, index * 2 + lax.rem(row, 2), col)
        if axis == "k":
            return (seq, row // 2 * 2 + index, col)
        return (seq, row, index)

    return lines, device


def greet(lines, device):
    barrier = pltpu.get_barrier_semaphore()
    count = 0
    for axis, (mine, size) in lines.items():
        for t in range(1, size):
            pl.semaphore_signal(barrier, inc=1, device_id=device(axis, lax.rem(mine + t, size)), device_id_type=MESH)
            count += 1
    pl.semaphore_wait(barrier, count)


class Post:
    def __init__(self, device, send_sems, recv_sems):
        self.device, self.send_sems, self.recv_sems = device, send_sems, recv_sems
        self.slots, self.sent = {}, []

    def slot(self, key):
        return self.slots.setdefault(key, len(self.slots))

    def copy(self, key, axis, index, source, target):
        n = self.slot(key)
        return pltpu.make_async_remote_copy(
            src_ref=source, dst_ref=target, send_sem=self.send_sems.at[n], recv_sem=self.recv_sems.at[n],
            device_id=self.device(axis, index), device_id_type=MESH,
        )

    def send(self, key, make):
        def run(act):
            axis, index, source, target, when = make()

            def go():
                act(self.copy(key, axis, index, source, target))

            if when is None:
                go()
            else:
                pl.when(when)(go)

        run(lambda copy: copy.start())
        self.sent.append(run)

    def wait(self, key, axis, index, target, when=None):
        def go():
            self.copy(key, axis, index, target, target).wait_recv()

        if when is None:
            go()
        else:
            pl.when(when)(go)

    def close(self):
        for run in self.sent:
            run(lambda copy: copy.wait_send())


def clip(index, size):
    return jnp.clip(index, 0, size - 1)


class LineGather:
    def __init__(self, post, name, axis, line, region, reach=None):
        self.post, self.name, self.axis, self.region = post, name, axis, region
        self.mine, self.size = line
        self.reach = min(self.size - 1, reach or self.size)

    def hop(self, way, t):
        mine, size = self.mine, self.size

        def make():
            origin, target = mine - way * t, mine + way
            ok = (origin >= 0) & (origin < size) & (target >= 0) & (target < size)
            here = self.region(clip(origin, size))
            return self.axis, clip(target, size), here, here, ok

        self.post.send((self.name, way, t + 1), make)

    def start(self):
        for way in (1, -1):
            if self.reach >= 1:
                self.hop(way, 0)

    def step(self, t):
        if t > self.reach:
            return
        for way in (1, -1):
            origin = self.mine - way * t
            ok = (origin >= 0) & (origin < self.size)
            self.post.wait((self.name, way, t), self.axis, clip(self.mine - way, self.size), self.region(clip(origin, self.size)), ok)
            if t < self.reach:
                self.hop(way, t)

    def finish(self, first=1):
        for t in range(first, self.reach + 1):
            self.step(t)


def gather_kernel(sizes, micro, own_ref, shard_ref, every_ref, full_ref, send_sems, recv_sems, local_sems):
    lines, device = place(sizes)
    (x, _), (y, _), (k, _), (z, cols) = (lines[a] for a in "xykz")
    half = shard_ref.shape[-1] // 2
    rows = own_ref.shape[1]
    reach = -(-(DOC_MOST - 1) // rows)
    parts = [pl.ds(p * half, half) for p in (0, 1)]
    local = [pltpu.make_async_copy(shard_ref.at[j], full_ref.at[j, z, x, y, k], local_sems.at[j]) for j in range(3)]
    local += [pltpu.make_async_copy(own_ref.at[m], every_ref.at[m, z], local_sems.at[3 + m]) for m in range(micro)]
    for copy in local:
        copy.start()
    greet(lines, device)
    post = Post(device, send_sems, recv_sems)
    for copy in local:
        copy.wait()
    zs = [LineGather(post, ("z", j), "z", lines["z"], lambda i, j=j: full_ref.at[j, i, x, y, k]) for j in range(3)]
    tokens = [LineGather(post, ("t", m), "z", lines["z"], lambda i, m=m: every_ref.at[m, i], reach) for m in range(micro)]
    second, third = {}, {}
    for j in range(3):
        second[j] = [
            LineGather(post, ("a", j), "y", lines["y"], lambda i, j=j: full_ref.at[j, :, x, i, k, :, parts[0]]),
            LineGather(post, ("b", j), "x", lines["x"], lambda i, j=j: full_ref.at[j, :, i, y, k, :, parts[1]]),
        ]
        third[j] = [
            LineGather(post, ("c", j), "x", lines["x"], lambda i, j=j: full_ref.at[j, :, i, :, k, :, parts[0]]),
            LineGather(post, ("d", j), "y", lines["y"], lambda i, j=j: full_ref.at[j, :, :, i, k, :, parts[1]]),
        ]

    def start(group):
        for line in group:
            line.start()

    def finish(group):
        for line in group:
            line.finish()

    def swap(j):
        plane = full_ref.at[j, :, :, :, k]
        post.send(("k", j), lambda: ("k", 1 - k, plane, plane, None))

    start(zs[:1])
    finish(zs[:1])
    start(second[0] + zs[1:2])
    finish(second[0])
    start(third[0])
    finish(zs[1:2])
    start(second[1] + tokens[:1])
    finish(third[0])
    swap(0)
    finish(second[1])
    start(third[1])
    finish(tokens[:1])
    start(zs[2:])
    finish(zs[2:])
    start(second[2] + tokens[1:])
    finish(third[1])
    swap(1)
    finish(second[2])
    start(third[2])
    finish(tokens[1:])
    finish(third[2])
    swap(2)
    for i in range(cols):
        far = (z - i > reach) | (i - z > reach)
        for m in range(micro):
            def fill(m=m, i=i):
                copy = pltpu.make_async_copy(own_ref.at[m], every_ref.at[m, i], local_sems.at[3 + m])
                copy.start()
                copy.wait()

            if i > reach or cols - 1 - i > reach:
                pl.when(far)(fill)
    for j in range(3):
        post.wait(("k", j), "k", 1 - k, full_ref.at[j, :, :, :, 1 - k])
    post.close()


def gather(sizes, own, shard):
    ns, nr, nc = sizes
    ny = nr // 2
    micro, rows, model = own.shape
    _, rb, w = shard.shape
    count = 3 * 2 * (nc - 1) + micro * 2 * (nc - 1) + 3 * (4 * (ny - 1) + 4 * (ns - 1) + 1)
    anywhere = pl.BlockSpec(memory_space=pl.ANY)
    every, full = pl.pallas_call(
        functools.partial(gather_kernel, sizes, micro),
        out_shape=[
            jax.ShapeDtypeStruct((micro, nc, rows, model), own.dtype),
            jax.ShapeDtypeStruct((3, nc, ns, ny, 2, rb, w), shard.dtype),
        ],
        in_specs=[pl.BlockSpec(memory_space=pltpu.VMEM)] * 2,
        out_specs=[anywhere] * 2,
        scratch_shapes=[pltpu.SemaphoreType.DMA((count,)), pltpu.SemaphoreType.DMA((count,)), pltpu.SemaphoreType.DMA((3 + micro,))],
        compiler_params=pltpu.CompilerParams(collective_id=0, has_side_effects=True),
        name="gather",
    )(own, shard)
    return every, full.reshape(3, nc, ns * nr * rb, w)


class LineReduce:
    def __init__(self, post, name, axis, line, region, inbox, add, reach=None):
        self.post, self.name, self.axis, self.region, self.inbox, self.add = post, name, axis, region, inbox, add
        self.mine, self.size = line
        self.reach = min(self.size - 1, reach or self.size)

    def arrived(self, way, e):
        behind, goal = self.mine - way, self.mine + way * e
        return (behind >= 0) & (behind < self.size) & (goal >= 0) & (goal < self.size)

    def take(self, way, e):
        ok = self.arrived(way, e)
        inbox = self.inbox(way, e)
        self.post.wait((self.name, way, e), self.axis, clip(self.mine - way, self.size), inbox, ok)

        @pl.when(ok)
        def _():
            self.add(self.region(clip(self.mine + way * e, self.size)), inbox)

    def forward(self, way, e):
        def make():
            goal = self.mine + way * e
            ok = (goal >= 0) & (goal < self.size)
            return self.axis, clip(self.mine + way, self.size), self.region(clip(goal, self.size)), self.inbox(way, e - 1), ok

        self.post.send((self.name, way, e - 1), make)

    def start(self):
        for way in (1, -1):
            if self.reach >= 1:
                self.forward(way, self.reach)

    def forward_from(self, nearest):
        for e in range(self.reach - 1, nearest - 1, -1):
            for way in (1, -1):
                self.take(way, e)
                self.forward(way, e)

    def finish(self, last=True):
        self.forward_from(1)
        if last:
            for way in (1, -1):
                if self.reach >= 1:
                    self.take(way, 0)


def reduce_to(post, name, axis, line, goal, e, region, inbox, add):
    mine, size = line
    for way in (1, -1):
        behind = mine - way
        arrives = (way * (goal - mine) == e) & (behind >= 0) & (behind < size)
        slot = inbox(way, min(e, size - 2))
        post.wait((name, way), axis, clip(behind, size), slot, arrives)

        @pl.when(arrives)
        def _():
            add(region, slot)

        def make(way=way):
            return axis, clip(mine + way, size), region, inbox(way, e - 1), way * (goal - mine) == e

        if e:
            post.send((name, way), make)


def reduce_kernel(sizes, micro, own_ref, spread_ref, part_ref, vec_ref, back_ref, block_ref, sums_ref,
                  mine_buf, core_buf, in_a, in_b, in_c, in_d, in_z, tok_buf, tok_in, vec_buf, send_sems, recv_sems, local_sems):
    floats, halves = jnp.float32, jnp.bfloat16
    lines, device = place(sizes)
    (x, ns), (y, ny), (k, _), (z, nc) = (lines[a] for a in "xykz")
    half = part_ref.shape[-1] // 2
    rows = own_ref.shape[1]
    reach = -(-(DOC_MOST - 1) // rows)
    parts = [pl.ds(p * half, half) for p in (0, 1)]
    local = [pltpu.make_async_copy(part_ref.at[j, :, :, :, k], mine_buf.at[j], local_sems.at[j]) for j in range(3)]
    local += [pltpu.make_async_copy(spread_ref.at[m], tok_buf.at[m], local_sems.at[3 + m]) for m in range(micro)]
    for copy in local:
        copy.start()
    greet(lines, device)
    post = Post(device, send_sems, recv_sems)
    for j in range(3):
        post.send(("k", j), lambda j=j: ("k", 1 - k, part_ref.at[j, :, :, :, 1 - k], core_buf.at[j], None))

    def plus(target, source):
        target[...] = (target[...].astype(floats) + source[...].astype(floats)).astype(halves)

    def plus_grid(target, source, first, second):
        @pl.loop(0, first * second)
        def _(n):
            plus(target.at[n // second, lax.rem(n, second)], source.at[n // second, lax.rem(n, second)])

    def plus_row(target, source, first):
        @pl.loop(0, first)
        def _(n):
            plus(target.at[n], source.at[n])

    vec_buf[0, 0] = vec_ref[...]

    def vector_start(stage, axis):
        mine, size = lines[axis]
        vec_buf[stage, 1 + mine] = vec_buf[stage, 0]
        for t in range(1, size):
            post.send(("v", stage, t), lambda t=t: (
                axis, lax.rem(mine + t, size), vec_buf.at[stage, 0], vec_buf.at[stage, 1 + mine], None))

    def vector_finish(stage, axis, out):
        mine, size = lines[axis]
        for t in range(1, size):
            origin = lax.rem(mine + size - t, size)
            post.wait(("v", stage, t), axis, origin, vec_buf.at[stage, 1 + origin])
        total = vec_buf[stage, 1]
        for i in range(1, size):
            total = total + vec_buf[stage, 1 + i]
        out[...] = total

    tokens = [
        LineReduce(post, ("t", m), "z", lines["z"], lambda i, m=m: tok_buf.at[m, i],
                   lambda way, e, m=m: tok_in.at[m, (1 - way) // 2, e], plus, reach)
        for m in range(micro)
    ]
    box = lambda way: (1 - way) // 2
    second, third, last = {}, {}, {}
    for j in range(3):
        second[j] = [
            LineReduce(post, ("a", j), "x", lines["x"], lambda i, j=j: mine_buf.at[j, :, i, :, :, parts[0]],
                       lambda way, e, j=j: in_a.at[j, box(way), e], lambda t, s: plus_grid(t, s, nc, ny)),
            LineReduce(post, ("b", j), "y", lines["y"], lambda i, j=j: mine_buf.at[j, :, :, i, :, parts[1]],
                       lambda way, e, j=j: in_b.at[j, box(way), e], lambda t, s: plus_grid(t, s, nc, ns)),
        ]
        third[j] = [
            LineReduce(post, ("c", j), "y", lines["y"], lambda i, j=j: mine_buf.at[j, :, x, i, :, parts[0]],
                       lambda way, e, j=j: in_c.at[j, box(way), e], lambda t, s: plus_row(t, s, nc)),
            LineReduce(post, ("d", j), "x", lines["x"], lambda i, j=j: mine_buf.at[j, :, i, y, :, parts[1]],
                       lambda way, e, j=j: in_d.at[j, box(way), e], lambda t, s: plus_row(t, s, nc)),
        ]
        last[j] = [
            LineReduce(post, ("z", j), "z", lines["z"], lambda i, j=j: mine_buf.at[j, i, x, y],
                       lambda way, e, j=j: in_z.at[j, box(way), e], plus)
        ]

    def start(group):
        for line in group:
            line.start()

    def finish(group):
        for line in group:
            line.finish()

    def core(j):
        local[j].wait()
        post.wait(("k", j), "k", 1 - k, core_buf.at[j])

        @pl.loop(0, nc * ns * ny)
        def _(n):
            at = (n // (ns * ny), lax.rem(n // ny, ns), lax.rem(n, ny))
            plus(mine_buf.at[(j, *at)], core_buf.at[(j, *at)])

    for m in range(micro):
        local[3 + m].wait()
    start(tokens)
    core(0)
    start(second[0])
    vector_start(0, "k")
    core(1)
    start(second[1])
    vector_finish(0, "k", vec_buf.at[1, 0])
    vector_start(1, "y")
    core(2)
    finish(second[0])
    start(third[0])
    start(second[2])
    vector_finish(1, "y", vec_buf.at[2, 0])
    vector_start(2, "x")
    finish(tokens)
    vector_finish(2, "x", vec_buf.at[3, 0])
    vector_start(3, "z")
    finish(second[1])
    start(third[1])
    finish(third[0])
    start(last[0])
    finish(second[2])
    start(third[2])
    finish(third[1])
    start(last[1])
    finish(last[0])
    finish(third[2])
    start(last[2])
    vector_finish(3, "z", sums_ref)
    for m in range(micro):
        back_ref[m] = own_ref[m] + tok_buf[m, z].astype(floats)
    finish(last[1])
    finish(last[2])
    for j in range(3):
        block_ref[j] = mine_buf[j, z, x, y].astype(floats)
    post.close()


def reduce(sizes, own_share, spread, partial, vectors):
    ns, nr, nc = sizes
    ny = nr // 2
    micro, rows, model = own_share.shape
    w = partial.shape[-1]
    rb = partial.shape[2] // (ns * nr)
    halves, floats = jnp.bfloat16, jnp.float32
    reach = min(nc - 1, -(-(DOC_MOST - 1) // rows))
    count = 3 + 2 * (ny - 1 + ns - 1) * 6 + 3 * 2 * (nc - 1) + micro * 2 * reach + (1 + ny - 1 + ns - 1 + nc - 1)
    widest = max(ns, ny, nc, 2)
    extra = -vectors.shape[0] % 8
    vectors = jnp.pad(vectors, ((0, extra), (0, 0)))
    vmem = pl.BlockSpec(memory_space=pltpu.VMEM)
    anywhere = pl.BlockSpec(memory_space=pl.ANY)
    back, blocks, sums = pl.pallas_call(
        functools.partial(reduce_kernel, sizes, micro),
        out_shape=[
            jax.ShapeDtypeStruct((micro, rows, model), floats),
            jax.ShapeDtypeStruct((3, rb, w), floats),
            jax.ShapeDtypeStruct(vectors.shape, floats),
        ],
        in_specs=[vmem, anywhere, anywhere, vmem],
        out_specs=[vmem] * 3,
        scratch_shapes=[
            pltpu.VMEM((3, nc, ns, ny, rb, w), halves),
            pltpu.VMEM((3, nc, ns, ny, rb, w), halves),
            pltpu.VMEM((3, 2, max(ns - 1, 1), nc, ny, rb, w // 2), halves),
            pltpu.VMEM((3, 2, max(ny - 1, 1), nc, ns, rb, w // 2), halves),
            pltpu.VMEM((3, 2, max(ny - 1, 1), nc, rb, w // 2), halves),
            pltpu.VMEM((3, 2, max(ns - 1, 1), nc, rb, w // 2), halves),
            pltpu.VMEM((3, 2, max(nc - 1, 1), rb, w), halves),
            pltpu.VMEM((micro, nc, rows, model), halves),
            pltpu.VMEM((micro, 2, max(reach, 1), rows, model), halves),
            pltpu.VMEM((4, 1 + widest, *vectors.shape), floats),
            pltpu.SemaphoreType.DMA((count,)),
            pltpu.SemaphoreType.DMA((count,)),
            pltpu.SemaphoreType.DMA((3 + micro,)),
        ],
        compiler_params=pltpu.CompilerParams(collective_id=1, has_side_effects=True, vmem_limit_bytes=60 << 20),
        name="reduce",
    )(own_share, spread, partial.reshape(3, nc, ns, ny, 2, rb, w), vectors)
    return back, blocks, sums


Q_AT, K_AT, V_AT, O_AT, WINDOW = 0, 128, 384, 512, 256


def plane(full_ref, c, at, size=WINDOW):
    value = full_ref[c, :, :, :, :, at : at + size]
    return value.reshape(-1, size)


def split_plan(plan):
    parts, order = [[]], []
    for task in plan:
        if task[0] == "U":
            order.append(task[1:])
            parts.append([])
        else:
            parts[-1].append(task)
    return parts[0], parts[1:], order


def pick(step, values):
    value = values[0]
    for i, other in enumerate(values[1:], 1):
        value = jnp.where(step == i, other, value)
    return value


def place_of(rows):
    return lax.broadcasted_iota(jnp.int32, (rows, WINDOW), 1) // HEAD_DIM


def keep(value, places, wanted):
    return jnp.where(places == wanted, value, jnp.zeros_like(value))


def forward_kernel(sizes, micro, own_ref, wq_ref, wk_ref, wv_ref, wo_ref, wh_ref, wd_ref, hidden_bias_ref, query_bias_ref, value_bias_ref, seg_ref,
                   rest_ref, first_ref, turned_ref, mask_ref, biases_ref, mixed_ref, lse_ref, q_ref, k_ref, v_ref,
                   weights, turned, bias_buf, mask, mixed_buf, lse_buf, q_buf, k_buf, v_buf, tokens_buf, acc, score_buf, prob_buf, values_t,
                   send_sems, recv_sems, local_sems, unit_sems):
    floats, halves = jnp.float32, jnp.bfloat16
    lines, device = place(sizes)
    (x, _), (y, _), (k, _), (z, cols) = (lines[a] for a in "xykz")
    half = wh_ref.shape[-1] // 2
    rows = own_ref.shape[1]
    reach = -(-(DOC_MOST - 1) // rows)
    parts = [pl.ds(p * half, half) for p in (0, 1)]
    low, high = jnp.maximum(z - reach, 0), jnp.minimum(z + reach + 1, cols)
    used = [0]

    class Local:
        def __init__(self, source, target):
            self.source, self.target, self.n = source, target, used[0]
            used[0] += 1
            self.describe().start()

        def describe(self):
            source = self.source() if callable(self.source) else self.source
            return pltpu.make_async_copy(source, self.target, local_sems.at[self.n])

        def wait(self):
            self.describe().wait()

    local = Local
    targets = [weights.at[0], rest_ref.at[0], rest_ref.at[1]]
    packed = [wq_ref[...], wk_ref[...], wv_ref[...], wo_ref[...].astype(floats).T.astype(halves)]
    weights[0, z, x, y, k] = jnp.concatenate(packed, 1)
    begin = [local(wh_ref, targets[1].at[z, x, y, k]), local(wd_ref, targets[2].at[z, x, y, k])]
    begin += [local(own_ref.at[m], tokens_buf.at[m, z]) for m in range(micro)]
    for i, ref in enumerate((hidden_bias_ref, query_bias_ref, value_bias_ref)):
        bias_buf[z, i : i + 1, 0 : ref.shape[0]] = ref[...].astype(floats).reshape(1, -1)
        if ref.shape[0] < WINDOW:
            bias_buf[z, i : i + 1, ref.shape[0] : WINDOW] = jnp.zeros((1, WINDOW - ref.shape[0]), floats)
    greet(lines, device)
    post = Post(device, send_sems, recv_sems)
    for copy in begin:
        copy.wait()
    tokens = [
        LineGather(post, ("t", q), "z", lines["z"],
                   lambda i, q=q: tokens_buf.at[q // 2, i, pl.ds(q % 2 * (rows // 2), rows // 2)], reach)
        for q in range(2 * micro)
    ]
    small = LineGather(post, "bias", "z", lines["z"], lambda i: bias_buf.at[i])
    rb = wh_ref.shape[0]
    zs, second, third = {}, {}, {}
    for n in range(6):
        j, r = n // 2, pl.ds(n % 2 * (rb // 2), rb // 2)
        zs[n] = LineGather(post, ("z", n), "z", lines["z"], lambda i, j=j, r=r: targets[j].at[i, x, y, k, r])
        second[n] = [
            LineGather(post, ("a", n), "y", lines["y"], lambda i, j=j, r=r: targets[j].at[:, x, i, k, r, parts[0]]),
            LineGather(post, ("b", n), "x", lines["x"], lambda i, j=j, r=r: targets[j].at[:, i, y, k, r, parts[1]]),
        ]
        third[n] = [
            LineGather(post, ("c", n), "x", lines["x"], lambda i, j=j, r=r: targets[j].at[:, i, :, k, r, parts[0]]),
            LineGather(post, ("d", n), "y", lines["y"], lambda i, j=j, r=r: targets[j].at[:, :, i, k, r, parts[1]]),
        ]

    def start(*group):
        for line in group:
            line.start()

    def finish(*group):
        for line in group:
            line.finish()

    def side(n, which):
        return targets[n // 2].at[:, :, :, which, pl.ds(n % 2 * (rb // 2), rb // 2)]

    def swap(n):
        post.send(("k", n), lambda: ("k", 1 - k, side(n, k), side(n, k), None))

    def swapped(n):
        post.wait(("k", n), "k", 1 - k, side(n, 1 - k))

    places = place_of(rows)

    def project(m, c, block):
        rows_at = tokens_buf[m, block]
        k_buf[m, c, block] = jnp.dot(rows_at, plane(weights.at[0], c, K_AT), preferred_element_type=floats).astype(halves)
        values = jnp.dot(rows_at, plane(weights.at[0], c, V_AT), preferred_element_type=floats) + bias_buf[c, 2:3, 0:WINDOW]
        v_buf[m, c, block] = values.astype(halves)

    def prepare(m, c):
        queries = jnp.dot(own_ref[m], plane(weights.at[0], c, Q_AT), preferred_element_type=floats) + bias_buf[c, 1:2, 0:WINDOW]
        queries = pltpu.roll(queries.astype(halves).astype(floats) * HEAD_DIM ** -0.5, HEAD_DIM, 1)
        q_buf[m, c] = jnp.where(places > 0, queries, 0.0).astype(halves)
        for way in (0, 1, 3):
            project(m, c, lax.rem(z + way, cols))

    def unit(m, c):
        project(m, c, lax.rem(z + 2, cols))
        queries = q_buf[m, c]
        heads = jnp.concatenate([keep(queries, places, h + 1) for h in range(3)], 0)
        largest = jnp.full((1, 3 * rows), 2 * MASK_VALUE, floats)
        for block in range(cols):
            keys = k_buf[m, c, block]
            values_t[:, block * rows : (block + 1) * rows] = v_buf[m, c, block].T
            hidden = mask[m, block].astype(floats)
            s = contract_cols(keys, heads) + jnp.concatenate([hidden] * 3, 1)
            score_buf[block] = s
            largest = jnp.maximum(largest, jnp.max(s, 0, keepdims=True))
        row_total = jnp.zeros((1, 3 * rows), floats)
        for block in range(cols):
            p = jnp.exp(score_buf[block] - largest)
            row_total = row_total + jnp.sum(p, 0, keepdims=True)
            prob_buf[block * rows : (block + 1) * rows] = p.astype(halves)
        log_total = largest + jnp.log(row_total)
        acc[0:HEAD_DIM] = jnp.zeros((HEAD_DIM, rows), floats)
        for h in range(3):
            lanes = slice(h * rows, (h + 1) * rows)
            product = jnp.dot(values_t[h * HEAD_DIM : (h + 1) * HEAD_DIM], prob_buf[:, lanes], preferred_element_type=floats)
            acc[pl.ds((h + 1) * HEAD_DIM, HEAD_DIM), :] = product / row_total[:, lanes]
            lse_buf[m, c, h : h + 1] = log_total[:, lanes]
        mixed_buf[c, m] = acc[...].T.astype(halves)

    def units(m, first, last):
        @pl.loop(first, last)
        def _(c):
            unit(m, c)

    def masks(m):
        asking = seg_ref[m, 0:1, pl.ds(pl.multiple_of(z * rows, 128), rows)].astype(floats)
        for block in range(cols):
            asked = seg_ref[m, 0:1, block * rows : (block + 1) * rows].astype(floats)
            same = jnp.broadcast_to(asked, (rows, rows)).T == asking
            mask[m, block] = jnp.where(same, 0.0, MASK_VALUE).astype(halves)

    done = []

    def turn(m):
        for block in range(cols):
            turned[:, (m * cols + block) * rows : (m * cols + block + 1) * rows] = tokens_buf[m, block].T
        if m == micro - 1:
            done.append(local(turned, turned_ref))

    keeps = ((q_buf, q_ref), (k_buf, k_ref), (v_buf, v_ref), (lse_buf, lse_ref))

    def take_z(n, t):
        zs[n].step(t)
        if n == 0:
            small.step(t)
        if t == cols - 1:
            start(*second[n])

    def take_second(n):
        finish(*second[n])
        start(*third[n])

    def take_third(n):
        finish(*third[n])
        swap(n)

    swaps = set()

    def take_core(n):
        swapped(n)
        swaps.add(n)
        if n < 2 and swaps >= {0, 1}:
            done.append(local(lambda: weights.at[0], first_ref))

    act = {
        "Zs": lambda n: zs[n].start(), "Z": take_z, "Ts": lambda q: tokens[q].start(), "T": lambda q, t: tokens[q].step(t),
        "B": take_second, "C": take_third, "K": take_core, "R": turn,
    }
    small.start()
    head, tail, order = split_plan([("U", *task) if task[0] == "P" else task for task in FORWARD_PLAN])
    kinds = [int(item[0] == "P") for item in order]
    micros, heads_of = [item[-2] for item in order], [item[-1] for item in order]
    act[head[0][0]](*head[0][1:])
    for block in range(cols):
        if block > reach or cols - 1 - block > reach:
            @pl.when(jnp.logical_not((low <= block) & (block < high)))
            def _(block=block):
                for m in range(micro):
                    tokens_buf[m, block] = jnp.zeros(own_ref.shape[1:], halves)
    for m in range(micro):
        masks(m)
    done.append(local(mask, mask_ref))
    for task in head[1:]:
        act[task[0]](*task[1:])

    def leave(m, c, go):
        for i, (source, target) in enumerate(keeps):
            go(pltpu.make_async_copy(source.at[m, c], target.at[m, c], unit_sems.at[i, m * cols + c]))
        go(pltpu.make_async_copy(mixed_buf.at[c, m], mixed_ref.at[c, m], unit_sems.at[len(keeps), m * cols + c]))

    @pl.loop(0, len(order))
    def _(step):
        m, c, kind = pick(step, micros), pick(step, heads_of), pick(step, kinds)

        @pl.when(kind == 1)
        def _():
            prepare(m, c)

        @pl.when(kind == 0)
        def _():
            unit(m, c)
            leave(m, c, lambda copy: copy.start())

        for i, tasks in enumerate(tail[:-1]):
            if tasks:
                @pl.when(step == i)
                def _(tasks=tasks):
                    for task in tasks:
                        act[task[0]](*task[1:])

    done.append(local(bias_buf, biases_ref))
    for task in tail[-1]:
        act[task[0]](*task[1:])
    for m in range(micro):
        for c in range(cols):
            leave(m, c, lambda copy: copy.wait())
    for copy in done:
        copy.wait()
    post.close()


def forward(sizes, own, shards, hidden_bias, query_bias, value_bias, segments):
    ns, nr, nc = sizes
    ny = nr // 2
    micro, rows, model = own.shape
    rb, w = shards[4].shape
    halves, floats = own.dtype, jnp.float32
    reach = min(nc - 1, -(-(DOC_MOST - 1) // rows))
    count = (6 + 1) * 2 * (nc - 1) + micro * 4 * reach + 6 * (4 * (ny - 1) + 4 * (ns - 1) + 1)
    anywhere = pl.BlockSpec(memory_space=pl.ANY)
    vmem = pl.BlockSpec(memory_space=pltpu.VMEM)
    length = nc * rows
    arrays = [
        ((2, nc, ns, ny, 2, rb, w), halves), ((nc, ns, ny, 2, rb, w), halves), ((model, micro * length), halves), ((micro, nc, rows, rows), halves),
        ((nc, 8, model), floats), ((nc, micro, rows, WINDOW), halves), ((micro, nc, 8, rows), floats),
        ((micro, nc, rows, WINDOW), halves), ((micro, nc, nc, rows, WINDOW), halves), ((micro, nc, nc, rows, WINDOW), halves),
    ]
    shapes = [pltpu.VMEM(shape, kind) for shape, kind in arrays]
    return pl.pallas_call(
        functools.partial(forward_kernel, sizes, micro),
        out_shape=[jax.ShapeDtypeStruct(shape, kind) for shape, kind in arrays],
        in_specs=[vmem] * 11,
        out_specs=[anywhere] * len(arrays),
        scratch_shapes=[
            pltpu.VMEM((1, nc, ns, ny, 2, rb, w), halves),
            shapes[2], shapes[4], shapes[3], *shapes[5:],
            pltpu.VMEM((micro, nc, rows, model), halves), pltpu.VMEM((WINDOW, rows), floats), pltpu.VMEM((nc, rows, 3 * rows), floats), pltpu.VMEM((length, 3 * rows), halves), pltpu.VMEM((WINDOW, length), halves),
            pltpu.SemaphoreType.DMA((count,)), pltpu.SemaphoreType.DMA((count,)), pltpu.SemaphoreType.DMA((20,)), pltpu.SemaphoreType.DMA((5, micro * nc)),
        ],
        compiler_params=pltpu.CompilerParams(collective_id=2, has_side_effects=True, vmem_limit_bytes=60 << 20),
        name="forward",
    )(own, *shards, hidden_bias, query_bias, value_bias, segments)


def middle_kernel(cols, own_ref, mixed_ref, out_ref, rest_ref, bias_ref, *refs):
    vector_refs = refs[:6]
    (cot_ref, outputs_ref, first_grad_ref, attn_grad_ref, part_ref, sums_ref,
     normal, scale, normed, normed_low, normed_t, grad_low, grad_t, act_buf, slope_buf, total, cot_buf, weight_buf, sems) = refs[6:]
    floats, halves = jnp.float32, jnp.bfloat16
    step = pl.program_id(0)
    rows, model = own_ref.shape
    chunks = [pl.ds(r * 256, 256) for r in range(rows // 256)]
    whole_rows = [pl.ds(0, rows)]
    bands = [pl.ds(n * 256, 256) for n in range(model // 256)]
    loads = [[pltpu.make_async_copy(rest_ref.at[j, c], weight_buf.at[j, c], sems.at[j, c]) for j in range(2)] for c in range(cols)]
    load_cot = pltpu.make_async_copy(cot_ref, cot_buf, sems.at[0, cols])
    vector = lambda i: vector_refs[i][...].astype(floats).reshape(1, -1)

    @pl.when(step == 0)
    def _():
        for pair in loads:
            for copy in pair:
                copy.start()
        load_cot.start()
        sums_ref[...] = jnp.zeros_like(sums_ref)
        for chunk in chunks:
            first_sum = own_ref[chunk].astype(floats) + vector(0)
            for c in range(cols):
                first_sum = first_sum + contract_cols(mixed_ref[c, chunk], out_ref[c])
            normal_one, scale_one = norm_parts(first_sum)
            normal[chunk] = normal_one
            scale[chunk] = jnp.broadcast_to(scale_one, (256, 128))
            norm_one = normal_one * vector(1) + vector(2)
            total[chunk] = norm_one + vector(3)
            normed_low[chunk] = norm_one.astype(halves)
            normed_t[:, chunk] = norm_one.astype(halves).T

    for c in range(cols):
        @pl.when(step == c)
        def _(c=c):
            for copy in loads[c]:
                copy.wait()

    @pl.when(step < cols)
    def _():
        for chunk in chunks:
            for band in bands:
                hidden = jnp.dot(normed_low[chunk], weight_buf[0, step, :, band], preferred_element_type=floats) + bias_ref[0, 0:1, band]
                half_erf = 0.5 * lax.erf(hidden * 0.7071067811865476) + 0.5
                act_buf[step, chunk, band] = (hidden * half_erf).astype(halves)
                slope_buf[step, chunk, band] = (half_erf + hidden * (jnp.exp(-0.5 * hidden * hidden) * 0.3989422804014327)).astype(halves)
        for chunk in chunks:
            for band in bands:
                total[chunk, band] += contract_cols(act_buf[step, chunk], weight_buf[1, step, band, :])

    @pl.when(step == cols - 1)
    def _():
        load_cot.wait()
        for chunk in chunks:
            normal_two, scale_two = norm_parts(total[chunk])
            outputs_ref[chunk] = (normal_two * vector(4) + vector(5)).astype(halves)
            cot = cot_buf[chunk].astype(floats)
            second_grad = norm_back(cot * vector(4), normal_two, scale_two)
            total[chunk] = second_grad
            grad_low[chunk] = second_grad.astype(halves)
            grad_t[:, chunk] = second_grad.astype(halves).T
            sums_ref[3:4] += jnp.sum(second_grad, 0, keepdims=True)
            sums_ref[4:5] += jnp.sum(cot * normal_two, 0, keepdims=True)
            sums_ref[5:6] += jnp.sum(cot, 0, keepdims=True)

    @pl.when(step >= cols)
    def _():
        c = step - cols
        bias_total = [jnp.zeros((1, 256), floats) for _ in bands]
        for chunk in chunks:
            for n, band in enumerate(bands):
                pre = jnp.dot(grad_low[chunk], weight_buf[1, c, :, band], preferred_element_type=floats)
                pre = (pre * slope_buf[c, chunk, band].astype(floats)).astype(halves)
                slope_buf[c, chunk, band] = pre
                bias_total[n] = bias_total[n] + jnp.sum(pre.astype(floats), 0, keepdims=True)
        for n, band in enumerate(bands):
            sums_ref[pl.ds(8 + c, 1), band] = bias_total[n]
        for band in bands:
            for side in [pl.ds(0, model)]:
                part_ref[0, 0, side, band] = jnp.dot(normed_t[side, :], slope_buf[c, :, band], preferred_element_type=floats).astype(halves)
                part_ref[1, 0, side, band] = jnp.dot(grad_t[side, :], act_buf[c, :, band], preferred_element_type=floats).astype(halves)
        for chunk in chunks:
            for band in bands:
                total[chunk, band] += contract_cols(slope_buf[c, chunk], weight_buf[0, c, band, :])

    @pl.when(step == 2 * cols - 1)
    def _():
        for chunk in chunks:
            normed_grad, normal_one = total[chunk], normal[chunk]
            first_grad = norm_back(normed_grad * vector(1), normal_one, scale[chunk, 0:1])
            first_grad_ref[chunk] = first_grad
            attn_grad_ref[chunk] = first_grad.astype(halves)
            sums_ref[0:1] += jnp.sum(first_grad, 0, keepdims=True)
            sums_ref[1:2] += jnp.sum(normed_grad * normal_one, 0, keepdims=True)
            sums_ref[2:3] += jnp.sum(normed_grad, 0, keepdims=True)


def middle(own, mixed, first, rest, biases, vectors, cot):
    rows, model = own.shape
    cols = first.shape[0]
    halves, floats = jnp.bfloat16, jnp.float32
    whole = lambda shape: pl.BlockSpec(shape, lambda i: (0,) * len(shape))
    wide = lambda kind: pltpu.VMEM((rows, model), kind)
    return pl.pallas_call(
        functools.partial(middle_kernel, cols),
        grid=(2 * cols,),
        in_specs=[
            whole((rows, model)), whole(mixed.shape),
            pl.BlockSpec((cols, model, WINDOW), lambda i: (0, 0, O_AT // WINDOW)),
            pl.BlockSpec(memory_space=pl.ANY),
            pl.BlockSpec((1, *biases.shape[1:]), lambda i: (lax.rem(i, cols), 0, 0)),
            *[whole((model,))] * 6, pl.BlockSpec(memory_space=pl.ANY),
        ],
        out_specs=[
            whole((rows, model)), whole((rows, model)), whole((rows, model)),
            pl.BlockSpec((2, 1, model, rest.shape[-1]), lambda i: (0, jnp.maximum(i - cols, 0), 0, 0)),
            whole((8 + cols + -cols % 8, model)),
        ],
        out_shape=[
            jax.ShapeDtypeStruct((rows, model), halves), jax.ShapeDtypeStruct((rows, model), floats),
            jax.ShapeDtypeStruct((rows, model), halves), jax.ShapeDtypeStruct(rest.shape, halves),
            jax.ShapeDtypeStruct((8 + cols + -cols % 8, model), floats),
        ],
        scratch_shapes=[
            wide(floats), pltpu.VMEM((rows, 128), floats), wide(floats), wide(halves), pltpu.VMEM((model, rows), halves), wide(halves),
            pltpu.VMEM((model, rows), halves), pltpu.VMEM((cols, rows, rest.shape[-1]), halves),
            pltpu.VMEM((cols, rows, rest.shape[-1]), halves), wide(floats), wide(halves),
            pltpu.VMEM(rest.shape, halves), pltpu.SemaphoreType.DMA((2, cols + 1)),
        ],
        compiler_params=pltpu.CompilerParams(vmem_limit_bytes=56 << 20),
        name="middle",
    )(own, mixed, first, rest, biases, *vectors, cot)


class Inbox:
    def __init__(self, ref, size):
        self.ref, self.size = ref, size

    def __call__(self, way, e):
        return self.ref.at[0 if self.size == 2 else (1 - way) // 2, e]


def backward_kernel(sizes, micro, grad_ref, share_ref, first_ref, turned_ref, mixed_ref, lse_ref, q_ref, k_ref, v_ref,
                    mask_ref, part_ref, vec_ref,
                    out_ref,
                    mine_buf, core_buf, stage_buf, in_a, in_b, in_c, in_d, in_z, tok_buf, tok_in, vec_buf,
                    weights, mixed_buf, q_buf, k_buf, v_buf, every_t, grad_t, mask, acc, spread, block_sum,
                    send_sems, recv_sems, local_sems, free_sem):
    floats, halves = jnp.float32, jnp.bfloat16
    lines, device = place(sizes)
    (x, ns), (y, ny), (k, _), (z, cols) = (lines[a] for a in "xykz")
    model = first_ref.shape[1]
    back_rows = micro * grad_ref.shape[1]
    block_rows = 3 * part_ref.shape[-2]
    sums_ref = out_ref.at[pl.ds(back_rows + block_rows, out_ref.shape[0] - back_rows - block_rows)]

    def back(m, begin=0, size=None):
        return pl.ds(pl.multiple_of(m * grad_ref.shape[1] + begin, 8), size or grad_ref.shape[1])

    half = part_ref.shape[-1] // 2
    rb = part_ref.shape[-2]
    rows = grad_ref.shape[1]
    reach = -(-(DOC_MOST - 1) // rows)
    parts = [pl.ds(p * half, half) for p in (0, 1)]
    used = [0]

    def local(source, target):
        copy = pltpu.make_async_copy(source, target, local_sems.at[used[0]])
        used[0] += 1
        copy.start()
        return copy

    def rows_of(n):
        return pl.ds(n % 2 * (rb // 2), rb // 2)

    planes = [local(part_ref.at[n // 2, :, :, :, k, rows_of(n)], mine_buf.at[n // 2 + 1, :, :, :, rows_of(n)]) for n in range(4)]
    loads = [local(*pair) for pair in ((first_ref, weights), (mixed_ref, mixed_buf), (q_ref, q_buf), (share_ref, out_ref.at[pl.ds(0, back_rows)]))]
    loads += [local(k_ref, k_buf), local(v_ref, v_buf)]
    loads += [local(mask_ref, mask)]
    late = [local(turned_ref, every_t)]
    greet(lines, device)
    post = Post(device, send_sems, recv_sems)

    def give(n):
        post.send(("k", n), lambda: (
            "k", 1 - k, part_ref.at[n // 2, :, :, :, 1 - k, rows_of(n)], core_buf.at[n // 2, :, :, :, rows_of(n)], None))

    def plus(target, source):
        target[...] = target[...] + source[...]

    def plus_grid(target, source, first, second):
        @pl.loop(0, first * second)
        def _(n):
            at = (n // second, lax.rem(n, second))
            plus(target.at[at], source.at[at])

    def plus_row(target, source, first):
        @pl.loop(0, first)
        def _(n):
            plus(target.at[n], source.at[n])

    class Stream:
        def __init__(self, name, j, begin, size, r):
            cs = pl.ds(begin, size)
            self.second = [
                LineReduce(post, (name, "a"), "x", lines["x"], lambda i: mine_buf.at[j, cs, i, :, r, parts[0]],
                           lambda way, e: Inbox(in_a.at[j], ns)(way, e).at[cs, :, r], lambda t, s: plus_grid(t, s, size, ny)),
                LineReduce(post, (name, "b"), "y", lines["y"], lambda i: mine_buf.at[j, cs, :, i, r, parts[1]],
                           lambda way, e: Inbox(in_b.at[j], ny)(way, e).at[cs, :, r], lambda t, s: plus_grid(t, s, size, ns)),
            ]
            self.third = [
                LineReduce(post, (name, "c"), "y", lines["y"], lambda i: mine_buf.at[j, cs, x, i, r, parts[0]],
                           lambda way, e: Inbox(in_c.at[j], ny)(way, e).at[cs, r], lambda t, s: plus_row(t, s, size)),
                LineReduce(post, (name, "d"), "x", lines["x"], lambda i: mine_buf.at[j, cs, i, y, r, parts[1]],
                           lambda way, e: Inbox(in_d.at[j], ns)(way, e).at[cs, r], lambda t, s: plus_row(t, s, size)),
            ]

    def line_z(name, j, r):
        return LineReduce(post, ("z", name), "z", lines["z"], lambda i: mine_buf.at[j, i, x, y, r],
                          lambda way, e: in_z.at[j, (1 - way) // 2, e, r], plus)

    ffn = [Stream(("s", n), n // 2 + 1, 0, cols, rows_of(n)) for n in range(4)]
    ffn_z = [line_z(n, n // 2 + 1, rows_of(n)) for n in range(4)]
    attn = [Stream(("u", c), 0, c, 1, pl.ds(0, rb)) for c in range(cols)]

    def take_y(c, e):
        reduce_to(post, ("y", c), "z", lines["z"], c, e, mine_buf.at[0, c, x, y], lambda way, e: in_z.at[0, (1 - way) // 2, e], plus)

    def half_of(h):
        return pl.ds(h * (rows // 2), rows // 2)

    def line_tokens(m, h):
        at = half_of(h)
        return LineReduce(post, ("t", m, h), "z", lines["z"], lambda i: tok_buf.at[m, i, at],
                          lambda way, e: tok_in.at[m, (1 - way) // 2, e, at], plus, reach)

    tokens = [[line_tokens(m, h) for h in range(2)] for m in range(micro)]

    def start(*group):
        for line in group:
            line.start()

    def finish(*group):
        for line in group:
            line.finish()

    def core(n):
        planes[n].wait()
        r = rows_of(n)
        post.wait(("k", n), "k", 1 - k, core_buf.at[n // 2, :, :, :, r])

        @pl.loop(0, cols * ns * ny)
        def _(i):
            at = (i // (ns * ny), lax.rem(i // ny, ns), lax.rem(i, ny), r)
            plus(mine_buf.at[(n // 2 + 1, *at)], core_buf.at[(n // 2, *at)])

    def vector_start(stage, axis):
        mine, size = lines[axis]
        vec_buf[stage, 1 + mine] = vec_buf[stage, 0]
        for t in range(1, size):
            post.send(("v", stage, t), lambda t=t: (
                axis, lax.rem(mine + t, size), vec_buf.at[stage, 0], vec_buf.at[stage, 1 + mine], None))

    def vector_finish(stage, axis, out):
        mine, size = lines[axis]
        for t in range(1, size):
            origin = lax.rem(mine + size - t, size)
            post.wait(("v", stage, t), axis, origin, vec_buf.at[stage, 1 + origin])
        total = vec_buf[stage, 1]
        for i in range(1, size):
            total = total + vec_buf[stage, 1 + i]
        out[...] = total

    places = place_of(rows)
    small = vec_ref.shape[0]
    vec_buf[0, 0] = jnp.zeros_like(vec_buf[0, 0])
    vec_buf[0, 0, 0:small] = vec_ref[...]

    def unit(m, c):
        mixed_grad = jnp.dot(grad_ref[m], weights[c, :, O_AT : O_AT + WINDOW], preferred_element_type=floats).astype(halves)
        mixed_grad = jnp.where(places > 0, mixed_grad.astype(floats), 0.0)
        product = mixed_grad * mixed_buf[c, m].astype(floats)
        product_high = product.astype(halves)
        product_low = (product - product_high.astype(floats)).astype(halves)
        pick = (
            lax.broadcasted_iota(jnp.int32, (8, WINDOW), 1) // HEAD_DIM == lax.broadcasted_iota(jnp.int32, (8, WINDOW), 0) + 1
        ).astype(floats).astype(halves)
        inner = contract_cols(pick, product_high) + contract_cols(pick, product_low)
        value_side = pltpu.roll(mixed_grad, WINDOW - HEAD_DIM, 1).astype(halves)
        queries = q_buf[m, c]
        query_heads = jnp.concatenate([keep(queries, places, h + 1) for h in range(3)], 0)
        grad_heads = jnp.concatenate([keep(value_side, places, h) for h in range(3)], 0)
        side_by_side = lambda ref_rows: jnp.concatenate([ref_rows(h) for h in range(3)], 1)
        log_total = side_by_side(lambda h: lse_ref[m, c, h : h + 1])
        inner_row = side_by_side(lambda h: inner[h : h + 1])
        acc[...] = jnp.zeros_like(acc)
        key_weight = weights[c, :, K_AT : K_AT + WINDOW]
        value_weight = weights[c, :, V_AT : V_AT + WINDOW]

        def step(block, value_bias):
            keys = k_buf[m, c, block]
            values = v_buf[m, c, block]
            keys_t = keys.T
            hidden = mask[m, block].astype(floats)
            hidden = jnp.concatenate([hidden] * 3, 1)
            p = jnp.exp(contract_cols(keys, query_heads) + hidden - log_total)
            prob_grad = contract_cols(values, grad_heads)
            score_grad = (p * (prob_grad - inner_row)).astype(halves)
            value_grad = jnp.dot(p.astype(halves), grad_heads, preferred_element_type=floats)
            key_grad = jnp.dot(score_grad, query_heads, preferred_element_type=floats)
            for h in range(3):
                acc[pl.ds(h * HEAD_DIM, HEAD_DIM), :] += jnp.dot(
                    keys_t[(h + 1) * HEAD_DIM : (h + 2) * HEAD_DIM], score_grad[:, h * rows : (h + 1) * rows], preferred_element_type=floats)
            key_low, value_low = key_grad.astype(halves), value_grad.astype(halves)
            k_buf[m, c, block] = key_low
            v_buf[m, c, block] = value_low
            spread[m, block] += contract_cols(key_low, key_weight) + contract_cols(value_low, value_weight)
            return value_bias + jnp.sum(value_low.astype(floats), 0, keepdims=True)

        value_bias = jnp.zeros((1, WINDOW), floats)
        for block in range(cols):
            value_bias = step(block, value_bias)
        query_low = (acc[...].T * HEAD_DIM ** -0.5).astype(halves)
        q_buf[m, c] = query_low
        vec_buf[0, 0, pl.ds(small + c, 1), 0:WINDOW] += jnp.sum(query_low.astype(floats), 0, keepdims=True)
        vec_buf[0, 0, pl.ds(small + c, 1), WINDOW : 2 * WINDOW] += value_bias
        out_ref[back(m)] += contract_cols(query_low, weights[c, :, Q_AT : Q_AT + WINDOW])

    def send_tokens(m):
        out_ref[back(m)] += spread[m, z]

        @pl.loop(0, cols)
        def _(block):
            tok_buf[m, block] = spread[m, block].astype(halves)

        start(*tokens[m])

    def weight_grads(c):
        strip = block_sum.shape[0]

        @pl.loop(0, model // strip)
        def _(part):
            base = pl.multiple_of(part * strip, strip)
            side = pl.ds(base, strip)
            block_sum[...] = jnp.zeros_like(block_sum)
            for m in range(micro):
                mine_at = pl.ds(pl.multiple_of((m * cols + z) * rows, rows), rows)
                block_sum[:, Q_AT : Q_AT + WINDOW] += jnp.dot(every_t[side, mine_at], q_buf[m, c], preferred_element_type=floats)
                all_at = pl.ds(m * cols * rows, cols * rows)
                block_sum[:, K_AT : K_AT + WINDOW] += jnp.dot(
                    every_t[side, all_at], k_buf[m, c].reshape(-1, WINDOW), preferred_element_type=floats)
                block_sum[:, V_AT : V_AT + WINDOW] += jnp.dot(
                    every_t[side, all_at], v_buf[m, c].reshape(-1, WINDOW), preferred_element_type=floats)
                block_sum[:, O_AT : O_AT + WINDOW] += jnp.dot(
                    grad_t[side, m * rows : (m + 1) * rows], mixed_buf[c, m], preferred_element_type=floats)
            for i in range(strip // (2 * rb)):
                ours = pl.ds(pl.multiple_of((2 * i + k) * rb, 16), rb)
                theirs = pl.ds(pl.multiple_of((2 * i + 1 - k) * rb, 16), rb)
                chip = part * (strip // (2 * rb)) + i
                mine_buf[0, c, chip // ny, lax.rem(chip, ny)] = block_sum[ours].astype(halves)
                stage_buf[c, chip // ny, lax.rem(chip, ny)] = block_sum[theirs].astype(halves)

    waited = []

    def attn_give(c):
        if not waited:
            pl.semaphore_wait(free_sem, 1)
            waited.append(c)
        post.send(("g", c), lambda: ("k", 1 - k, stage_buf.at[c], core_buf.at[0, c], None))

    def attn_add(c):
        post.wait(("g", c), "k", 1 - k, core_buf.at[0, c])

        @pl.loop(0, ns * ny)
        def _(n):
            at = (c, n // ny, lax.rem(n, ny))
            plus(mine_buf.at[(0, *at)], core_buf.at[(0, *at)])

    streams = ffn + attn
    added = set()

    def take_core(n):
        if n < 4:
            core(n)
            added.add(n)
            if added >= {0, 1} and n in (0, 1):
                pl.semaphore_signal(free_sem, 1, device_id=device("k", 1 - k), device_id_type=MESH)
        else:
            attn_add(n - 4)
        start(*streams[n].second)

    def take_second(n):
        finish(*streams[n].second)
        start(*streams[n].third)

    def take_third(n):
        finish(*streams[n].third)
        if n < 4:
            start(ffn_z[n])

    def along(line, e):
        for way in (1, -1):
            line.take(way, e)
            if e:
                line.forward(way, e)

    def take_tokens(m, h, e):
        line = tokens[m][h]
        if e == 0:
            def add(target, source):
                out_ref[back(m, h * (rows // 2), rows // 2)] += source[...].astype(floats)

            line.add = add
        along(line, e)

    def vectors(stage):
        if stage:
            vector_finish(stage - 1, "kyxz"[stage - 1], vec_buf.at[stage, 0] if stage < 4 else sums_ref)
        if stage < 4:
            vector_start(stage, "kyxz"[stage])

    def load():
        for copy in loads:
            copy.wait()

    act = {
        "L": load, "G": lambda n: give(n) if n < 4 else attn_give(n - 4), "A": take_core, "B": take_second, "C": take_third,
        "Z": lambda n, e: along(ffn_z[n], e), "S": send_tokens, "T": take_tokens, "Y": take_y, "V": vectors,
    }
    head, tail, order = split_plan([("U", "W", task[1], 0) if task[0] == "W" else task for task in BACKWARD_PLAN])
    kinds = [item[0] == "W" for item in order]
    heads = [item[1] if item[0] == "W" else item[0] for item in order]
    micros = [0 if item[0] == "W" else item[1] for item in order]
    act[head[0][0]](*head[0][1:])
    spread[...] = jnp.zeros_like(spread)
    for m in range(micro):
        grad_t[:, m * rows : (m + 1) * rows] = grad_ref[m].T
    for task in head[1:]:
        act[task[0]](*task[1:])

    @pl.loop(0, len(order))
    def _(step):
        c, m, kind = pick(step, heads), pick(step, micros), pick(step, [int(k_) for k_ in kinds])

        @pl.when(kind == 0)
        def _():
            unit(m, c)

        @pl.when(kind == 1)
        def _():
            @pl.when(step == kinds.index(True))
            def _():
                for copy in late:
                    copy.wait()

            weight_grads(c)

        for i, tasks in enumerate(tail[:-1]):
            if tasks:
                @pl.when(step == i)
                def _(tasks=tasks):
                    for task in tasks:
                        act[task[0]](*task[1:])

    for task in tail[-1]:
        act[task[0]](*task[1:])
    for j in range(3):
        out_ref[pl.ds(back_rows + j * rb, rb)] = mine_buf[j, z, x, y].astype(floats)
    post.close()


def backward(sizes, grad, share, first, turned, mixed, lse, q, k, v, mask, part, vectors):
    ns, nr, nc = sizes
    ny = nr // 2
    micro, rows, model = grad.shape
    w = part.shape[-1]
    rb = model // (ns * nr)
    halves, floats = jnp.bfloat16, jnp.float32
    reach = min(nc - 1, -(-(DOC_MOST - 1) // rows))
    streams = 4 + nc
    count = 4 + nc + 4 * (ny - 1 + ns - 1) * streams + 4 * 2 * (nc - 1) + 2 * nc * 2 + micro * 4 * reach + (1 + ny - 1 + ns - 1 + nc - 1)
    widest = max(ns, ny, nc, 2)
    ways = lambda n: 1 if n == 2 else 2
    vec_shape = (vectors.shape[0] + nc + -nc % 8, model)
    vmem = pl.BlockSpec(memory_space=pltpu.VMEM)
    anywhere = pl.BlockSpec(memory_space=pl.ANY)
    buf = lambda *shape, kind=halves: pltpu.VMEM(shape, kind)
    total = micro * rows + 3 * rb + vec_shape[0]
    return pl.pallas_call(
        functools.partial(backward_kernel, sizes, micro),
        out_shape=jax.ShapeDtypeStruct((total, model), floats),
        in_specs=[vmem, anywhere, anywhere, anywhere, anywhere, vmem, anywhere, anywhere, anywhere, anywhere, anywhere, vmem],
        out_specs=vmem,
        scratch_shapes=[
            buf(3, nc, ns, ny, rb, w), buf(2, nc, ns, ny, rb, w), buf(nc, ns, ny, rb, w),
            buf(3, ways(ns), max(ns - 1, 1), nc, ny, rb, w // 2), buf(3, ways(ny), max(ny - 1, 1), nc, ns, rb, w // 2),
            buf(3, ways(ny), max(ny - 1, 1), nc, rb, w // 2), buf(3, ways(ns), max(ns - 1, 1), nc, rb, w // 2),
            buf(3, 2, max(nc - 1, 1), rb, w), buf(micro, nc, rows, model), buf(micro, 2, max(reach, 1), rows, model),
            buf(4, 1 + widest, *vec_shape, kind=floats),
            buf(nc, model, w), buf(nc, micro, rows, WINDOW), buf(micro, nc, rows, WINDOW),
            buf(micro, nc, nc, rows, WINDOW), buf(micro, nc, nc, rows, WINDOW),
            buf(model, micro * nc * rows), buf(model, micro * rows),
            buf(micro, nc, rows, rows), buf(WINDOW, rows, kind=floats), buf(micro, nc, rows, model, kind=floats), buf(model // 2, w, kind=floats),
            pltpu.SemaphoreType.DMA((count,)), pltpu.SemaphoreType.DMA((count,)), pltpu.SemaphoreType.DMA((24,)), pltpu.SemaphoreType.REGULAR,
        ],
        compiler_params=pltpu.CompilerParams(collective_id=3, has_side_effects=True, vmem_limit_bytes=62 << 20),
        name="backward",
    )(grad, share.reshape(micro * rows, model), first, turned, mixed, lse, q, k, v, mask,
      part.reshape(2, nc, ns, ny, 2, rb, w), vectors)


def per_device_plain(sizes, inputs, segment_ids, query_weight, key_weight, value_weight, query_bias, value_bias,
               output_weight, output_bias, first_gain, first_shift, hidden_weight, hidden_bias, down_weight,
               down_bias, second_gain, second_shift, cotangent):
    floats, halves = jnp.float32, jnp.bfloat16
    cols = sizes[2]
    micro, _, rows, model = inputs.shape
    length = segment_ids.shape[-1]
    width = query_weight.shape[1]
    here = lax.axis_index("col")
    own = inputs[:, 0]
    shard = jnp.stack([
        jnp.concatenate([query_weight, key_weight, value_weight, output_weight.T], 1),
        hidden_weight,
        down_weight.T,
    ])
    biases = lax.all_gather(jnp.concatenate([query_bias, value_bias, hidden_bias]), "col", axis=0)
    everything, gathered = gather(sizes, own, shard)
    everything = everything.reshape(micro, length, model)
    attn_weights = gathered[0]
    wq, wk, wv, wot = (attn_weights[:, :, i * width : (i + 1) * width] for i in range(4))
    hidden_full, down_full = gathered[1], gathered[2]
    bq, bv, bh = biases[:, :width], biases[:, width : 2 * width], biases[:, 2 * width :]
    seg_all = segment_ids[:, 0]
    seg_own = lax.dynamic_slice_in_dim(seg_all, here * rows, rows, 1)
    first_key = jnp.sum((seg_all < seg_own[:, :1]).astype(jnp.int32), 1)
    last_key = jnp.sum((seg_all <= seg_own[:, -1:]).astype(jnp.int32), 1)
    bounds = jnp.stack([first_key // KEY_BLOCK, (last_key + KEY_BLOCK - 1) // KEY_BLOCK], 1)

    mixed, lse, q, k, v = attend(bounds, own, everything, wq, wk, wv, bq.astype(floats), bv.astype(floats), seg_own, seg_all)
    total = micro * rows
    flat = lambda a: a.reshape(total, -1)
    mixed_flat = mixed.reshape(cols, total, width)
    attn = sum(contract_cols(mixed_flat[c], wot[c]) for c in range(cols))
    first_sum = flat(own).astype(floats) + attn + output_bias.astype(floats)
    normal_one, scale_one = norm_parts(first_sum)
    gain_one = first_gain.astype(floats)
    normed = normal_one * gain_one + first_shift.astype(floats)
    normed_low = normed.astype(halves)
    ffn = 0
    activated, slopes = [], []
    for c in range(cols):
        hidden = jnp.dot(normed_low, hidden_full[c], preferred_element_type=floats) + bh[c].astype(floats)
        half_erf = 0.5 * lax.erf(hidden * 0.7071067811865476) + 0.5
        act = (hidden * half_erf).astype(halves)
        slope = half_erf + hidden * (jnp.exp(-0.5 * hidden * hidden) * 0.3989422804014327)
        activated.append(act)
        slopes.append(slope.astype(halves))
        ffn = ffn + contract_cols(act, down_full[c])
    second_sum = normed + ffn + down_bias.astype(floats)
    normal_two, scale_two = norm_parts(second_sum)
    gain_two = second_gain.astype(floats)
    outputs = (normal_two * gain_two + second_shift.astype(floats)).astype(halves)
    cot = flat(cotangent[:, 0]).astype(floats)
    second_grad = norm_back(cot * gain_two, normal_two, scale_two)
    ffn_grad = second_grad.astype(halves)
    hidden_grads, down_grads, hidden_bias_grads = [], [], []
    normed_grad = second_grad
    for c in range(cols):
        pre = (jnp.dot(ffn_grad, down_full[c], preferred_element_type=floats) * slopes[c].astype(floats)).astype(halves)
        hidden_grads.append(contract_rows(normed_low, pre).astype(halves))
        down_grads.append(contract_rows(ffn_grad, activated[c]).astype(halves))
        hidden_bias_grads.append(jnp.sum(pre.astype(floats), 0))
        normed_grad = normed_grad + contract_cols(pre, hidden_full[c])
    first_grad = norm_back(normed_grad * gain_one, normal_one, scale_one)
    attn_grad = first_grad.astype(halves)
    dq, dk, dv = attend_back(bounds, attn_grad.reshape(micro, rows, model), wot, mixed, lse, q, k, v, seg_own, seg_all)
    every_flat = everything.reshape(micro * length, model)
    attn_grads = []
    own_share = first_grad
    spread = 0
    for c in range(cols):
        dq_c, dk_c, dv_c = dq[c].reshape(total, width), dk[c].reshape(micro * length, width), dv[c].reshape(micro * length, width)
        attn_grads.append(jnp.concatenate([
            contract_rows(flat(own), dq_c), contract_rows(every_flat, dk_c), contract_rows(every_flat, dv_c),
            contract_rows(attn_grad, mixed_flat[c]),
        ], 1).astype(halves))
        own_share = own_share + contract_cols(dq_c, wq[c])
        spread = spread + contract_cols(dk_c, wk[c]) + contract_cols(dv_c, wv[c])
    bias_q = jnp.sum(dq.astype(floats), (1, 2)).reshape(-1)
    bias_v = jnp.sum(dv.astype(floats), (1, 2)).reshape(-1)
    vectors = jnp.concatenate([
        jnp.sum(first_grad, 0), jnp.sum(normed_grad * normal_one, 0), jnp.sum(normed_grad, 0), jnp.sum(second_grad, 0),
        jnp.sum(cot * normal_two, 0), jnp.sum(cot, 0), bias_q, bias_v, *hidden_bias_grads,
    ]).reshape(-1, model)
    partial = jnp.stack([jnp.stack(attn_grads), jnp.stack(hidden_grads), jnp.stack(down_grads)])
    input_grad, reduced, sums = reduce(sizes, own_share.reshape(micro, rows, model),
                                       spread.astype(halves).reshape(micro, cols, rows, model), partial, vectors)
    attn_block = reduced[0]
    piece = lambda i: attn_block[:, i * width : (i + 1) * width]
    mine = lambda vector, size: lax.dynamic_slice_in_dim(vector.reshape(-1), here * size, size, 0)
    return (
        outputs.reshape(micro, 1, rows, model), input_grad[:, None],
        piece(0), piece(1), piece(2), mine(sums[6], width), mine(sums[7], width), piece(3).T,
        sums[0], sums[1], sums[2], reduced[1], mine(sums[8:], hidden_bias.shape[0]), reduced[2].T,
        sums[3], sums[4], sums[5],
    )


def deliver_kernel(sizes, width, results, *refs):
    *outs, back_ref, block_ref, sums_ref, sems = refs
    micro, rows, _ = back_ref.shape
    rb = block_ref.shape[1]
    at = micro * rows
    pieces = [(results.at[pl.ds(at + j * rb, rb)], block_ref.at[j]) for j in range(3)]
    pieces += [(results.at[pl.ds(at + 3 * rb, sums_ref.shape[0])], sums_ref)]
    pieces += [(results.at[pl.ds(m * rows, rows)], back_ref.at[m]) for m in range(micro)]
    copies = [
        pltpu.make_async_copy(source, target, sems.at[i])
        for i, (source, target) in enumerate(pieces)
    ]
    for copy in copies:
        copy.start()
    (input_grad, query, key, value, query_bias, value_bias, output, output_bias, first_gain, first_shift, hidden, hidden_bias, down,
     down_bias, second_gain, second_shift) = outs
    here = lax.axis_index("col")
    for copy in copies[:4]:
        copy.wait()
    for i, ref in enumerate((query, key, value)):
        ref[...] = block_ref[0, :, i * width : (i + 1) * width]
    output[...] = block_ref[0, :, 3 * width : 4 * width].T
    hidden[...] = block_ref[1]
    down[...] = block_ref[2]
    for i, ref in enumerate((output_bias, first_gain, first_shift, down_bias, second_gain, second_shift)):
        ref[...] = sums_ref[i : i + 1].reshape(-1)
    hidden_bias[...] = sums_ref[pl.ds(8 + here, 1)].reshape(-1)
    heads_at = sums_ref.shape[0] - (sizes[2] + -sizes[2] % 8)
    row = sums_ref[pl.ds(heads_at + here, 1)]
    query_bias[...] = row[:, 0:width].reshape(-1)
    value_bias[...] = row[:, WINDOW : WINDOW + width].reshape(-1)
    for copy in copies[4:]:
        copy.wait()
    input_grad[...] = back_ref[...]


def deliver(sizes, width, tokens_shape, block_shape, results):
    micro, rows, model = tokens_shape
    rb, w = block_shape
    sums_rows = results.shape[0] - micro * rows - 3 * rb
    vmem = pl.BlockSpec(memory_space=pltpu.VMEM)
    square, vector = (rb, width), (model,)
    shapes = [tokens_shape, square, square, square, (width,), (width,), (width, rb), vector, vector, vector, (rb, w), (w,), (rb, w),
              vector, vector, vector]
    return pl.pallas_call(
        functools.partial(deliver_kernel, sizes, width),
        out_shape=[jax.ShapeDtypeStruct(shape, jnp.float32) for shape in shapes],
        in_specs=[pl.BlockSpec(memory_space=pltpu.MemorySpace.HBM)],
        out_specs=[vmem] * len(shapes),
        scratch_shapes=[pltpu.VMEM(a, jnp.float32) for a in (tokens_shape, (3, rb, w), (sums_rows, model))] + [pltpu.SemaphoreType.DMA((4 + micro,))],
        compiler_params=pltpu.CompilerParams(vmem_limit_bytes=32 << 20),
        name="deliver",
    )(results)


def per_device_fused(sizes, inputs, segment_ids, query_weight, key_weight, value_weight, query_bias, value_bias,
               output_weight, output_bias, first_gain, first_shift, hidden_weight, hidden_bias, down_weight,
               down_bias, second_gain, second_shift, cotangent):
    floats, halves = jnp.float32, jnp.bfloat16
    cols = sizes[2]
    micro, _, rows, model = inputs.shape
    length = segment_ids.shape[-1]
    width = query_weight.shape[1]
    here = lax.axis_index("col")
    own = inputs[:, 0]
    rest, first, turned, mask, biases, mixed, lse, q, k, v = forward(
        sizes, own, (query_weight, key_weight, value_weight, output_weight, hidden_weight, down_weight.T), hidden_bias, query_bias, value_bias, segment_ids)
    first = first.reshape(cols, model, 4 * width)
    total = micro * rows
    flat = lambda a: a.reshape(total, -1)
    outputs, first_grad, attn_grad, part, sums = middle(
        flat(own), mixed.reshape(cols, total, WINDOW), first, rest.reshape(2, cols, model, -1), biases,
        (output_bias, first_gain, first_shift, down_bias, second_gain, second_shift), flat(cotangent[:, 0]))
    parted = lambda a: a.reshape(micro, rows, model)
    results = backward(sizes, parted(attn_grad), parted(first_grad), first, turned, mixed, lse, q, k, v,
                                         mask, part, sums)
    grads = deliver(sizes, width, own.shape, hidden_weight.shape, results)
    return (outputs.reshape(micro, 1, rows, model), grads[0][:, None], *grads[1:12], grads[12].T, *grads[13:])


def per_device(sizes, inputs, segment_ids, query_weight, *rest):
    micro, _, rows, _ = inputs.shape
    fits = (query_weight.shape == (query_weight.shape[0] // 32 * 32, 3 * HEAD_DIM) and micro == 2 and sizes[2] == 4
            and DOC_MOST // 2 == rows)
    return (per_device_fused if fits else per_device_plain)(sizes, inputs, segment_ids, query_weight, *rest)


def solution(mesh):
    sizes = tuple(mesh.shape[name] for name in ("seq", "row", "col"))
    block, line = P(("seq", "row"), "col"), P("col", ("seq", "row"))
    tokens = P(None, ("seq", "row"), "col", None)
    placed = (tokens, P(None, ("seq", "row"), None), block, block, block, P("col"), P("col"), line, P(), P(), P(),
              block, P("col"), line, P(), P(), P(), tokens)
    given = (tokens, tokens, block, block, block, P("col"), P("col"), line, P(), P(), P(), block, P("col"), line,
             P(), P(), P())
    return jax.shard_map(functools.partial(per_device, sizes), mesh=mesh, in_specs=placed, out_specs=given, check_vma=False)
```

```python
import functools

import jax
import jax.numpy as jnp
from jax import lax
from jax.experimental import pallas as pl
from jax.experimental.pallas import tpu as pltpu
from jax.sharding import PartitionSpec as P

HEAD_DIM = 64
NORM_EPS = 1e-05
MASK_VALUE = -1000000000.0
DOC_MOST = 512
KEY_BLOCK = 256
MESH = pl.DeviceIdType.MESH


def contract_rows(left, right):
    return lax.dot_general(
        left, right, (((0,), (0,)), ((), ())), preferred_element_type=jnp.float32
    )


def contract_cols(left, right):
    return lax.dot_general(
        left, right, (((1,), (1,)), ((), ())), preferred_element_type=jnp.float32
    )


def norm_parts(summed):
    deviation = summed - jnp.mean(summed, -1, keepdims=True)
    scale = lax.rsqrt(jnp.mean(deviation * deviation, -1, keepdims=True) + NORM_EPS)
    return deviation * scale, scale


def norm_back(pull, normal, scale):
    return scale * (
        pull - jnp.mean(pull, -1, keepdims=True) - normal * jnp.mean(pull * normal, -1, keepdims=True)
    )

FORWARD_PLAN = (
    ("Zs", 1), ("Zs", 0), ("Z", 1, 1), ("Z", 0, 1), ("Z", 1, 2), ("Z", 1, 3), ("Z", 0, 2), ("Zs", 4), ("Z", 0, 3),
    ("Zs", 2), ("B", 1), ("Ts", 1), ("Z", 4, 1), ("Z", 2, 1), ("Zs", 5), ("Zs", 3), ("B", 0), ("Z", 4, 2),
    ("Z", 2, 2), ("Ts", 0), ("Z", 5, 1), ("Z", 4, 3), ("C", 0), ("Z", 2, 3), ("Z", 3, 1), ("B", 4), ("Z", 3, 2),
    ("Z", 3, 3), ("T", 1, 1), ("T", 0, 1), ("B", 2), ("K", 0), ("C", 1), ("Z", 5, 2), ("T", 1, 2), ("Ts", 3),
    ("C", 4), ("K", 1), ("T", 0, 2), ("P", 0, 0), ("Ts", 2), ("Z", 5, 3), ("R", 0), ("B", 3), ("U", 0, 0),
    ("P", 0, 1), ("T", 3, 1), ("U", 0, 1), ("P", 0, 2), ("C", 2), ("P", 0, 3), ("T", 2, 1), ("P", 1, 0), ("B", 5),
    ("U", 0, 2), ("K", 2), ("P", 1, 1), ("U", 0, 3), ("K", 4), ("P", 1, 2), ("P", 1, 3), ("C", 3), ("T", 3, 2),
    ("T", 2, 2), ("R", 1), ("U", 1, 0), ("U", 1, 1), ("C", 5), ("U", 1, 2), ("K", 3), ("U", 1, 3), ("K", 5),
)
BACKWARD_PLAN = (
    ("G", 1), ("G", 3), ("L",), ("U", 2, 0), ("A", 1), ("G", 0), ("U", 0, 0), ("A", 3), ("U", 1, 0), ("U", 3, 0),
    ("S", 0), ("G", 2), ("B", 1), ("A", 0), ("U", 0, 1), ("A", 2), ("B", 3), ("T", 0, 0, 1), ("C", 1), ("U", 2, 1),
    ("U", 1, 1), ("T", 0, 1, 1), ("U", 3, 1), ("S", 1), ("B", 2), ("W", 2), ("V", 0), ("G", 6), ("B", 0), ("W", 3),
    ("V", 1), ("Z", 1, 2), ("A", 6), ("G", 7), ("C", 3), ("W", 0), ("C", 2), ("G", 4), ("A", 7), ("T", 1, 1, 1),
    ("W", 1), ("Z", 3, 2), ("V", 2), ("G", 5), ("C", 0), ("A", 4), ("B", 7), ("V", 3), ("A", 5), ("Z", 1, 1),
    ("B", 4), ("Z", 2, 2), ("C", 7), ("T", 1, 0, 1), ("B", 6), ("Y", 3, 3), ("B", 5), ("T", 1, 1, 0), ("Z", 3, 1),
    ("C", 4), ("C", 6), ("Y", 0, 3), ("Z", 0, 2), ("Y", 2, 2), ("T", 0, 1, 0), ("C", 5), ("Y", 1, 2), ("V", 4),
    ("Y", 3, 2), ("Y", 0, 2), ("Z", 0, 1), ("Z", 1, 0), ("T", 1, 0, 0), ("Z", 2, 1), ("Z", 3, 0), ("Y", 3, 1),
    ("Y", 2, 1), ("Y", 1, 1), ("T", 0, 0, 0), ("Y", 0, 1), ("Z", 0, 0), ("Z", 2, 0), ("Y", 2, 0), ("Y", 3, 0),
    ("Y", 1, 0), ("Y", 0, 0),
)
def attend_kernel(bounds, own_ref, all_ref, wq_ref, wk_ref, wv_ref, bq_ref, bv_ref,
                  segq_ref, segk_ref, mixed_ref, lse_ref, q_ref, k_ref, v_ref, bias, acc, top, total):
    micro = pl.program_id(0)
    low, high = bounds[micro, 0], bounds[micro, 1]
    floats, halves = jnp.float32, jnp.bfloat16
    width = wq_ref.shape[-1]
    heads = width // HEAD_DIM
    rows = own_ref.shape[1]

    @pl.when(pl.program_id(1) == 0)
    def _():
        same = segk_ref[0] == segq_ref[0, 0:1]
        bias[...] = jnp.where(same, 0.0, MASK_VALUE)

    queries = jnp.dot(own_ref[0], wq_ref[0], preferred_element_type=floats) + bq_ref[0]
    queries = queries.astype(halves) * jnp.asarray(HEAD_DIM ** -0.5, halves)
    q_ref[0, 0] = queries
    lane = lax.broadcasted_iota(jnp.int32, (rows, width), 1) // HEAD_DIM
    query_heads = [jnp.where(lane == h, queries, jnp.zeros_like(queries)) for h in range(heads)]
    acc[...] = jnp.zeros_like(acc)
    total[...] = jnp.zeros_like(total)
    top[...] = jnp.full_like(top, 2 * MASK_VALUE)

    def step(block, carry):
        at = pl.ds(pl.multiple_of(block * KEY_BLOCK, KEY_BLOCK), KEY_BLOCK)
        x = all_ref[0, at, :]
        keys = jnp.dot(x, wk_ref[0], preferred_element_type=floats).astype(halves)
        k_ref[0, 0, at, :] = keys
        values = (jnp.dot(x, wv_ref[0], preferred_element_type=floats) + bv_ref[0]).astype(halves)
        v_ref[0, 0, at, :] = values
        values_t = values.T
        mask = bias[at, :]
        for h in range(heads):
            s = contract_cols(keys, query_heads[h]) + mask
            old = top[h : h + 1]
            new = jnp.maximum(old, jnp.max(s, 0, keepdims=True))
            p = jnp.exp(s - new)
            shrink = jnp.exp(old - new)
            top[h : h + 1] = new
            total[h : h + 1] = total[h : h + 1] * shrink + jnp.sum(p, 0, keepdims=True)
            part = pl.ds(h * HEAD_DIM, HEAD_DIM)
            acc[part, :] = acc[part, :] * shrink + jnp.dot(
                values_t[h * HEAD_DIM : (h + 1) * HEAD_DIM], p.astype(halves), preferred_element_type=floats
            )
        return carry

    lax.fori_loop(low, high, step, 0)
    for h in range(heads):
        part = pl.ds(h * HEAD_DIM, HEAD_DIM)
        acc[part, :] = acc[part, :] / total[h : h + 1]
    mixed_ref[0, 0] = acc[...].T.astype(halves)
    lse_ref[0, 0] = top[...] + jnp.log(jnp.maximum(total[...], 1e-30))


def attend(bounds, own, everything, wq, wk, wv, bq, bv, seg_own, seg_all):
    micro, rows, model = own.shape
    length = everything.shape[1]
    cols, _, width = wq.shape
    halves = jnp.bfloat16
    weight = pl.BlockSpec((1, model, width), lambda m, c, b: (c, 0, 0))
    per = lambda a, b_: pl.BlockSpec((1, 1, a, b_), lambda m, c, b: (c, m, 0, 0))
    spec = pltpu.PrefetchScalarGridSpec(
        num_scalar_prefetch=1,
        grid=(micro, cols),
        in_specs=[
            pl.BlockSpec((1, rows, model), lambda m, c, b: (m, 0, 0)),
            pl.BlockSpec((1, length, model), lambda m, c, b: (m, 0, 0)),
            weight, weight, weight,
            pl.BlockSpec((1, 1, width), lambda m, c, b: (c, 0, 0)),
            pl.BlockSpec((1, 1, width), lambda m, c, b: (c, 0, 0)),
            pl.BlockSpec((1, 1, rows), lambda m, c, b: (m, 0, 0)),
            pl.BlockSpec((1, length, 1), lambda m, c, b: (m, 0, 0)),
        ],
        out_specs=[per(rows, width), per(8, rows), per(rows, width), per(length, width), per(length, width)],
        scratch_shapes=[
            pltpu.VMEM((length, rows), jnp.float32),
            pltpu.VMEM((width, rows), jnp.float32),
            pltpu.VMEM((8, rows), jnp.float32),
            pltpu.VMEM((8, rows), jnp.float32),
        ],
    )
    shape = lambda a, b_, d=halves: jax.ShapeDtypeStruct((cols, micro, a, b_), d)
    return pl.pallas_call(
        attend_kernel,
        grid_spec=spec,
        out_shape=[shape(rows, width), shape(8, rows, jnp.float32), shape(rows, width), shape(length, width), shape(length, width)],
        compiler_params=pltpu.CompilerParams(vmem_limit_bytes=48 << 20),
        name="attend",
    )(bounds, own, everything, wq, wk, wv, bq[:, None], bv[:, None],
      seg_own[:, None], seg_all[:, :, None])


def attend_back_kernel(bounds, grad_ref, wot_ref, mixed_ref, lse_ref, q_ref, k_ref, v_ref, segq_ref, segk_ref,
                       dq_ref, dk_ref, dv_ref, bias, acc):
    micro = pl.program_id(0)
    low, high = bounds[micro, 0], bounds[micro, 1]
    floats, halves = jnp.float32, jnp.bfloat16
    rows, width = q_ref.shape[2:]
    heads = width // HEAD_DIM

    @pl.when(pl.program_id(1) == 0)
    def _():
        same = segk_ref[0] == segq_ref[0, 0:1]
        bias[...] = jnp.where(same, 0.0, MASK_VALUE)

    mixed_grad = jnp.dot(grad_ref[0], wot_ref[0], preferred_element_type=floats).astype(halves)
    product = mixed_grad.astype(floats) * mixed_ref[0, 0].astype(floats)
    product_high = product.astype(halves)
    product_low = (product - product_high.astype(floats)).astype(halves)
    pick = (
        lax.broadcasted_iota(jnp.int32, (8, width), 1) // HEAD_DIM == lax.broadcasted_iota(jnp.int32, (8, width), 0)
    ).astype(halves)
    inner = contract_cols(pick, product_high) + contract_cols(pick, product_low)
    lane = lax.broadcasted_iota(jnp.int32, (rows, width), 1) // HEAD_DIM
    queries = q_ref[0, 0]
    query_heads = [jnp.where(lane == h, queries, jnp.zeros_like(queries)) for h in range(heads)]
    grad_heads = [jnp.where(lane == h, mixed_grad, jnp.zeros_like(mixed_grad)) for h in range(heads)]
    acc[...] = jnp.zeros_like(acc)
    dk_ref[...] = jnp.zeros_like(dk_ref)
    dv_ref[...] = jnp.zeros_like(dv_ref)

    def step(block, carry):
        at = pl.ds(pl.multiple_of(block * KEY_BLOCK, KEY_BLOCK), KEY_BLOCK)
        keys = k_ref[0, 0, at, :]
        values = v_ref[0, 0, at, :]
        keys_t = keys.T
        mask = bias[at, :]
        key_grad = jnp.zeros((KEY_BLOCK, width), floats)
        value_grad = jnp.zeros((KEY_BLOCK, width), floats)
        for h in range(heads):
            s = contract_cols(keys, query_heads[h]) + mask
            p = jnp.exp(s - lse_ref[0, 0, h : h + 1])
            prob_grad = contract_cols(values, grad_heads[h])
            score_grad = (p * (prob_grad - inner[h : h + 1])).astype(halves)
            value_grad = value_grad + jnp.dot(p.astype(halves), grad_heads[h], preferred_element_type=floats)
            key_grad = key_grad + jnp.dot(score_grad, query_heads[h], preferred_element_type=floats)
            part = pl.ds(h * HEAD_DIM, HEAD_DIM)
            acc[part, :] += jnp.dot(keys_t[h * HEAD_DIM : (h + 1) * HEAD_DIM], score_grad, preferred_element_type=floats)
        dk_ref[0, 0, at, :] = key_grad.astype(halves)
        dv_ref[0, 0, at, :] = value_grad.astype(halves)
        return carry

    lax.fori_loop(low, high, step, 0)
    dq_ref[0, 0] = (acc[...].T * HEAD_DIM ** -0.5).astype(halves)


def attend_back(bounds, grad, wot, mixed, lse, q, k, v, seg_own, seg_all):
    micro, rows, model = grad.shape
    cols, _, length, width = k.shape
    halves = jnp.bfloat16
    per = lambda a, b_: pl.BlockSpec((1, 1, a, b_), lambda m, c, b: (c, m, 0, 0))
    spec = pltpu.PrefetchScalarGridSpec(
        num_scalar_prefetch=1,
        grid=(micro, cols),
        in_specs=[
            pl.BlockSpec((1, rows, model), lambda m, c, b: (m, 0, 0)),
            pl.BlockSpec((1, model, width), lambda m, c, b: (c, 0, 0)),
            per(rows, width), per(8, rows), per(rows, width), per(length, width), per(length, width),
            pl.BlockSpec((1, 1, rows), lambda m, c, b: (m, 0, 0)),
            pl.BlockSpec((1, length, 1), lambda m, c, b: (m, 0, 0)),
        ],
        out_specs=[per(rows, width), per(length, width), per(length, width)],
        scratch_shapes=[pltpu.VMEM((length, rows), jnp.float32), pltpu.VMEM((width, rows), jnp.float32)],
    )
    shape = lambda a, b_, d=halves: jax.ShapeDtypeStruct((cols, micro, a, b_), d)
    return pl.pallas_call(
        attend_back_kernel,
        grid_spec=spec,
        out_shape=[shape(rows, width), shape(length, width), shape(length, width)],
        compiler_params=pltpu.CompilerParams(vmem_limit_bytes=48 << 20),
        name="attend_back",
    )(bounds, grad, wot, mixed, lse, q, k, v, seg_own[:, None], seg_all[:, :, None])


def place(sizes):
    seq, row, col = (lax.axis_index(name) for name in ("seq", "row", "col"))
    lines = {"x": (seq, sizes[0]), "y": (row // 2, sizes[1] // 2), "k": (lax.rem(row, 2), 2), "z": (col, sizes[2])}

    def device(axis, index):
        if axis == "x":
            return (index, row, col)
        if axis == "y":
            return (seq, index * 2 + lax.rem(row, 2), col)
        if axis == "k":
            return (seq, row // 2 * 2 + index, col)
        return (seq, row, index)

    return lines, device


def greet(lines, device):
    barrier = pltpu.get_barrier_semaphore()
    count = 0
    for axis, (mine, size) in lines.items():
        for t in range(1, size):
            pl.semaphore_signal(barrier, inc=1, device_id=device(axis, lax.rem(mine + t, size)), device_id_type=MESH)
            count += 1
    pl.semaphore_wait(barrier, count)


class Post:
    def __init__(self, device, send_sems, recv_sems):
        self.device, self.send_sems, self.recv_sems = device, send_sems, recv_sems
        self.slots, self.sent = {}, []

    def slot(self, key):
        return self.slots.setdefault(key, len(self.slots))

    def copy(self, key, axis, index, source, target):
        n = self.slot(key)
        return pltpu.make_async_remote_copy(
            src_ref=source, dst_ref=target, send_sem=self.send_sems.at[n], recv_sem=self.recv_sems.at[n],
            device_id=self.device(axis, index), device_id_type=MESH,
        )

    def send(self, key, make):
        def run(act):
            axis, index, source, target, when = make()

            def go():
                act(self.copy(key, axis, index, source, target))

            if when is None:
                go()
            else:
                pl.when(when)(go)

        run(lambda copy: copy.start())
        self.sent.append(run)

    def wait(self, key, axis, index, target, when=None):
        def go():
            self.copy(key, axis, index, target, target).wait_recv()

        if when is None:
            go()
        else:
            pl.when(when)(go)

    def close(self):
        for run in self.sent:
            run(lambda copy: copy.wait_send())


def clip(index, size):
    return jnp.clip(index, 0, size - 1)


class LineGather:
    def __init__(self, post, name, axis, line, region, reach=None):
        self.post, self.name, self.axis, self.region = post, name, axis, region
        self.mine, self.size = line
        self.reach = min(self.size - 1, reach or self.size)

    def hop(self, way, t):
        mine, size = self.mine, self.size

        def make():
            origin, target = mine - way * t, mine + way
            ok = (origin >= 0) & (origin < size) & (target >= 0) & (target < size)
            here = self.region(clip(origin, size))
            return self.axis, clip(target, size), here, here, ok

        self.post.send((self.name, way, t + 1), make)

    def start(self):
        for way in (1, -1):
            if self.reach >= 1:
                self.hop(way, 0)

    def step(self, t):
        if t > self.reach:
            return
        for way in (1, -1):
            origin = self.mine - way * t
            ok = (origin >= 0) & (origin < self.size)
            self.post.wait((self.name, way, t), self.axis, clip(self.mine - way, self.size), self.region(clip(origin, self.size)), ok)
            if t < self.reach:
                self.hop(way, t)

    def finish(self, first=1):
        for t in range(first, self.reach + 1):
            self.step(t)


def gather_kernel(sizes, micro, own_ref, shard_ref, every_ref, full_ref, send_sems, recv_sems, local_sems):
    lines, device = place(sizes)
    (x, _), (y, _), (k, _), (z, cols) = (lines[a] for a in "xykz")
    half = shard_ref.shape[-1] // 2
    rows = own_ref.shape[1]
    reach = -(-(DOC_MOST - 1) // rows)
    parts = [pl.ds(p * half, half) for p in (0, 1)]
    local = [pltpu.make_async_copy(shard_ref.at[j], full_ref.at[j, z, x, y, k], local_sems.at[j]) for j in range(3)]
    local += [pltpu.make_async_copy(own_ref.at[m], every_ref.at[m, z], local_sems.at[3 + m]) for m in range(micro)]
    for copy in local:
        copy.start()
    greet(lines, device)
    post = Post(device, send_sems, recv_sems)
    for copy in local:
        copy.wait()
    zs = [LineGather(post, ("z", j), "z", lines["z"], lambda i, j=j: full_ref.at[j, i, x, y, k]) for j in range(3)]
    tokens = [LineGather(post, ("t", m), "z", lines["z"], lambda i, m=m: every_ref.at[m, i], reach) for m in range(micro)]
    second, third = {}, {}
    for j in range(3):
        second[j] = [
            LineGather(post, ("a", j), "y", lines["y"], lambda i, j=j: full_ref.at[j, :, x, i, k, :, parts[0]]),
            LineGather(post, ("b", j), "x", lines["x"], lambda i, j=j: full_ref.at[j, :, i, y, k, :, parts[1]]),
        ]
        third[j] = [
            LineGather(post, ("c", j), "x", lines["x"], lambda i, j=j: full_ref.at[j, :, i, :, k, :, parts[0]]),
            LineGather(post, ("d", j), "y", lines["y"], lambda i, j=j: full_ref.at[j, :, :, i, k, :, parts[1]]),
        ]

    def start(group):
        for line in group:
            line.start()

    def finish(group):
        for line in group:
            line.finish()

    def swap(j):
        plane = full_ref.at[j, :, :, :, k]
        post.send(("k", j), lambda: ("k", 1 - k, plane, plane, None))

    start(zs[:1])
    finish(zs[:1])
    start(second[0] + zs[1:2])
    finish(second[0])
    start(third[0])
    finish(zs[1:2])
    start(second[1] + tokens[:1])
    finish(third[0])
    swap(0)
    finish(second[1])
    start(third[1])
    finish(tokens[:1])
    start(zs[2:])
    finish(zs[2:])
    start(second[2] + tokens[1:])
    finish(third[1])
    swap(1)
    finish(second[2])
    start(third[2])
    finish(tokens[1:])
    finish(third[2])
    swap(2)
    for i in range(cols):
        far = (z - i > reach) | (i - z > reach)
        for m in range(micro):
            def fill(m=m, i=i):
                copy = pltpu.make_async_copy(own_ref.at[m], every_ref.at[m, i], local_sems.at[3 + m])
                copy.start()
                copy.wait()

            if i > reach or cols - 1 - i > reach:
                pl.when(far)(fill)
    for j in range(3):
        post.wait(("k", j), "k", 1 - k, full_ref.at[j, :, :, :, 1 - k])
    post.close()


def gather(sizes, own, shard):
    ns, nr, nc = sizes
    ny = nr // 2
    micro, rows, model = own.shape
    _, rb, w = shard.shape
    count = 3 * 2 * (nc - 1) + micro * 2 * (nc - 1) + 3 * (4 * (ny - 1) + 4 * (ns - 1) + 1)
    anywhere = pl.BlockSpec(memory_space=pl.ANY)
    every, full = pl.pallas_call(
        functools.partial(gather_kernel, sizes, micro),
        out_shape=[
            jax.ShapeDtypeStruct((micro, nc, rows, model), own.dtype),
            jax.ShapeDtypeStruct((3, nc, ns, ny, 2, rb, w), shard.dtype),
        ],
        in_specs=[pl.BlockSpec(memory_space=pltpu.VMEM)] * 2,
        out_specs=[anywhere] * 2,
        scratch_shapes=[pltpu.SemaphoreType.DMA((count,)), pltpu.SemaphoreType.DMA((count,)), pltpu.SemaphoreType.DMA((3 + micro,))],
        compiler_params=pltpu.CompilerParams(collective_id=0, has_side_effects=True),
        name="gather",
    )(own, shard)
    return every, full.reshape(3, nc, ns * nr * rb, w)


class LineReduce:
    def __init__(self, post, name, axis, line, region, inbox, add, reach=None):
        self.post, self.name, self.axis, self.region, self.inbox, self.add = post, name, axis, region, inbox, add
        self.mine, self.size = line
        self.reach = min(self.size - 1, reach or self.size)

    def arrived(self, way, e):
        behind, goal = self.mine - way, self.mine + way * e
        return (behind >= 0) & (behind < self.size) & (goal >= 0) & (goal < self.size)

    def take(self, way, e):
        ok = self.arrived(way, e)
        inbox = self.inbox(way, e)
        self.post.wait((self.name, way, e), self.axis, clip(self.mine - way, self.size), inbox, ok)

        @pl.when(ok)
        def _():
            self.add(self.region(clip(self.mine + way * e, self.size)), inbox)

    def forward(self, way, e):
        def make():
            goal = self.mine + way * e
            ok = (goal >= 0) & (goal < self.size)
            return self.axis, clip(self.mine + way, self.size), self.region(clip(goal, self.size)), self.inbox(way, e - 1), ok

        self.post.send((self.name, way, e - 1), make)

    def start(self):
        for way in (1, -1):
            if self.reach >= 1:
                self.forward(way, self.reach)

    def forward_from(self, nearest):
        for e in range(self.reach - 1, nearest - 1, -1):
            for way in (1, -1):
                self.take(way, e)
                self.forward(way, e)

    def finish(self, last=True):
        self.forward_from(1)
        if last:
            for way in (1, -1):
                if self.reach >= 1:
                    self.take(way, 0)


def reduce_to(post, name, axis, line, goal, e, region, inbox, add):
    mine, size = line
    for way in (1, -1):
        behind = mine - way
        arrives = (way * (goal - mine) == e) & (behind >= 0) & (behind < size)
        slot = inbox(way, min(e, size - 2))
        post.wait((name, way), axis, clip(behind, size), slot, arrives)

        @pl.when(arrives)
        def _():
            add(region, slot)

        def make(way=way):
            return axis, clip(mine + way, size), region, inbox(way, e - 1), way * (goal - mine) == e

        if e:
            post.send((name, way), make)


def reduce_kernel(sizes, micro, own_ref, spread_ref, part_ref, vec_ref, back_ref, block_ref, sums_ref,
                  mine_buf, core_buf, in_a, in_b, in_c, in_d, in_z, tok_buf, tok_in, vec_buf, send_sems, recv_sems, local_sems):
    floats, halves = jnp.float32, jnp.bfloat16
    lines, device = place(sizes)
    (x, ns), (y, ny), (k, _), (z, nc) = (lines[a] for a in "xykz")
    half = part_ref.shape[-1] // 2
    rows = own_ref.shape[1]
    reach = -(-(DOC_MOST - 1) // rows)
    parts = [pl.ds(p * half, half) for p in (0, 1)]
    local = [pltpu.make_async_copy(part_ref.at[j, :, :, :, k], mine_buf.at[j], local_sems.at[j]) for j in range(3)]
    local += [pltpu.make_async_copy(spread_ref.at[m], tok_buf.at[m], local_sems.at[3 + m]) for m in range(micro)]
    for copy in local:
        copy.start()
    greet(lines, device)
    post = Post(device, send_sems, recv_sems)
    for j in range(3):
        post.send(("k", j), lambda j=j: ("k", 1 - k, part_ref.at[j, :, :, :, 1 - k], core_buf.at[j], None))

    def plus(target, source):
        target[...] = (target[...].astype(floats) + source[...].astype(floats)).astype(halves)

    def plus_grid(target, source, first, second):
        @pl.loop(0, first * second)
        def _(n):
            plus(target.at[n // second, lax.rem(n, second)], source.at[n // second, lax.rem(n, second)])

    def plus_row(target, source, first):
        @pl.loop(0, first)
        def _(n):
            plus(target.at[n], source.at[n])

    vec_buf[0, 0] = vec_ref[...]

    def vector_start(stage, axis):
        mine, size = lines[axis]
        vec_buf[stage, 1 + mine] = vec_buf[stage, 0]
        for t in range(1, size):
            post.send(("v", stage, t), lambda t=t: (
                axis, lax.rem(mine + t, size), vec_buf.at[stage, 0], vec_buf.at[stage, 1 + mine], None))

    def vector_finish(stage, axis, out):
        mine, size = lines[axis]
        for t in range(1, size):
            origin = lax.rem(mine + size - t, size)
            post.wait(("v", stage, t), axis, origin, vec_buf.at[stage, 1 + origin])
        total = vec_buf[stage, 1]
        for i in range(1, size):
            total = total + vec_buf[stage, 1 + i]
        out[...] = total

    tokens = [
        LineReduce(post, ("t", m), "z", lines["z"], lambda i, m=m: tok_buf.at[m, i],
                   lambda way, e, m=m: tok_in.at[m, (1 - way) // 2, e], plus, reach)
        for m in range(micro)
    ]
    box = lambda way: (1 - way) // 2
    second, third, last = {}, {}, {}
    for j in range(3):
        second[j] = [
            LineReduce(post, ("a", j), "x", lines["x"], lambda i, j=j: mine_buf.at[j, :, i, :, :, parts[0]],
                       lambda way, e, j=j: in_a.at[j, box(way), e], lambda t, s: plus_grid(t, s, nc, ny)),
            LineReduce(post, ("b", j), "y", lines["y"], lambda i, j=j: mine_buf.at[j, :, :, i, :, parts[1]],
                       lambda way, e, j=j: in_b.at[j, box(way), e], lambda t, s: plus_grid(t, s, nc, ns)),
        ]
        third[j] = [
            LineReduce(post, ("c", j), "y", lines["y"], lambda i, j=j: mine_buf.at[j, :, x, i, :, parts[0]],
                       lambda way, e, j=j: in_c.at[j, box(way), e], lambda t, s: plus_row(t, s, nc)),
            LineReduce(post, ("d", j), "x", lines["x"], lambda i, j=j: mine_buf.at[j, :, i, y, :, parts[1]],
                       lambda way, e, j=j: in_d.at[j, box(way), e], lambda t, s: plus_row(t, s, nc)),
        ]
        last[j] = [
            LineReduce(post, ("z", j), "z", lines["z"], lambda i, j=j: mine_buf.at[j, i, x, y],
                       lambda way, e, j=j: in_z.at[j, box(way), e], plus)
        ]

    def start(group):
        for line in group:
            line.start()

    def finish(group):
        for line in group:
            line.finish()

    def core(j):
        local[j].wait()
        post.wait(("k", j), "k", 1 - k, core_buf.at[j])

        @pl.loop(0, nc * ns * ny)
        def _(n):
            at = (n // (ns * ny), lax.rem(n // ny, ns), lax.rem(n, ny))
            plus(mine_buf.at[(j, *at)], core_buf.at[(j, *at)])

    for m in range(micro):
        local[3 + m].wait()
    start(tokens)
    core(0)
    start(second[0])
    vector_start(0, "k")
    core(1)
    start(second[1])
    vector_finish(0, "k", vec_buf.at[1, 0])
    vector_start(1, "y")
    core(2)
    finish(second[0])
    start(third[0])
    start(second[2])
    vector_finish(1, "y", vec_buf.at[2, 0])
    vector_start(2, "x")
    finish(tokens)
    vector_finish(2, "x", vec_buf.at[3, 0])
    vector_start(3, "z")
    finish(second[1])
    start(third[1])
    finish(third[0])
    start(last[0])
    finish(second[2])
    start(third[2])
    finish(third[1])
    start(last[1])
    finish(last[0])
    finish(third[2])
    start(last[2])
    vector_finish(3, "z", sums_ref)
    for m in range(micro):
        back_ref[m] = own_ref[m] + tok_buf[m, z].astype(floats)
    finish(last[1])
    finish(last[2])
    for j in range(3):
        block_ref[j] = mine_buf[j, z, x, y].astype(floats)
    post.close()


def reduce(sizes, own_share, spread, partial, vectors):
    ns, nr, nc = sizes
    ny = nr // 2
    micro, rows, model = own_share.shape
    w = partial.shape[-1]
    rb = partial.shape[2] // (ns * nr)
    halves, floats = jnp.bfloat16, jnp.float32
    reach = min(nc - 1, -(-(DOC_MOST - 1) // rows))
    count = 3 + 2 * (ny - 1 + ns - 1) * 6 + 3 * 2 * (nc - 1) + micro * 2 * reach + (1 + ny - 1 + ns - 1 + nc - 1)
    widest = max(ns, ny, nc, 2)
    extra = -vectors.shape[0] % 8
    vectors = jnp.pad(vectors, ((0, extra), (0, 0)))
    vmem = pl.BlockSpec(memory_space=pltpu.VMEM)
    anywhere = pl.BlockSpec(memory_space=pl.ANY)
    back, blocks, sums = pl.pallas_call(
        functools.partial(reduce_kernel, sizes, micro),
        out_shape=[
            jax.ShapeDtypeStruct((micro, rows, model), floats),
            jax.ShapeDtypeStruct((3, rb, w), floats),
            jax.ShapeDtypeStruct(vectors.shape, floats),
        ],
        in_specs=[vmem, anywhere, anywhere, vmem],
        out_specs=[vmem] * 3,
        scratch_shapes=[
            pltpu.VMEM((3, nc, ns, ny, rb, w), halves),
            pltpu.VMEM((3, nc, ns, ny, rb, w), halves),
            pltpu.VMEM((3, 2, max(ns - 1, 1), nc, ny, rb, w // 2), halves),
            pltpu.VMEM((3, 2, max(ny - 1, 1), nc, ns, rb, w // 2), halves),
            pltpu.VMEM((3, 2, max(ny - 1, 1), nc, rb, w // 2), halves),
            pltpu.VMEM((3, 2, max(ns - 1, 1), nc, rb, w // 2), halves),
            pltpu.VMEM((3, 2, max(nc - 1, 1), rb, w), halves),
            pltpu.VMEM((micro, nc, rows, model), halves),
            pltpu.VMEM((micro, 2, max(reach, 1), rows, model), halves),
            pltpu.VMEM((4, 1 + widest, *vectors.shape), floats),
            pltpu.SemaphoreType.DMA((count,)),
            pltpu.SemaphoreType.DMA((count,)),
            pltpu.SemaphoreType.DMA((3 + micro,)),
        ],
        compiler_params=pltpu.CompilerParams(collective_id=1, has_side_effects=True, vmem_limit_bytes=60 << 20),
        name="reduce",
    )(own_share, spread, partial.reshape(3, nc, ns, ny, 2, rb, w), vectors)
    return back, blocks, sums


Q_AT, K_AT, V_AT, O_AT, WINDOW = 0, 128, 384, 512, 256


def plane(full_ref, c, at, size=WINDOW):
    value = full_ref[c, :, :, :, :, at : at + size]
    return value.reshape(-1, size)


def split_plan(plan):
    parts, order = [[]], []
    for task in plan:
        if task[0] == "U":
            order.append(task[1:])
            parts.append([])
        else:
            parts[-1].append(task)
    return parts[0], parts[1:], order


def pick(step, values):
    value = values[0]
    for i, other in enumerate(values[1:], 1):
        value = jnp.where(step == i, other, value)
    return value


def place_of(rows):
    return lax.broadcasted_iota(jnp.int32, (rows, WINDOW), 1) // HEAD_DIM


def keep(value, places, wanted):
    return jnp.where(places == wanted, value, jnp.zeros_like(value))


def forward_kernel(sizes, micro, own_ref, wq_ref, wk_ref, wv_ref, wo_ref, wh_ref, wd_ref, hidden_bias_ref, query_bias_ref, value_bias_ref, seg_ref,
                   rest_ref, first_ref, turned_ref, mask_ref, biases_ref, mixed_ref, lse_ref, q_ref, k_ref, v_ref,
                   weights, turned, bias_buf, mask, mixed_buf, lse_buf, q_buf, k_buf, v_buf, tokens_buf, acc, score_buf, prob_buf, values_t,
                   send_sems, recv_sems, local_sems, unit_sems):
    floats, halves = jnp.float32, jnp.bfloat16
    lines, device = place(sizes)
    (x, _), (y, _), (k, _), (z, cols) = (lines[a] for a in "xykz")
    half = wh_ref.shape[-1] // 2
    rows = own_ref.shape[1]
    reach = -(-(DOC_MOST - 1) // rows)
    parts = [pl.ds(p * half, half) for p in (0, 1)]
    low, high = jnp.maximum(z - reach, 0), jnp.minimum(z + reach + 1, cols)
    used = [0]

    class Local:
        def __init__(self, source, target):
            self.source, self.target, self.n = source, target, used[0]
            used[0] += 1
            self.describe().start()

        def describe(self):
            source = self.source() if callable(self.source) else self.source
            return pltpu.make_async_copy(source, self.target, local_sems.at[self.n])

        def wait(self):
            self.describe().wait()

    local = Local
    targets = [weights.at[0], rest_ref.at[0], rest_ref.at[1]]
    packed = [wq_ref[...], wk_ref[...], wv_ref[...], wo_ref[...].astype(floats).T.astype(halves)]
    weights[0, z, x, y, k] = jnp.concatenate(packed, 1)
    begin = [local(wh_ref, targets[1].at[z, x, y, k]), local(wd_ref, targets[2].at[z, x, y, k])]
    begin += [local(own_ref.at[m], tokens_buf.at[m, z]) for m in range(micro)]
    for i, ref in enumerate((hidden_bias_ref, query_bias_ref, value_bias_ref)):
        bias_buf[z, i : i + 1, 0 : ref.shape[0]] = ref[...].astype(floats).reshape(1, -1)
        if ref.shape[0] < WINDOW:
            bias_buf[z, i : i + 1, ref.shape[0] : WINDOW] = jnp.zeros((1, WINDOW - ref.shape[0]), floats)
    greet(lines, device)
    post = Post(device, send_sems, recv_sems)
    for copy in begin:
        copy.wait()
    tokens = [
        LineGather(post, ("t", q), "z", lines["z"],
                   lambda i, q=q: tokens_buf.at[q // 2, i, pl.ds(q % 2 * (rows // 2), rows // 2)], reach)
        for q in range(2 * micro)
    ]
    small = LineGather(post, "bias", "z", lines["z"], lambda i: bias_buf.at[i])
    rb = wh_ref.shape[0]
    zs, second, third = {}, {}, {}
    for n in range(6):
        j, r = n // 2, pl.ds(n % 2 * (rb // 2), rb // 2)
        zs[n] = LineGather(post, ("z", n), "z", lines["z"], lambda i, j=j, r=r: targets[j].at[i, x, y, k, r])
        second[n] = [
            LineGather(post, ("a", n), "y", lines["y"], lambda i, j=j, r=r: targets[j].at[:, x, i, k, r, parts[0]]),
            LineGather(post, ("b", n), "x", lines["x"], lambda i, j=j, r=r: targets[j].at[:, i, y, k, r, parts[1]]),
        ]
        third[n] = [
            LineGather(post, ("c", n), "x", lines["x"], lambda i, j=j, r=r: targets[j].at[:, i, :, k, r, parts[0]]),
            LineGather(post, ("d", n), "y", lines["y"], lambda i, j=j, r=r: targets[j].at[:, :, i, k, r, parts[1]]),
        ]

    def start(*group):
        for line in group:
            line.start()

    def finish(*group):
        for line in group:
            line.finish()

    def side(n, which):
        return targets[n // 2].at[:, :, :, which, pl.ds(n % 2 * (rb // 2), rb // 2)]

    def swap(n):
        post.send(("k", n), lambda: ("k", 1 - k, side(n, k), side(n, k), None))

    def swapped(n):
        post.wait(("k", n), "k", 1 - k, side(n, 1 - k))

    places = place_of(rows)

    def project(m, c, block):
        rows_at = tokens_buf[m, block]
        k_buf[m, c, block] = jnp.dot(rows_at, plane(weights.at[0], c, K_AT), preferred_element_type=floats).astype(halves)
        values = jnp.dot(rows_at, plane(weights.at[0], c, V_AT), preferred_element_type=floats) + bias_buf[c, 2:3, 0:WINDOW]
        v_buf[m, c, block] = values.astype(halves)

    def prepare(m, c):
        queries = jnp.dot(own_ref[m], plane(weights.at[0], c, Q_AT), preferred_element_type=floats) + bias_buf[c, 1:2, 0:WINDOW]
        queries = pltpu.roll(queries.astype(halves).astype(floats) * HEAD_DIM ** -0.5, HEAD_DIM, 1)
        q_buf[m, c] = jnp.where(places > 0, queries, 0.0).astype(halves)
        for way in (0, 1, 3):
            project(m, c, lax.rem(z + way, cols))

    def unit(m, c):
        project(m, c, lax.rem(z + 2, cols))
        queries = q_buf[m, c]
        heads = jnp.concatenate([keep(queries, places, h + 1) for h in range(3)], 0)
        largest = jnp.full((1, 3 * rows), 2 * MASK_VALUE, floats)
        for block in range(cols):
            keys = k_buf[m, c, block]
            values_t[:, block * rows : (block + 1) * rows] = v_buf[m, c, block].T
            hidden = mask[m, block].astype(floats)
            s = contract_cols(keys, heads) + jnp.concatenate([hidden] * 3, 1)
            score_buf[block] = s
            largest = jnp.maximum(largest, jnp.max(s, 0, keepdims=True))
        row_total = jnp.zeros((1, 3 * rows), floats)
        for block in range(cols):
            p = jnp.exp(score_buf[block] - largest)
            row_total = row_total + jnp.sum(p, 0, keepdims=True)
            prob_buf[block * rows : (block + 1) * rows] = p.astype(halves)
        log_total = largest + jnp.log(row_total)
        acc[0:HEAD_DIM] = jnp.zeros((HEAD_DIM, rows), floats)
        for h in range(3):
            lanes = slice(h * rows, (h + 1) * rows)
            product = jnp.dot(values_t[h * HEAD_DIM : (h + 1) * HEAD_DIM], prob_buf[:, lanes], preferred_element_type=floats)
            acc[pl.ds((h + 1) * HEAD_DIM, HEAD_DIM), :] = product / row_total[:, lanes]
            lse_buf[m, c, h : h + 1] = log_total[:, lanes]
        mixed_buf[c, m] = acc[...].T.astype(halves)

    def units(m, first, last):
        @pl.loop(first, last)
        def _(c):
            unit(m, c)

    def masks(m):
        asking = seg_ref[m, 0:1, pl.ds(pl.multiple_of(z * rows, 128), rows)].astype(floats)
        for block in range(cols):
            asked = seg_ref[m, 0:1, block * rows : (block + 1) * rows].astype(floats)
            same = jnp.broadcast_to(asked, (rows, rows)).T == asking
            mask[m, block] = jnp.where(same, 0.0, MASK_VALUE).astype(halves)

    done = []

    def turn(m):
        for block in range(cols):
            turned[:, (m * cols + block) * rows : (m * cols + block + 1) * rows] = tokens_buf[m, block].T
        if m == micro - 1:
            done.append(local(turned, turned_ref))

    keeps = ((q_buf, q_ref), (k_buf, k_ref), (v_buf, v_ref), (lse_buf, lse_ref))

    def take_z(n, t):
        zs[n].step(t)
        if n == 0:
            small.step(t)
        if t == cols - 1:
            start(*second[n])

    def take_second(n):
        finish(*second[n])
        start(*third[n])

    def take_third(n):
        finish(*third[n])
        swap(n)

    swaps = set()

    def take_core(n):
        swapped(n)
        swaps.add(n)
        if n < 2 and swaps >= {0, 1}:
            done.append(local(lambda: weights.at[0], first_ref))

    act = {
        "Zs": lambda n: zs[n].start(), "Z": take_z, "Ts": lambda q: tokens[q].start(), "T": lambda q, t: tokens[q].step(t),
        "B": take_second, "C": take_third, "K": take_core, "R": turn,
    }
    small.start()
    head, tail, order = split_plan([("U", *task) if task[0] == "P" else task for task in FORWARD_PLAN])
    kinds = [int(item[0] == "P") for item in order]
    micros, heads_of = [item[-2] for item in order], [item[-1] for item in order]
    act[head[0][0]](*head[0][1:])
    for block in range(cols):
        if block > reach or cols - 1 - block > reach:
            @pl.when(jnp.logical_not((low <= block) & (block < high)))
            def _(block=block):
                for m in range(micro):
                    tokens_buf[m, block] = jnp.zeros(own_ref.shape[1:], halves)
    for m in range(micro):
        masks(m)
    done.append(local(mask, mask_ref))
    for task in head[1:]:
        act[task[0]](*task[1:])

    def leave(m, c, go):
        for i, (source, target) in enumerate(keeps):
            go(pltpu.make_async_copy(source.at[m, c], target.at[m, c], unit_sems.at[i, m * cols + c]))
        go(pltpu.make_async_copy(mixed_buf.at[c, m], mixed_ref.at[c, m], unit_sems.at[len(keeps), m * cols + c]))

    @pl.loop(0, len(order))
    def _(step):
        m, c, kind = pick(step, micros), pick(step, heads_of), pick(step, kinds)

        @pl.when(kind == 1)
        def _():
            prepare(m, c)

        @pl.when(kind == 0)
        def _():
            unit(m, c)
            leave(m, c, lambda copy: copy.start())

        for i, tasks in enumerate(tail[:-1]):
            if tasks:
                @pl.when(step == i)
                def _(tasks=tasks):
                    for task in tasks:
                        act[task[0]](*task[1:])

    done.append(local(bias_buf, biases_ref))
    for task in tail[-1]:
        act[task[0]](*task[1:])
    for m in range(micro):
        for c in range(cols):
            leave(m, c, lambda copy: copy.wait())
    for copy in done:
        copy.wait()
    post.close()


def forward(sizes, own, shards, hidden_bias, query_bias, value_bias, segments):
    ns, nr, nc = sizes
    ny = nr // 2
    micro, rows, model = own.shape
    rb, w = shards[4].shape
    halves, floats = own.dtype, jnp.float32
    reach = min(nc - 1, -(-(DOC_MOST - 1) // rows))
    count = (6 + 1) * 2 * (nc - 1) + micro * 4 * reach + 6 * (4 * (ny - 1) + 4 * (ns - 1) + 1)
    anywhere = pl.BlockSpec(memory_space=pl.ANY)
    vmem = pl.BlockSpec(memory_space=pltpu.VMEM)
    length = nc * rows
    arrays = [
        ((2, nc, ns, ny, 2, rb, w), halves), ((nc, ns, ny, 2, rb, w), halves), ((model, micro * length), halves), ((micro, nc, rows, rows), halves),
        ((nc, 8, model), floats), ((nc, micro, rows, WINDOW), halves), ((micro, nc, 8, rows), floats),
        ((micro, nc, rows, WINDOW), halves), ((micro, nc, nc, rows, WINDOW), halves), ((micro, nc, nc, rows, WINDOW), halves),
    ]
    shapes = [pltpu.VMEM(shape, kind) for shape, kind in arrays]
    return pl.pallas_call(
        functools.partial(forward_kernel, sizes, micro),
        out_shape=[jax.ShapeDtypeStruct(shape, kind) for shape, kind in arrays],
        in_specs=[vmem] * 11,
        out_specs=[anywhere] * len(arrays),
        scratch_shapes=[
            pltpu.VMEM((1, nc, ns, ny, 2, rb, w), halves),
            shapes[2], shapes[4], shapes[3], *shapes[5:],
            pltpu.VMEM((micro, nc, rows, model), halves), pltpu.VMEM((WINDOW, rows), floats), pltpu.VMEM((nc, rows, 3 * rows), floats), pltpu.VMEM((length, 3 * rows), halves), pltpu.VMEM((WINDOW, length), halves),
            pltpu.SemaphoreType.DMA((count,)), pltpu.SemaphoreType.DMA((count,)), pltpu.SemaphoreType.DMA((20,)), pltpu.SemaphoreType.DMA((5, micro * nc)),
        ],
        compiler_params=pltpu.CompilerParams(collective_id=2, has_side_effects=True, vmem_limit_bytes=60 << 20),
        name="forward",
    )(own, *shards, hidden_bias, query_bias, value_bias, segments)


def middle_kernel(cols, own_ref, mixed_ref, out_ref, rest_ref, bias_ref, *refs):
    vector_refs = refs[:6]
    (cot_ref, outputs_ref, first_grad_ref, attn_grad_ref, part_ref, sums_ref,
     normal, scale, normed, normed_low, normed_t, grad_low, grad_t, act_buf, slope_buf, total, cot_buf, weight_buf, sems) = refs[6:]
    floats, halves = jnp.float32, jnp.bfloat16
    step = pl.program_id(0)
    rows, model = own_ref.shape
    chunks = [pl.ds(r * 256, 256) for r in range(rows // 256)]
    whole_rows = [pl.ds(0, rows)]
    bands = [pl.ds(n * 256, 256) for n in range(model // 256)]
    loads = [[pltpu.make_async_copy(rest_ref.at[j, c], weight_buf.at[j, c], sems.at[j, c]) for j in range(2)] for c in range(cols)]
    load_cot = pltpu.make_async_copy(cot_ref, cot_buf, sems.at[0, cols])
    vector = lambda i: vector_refs[i][...].astype(floats).reshape(1, -1)

    @pl.when(step == 0)
    def _():
        for pair in loads:
            for copy in pair:
                copy.start()
        load_cot.start()
        sums_ref[...] = jnp.zeros_like(sums_ref)
        for chunk in chunks:
            first_sum = own_ref[chunk].astype(floats) + vector(0)
            for c in range(cols):
                first_sum = first_sum + contract_cols(mixed_ref[c, chunk], out_ref[c])
            normal_one, scale_one = norm_parts(first_sum)
            normal[chunk] = normal_one
            scale[chunk] = jnp.broadcast_to(scale_one, (256, 128))
            norm_one = normal_one * vector(1) + vector(2)
            total[chunk] = norm_one + vector(3)
            normed_low[chunk] = norm_one.astype(halves)
            normed_t[:, chunk] = norm_one.astype(halves).T

    for c in range(cols):
        @pl.when(step == c)
        def _(c=c):
            for copy in loads[c]:
                copy.wait()

    @pl.when(step < cols)
    def _():
        for chunk in chunks:
            for band in bands:
                hidden = jnp.dot(normed_low[chunk], weight_buf[0, step, :, band], preferred_element_type=floats) + bias_ref[0, 0:1, band]
                half_erf = 0.5 * lax.erf(hidden * 0.7071067811865476) + 0.5
                act_buf[step, chunk, band] = (hidden * half_erf).astype(halves)
                slope_buf[step, chunk, band] = (half_erf + hidden * (jnp.exp(-0.5 * hidden * hidden) * 0.3989422804014327)).astype(halves)
        for chunk in chunks:
            for band in bands:
                total[chunk, band] += contract_cols(act_buf[step, chunk], weight_buf[1, step, band, :])

    @pl.when(step == cols - 1)
    def _():
        load_cot.wait()
        for chunk in chunks:
            normal_two, scale_two = norm_parts(total[chunk])
            outputs_ref[chunk] = (normal_two * vector(4) + vector(5)).astype(halves)
            cot = cot_buf[chunk].astype(floats)
            second_grad = norm_back(cot * vector(4), normal_two, scale_two)
            total[chunk] = second_grad
            grad_low[chunk] = second_grad.astype(halves)
            grad_t[:, chunk] = second_grad.astype(halves).T
            sums_ref[3:4] += jnp.sum(second_grad, 0, keepdims=True)
            sums_ref[4:5] += jnp.sum(cot * normal_two, 0, keepdims=True)
            sums_ref[5:6] += jnp.sum(cot, 0, keepdims=True)

    @pl.when(step >= cols)
    def _():
        c = step - cols
        bias_total = [jnp.zeros((1, 256), floats) for _ in bands]
        for chunk in chunks:
            for n, band in enumerate(bands):
                pre = jnp.dot(grad_low[chunk], weight_buf[1, c, :, band], preferred_element_type=floats)
                pre = (pre * slope_buf[c, chunk, band].astype(floats)).astype(halves)
                slope_buf[c, chunk, band] = pre
                bias_total[n] = bias_total[n] + jnp.sum(pre.astype(floats), 0, keepdims=True)
        for n, band in enumerate(bands):
            sums_ref[pl.ds(8 + c, 1), band] = bias_total[n]
        for band in bands:
            for side in [pl.ds(0, model)]:
                part_ref[0, 0, side, band] = jnp.dot(normed_t[side, :], slope_buf[c, :, band], preferred_element_type=floats).astype(halves)
                part_ref[1, 0, side, band] = jnp.dot(grad_t[side, :], act_buf[c, :, band], preferred_element_type=floats).astype(halves)
        for chunk in chunks:
            for band in bands:
                total[chunk, band] += contract_cols(slope_buf[c, chunk], weight_buf[0, c, band, :])

    @pl.when(step == 2 * cols - 1)
    def _():
        for chunk in chunks:
            normed_grad, normal_one = total[chunk], normal[chunk]
            first_grad = norm_back(normed_grad * vector(1), normal_one, scale[chunk, 0:1])
            first_grad_ref[chunk] = first_grad
            attn_grad_ref[chunk] = first_grad.astype(halves)
            sums_ref[0:1] += jnp.sum(first_grad, 0, keepdims=True)
            sums_ref[1:2] += jnp.sum(normed_grad * normal_one, 0, keepdims=True)
            sums_ref[2:3] += jnp.sum(normed_grad, 0, keepdims=True)


def middle(own, mixed, first, rest, biases, vectors, cot):
    rows, model = own.shape
    cols = first.shape[0]
    halves, floats = jnp.bfloat16, jnp.float32
    whole = lambda shape: pl.BlockSpec(shape, lambda i: (0,) * len(shape))
    wide = lambda kind: pltpu.VMEM((rows, model), kind)
    return pl.pallas_call(
        functools.partial(middle_kernel, cols),
        grid=(2 * cols,),
        in_specs=[
            whole((rows, model)), whole(mixed.shape),
            pl.BlockSpec((cols, model, WINDOW), lambda i: (0, 0, O_AT // WINDOW)),
            pl.BlockSpec(memory_space=pl.ANY),
            pl.BlockSpec((1, *biases.shape[1:]), lambda i: (lax.rem(i, cols), 0, 0)),
            *[whole((model,))] * 6, pl.BlockSpec(memory_space=pl.ANY),
        ],
        out_specs=[
            whole((rows, model)), whole((rows, model)), whole((rows, model)),
            pl.BlockSpec((2, 1, model, rest.shape[-1]), lambda i: (0, jnp.maximum(i - cols, 0), 0, 0)),
            whole((8 + cols + -cols % 8, model)),
        ],
        out_shape=[
            jax.ShapeDtypeStruct((rows, model), halves), jax.ShapeDtypeStruct((rows, model), floats),
            jax.ShapeDtypeStruct((rows, model), halves), jax.ShapeDtypeStruct(rest.shape, halves),
            jax.ShapeDtypeStruct((8 + cols + -cols % 8, model), floats),
        ],
        scratch_shapes=[
            wide(floats), pltpu.VMEM((rows, 128), floats), wide(floats), wide(halves), pltpu.VMEM((model, rows), halves), wide(halves),
            pltpu.VMEM((model, rows), halves), pltpu.VMEM((cols, rows, rest.shape[-1]), halves),
            pltpu.VMEM((cols, rows, rest.shape[-1]), halves), wide(floats), wide(halves),
            pltpu.VMEM(rest.shape, halves), pltpu.SemaphoreType.DMA((2, cols + 1)),
        ],
        compiler_params=pltpu.CompilerParams(vmem_limit_bytes=56 << 20),
        name="middle",
    )(own, mixed, first, rest, biases, *vectors, cot)


class Inbox:
    def __init__(self, ref, size):
        self.ref, self.size = ref, size

    def __call__(self, way, e):
        return self.ref.at[0 if self.size == 2 else (1 - way) // 2, e]


def backward_kernel(sizes, micro, grad_ref, share_ref, first_ref, turned_ref, mixed_ref, lse_ref, q_ref, k_ref, v_ref,
                    mask_ref, part_ref, vec_ref,
                    out_ref,
                    mine_buf, core_buf, stage_buf, in_a, in_b, in_c, in_d, in_z, tok_buf, tok_in, vec_buf,
                    weights, mixed_buf, q_buf, k_buf, v_buf, every_t, grad_t, mask, acc, spread, block_sum,
                    send_sems, recv_sems, local_sems, free_sem):
    floats, halves = jnp.float32, jnp.bfloat16
    lines, device = place(sizes)
    (x, ns), (y, ny), (k, _), (z, cols) = (lines[a] for a in "xykz")
    model = first_ref.shape[1]
    back_rows = micro * grad_ref.shape[1]
    block_rows = 3 * part_ref.shape[-2]
    sums_ref = out_ref.at[pl.ds(back_rows + block_rows, out_ref.shape[0] - back_rows - block_rows)]

    def back(m, begin=0, size=None):
        return pl.ds(pl.multiple_of(m * grad_ref.shape[1] + begin, 8), size or grad_ref.shape[1])

    half = part_ref.shape[-1] // 2
    rb = part_ref.shape[-2]
    rows = grad_ref.shape[1]
    reach = -(-(DOC_MOST - 1) // rows)
    parts = [pl.ds(p * half, half) for p in (0, 1)]
    used = [0]

    def local(source, target):
        copy = pltpu.make_async_copy(source, target, local_sems.at[used[0]])
        used[0] += 1
        copy.start()
        return copy

    def rows_of(n):
        return pl.ds(n % 2 * (rb // 2), rb // 2)

    planes = [local(part_ref.at[n // 2, :, :, :, k, rows_of(n)], mine_buf.at[n // 2 + 1, :, :, :, rows_of(n)]) for n in range(4)]
    loads = [local(*pair) for pair in ((first_ref, weights), (mixed_ref, mixed_buf), (q_ref, q_buf), (share_ref, out_ref.at[pl.ds(0, back_rows)]))]
    loads += [local(k_ref, k_buf), local(v_ref, v_buf)]
    loads += [local(mask_ref, mask)]
    late = [local(turned_ref, every_t)]
    greet(lines, device)
    post = Post(device, send_sems, recv_sems)

    def give(n):
        post.send(("k", n), lambda: (
            "k", 1 - k, part_ref.at[n // 2, :, :, :, 1 - k, rows_of(n)], core_buf.at[n // 2, :, :, :, rows_of(n)], None))

    def plus(target, source):
        target[...] = target[...] + source[...]

    def plus_grid(target, source, first, second):
        @pl.loop(0, first * second)
        def _(n):
            at = (n // second, lax.rem(n, second))
            plus(target.at[at], source.at[at])

    def plus_row(target, source, first):
        @pl.loop(0, first)
        def _(n):
            plus(target.at[n], source.at[n])

    class Stream:
        def __init__(self, name, j, begin, size, r):
            cs = pl.ds(begin, size)
            self.second = [
                LineReduce(post, (name, "a"), "x", lines["x"], lambda i: mine_buf.at[j, cs, i, :, r, parts[0]],
                           lambda way, e: Inbox(in_a.at[j], ns)(way, e).at[cs, :, r], lambda t, s: plus_grid(t, s, size, ny)),
                LineReduce(post, (name, "b"), "y", lines["y"], lambda i: mine_buf.at[j, cs, :, i, r, parts[1]],
                           lambda way, e: Inbox(in_b.at[j], ny)(way, e).at[cs, :, r], lambda t, s: plus_grid(t, s, size, ns)),
            ]
            self.third = [
                LineReduce(post, (name, "c"), "y", lines["y"], lambda i: mine_buf.at[j, cs, x, i, r, parts[0]],
                           lambda way, e: Inbox(in_c.at[j], ny)(way, e).at[cs, r], lambda t, s: plus_row(t, s, size)),
                LineReduce(post, (name, "d"), "x", lines["x"], lambda i: mine_buf.at[j, cs, i, y, r, parts[1]],
                           lambda way, e: Inbox(in_d.at[j], ns)(way, e).at[cs, r], lambda t, s: plus_row(t, s, size)),
            ]

    def line_z(name, j, r):
        return LineReduce(post, ("z", name), "z", lines["z"], lambda i: mine_buf.at[j, i, x, y, r],
                          lambda way, e: in_z.at[j, (1 - way) // 2, e, r], plus)

    ffn = [Stream(("s", n), n // 2 + 1, 0, cols, rows_of(n)) for n in range(4)]
    ffn_z = [line_z(n, n // 2 + 1, rows_of(n)) for n in range(4)]
    attn = [Stream(("u", c), 0, c, 1, pl.ds(0, rb)) for c in range(cols)]

    def take_y(c, e):
        reduce_to(post, ("y", c), "z", lines["z"], c, e, mine_buf.at[0, c, x, y], lambda way, e: in_z.at[0, (1 - way) // 2, e], plus)

    def half_of(h):
        return pl.ds(h * (rows // 2), rows // 2)

    def line_tokens(m, h):
        at = half_of(h)
        return LineReduce(post, ("t", m, h), "z", lines["z"], lambda i: tok_buf.at[m, i, at],
                          lambda way, e: tok_in.at[m, (1 - way) // 2, e, at], plus, reach)

    tokens = [[line_tokens(m, h) for h in range(2)] for m in range(micro)]

    def start(*group):
        for line in group:
            line.start()

    def finish(*group):
        for line in group:
            line.finish()

    def core(n):
        planes[n].wait()
        r = rows_of(n)
        post.wait(("k", n), "k", 1 - k, core_buf.at[n // 2, :, :, :, r])

        @pl.loop(0, cols * ns * ny)
        def _(i):
            at = (i // (ns * ny), lax.rem(i // ny, ns), lax.rem(i, ny), r)
            plus(mine_buf.at[(n // 2 + 1, *at)], core_buf.at[(n // 2, *at)])

    def vector_start(stage, axis):
        mine, size = lines[axis]
        vec_buf[stage, 1 + mine] = vec_buf[stage, 0]
        for t in range(1, size):
            post.send(("v", stage, t), lambda t=t: (
                axis, lax.rem(mine + t, size), vec_buf.at[stage, 0], vec_buf.at[stage, 1 + mine], None))

    def vector_finish(stage, axis, out):
        mine, size = lines[axis]
        for t in range(1, size):
            origin = lax.rem(mine + size - t, size)
            post.wait(("v", stage, t), axis, origin, vec_buf.at[stage, 1 + origin])
        total = vec_buf[stage, 1]
        for i in range(1, size):
            total = total + vec_buf[stage, 1 + i]
        out[...] = total

    places = place_of(rows)
    small = vec_ref.shape[0]
    vec_buf[0, 0] = jnp.zeros_like(vec_buf[0, 0])
    vec_buf[0, 0, 0:small] = vec_ref[...]

    def unit(m, c):
        mixed_grad = jnp.dot(grad_ref[m], weights[c, :, O_AT : O_AT + WINDOW], preferred_element_type=floats).astype(halves)
        mixed_grad = jnp.where(places > 0, mixed_grad.astype(floats), 0.0)
        product = mixed_grad * mixed_buf[c, m].astype(floats)
        product_high = product.astype(halves)
        product_low = (product - product_high.astype(floats)).astype(halves)
        pick = (
            lax.broadcasted_iota(jnp.int32, (8, WINDOW), 1) // HEAD_DIM == lax.broadcasted_iota(jnp.int32, (8, WINDOW), 0) + 1
        ).astype(floats).astype(halves)
        inner = contract_cols(pick, product_high) + contract_cols(pick, product_low)
        value_side = pltpu.roll(mixed_grad, WINDOW - HEAD_DIM, 1).astype(halves)
        queries = q_buf[m, c]
        query_heads = jnp.concatenate([keep(queries, places, h + 1) for h in range(3)], 0)
        grad_heads = jnp.concatenate([keep(value_side, places, h) for h in range(3)], 0)
        side_by_side = lambda ref_rows: jnp.concatenate([ref_rows(h) for h in range(3)], 1)
        log_total = side_by_side(lambda h: lse_ref[m, c, h : h + 1])
        inner_row = side_by_side(lambda h: inner[h : h + 1])
        acc[...] = jnp.zeros_like(acc)
        key_weight = weights[c, :, K_AT : K_AT + WINDOW]
        value_weight = weights[c, :, V_AT : V_AT + WINDOW]

        def step(block, value_bias):
            keys = k_buf[m, c, block]
            values = v_buf[m, c, block]
            keys_t = keys.T
            hidden = mask[m, block].astype(floats)
            hidden = jnp.concatenate([hidden] * 3, 1)
            p = jnp.exp(contract_cols(keys, query_heads) + hidden - log_total)
            prob_grad = contract_cols(values, grad_heads)
            score_grad = (p * (prob_grad - inner_row)).astype(halves)
            value_grad = jnp.dot(p.astype(halves), grad_heads, preferred_element_type=floats)
            key_grad = jnp.dot(score_grad, query_heads, preferred_element_type=floats)
            for h in range(3):
                acc[pl.ds(h * HEAD_DIM, HEAD_DIM), :] += jnp.dot(
                    keys_t[(h + 1) * HEAD_DIM : (h + 2) * HEAD_DIM], score_grad[:, h * rows : (h + 1) * rows], preferred_element_type=floats)
            key_low, value_low = key_grad.astype(halves), value_grad.astype(halves)
            k_buf[m, c, block] = key_low
            v_buf[m, c, block] = value_low
            spread[m, block] += contract_cols(key_low, key_weight) + contract_cols(value_low, value_weight)
            return value_bias + jnp.sum(value_low.astype(floats), 0, keepdims=True)

        value_bias = jnp.zeros((1, WINDOW), floats)
        for block in range(cols):
            value_bias = step(block, value_bias)
        query_low = (acc[...].T * HEAD_DIM ** -0.5).astype(halves)
        q_buf[m, c] = query_low
        vec_buf[0, 0, pl.ds(small + c, 1), 0:WINDOW] += jnp.sum(query_low.astype(floats), 0, keepdims=True)
        vec_buf[0, 0, pl.ds(small + c, 1), WINDOW : 2 * WINDOW] += value_bias
        out_ref[back(m)] += contract_cols(query_low, weights[c, :, Q_AT : Q_AT + WINDOW])

    def send_tokens(m):
        out_ref[back(m)] += spread[m, z]

        @pl.loop(0, cols)
        def _(block):
            tok_buf[m, block] = spread[m, block].astype(halves)

        start(*tokens[m])

    def weight_grads(c):
        strip = block_sum.shape[0]

        @pl.loop(0, model // strip)
        def _(part):
            base = pl.multiple_of(part * strip, strip)
            side = pl.ds(base, strip)
            block_sum[...] = jnp.zeros_like(block_sum)
            for m in range(micro):
                mine_at = pl.ds(pl.multiple_of((m * cols + z) * rows, rows), rows)
                block_sum[:, Q_AT : Q_AT + WINDOW] += jnp.dot(every_t[side, mine_at], q_buf[m, c], preferred_element_type=floats)
                all_at = pl.ds(m * cols * rows, cols * rows)
                block_sum[:, K_AT : K_AT + WINDOW] += jnp.dot(
                    every_t[side, all_at], k_buf[m, c].reshape(-1, WINDOW), preferred_element_type=floats)
                block_sum[:, V_AT : V_AT + WINDOW] += jnp.dot(
                    every_t[side, all_at], v_buf[m, c].reshape(-1, WINDOW), preferred_element_type=floats)
                block_sum[:, O_AT : O_AT + WINDOW] += jnp.dot(
                    grad_t[side, m * rows : (m + 1) * rows], mixed_buf[c, m], preferred_element_type=floats)
            for i in range(strip // (2 * rb)):
                ours = pl.ds(pl.multiple_of((2 * i + k) * rb, 16), rb)
                theirs = pl.ds(pl.multiple_of((2 * i + 1 - k) * rb, 16), rb)
                chip = part * (strip // (2 * rb)) + i
                mine_buf[0, c, chip // ny, lax.rem(chip, ny)] = block_sum[ours].astype(halves)
                stage_buf[c, chip // ny, lax.rem(chip, ny)] = block_sum[theirs].astype(halves)

    waited = []

    def attn_give(c):
        if not waited:
            pl.semaphore_wait(free_sem, 1)
            waited.append(c)
        post.send(("g", c), lambda: ("k", 1 - k, stage_buf.at[c], core_buf.at[0, c], None))

    def attn_add(c):
        post.wait(("g", c), "k", 1 - k, core_buf.at[0, c])

        @pl.loop(0, ns * ny)
        def _(n):
            at = (c, n // ny, lax.rem(n, ny))
            plus(mine_buf.at[(0, *at)], core_buf.at[(0, *at)])

    streams = ffn + attn
    added = set()

    def take_core(n):
        if n < 4:
            core(n)
            added.add(n)
            if added >= {0, 1} and n in (0, 1):
                pl.semaphore_signal(free_sem, 1, device_id=device("k", 1 - k), device_id_type=MESH)
        else:
            attn_add(n - 4)
        start(*streams[n].second)

    def take_second(n):
        finish(*streams[n].second)
        start(*streams[n].third)

    def take_third(n):
        finish(*streams[n].third)
        if n < 4:
            start(ffn_z[n])

    def along(line, e):
        for way in (1, -1):
            line.take(way, e)
            if e:
                line.forward(way, e)

    def take_tokens(m, h, e):
        line = tokens[m][h]
        if e == 0:
            def add(target, source):
                out_ref[back(m, h * (rows // 2), rows // 2)] += source[...].astype(floats)

            line.add = add
        along(line, e)

    def vectors(stage):
        if stage:
            vector_finish(stage - 1, "kyxz"[stage - 1], vec_buf.at[stage, 0] if stage < 4 else sums_ref)
        if stage < 4:
            vector_start(stage, "kyxz"[stage])

    def load():
        for copy in loads:
            copy.wait()

    act = {
        "L": load, "G": lambda n: give(n) if n < 4 else attn_give(n - 4), "A": take_core, "B": take_second, "C": take_third,
        "Z": lambda n, e: along(ffn_z[n], e), "S": send_tokens, "T": take_tokens, "Y": take_y, "V": vectors,
    }
    head, tail, order = split_plan([("U", "W", task[1], 0) if task[0] == "W" else task for task in BACKWARD_PLAN])
    kinds = [item[0] == "W" for item in order]
    heads = [item[1] if item[0] == "W" else item[0] for item in order]
    micros = [0 if item[0] == "W" else item[1] for item in order]
    act[head[0][0]](*head[0][1:])
    spread[...] = jnp.zeros_like(spread)
    for m in range(micro):
        grad_t[:, m * rows : (m + 1) * rows] = grad_ref[m].T
    for task in head[1:]:
        act[task[0]](*task[1:])

    @pl.loop(0, len(order))
    def _(step):
        c, m, kind = pick(step, heads), pick(step, micros), pick(step, [int(k_) for k_ in kinds])

        @pl.when(kind == 0)
        def _():
            unit(m, c)

        @pl.when(kind == 1)
        def _():
            @pl.when(step == kinds.index(True))
            def _():
                for copy in late:
                    copy.wait()

            weight_grads(c)

        for i, tasks in enumerate(tail[:-1]):
            if tasks:
                @pl.when(step == i)
                def _(tasks=tasks):
                    for task in tasks:
                        act[task[0]](*task[1:])

    for task in tail[-1]:
        act[task[0]](*task[1:])
    for j in range(3):
        out_ref[pl.ds(back_rows + j * rb, rb)] = mine_buf[j, z, x, y].astype(floats)
    post.close()


def backward(sizes, grad, share, first, turned, mixed, lse, q, k, v, mask, part, vectors):
    ns, nr, nc = sizes
    ny = nr // 2
    micro, rows, model = grad.shape
    w = part.shape[-1]
    rb = model // (ns * nr)
    halves, floats = jnp.bfloat16, jnp.float32
    reach = min(nc - 1, -(-(DOC_MOST - 1) // rows))
    streams = 4 + nc
    count = 4 + nc + 4 * (ny - 1 + ns - 1) * streams + 4 * 2 * (nc - 1) + 2 * nc * 2 + micro * 4 * reach + (1 + ny - 1 + ns - 1 + nc - 1)
    widest = max(ns, ny, nc, 2)
    ways = lambda n: 1 if n == 2 else 2
    vec_shape = (vectors.shape[0] + nc + -nc % 8, model)
    vmem = pl.BlockSpec(memory_space=pltpu.VMEM)
    anywhere = pl.BlockSpec(memory_space=pl.ANY)
    buf = lambda *shape, kind=halves: pltpu.VMEM(shape, kind)
    total = micro * rows + 3 * rb + vec_shape[0]
    return pl.pallas_call(
        functools.partial(backward_kernel, sizes, micro),
        out_shape=jax.ShapeDtypeStruct((total, model), floats),
        in_specs=[vmem, anywhere, anywhere, anywhere, anywhere, vmem, anywhere, anywhere, anywhere, anywhere, anywhere, vmem],
        out_specs=vmem,
        scratch_shapes=[
            buf(3, nc, ns, ny, rb, w), buf(2, nc, ns, ny, rb, w), buf(nc, ns, ny, rb, w),
            buf(3, ways(ns), max(ns - 1, 1), nc, ny, rb, w // 2), buf(3, ways(ny), max(ny - 1, 1), nc, ns, rb, w // 2),
            buf(3, ways(ny), max(ny - 1, 1), nc, rb, w // 2), buf(3, ways(ns), max(ns - 1, 1), nc, rb, w // 2),
            buf(3, 2, max(nc - 1, 1), rb, w), buf(micro, nc, rows, model), buf(micro, 2, max(reach, 1), rows, model),
            buf(4, 1 + widest, *vec_shape, kind=floats),
            buf(nc, model, w), buf(nc, micro, rows, WINDOW), buf(micro, nc, rows, WINDOW),
            buf(micro, nc, nc, rows, WINDOW), buf(micro, nc, nc, rows, WINDOW),
            buf(model, micro * nc * rows), buf(model, micro * rows),
            buf(micro, nc, rows, rows), buf(WINDOW, rows, kind=floats), buf(micro, nc, rows, model, kind=floats), buf(model // 2, w, kind=floats),
            pltpu.SemaphoreType.DMA((count,)), pltpu.SemaphoreType.DMA((count,)), pltpu.SemaphoreType.DMA((24,)), pltpu.SemaphoreType.REGULAR,
        ],
        compiler_params=pltpu.CompilerParams(collective_id=3, has_side_effects=True, vmem_limit_bytes=62 << 20),
        name="backward",
    )(grad, share.reshape(micro * rows, model), first, turned, mixed, lse, q, k, v, mask,
      part.reshape(2, nc, ns, ny, 2, rb, w), vectors)


def per_device_plain(sizes, inputs, segment_ids, query_weight, key_weight, value_weight, query_bias, value_bias,
               output_weight, output_bias, first_gain, first_shift, hidden_weight, hidden_bias, down_weight,
               down_bias, second_gain, second_shift, cotangent):
    floats, halves = jnp.float32, jnp.bfloat16
    cols = sizes[2]
    micro, _, rows, model = inputs.shape
    length = segment_ids.shape[-1]
    width = query_weight.shape[1]
    here = lax.axis_index("col")
    own = inputs[:, 0]
    shard = jnp.stack([
        jnp.concatenate([query_weight, key_weight, value_weight, output_weight.T], 1),
        hidden_weight,
        down_weight.T,
    ])
    biases = lax.all_gather(jnp.concatenate([query_bias, value_bias, hidden_bias]), "col", axis=0)
    everything, gathered = gather(sizes, own, shard)
    everything = everything.reshape(micro, length, model)
    attn_weights = gathered[0]
    wq, wk, wv, wot = (attn_weights[:, :, i * width : (i + 1) * width] for i in range(4))
    hidden_full, down_full = gathered[1], gathered[2]
    bq, bv, bh = biases[:, :width], biases[:, width : 2 * width], biases[:, 2 * width :]
    seg_all = segment_ids[:, 0]
    seg_own = lax.dynamic_slice_in_dim(seg_all, here * rows, rows, 1)
    first_key = jnp.sum((seg_all < seg_own[:, :1]).astype(jnp.int32), 1)
    last_key = jnp.sum((seg_all <= seg_own[:, -1:]).astype(jnp.int32), 1)
    bounds = jnp.stack([first_key // KEY_BLOCK, (last_key + KEY_BLOCK - 1) // KEY_BLOCK], 1)

    mixed, lse, q, k, v = attend(bounds, own, everything, wq, wk, wv, bq.astype(floats), bv.astype(floats), seg_own, seg_all)
    total = micro * rows
    flat = lambda a: a.reshape(total, -1)
    mixed_flat = mixed.reshape(cols, total, width)
    attn = sum(contract_cols(mixed_flat[c], wot[c]) for c in range(cols))
    first_sum = flat(own).astype(floats) + attn + output_bias.astype(floats)
    normal_one, scale_one = norm_parts(first_sum)
    gain_one = first_gain.astype(floats)
    normed = normal_one * gain_one + first_shift.astype(floats)
    normed_low = normed.astype(halves)
    ffn = 0
    activated, slopes = [], []
    for c in range(cols):
        hidden = jnp.dot(normed_low, hidden_full[c], preferred_element_type=floats) + bh[c].astype(floats)
        half_erf = 0.5 * lax.erf(hidden * 0.7071067811865476) + 0.5
        act = (hidden * half_erf).astype(halves)
        slope = half_erf + hidden * (jnp.exp(-0.5 * hidden * hidden) * 0.3989422804014327)
        activated.append(act)
        slopes.append(slope.astype(halves))
        ffn = ffn + contract_cols(act, down_full[c])
    second_sum = normed + ffn + down_bias.astype(floats)
    normal_two, scale_two = norm_parts(second_sum)
    gain_two = second_gain.astype(floats)
    outputs = (normal_two * gain_two + second_shift.astype(floats)).astype(halves)
    cot = flat(cotangent[:, 0]).astype(floats)
    second_grad = norm_back(cot * gain_two, normal_two, scale_two)
    ffn_grad = second_grad.astype(halves)
    hidden_grads, down_grads, hidden_bias_grads = [], [], []
    normed_grad = second_grad
    for c in range(cols):
        pre = (jnp.dot(ffn_grad, down_full[c], preferred_element_type=floats) * slopes[c].astype(floats)).astype(halves)
        hidden_grads.append(contract_rows(normed_low, pre).astype(halves))
        down_grads.append(contract_rows(ffn_grad, activated[c]).astype(halves))
        hidden_bias_grads.append(jnp.sum(pre.astype(floats), 0))
        normed_grad = normed_grad + contract_cols(pre, hidden_full[c])
    first_grad = norm_back(normed_grad * gain_one, normal_one, scale_one)
    attn_grad = first_grad.astype(halves)
    dq, dk, dv = attend_back(bounds, attn_grad.reshape(micro, rows, model), wot, mixed, lse, q, k, v, seg_own, seg_all)
    every_flat = everything.reshape(micro * length, model)
    attn_grads = []
    own_share = first_grad
    spread = 0
    for c in range(cols):
        dq_c, dk_c, dv_c = dq[c].reshape(total, width), dk[c].reshape(micro * length, width), dv[c].reshape(micro * length, width)
        attn_grads.append(jnp.concatenate([
            contract_rows(flat(own), dq_c), contract_rows(every_flat, dk_c), contract_rows(every_flat, dv_c),
            contract_rows(attn_grad, mixed_flat[c]),
        ], 1).astype(halves))
        own_share = own_share + contract_cols(dq_c, wq[c])
        spread = spread + contract_cols(dk_c, wk[c]) + contract_cols(dv_c, wv[c])
    bias_q = jnp.sum(dq.astype(floats), (1, 2)).reshape(-1)
    bias_v = jnp.sum(dv.astype(floats), (1, 2)).reshape(-1)
    vectors = jnp.concatenate([
        jnp.sum(first_grad, 0), jnp.sum(normed_grad * normal_one, 0), jnp.sum(normed_grad, 0), jnp.sum(second_grad, 0),
        jnp.sum(cot * normal_two, 0), jnp.sum(cot, 0), bias_q, bias_v, *hidden_bias_grads,
    ]).reshape(-1, model)
    partial = jnp.stack([jnp.stack(attn_grads), jnp.stack(hidden_grads), jnp.stack(down_grads)])
    input_grad, reduced, sums = reduce(sizes, own_share.reshape(micro, rows, model),
                                       spread.astype(halves).reshape(micro, cols, rows, model), partial, vectors)
    attn_block = reduced[0]
    piece = lambda i: attn_block[:, i * width : (i + 1) * width]
    mine = lambda vector, size: lax.dynamic_slice_in_dim(vector.reshape(-1), here * size, size, 0)
    return (
        outputs.reshape(micro, 1, rows, model), input_grad[:, None],
        piece(0), piece(1), piece(2), mine(sums[6], width), mine(sums[7], width), piece(3).T,
        sums[0], sums[1], sums[2], reduced[1], mine(sums[8:], hidden_bias.shape[0]), reduced[2].T,
        sums[3], sums[4], sums[5],
    )


def deliver_kernel(sizes, width, results, *refs):
    *outs, back_ref, block_ref, sums_ref, sems = refs
    micro, rows, _ = back_ref.shape
    rb = block_ref.shape[1]
    at = micro * rows
    pieces = [(results.at[pl.ds(at + j * rb, rb)], block_ref.at[j]) for j in range(3)]
    pieces += [(results.at[pl.ds(at + 3 * rb, sums_ref.shape[0])], sums_ref)]
    pieces += [(results.at[pl.ds(m * rows, rows)], back_ref.at[m]) for m in range(micro)]
    copies = [
        pltpu.make_async_copy(source, target, sems.at[i])
        for i, (source, target) in enumerate(pieces)
    ]
    for copy in copies:
        copy.start()
    (input_grad, query, key, value, query_bias, value_bias, output, output_bias, first_gain, first_shift, hidden, hidden_bias, down,
     down_bias, second_gain, second_shift) = outs
    here = lax.axis_index("col")
    for copy in copies[:4]:
        copy.wait()
    for i, ref in enumerate((query, key, value)):
        ref[...] = block_ref[0, :, i * width : (i + 1) * width]
    output[...] = block_ref[0, :, 3 * width : 4 * width].T
    hidden[...] = block_ref[1]
    down[...] = block_ref[2]
    for i, ref in enumerate((output_bias, first_gain, first_shift, down_bias, second_gain, second_shift)):
        ref[...] = sums_ref[i : i + 1].reshape(-1)
    hidden_bias[...] = sums_ref[pl.ds(8 + here, 1)].reshape(-1)
    heads_at = sums_ref.shape[0] - (sizes[2] + -sizes[2] % 8)
    row = sums_ref[pl.ds(heads_at + here, 1)]
    query_bias[...] = row[:, 0:width].reshape(-1)
    value_bias[...] = row[:, WINDOW : WINDOW + width].reshape(-1)
    for copy in copies[4:]:
        copy.wait()
    input_grad[...] = back_ref[...]


def deliver(sizes, width, tokens_shape, block_shape, results):
    micro, rows, model = tokens_shape
    rb, w = block_shape
    sums_rows = results.shape[0] - micro * rows - 3 * rb
    vmem = pl.BlockSpec(memory_space=pltpu.VMEM)
    square, vector = (rb, width), (model,)
    shapes = [tokens_shape, square, square, square, (width,), (width,), (width, rb), vector, vector, vector, (rb, w), (w,), (rb, w),
              vector, vector, vector]
    return pl.pallas_call(
        functools.partial(deliver_kernel, sizes, width),
        out_shape=[jax.ShapeDtypeStruct(shape, jnp.float32) for shape in shapes],
        in_specs=[pl.BlockSpec(memory_space=pltpu.MemorySpace.HBM)],
        out_specs=[vmem] * len(shapes),
        scratch_shapes=[pltpu.VMEM(a, jnp.float32) for a in (tokens_shape, (3, rb, w), (sums_rows, model))] + [pltpu.SemaphoreType.DMA((4 + micro,))],
        compiler_params=pltpu.CompilerParams(vmem_limit_bytes=32 << 20),
        name="deliver",
    )(results)


def per_device_fused(sizes, inputs, segment_ids, query_weight, key_weight, value_weight, query_bias, value_bias,
               output_weight, output_bias, first_gain, first_shift, hidden_weight, hidden_bias, down_weight,
               down_bias, second_gain, second_shift, cotangent):
    floats, halves = jnp.float32, jnp.bfloat16
    cols = sizes[2]
    micro, _, rows, model = inputs.shape
    length = segment_ids.shape[-1]
    width = query_weight.shape[1]
    here = lax.axis_index("col")
    own = inputs[:, 0]
    rest, first, turned, mask, biases, mixed, lse, q, k, v = forward(
        sizes, own, (query_weight, key_weight, value_weight, output_weight, hidden_weight, down_weight.T), hidden_bias, query_bias, value_bias, segment_ids)
    first = first.reshape(cols, model, 4 * width)
    total = micro * rows
    flat = lambda a: a.reshape(total, -1)
    outputs, first_grad, attn_grad, part, sums = middle(
        flat(own), mixed.reshape(cols, total, WINDOW), first, rest.reshape(2, cols, model, -1), biases,
        (output_bias, first_gain, first_shift, down_bias, second_gain, second_shift), flat(cotangent[:, 0]))
    parted = lambda a: a.reshape(micro, rows, model)
    results = backward(sizes, parted(attn_grad), parted(first_grad), first, turned, mixed, lse, q, k, v,
                                         mask, part, sums)
    grads = deliver(sizes, width, own.shape, hidden_weight.shape, results)
    return (outputs.reshape(micro, 1, rows, model), grads[0][:, None], *grads[1:12], grads[12].T, *grads[13:])


def per_device(sizes, inputs, segment_ids, query_weight, *rest):
    micro, _, rows, _ = inputs.shape
    fits = (query_weight.shape == (query_weight.shape[0] // 32 * 32, 3 * HEAD_DIM) and micro == 2 and sizes[2] == 4
            and DOC_MOST // 2 == rows)
    return (per_device_fused if fits else per_device_plain)(sizes, inputs, segment_ids, query_weight, *rest)


def solution(mesh):
    sizes = tuple(mesh.shape[name] for name in ("seq", "row", "col"))
    block, line = P(("seq", "row"), "col"), P("col", ("seq", "row"))
    tokens = P(None, ("seq", "row"), "col", None)
    placed = (tokens, P(None, ("seq", "row"), None), block, block, block, P("col"), P("col"), line, P(), P(), P(),
              block, P("col"), line, P(), P(), P(), tokens)
    given = (tokens, tokens, block, block, block, P("col"), P("col"), line, P(), P(), P(), block, P("col"), line,
             P(), P(), P())
    return jax.shard_map(functools.partial(per_device, sizes), mesh=mesh, in_specs=placed, out_specs=given, check_vma=False)
```
